128 devices in a mesh: ep: 64 (over z, x, y), tp: 2 (over core).
Axes of the slice: x: 4, y: 4, z: 4, core: 2. Of those that a mesh axis runs over, the one named last changes fastest.
Arguments:
- residual_in: bfloat16 [16384, 2048], P(('ep', 'tp')), may hold values from -24 to 24
- routes: int32 [16384, 8], P('ep'), may hold values from 0 to 63, all different within a row
- segment_ids: int32 [64, 256], P('ep'), may hold values from 0 to 3, never falling along the last dimension, each value on 1 to 128 neighbouring positions
- gain_attn: float32 [2048], replicated, may hold values from 0.5 to 1.5
- w_query: bfloat16 [2048, 2048], P(None, 'tp'), may hold values from -0.125 to 0.125
- w_key: bfloat16 [2048, 2048], P(None, 'tp'), may hold values from -0.125 to 0.125
- w_value: bfloat16 [2048, 2048], P(None, 'tp'), may hold values from -0.125 to 0.125
- gain_query: float32 [16, 128], P('tp'), may hold values from 0.5 to 1.5
- gain_key: float32 [16, 128], P('tp'), may hold values from 0.5 to 1.5
- w_out: bfloat16 [2048, 2048], P('tp'), may hold values from -1 to 1
- gain_moe: float32 [2048], replicated, may hold values from 0.5 to 1.5
- w_router: bfloat16 [2048, 64], replicated, may hold values from -0.25 to 0.25
- w_gate: bfloat16 [64, 2048, 1024], P('ep', None, 'tp'), may hold values from -0.125 to 0.125
- w_up: bfloat16 [64, 2048, 1024], P('ep', None, 'tp'), may hold values from -0.125 to 0.125
- w_down: bfloat16 [64, 1024, 2048], P('ep', 'tp'), may hold values from -1.5 to 1.5
- cotangent: bfloat16 [16384, 2048], P(('ep', 'tp')), may hold values from -24 to 24
Outputs:
- output: bfloat16 [16384, 2048], P(('ep', 'tp'))
- grad_input: float32 [16384, 2048], P(('ep', 'tp'))
- grad_gain_attn: float32 [2048], P(('ep', 'tp'))
- grad_w_query: float32 [2048, 2048], P('ep', 'tp')
- grad_w_key: float32 [2048, 2048], P('ep', 'tp')
- grad_w_value: float32 [2048, 2048], P('ep', 'tp')
- grad_gain_query: float32 [16, 128], P('tp', 'ep')
- grad_gain_key: float32 [16, 128], P('tp', 'ep')
- grad_w_out: float32 [2048, 2048], P('tp', 'ep')
- grad_gain_moe: float32 [2048], P(('ep', 'tp'))
- grad_w_router: float32 [2048, 64], P(('ep', 'tp'))
- grad_w_gate: float32 [64, 2048, 1024], P('ep', None, 'tp')
- grad_w_up: float32 [64, 2048, 1024], P('ep', None, 'tp')
- grad_w_down: float32 [64, 1024, 2048], P('ep', 'tp')
- counts: int32 [64], P('ep')
The draws below stay inside these ranges and needn't reach their ends.
Inputs may be any that keep to these rules, and one draw needn't show every extreme that they name: `routes`: each token names 8 different experts. `segment_ids`: ids never fall along a row; every row holds 4 documents of at most 128 tokens, one of exactly that many.
All inputs are finite; a program needn't handle non-finite values.
Results may differ from the reference program's by a relative error of at most 0.02.
Values may be sent and summed in bfloat16 or wider, within the bound.
No kernel may reach another device: no remote copies, remote signals or barrier semaphores. Data moves between devices by JAX's collectives and lax.ppermute only.
A program may use at most 256 MiB of HBM per device.

```python
import math
import jax
import jax.numpy as jnp
import numpy as np
from jax import lax

D = 2048
H = 16
HD = 128
FF = 1024
TOPK = 8
SEQ = 256
DOCS = 4
HH = 2048
EXPERTS = 64
TOKENS = 16384
CAP = 32
N_EP = 64
N_TP = 2


def spiked(values, stream_key, source, target, shards_of, factor):
    owner, partner = [(jnp.arange(values.shape[position]) // (values.shape[position] // shards_of)).reshape([-1 if axis == position else 1 for axis in range(values.ndim)]) for position in (source, target)]
    chosen = jax.random.permutation(stream_key, shards_of)[partner]
    strong = (owner == chosen) | (owner == (partner + shards_of // 2) % shards_of)
    return jnp.where(strong, factor * values, values)


def levels(rng, shape, pieces, low, top_value):
    def one(position, shards_of):
        draws = jax.random.uniform(jax.random.fold_in(jax.random.fold_in(rng, 6), position), (shards_of,), jnp.float32, low / len(pieces), top_value / len(pieces))
        return jnp.repeat(jnp.exp(draws), shape[position] // shards_of).reshape((-1,) + (1,) * (len(shape) - position - 1))

    factor_of = one(*pieces[0])
    for cut in pieces[1:]:
        factor_of = factor_of * one(*cut)
    return factor_of


def distinct(rng, rows, number_of, top, lift):
    order = jax.random.permutation(jax.random.fold_in(rng, 1), number_of)
    pull = order
    for power in range(3):
        pull = pull * pull // number_of
    pull = pull * lift // number_of
    tickets = jax.random.randint(jax.random.fold_in(rng, 2), (rows, number_of), 0, 4096) + pull
    sure = jax.random.permutation(jax.random.fold_in(rng, 3), rows)[jnp.arange(number_of) % rows]
    tickets = jnp.where(jnp.arange(rows)[:, None] == sure[None, :], 1 << 14, tickets)
    merit = tickets * number_of + jnp.arange(number_of)
    return lax.top_k(merit.astype(jnp.int32), top)[1].astype(jnp.int32)


def split_up(amount, total, bound, lean):
    weights = [(1 << 20) // math.isqrt(standing ** lean) + 1 for standing in range(2, amount + 1)]
    spare, holding = total - bound - (amount - 1), [1] * (amount - 1)
    while spare > 0:
        movable = [i for i in range(amount - 1) if holding[i] < bound]
        whole, budget = sum([weights[i] for i in movable]), spare
        for i in movable:
            addition = min(bound - holding[i], max(1, budget * weights[i] // whole), spare)
            holding[i] = holding[i] + addition
            spare = spare - addition
    return np.array([bound] + holding)


def uneven_parts(stream_key, count, total, limit, skew):
    if count == 2:
        one = jax.random.randint(stream_key, (), max(1, total - limit), min(limit, total - 1) + 1)
        return jnp.stack([one, total - one])
    sizes = jnp.asarray(split_up(count, total, limit, skew), jnp.int32)
    pairs = (count - 1) // 2
    donor, sink = sizes[1:1 + 2 * pairs:2], sizes[2:2 + 2 * pairs:2]
    slack = jnp.minimum(donor - 1, limit - sink)
    passed = jax.random.randint(jax.random.fold_in(stream_key, 1), (pairs,), 0, 1 << 20) % (slack + 1)
    sizes = sizes.at[1:1 + 2 * pairs:2].set(donor - passed).at[2:2 + 2 * pairs:2].set(sink + passed)
    return sizes[jax.random.permutation(jax.random.fold_in(stream_key, 2), count)]


def scatter_about(own_key, extent, scale, reach, cuts=(), kind=jnp.bfloat16):
    entries = jax.random.normal(own_key, extent, jnp.float32) * scale
    if len(cuts) > 0:
        entries = levels(own_key, extent, cuts, -0.22, 0.18) * entries
    return jnp.clip(entries, min=-reach, max=reach).astype(kind)


def heavy_noise(rng, extent, spread, reach, split, heavy, kind=jnp.bfloat16):
    result = spread * jax.random.normal(rng, extent, jnp.float32)
    if split:
        result = result * levels(rng, extent, split, -0.22, 0.18)
    return jnp.clip(spiked(result, jax.random.fold_in(rng, 3), *heavy), -reach, reach).astype(kind)


def setup_inputs(seed: int = 0) -> dict:
    key_list = jax.random.split(jax.random.key(seed), 17)
    return {
        "residual_in": heavy_noise(key_list[0], (TOKENS, D), 1.0, 24.0, ((0, 128),), (0, 1, 128, 5.5)),
        "routes": distinct(key_list[1], TOKENS, EXPERTS, TOPK, 1024),
        "segment_ids": jax.vmap(lambda own: jnp.searchsorted(jnp.cumsum(uneven_parts(own, DOCS, SEQ, SEQ // 2, 1)), jnp.arange(SEQ), side="right"))(jax.random.split(key_list[2], N_EP)).reshape((N_EP, SEQ)).astype(jnp.int32),
        "gain_attn": jnp.clip(1.0 + 0.1 * jax.random.normal(key_list[3], (D,), jnp.float32), 0.5, 1.5),
        "w_query": scatter_about(key_list[4], (D, HH), D ** -0.5, 0.125, ((1, 2),)),
        "w_key": scatter_about(key_list[5], (D, HH), D ** -0.5, 0.125, ((1, 2),)),
        "w_value": scatter_about(key_list[6], (D, HH), D ** -0.5, 0.125, ((1, 2),)),
        "gain_query": jnp.clip(1.0 + 0.1 * jax.random.normal(key_list[7], (H, HD), jnp.float32), 0.5, 1.5),
        "gain_key": jnp.clip(1.0 + 0.1 * jax.random.normal(key_list[8], (H, HD), jnp.float32), 0.5, 1.5),
        "w_out": scatter_about(key_list[9], (HH, D), (HH // 64) ** -0.5, 1.0, ((0, 2),)),
        "gain_moe": jnp.clip(1.0 + 0.1 * jax.random.normal(key_list[10], (D,), jnp.float32), 0.5, 1.5),
        "w_router": scatter_about(key_list[11], (D, EXPERTS), (D // 4) ** -0.5, 0.25),
        "w_gate": scatter_about(key_list[12], (EXPERTS, D, FF), D ** -0.5, 0.125, ((0, 64), (2, 2))),
        "w_up": scatter_about(key_list[13], (EXPERTS, D, FF), D ** -0.5, 0.125, ((0, 64), (2, 2))),
        "w_down": scatter_about(key_list[14], (EXPERTS, FF, D), (FF // 64) ** -0.5, 1.5, ((0, 64), (1, 2))),
        "cotangent": heavy_noise(key_list[15], (TOKENS, D), 1.0, 24.0, ((0, 128),), (0, 1, 128, 5.5)),
    }


norm_eps = 1e-05
rope_base = 10000.0
mask_fill = -1e+30

@jax.custom_vjp
def low(v):
    return lax.optimization_barrier(v.astype(jnp.bfloat16)).astype(jnp.float32)

@jax.custom_vjp
def low_back(v):
    return v

def low_keep(v):
    return (low(v), None)

def low_pass(kept, grad):
    return (grad,)

def back_keep(v):
    return (v, None)

def back_low(kept, grad):
    return (low(grad),)
low.defvjp(low_keep, low_pass)
low_back.defvjp(back_keep, back_low)

def highest_dot(left, right):
    return jnp.dot(left, right, precision=lax.Precision.HIGHEST, preferred_element_type=jnp.float32)

def rms_scale(values):
    return lax.rsqrt(lax.optimization_barrier(jnp.mean(values * values, axis=-1, keepdims=True)) + norm_eps)

def positions_of(segment_row):
    places = jnp.arange(segment_row.shape[0], dtype=jnp.int32)
    fresh = jnp.concatenate([jnp.ones((1,), dtype=jnp.bool_), segment_row[1:] != segment_row[:-1]])
    starts = jnp.where(fresh, places, jnp.zeros_like(places))
    return places - lax.cummax(starts, axis=0)

def rope_angles(positions, head_dim):
    half_dim = head_dim // 2
    exponent = jnp.arange(half_dim, dtype=jnp.float32) * (2.0 / head_dim)
    inverse = jnp.power(jnp.float32(rope_base), -exponent)
    angles = positions.astype(jnp.float32)[:, None] * inverse[None, :]
    return (jnp.cos(angles), jnp.sin(angles))

def rotate(values, cosine, sine):
    half_dim = values.shape[-1] // 2
    first_half = values[..., :half_dim]
    second_half = values[..., half_dim:]
    cos_b = cosine[:, None, :]
    sin_b = sine[:, None, :]
    return jnp.concatenate([first_half * cos_b - second_half * sin_b, second_half * cos_b + first_half * sin_b], axis=-1)

def slot_tables(route_row):
    seq_len, top_count = route_row.shape
    route_hits = (route_row[:, :, None] == jnp.arange(EXPERTS, dtype=jnp.int32)[None, None, :]).astype(jnp.int32)
    per_token = lax.optimization_barrier(jnp.sum(route_hits, axis=1))
    earlier = jnp.cumsum(per_token, axis=0) - per_token
    rank_ids = lax.optimization_barrier(jnp.sum(route_hits * earlier[:, None, :], axis=2))
    kept_pair = rank_ids < CAP
    slot_ids = jnp.where(kept_pair, route_row * CAP + rank_ids, EXPERTS * CAP).astype(jnp.int32)
    owners = jnp.repeat(jnp.arange(seq_len, dtype=jnp.int32), top_count)
    slot_token = jnp.full((EXPERTS * CAP + 1,), seq_len, dtype=jnp.int32).at[slot_ids.reshape(-1)].set(owners)
    return (slot_ids, kept_pair, slot_token[:EXPERTS * CAP], lax.optimization_barrier(jnp.sum(per_token, axis=0)))

def layer_row(row_items, params):
    x_row, seg_row, route_row, slot_ids, kept_pair, slot_token = row_items
    gain_attn, w_query, w_key, w_value, gain_query, gain_key, w_out, gain_moe, w_router, w_gate, w_up, w_down = params
    seq_len = x_row.shape[0]
    places = jnp.arange(seq_len, dtype=jnp.int32)
    cosine, sine = rope_angles(positions_of(seg_row), HD)
    normed = low(x_row * rms_scale(x_row) * gain_attn)
    queries = low_back(highest_dot(normed, w_query))
    key_proj = low_back(highest_dot(normed, w_key))
    values = low(low_back(highest_dot(normed, w_value)))
    q_normed = queries * rms_scale(queries) * gain_query.reshape(-1)
    k_normed = key_proj * rms_scale(key_proj) * gain_key.reshape(-1)
    q_rot = low(rotate(q_normed.reshape(seq_len, H, HD), cosine, sine))
    k_rot = low(rotate(k_normed.reshape(seq_len, H, HD), cosine, sine))
    scores = jnp.einsum('qhd,khd->hqk', q_rot, k_rot, precision=lax.Precision.HIGHEST) * HD ** (-0.5)
    scores = low_back(scores)
    allowed = (seg_row[:, None] == seg_row[None, :]) & (places[None, :] <= places[:, None])
    scores = jnp.where(allowed[None], scores, mask_fill)
    probs = jax.nn.softmax(scores, axis=-1)
    mixed = jnp.einsum('hqk,khd->qhd', low(probs), values.reshape(seq_len, H, HD), precision=lax.Precision.HIGHEST)
    mixed = low(low_back(mixed.reshape(seq_len, HH)))
    branch = low_back(highest_dot(mixed, w_out))
    hidden_row = x_row + branch
    normed_moe = low(hidden_row * rms_scale(hidden_row) * gain_moe)
    router_probs = jax.nn.softmax(highest_dot(normed_moe, w_router), axis=-1)
    pair_weight = jnp.take_along_axis(router_probs, route_row, axis=1) * kept_pair.astype(jnp.float32)
    padded = jnp.concatenate([normed_moe, jnp.zeros((1, D), jnp.float32)], axis=0)
    slot_inputs = padded[slot_token].reshape(EXPERTS, CAP, D)
    expert_out = jnp.zeros((EXPERTS, CAP, D), jnp.float32)
    part_width = FF // N_TP
    for part_index in range(N_TP):
        lower_col = part_index * part_width
        part_inputs = low_back(slot_inputs)
        gate_act = low_back(jnp.einsum('ecd,edf->ecf', part_inputs, w_gate[:, :, lower_col:lower_col + part_width], precision=lax.Precision.HIGHEST))
        up_act = low_back(jnp.einsum('ecd,edf->ecf', part_inputs, w_up[:, :, lower_col:lower_col + part_width], precision=lax.Precision.HIGHEST))
        inner_act = low(jax.nn.silu(gate_act) * up_act)
        part_out = jnp.einsum('ecf,efd->ecd', inner_act, w_down[:, lower_col:lower_col + part_width, :], precision=lax.Precision.HIGHEST)
        expert_out = expert_out + low(low_back(part_out))
    out_rows = jnp.concatenate([expert_out.reshape(EXPERTS * CAP, D), jnp.zeros((1, D), jnp.float32)], axis=0)
    picked = out_rows[slot_ids]
    moe = jnp.einsum('sk,skd->sd', pair_weight, picked, precision=lax.Precision.HIGHEST)
    return hidden_row + moe

def reference(residual_in, routes, segment_ids, gain_attn, w_query, w_key, w_value, gain_query, gain_key, w_out, gain_moe, w_router, w_gate, w_up, w_down, cotangent):
    route_rows = routes.reshape(N_EP, SEQ, TOPK)
    slot_ids, kept_pair, slot_token, route_counts = jax.vmap(slot_tables)(route_rows)
    weights_in = tuple((weight_arg.astype(jnp.float32) for weight_arg in (gain_attn, w_query, w_key, w_value, gain_query, gain_key, w_out, gain_moe, w_router, w_gate, w_up, w_down)))

    def whole_layer(inputs_float, *params):

        def one_row(row_items):
            return layer_row(row_items, params)
        rows_out = lax.map(jax.checkpoint(one_row), (inputs_float.reshape(N_EP, SEQ, D), segment_ids, route_rows, slot_ids, kept_pair, slot_token))
        return rows_out.reshape(TOKENS, D)
    output, pullback = jax.vjp(whole_layer, residual_in.astype(jnp.float32), *weights_in)
    gradients = pullback(cotangent.astype(jnp.float32))
    counts = lax.optimization_barrier(jnp.sum(route_counts, axis=0)).astype(jnp.int32)
    return (output.astype(jnp.bfloat16), gradients[0], gradients[1], gradients[2], gradients[3], gradients[4], gradients[5], gradients[6], gradients[7], gradients[8], gradients[9], gradients[10], gradients[11], gradients[12], counts)
```

```python
import jax
import jax.numpy as jnp
from jax import lax
from jax.sharding import Mesh, PartitionSpec as P

norm_eps = 1e-05
rope_base = 10000.0
mask_fill = -1e30
bf16 = jnp.bfloat16
f32 = jnp.float32
rows_of_chips = ("z", "x", "y")


def swap(value):
    return lax.ppermute(value, "tp", [(0, 1), (1, 0)])


def dot(left, right):
    return lax.dot_general(left, right, (((1,), (0,)), ((), ())), preferred_element_type=f32)


def dot_rows(left, right):
    return lax.dot_general(left, right, (((0,), (0,)), ((), ())), preferred_element_type=f32)


def dot_cols(left, right):
    return lax.dot_general(left, right, (((1,), (1,)), ((), ())), preferred_element_type=f32)


def all_to_all(value, axes):
    return lax.all_to_all(value, axes, split_axis=0, concat_axis=0, tiled=True)


def rms_scale(values):
    return lax.rsqrt(jnp.mean(values * values, axis=-1, keepdims=True) + norm_eps)


def halves(value):
    high = value.astype(bf16)
    return high, (value - high.astype(f32)).astype(bf16)


def rope_angles(positions, head_dim):
    half_dim = head_dim // 2
    exponent = jnp.arange(half_dim, dtype=f32) * (2.0 / head_dim)
    inverse = jnp.power(f32(rope_base), -exponent)
    angles = positions.astype(f32)[:, None] * inverse[None, :]
    return jnp.cos(angles), jnp.sin(angles)


def rotate(values, cosine, sine):
    half_dim = values.shape[-1] // 2
    first_half = values[..., :half_dim]
    second_half = values[..., half_dim:]
    cos_b = cosine[:, None, :]
    sin_b = sine[:, None, :]
    return jnp.concatenate(
        [first_half * cos_b - second_half * sin_b, second_half * cos_b + first_half * sin_b],
        axis=-1,
    )


def local(
    residual_in,
    routes,
    segment_ids,
    gain_attn,
    w_query,
    w_key,
    w_value,
    gain_query,
    gain_key,
    w_out,
    gain_moe,
    w_router,
    w_gate,
    w_up,
    w_down,
    cotangent,
):
    core = lax.axis_index("tp")
    planes = lax.axis_size("z")
    chips = lax.axis_size(rows_of_chips)
    chip = lax.axis_index(rows_of_chips)
    own_rows, width = residual_in.shape
    seq_len, top_count = routes.shape
    local_width = w_query.shape[1]
    local_heads, head_dim = gain_query.shape
    full_width = 2 * local_width
    experts = chips
    capacity = seq_len * top_count // experts
    own_slots = capacity // 2
    score_scale = head_dim ** (-0.5)
    quarter = local_width // planes
    out_rows = width // chips

    def own_first(value):
        return jnp.where(
            core == 0, value, jnp.concatenate([value[own_rows:], value[:own_rows]], axis=0)
        )

    def other_order(value):
        return jnp.concatenate([value[own_rows:], value[:own_rows]], axis=0)

    place = own_first(jnp.arange(seq_len, dtype=jnp.int32))
    seg = own_first(segment_ids[0])
    route = own_first(routes)
    same_doc = seg[:, None] == seg[None, :]
    position = place - jnp.min(jnp.where(same_doc, place[None, :], seq_len), axis=1)
    cosine, sine = rope_angles(position, head_dim)
    allowed = same_doc & (place[None, :] <= place[:, None])

    hits = jnp.any(
        route[:, :, None] == jnp.arange(experts, dtype=jnp.int32)[None, None, :], axis=1
    )
    before = (place[None, :] < place[:, None]).astype(bf16)
    rank = dot(before, hits.astype(bf16)).astype(jnp.int32)
    rank = jnp.where(hits, rank, -1)
    counts = jnp.sum(hits.astype(f32), axis=0)
    slot_number = core * own_slots + jnp.arange(own_slots, dtype=jnp.int32)
    pick = (rank.T[:, None, :] == slot_number[None, :, None]).astype(bf16)
    pick = pick.reshape(experts * own_slots, seq_len)

    cot = jnp.concatenate([cotangent, swap(cotangent)], axis=0)
    cot_slots = dot(pick, cot).astype(bf16).reshape(experts, own_slots, width)
    cot_arrived = all_to_all(cot_slots, rows_of_chips).reshape(experts * own_slots, width)

    whole_in = jnp.concatenate([residual_in, swap(residual_in)], axis=0).astype(f32)
    scale_attn = rms_scale(whole_in)
    normed = (whole_in * scale_attn * gain_attn).astype(bf16)
    normed_own = normed[:own_rows]
    normed_planes = lax.all_gather(normed_own, "z", axis=0, tiled=False)
    normed_planes = jnp.concatenate([normed_planes, swap(normed_planes)], axis=1).reshape(
        planes * seq_len, width
    )
    queries = dot(normed, w_query)
    key_proj = dot(normed, w_key)
    values = dot(normed, w_value).astype(bf16)
    squares = jnp.stack([jnp.sum(queries * queries, axis=1), jnp.sum(key_proj * key_proj, axis=1)])
    squares = squares + other_order(swap(squares).T).T
    query_scale = lax.rsqrt(squares[0] / full_width + norm_eps)[:, None]
    key_scale = lax.rsqrt(squares[1] / full_width + norm_eps)[:, None]
    query_gain = gain_query.reshape(-1)
    key_gain = gain_key.reshape(-1)
    heads = (seq_len, local_heads, head_dim)
    q_rot = rotate((queries * query_scale * query_gain).reshape(heads), cosine, sine).astype(bf16)
    k_rot = rotate((key_proj * key_scale * key_gain).reshape(heads), cosine, sine).astype(bf16)
    v_heads = values.reshape(heads)
    scores = jnp.einsum("qhd,khd->hqk", q_rot, k_rot, preferred_element_type=f32) * score_scale
    scores = jnp.where(allowed[None], scores, mask_fill)
    grown = jnp.exp(scores - jnp.max(scores, axis=-1, keepdims=True))
    probs = grown / jnp.sum(grown, axis=-1, keepdims=True)
    probs_low = probs.astype(bf16)
    mixed = (
        jnp.einsum("hqk,khd->qhd", probs_low, v_heads, preferred_element_type=f32)
        .reshape(seq_len, local_width)
        .astype(bf16)
    )
    mixed_planes = all_to_all(
        jnp.stack([mixed[:, k * quarter : (k + 1) * quarter] for k in range(planes)]), "z"
    ).reshape(planes * seq_len, quarter)
    branch = dot(mixed, w_out)
    branch = branch + other_order(swap(branch))
    hidden = whole_in + branch
    scale_moe = rms_scale(hidden)
    normed_moe = (hidden * scale_moe * gain_moe).astype(bf16)

    moe_slots = dot(pick, normed_moe).astype(bf16).reshape(experts, own_slots, width)
    arrived = all_to_all(moe_slots, rows_of_chips).reshape(experts * own_slots, width)
    router_probs = jax.nn.softmax(dot(normed_moe, w_router), axis=-1)

    gate_parts = (w_gate[0], swap(w_gate[0]))
    up_parts = (w_up[0], swap(w_up[0]))
    down_parts = (w_down[0], swap(w_down[0]))
    slot_probs = jax.nn.softmax(dot(arrived, w_router), axis=-1)
    own_expert = jnp.arange(experts, dtype=jnp.int32) == chip
    slot_weight = jnp.sum(jnp.where(own_expert[None, :], slot_probs, 0.0), axis=1, keepdims=True)
    slot_grad = (slot_weight * cot_arrived.astype(f32)).astype(bf16)
    saved = []
    slot_out = None
    for w_g, w_u, w_d in zip(gate_parts, up_parts, down_parts):
        gate_act = dot(arrived, w_g)
        up_act = dot(arrived, w_u)
        sigmoid_gate = jax.nn.sigmoid(gate_act)
        silu_gate = gate_act * sigmoid_gate
        inner_act = (silu_gate * up_act).astype(bf16)
        part_out = dot(inner_act, w_d)
        slot_out = part_out if slot_out is None else slot_out + part_out
        saved.append((gate_act, up_act, sigmoid_gate, silu_gate, inner_act))
    returned = all_to_all(
        slot_out.astype(bf16).reshape(experts, own_slots, width), rows_of_chips
    ).reshape(experts * own_slots, width)
    part_grads = []
    slot_in_grad = None
    for (gate_act, up_act, sigmoid_gate, silu_gate, inner_act), w_g, w_u, w_d in zip(
        saved, gate_parts, up_parts, down_parts
    ):
        inner_grad = dot_cols(slot_grad, w_d)
        up_grad = (inner_grad * silu_gate).astype(bf16)
        gate_grad = (
            inner_grad * up_act * sigmoid_gate * (1.0 + gate_act * (1.0 - sigmoid_gate))
        ).astype(bf16)
        part_in = dot_cols(gate_grad, w_g) + dot_cols(up_grad, w_u)
        slot_in_grad = part_in if slot_in_grad is None else slot_in_grad + part_in
        part_grads.append((inner_act, gate_grad, up_grad))
    grads_back = all_to_all(
        slot_in_grad.astype(bf16).reshape(experts, own_slots, width), rows_of_chips
    ).reshape(experts * own_slots, width)
    (inner_own, gate_own, up_own), (inner_other, gate_other, up_other) = part_grads
    grad_w_gate = dot_rows(arrived, gate_own) + swap(
        dot_rows(arrived, gate_other).astype(bf16)
    ).astype(f32)
    grad_w_up = dot_rows(arrived, up_own) + swap(dot_rows(arrived, up_other).astype(bf16)).astype(
        f32
    )
    grad_w_down = dot_rows(inner_own, slot_grad) + swap(
        dot_rows(inner_other, slot_grad).astype(bf16)
    ).astype(f32)

    pick_pairs = pick.reshape(experts, own_slots, seq_len)
    weighted = pick_pairs.astype(f32) * router_probs.T[:, None, :]
    weight_high, weight_low = halves(weighted.reshape(experts * own_slots, seq_len))
    moe_part = dot_rows(weight_high, returned) + dot_rows(weight_low, returned)
    moe_own = moe_part[:own_rows] + swap(moe_part[own_rows:].astype(bf16)).astype(f32)
    output = (hidden[:own_rows] + moe_own).astype(bf16)
    pair_products = dot_cols(returned, cot).reshape(experts, own_slots, seq_len)
    prob_part = jnp.sum(pair_products * pick_pairs.astype(f32), axis=1).T
    prob_grad = prob_part + other_order(swap(prob_part))
    logit_grad = router_probs * (
        prob_grad - jnp.sum(router_probs * prob_grad, axis=1, keepdims=True)
    )
    logit_high, logit_low = halves(logit_grad)
    router_grad = dot_rows(normed_moe, logit_high) + dot_rows(normed_moe, logit_low)
    moe_in_part = dot_rows(pick, grads_back)
    moe_in_grad = (
        moe_in_part[:own_rows]
        + swap(moe_in_part[own_rows:])
        + dot_cols(logit_high[:own_rows], w_router)
        + dot_cols(logit_low[:own_rows], w_router)
    )
    cot_own = cotangent.astype(f32)
    hidden_own = hidden[:own_rows]
    scale_own = scale_moe[:own_rows]
    weighted_moe = moe_in_grad * gain_moe
    hidden_grad = (
        cot_own
        + scale_own * weighted_moe
        - hidden_own * scale_own**3 * jnp.mean(hidden_own * weighted_moe, axis=1, keepdims=True)
    )
    gain_moe_grad = jnp.sum(hidden_own * scale_own * moe_in_grad, axis=0)
    hidden_low_own = hidden_grad.astype(bf16)
    hidden_low = jnp.concatenate([hidden_low_own, swap(hidden_low_own)], axis=0)

    low_planes = lax.all_gather(hidden_low_own, "z", axis=0, tiled=False)
    low_planes = jnp.concatenate([low_planes, swap(low_planes)], axis=1).reshape(
        planes * seq_len, width
    )

    def for_cores(vector):
        pieces = vector.reshape(chips, 2, -1)
        mine = jnp.where(core == 0, pieces[:, 0], pieces[:, 1])
        others = jnp.where(core == 0, pieces[:, 1], pieces[:, 0])
        return mine + swap(others)

    lanes = 128

    def lane_blocks(matrix):
        pieces = matrix.reshape(chips, -1, matrix.shape[1])
        return [
            pieces[:, :, k * lanes : (k + 1) * lanes] for k in range(matrix.shape[1] // lanes)
        ]

    def small_rows(values):
        high, low = halves(jnp.pad(values, ((0, 0), (0, lanes - values.shape[1]))))
        return jnp.pad(jnp.stack([high, low], axis=1), ((0, 0), (0, 14), (0, 0)))

    out_grad = dot_rows(low_planes, mixed_planes).astype(bf16)
    router_pieces = router_grad.reshape(chips, 2, out_rows // 2, experts)
    router_mine = jnp.where(core == 0, router_pieces[:, 0], router_pieces[:, 1])
    router_mine = router_mine.reshape(chips, -1, lanes).astype(bf16)
    router_len = router_mine.shape[1]
    first_small = small_rows(
        jnp.concatenate([for_cores(gain_moe_grad), counts[:, None]], axis=1)
    )
    first_parcel = jnp.concatenate(lane_blocks(out_grad) + [router_mine, first_small], axis=1)
    first_sums = all_to_all(first_parcel, rows_of_chips).astype(f32)
    first_sums = jnp.sum(
        first_sums.reshape((planes, chips // planes) + first_sums.shape[1:]), axis=1
    )

    grad_mixed = dot_cols(hidden_low, w_out).astype(bf16).reshape(heads)
    grad_probs = jnp.einsum("qhd,khd->hqk", grad_mixed, v_heads, preferred_element_type=f32)
    grad_scores = (
        probs * (grad_probs - jnp.sum(probs * grad_probs, axis=-1, keepdims=True))
    ).astype(bf16)
    grad_q_rot = (
        jnp.einsum("hqk,khd->qhd", grad_scores, k_rot, preferred_element_type=f32) * score_scale
    )
    grad_k_rot = (
        jnp.einsum("hqk,qhd->khd", grad_scores, q_rot, preferred_element_type=f32) * score_scale
    )
    value_grad = (
        jnp.einsum("hqk,qhd->khd", probs_low, grad_mixed, preferred_element_type=f32)
        .reshape(seq_len, local_width)
        .astype(bf16)
    )
    grad_q_normed = rotate(grad_q_rot, cosine, -sine).reshape(seq_len, local_width)
    grad_k_normed = rotate(grad_k_rot, cosine, -sine).reshape(seq_len, local_width)
    gain_query_grad = jnp.sum(queries * query_scale * grad_q_normed, axis=0)
    gain_key_grad = jnp.sum(key_proj * key_scale * grad_k_normed, axis=0)
    weighted_query = grad_q_normed * query_gain
    weighted_key = grad_k_normed * key_gain
    inner = jnp.stack(
        [jnp.sum(queries * weighted_query, axis=1), jnp.sum(key_proj * weighted_key, axis=1)]
    )
    inner = (inner + other_order(swap(inner).T).T) / full_width
    query_grad = (
        query_scale * weighted_query - queries * query_scale**3 * inner[0][:, None]
    ).astype(bf16)
    key_grad = (
        key_scale * weighted_key - key_proj * key_scale**3 * inner[1][:, None]
    ).astype(bf16)

    to_planes = jnp.stack(
        [
            jnp.concatenate(
                [g[:, k * quarter : (k + 1) * quarter] for g in (query_grad, key_grad, value_grad)],
                axis=1,
            )
            for k in range(planes)
        ]
    )
    grads_planes = all_to_all(to_planes, "z").reshape(planes * seq_len, 3 * quarter)
    in_grads = dot_rows(normed_planes, grads_planes).astype(bf16)
    normed_grad = (
        dot_cols(query_grad, w_query) + dot_cols(key_grad, w_key) + dot_cols(value_grad, w_value)
    )
    normed_grad = normed_grad[:own_rows] + swap(normed_grad[own_rows:])
    in_own = whole_in[:own_rows]
    in_scale = scale_attn[:own_rows]
    weighted_attn = normed_grad * gain_attn
    grad_input = (
        hidden_grad
        + in_scale * weighted_attn
        - in_own * in_scale**3 * jnp.mean(in_own * weighted_attn, axis=1, keepdims=True)
    )
    gain_attn_grad = jnp.sum(in_own * in_scale * normed_grad, axis=0)

    def by_lane(vector):
        pieces = vector.reshape(local_heads, chips, head_dim // chips)
        return jnp.swapaxes(pieces, 0, 1).reshape(chips, -1)

    last_small = small_rows(
        jnp.concatenate(
            [for_cores(gain_attn_grad), by_lane(gain_query_grad), by_lane(gain_key_grad)], axis=1
        )
    )
    last_parcel = jnp.concatenate(lane_blocks(in_grads) + [last_small], axis=1)
    last_sums = all_to_all(last_parcel, rows_of_chips).astype(f32)
    last_sums = jnp.sum(last_sums.reshape((planes, chips // planes) + last_sums.shape[1:]), axis=1)

    def matrix_of(blocks):
        pieces = blocks.reshape(planes, -1, out_rows, lanes)
        return jnp.transpose(pieces, (2, 0, 1, 3)).reshape(out_rows, -1)

    block_len = quarter // lanes * out_rows
    grad_w_query, grad_w_key, grad_w_value = (
        matrix_of(last_sums[:, k * block_len : (k + 1) * block_len]) for k in range(3)
    )
    grad_w_out = matrix_of(first_sums[:, :block_len]).T
    grad_w_router = jnp.sum(first_sums[:, block_len : block_len + router_len], axis=0).reshape(
        out_rows // 2, experts
    )
    first_tail = jnp.sum(first_sums[:, block_len + router_len :], axis=0)
    first_tail = first_tail[0] + first_tail[1]
    last_tail = jnp.sum(last_sums[:, 3 * block_len :], axis=0)
    last_tail = last_tail[0] + last_tail[1]
    own_gain = out_rows // 2
    own_lanes = local_heads * head_dim // chips
    lane_shape = (local_heads, head_dim // chips)
    return (
        output,
        grad_input,
        last_tail[:own_gain],
        grad_w_query,
        grad_w_key,
        grad_w_value,
        last_tail[own_gain : own_gain + own_lanes].reshape(lane_shape),
        last_tail[own_gain + own_lanes : own_gain + 2 * own_lanes].reshape(lane_shape),
        grad_w_out,
        first_tail[:own_gain],
        grad_w_router,
        grad_w_gate[None],
        grad_w_up[None],
        grad_w_down[None],
        first_tail[own_gain : own_gain + 1].astype(jnp.int32),
    )


def solution(mesh):
    side = round(mesh.shape["ep"] ** (1 / 3))
    cube = Mesh(mesh.devices.reshape(side, side, side, 2), rows_of_chips + ("tp",))
    ep = rows_of_chips
    both = rows_of_chips + ("tp",)
    in_specs = (
        P(both, None),
        P(ep, None),
        P(ep, None),
        P(),
        P(None, "tp"),
        P(None, "tp"),
        P(None, "tp"),
        P("tp", None),
        P("tp", None),
        P("tp", None),
        P(),
        P(),
        P(ep, None, "tp"),
        P(ep, None, "tp"),
        P(ep, "tp", None),
        P(both, None),
    )
    out_specs = (
        P(both, None),
        P(both, None),
        P(both),
        P(ep, "tp"),
        P(ep, "tp"),
        P(ep, "tp"),
        P("tp", ep),
        P("tp", ep),
        P("tp", ep),
        P(both),
        P(both, None),
        P(ep, None, "tp"),
        P(ep, None, "tp"),
        P(ep, "tp", None),
        P(ep),
    )
    return jax.shard_map(local, mesh=cube, in_specs=in_specs, out_specs=out_specs, check_vma=False)
```

```python
import jax
import jax.numpy as jnp
from jax import lax
from jax.experimental import pallas as pl
from jax.experimental.pallas import tpu as pltpu
from jax.sharding import Mesh, PartitionSpec as P

norm_eps = 1e-05
rope_base = 10000.0
mask_fill = -1e30
bf16 = jnp.bfloat16
f32 = jnp.float32
rows_of_chips = ("z", "x", "y")


def swap(value):
    return lax.ppermute(value, "tp", [(0, 1), (1, 0)])


def dot(left, right):
    return lax.dot_general(left, right, (((1,), (0,)), ((), ())), preferred_element_type=f32)


def dot_rows(left, right):
    return lax.dot_general(left, right, (((0,), (0,)), ((), ())), preferred_element_type=f32)


def dot_cols(left, right):
    return lax.dot_general(left, right, (((1,), (1,)), ((), ())), preferred_element_type=f32)


def all_to_all(value, axes):
    return lax.all_to_all(value, axes, split_axis=0, concat_axis=0, tiled=True)


def rms_scale(values):
    return lax.rsqrt(jnp.mean(values * values, axis=-1, keepdims=True) + norm_eps)


def halves(value):
    high = value.astype(bf16)
    return high, (value - high.astype(f32)).astype(bf16)


def rope_angles(positions, head_dim):
    half_dim = head_dim // 2
    exponent = jnp.arange(half_dim, dtype=f32) * (2.0 / head_dim)
    inverse = jnp.power(f32(rope_base), -exponent)
    angles = positions.astype(f32)[:, None] * inverse[None, :]
    return jnp.cos(angles), jnp.sin(angles)


lanes = 128
vmem_bytes = 56 * 1024 * 1024
cheap = 64


def params():
    return pltpu.CompilerParams(vmem_limit_bytes=vmem_bytes)


def turn(value, cosine, sine):
    return value * cosine + pltpu.roll(value, value.shape[1] // 2, 1) * sine


def attention_forward_body(
    scale,
    query_ref,
    key_ref,
    value_ref,
    query_gain_ref,
    key_gain_ref,
    query_scale_ref,
    key_scale_ref,
    cosine_ref,
    sine_ref,
    bias_ref,
    q_rot_ref,
    k_rot_ref,
    probs_ref,
    mixed_ref,
):
    cosine, sine = cosine_ref[...], sine_ref[...]
    query = query_ref[...] * query_scale_ref[...] * query_gain_ref[...]
    key = key_ref[...] * key_scale_ref[...] * key_gain_ref[...]
    q_rot = turn(query, cosine, sine).astype(bf16)
    k_rot = turn(key, cosine, sine).astype(bf16)
    q_rot_ref[...] = q_rot
    k_rot_ref[...] = k_rot
    scores = dot_cols(q_rot, k_rot) * scale + bias_ref[...]
    grown = jnp.exp(scores - jnp.max(scores, axis=1, keepdims=True))
    probs = grown / jnp.sum(grown, axis=1, keepdims=True)
    probs_ref[...] = probs
    mixed_ref[...] = dot(probs.astype(bf16), value_ref[...]).astype(bf16)


def attention_forward(
    queries, keys, values, query_gain, key_gain, query_scale, key_scale, cosine, sine, bias, heads
):
    seq_len, width = queries.shape
    head = width // heads
    column = pl.BlockSpec((seq_len, head), lambda h: (0, h))
    gain = pl.BlockSpec((1, head), lambda h: (0, h))

    def whole(array):
        return pl.BlockSpec(array.shape, lambda h: (0, 0))

    return pl.pallas_call(
        lambda *refs: attention_forward_body(head**-0.5, *refs),
        grid=(heads,),
        in_specs=[column, column, column, gain, gain]
        + [whole(a) for a in (query_scale, key_scale, cosine, sine, bias)],
        out_specs=[
            column,
            column,
            pl.BlockSpec((None, seq_len, seq_len), lambda h: (h, 0, 0)),
            column,
        ],
        out_shape=[
            jax.ShapeDtypeStruct((seq_len, width), bf16),
            jax.ShapeDtypeStruct((seq_len, width), bf16),
            jax.ShapeDtypeStruct((heads, seq_len, seq_len), f32),
            jax.ShapeDtypeStruct((seq_len, width), bf16),
        ],
        compiler_params=params(),
        cost_estimate=pl.CostEstimate(
            flops=4 * seq_len * seq_len * width,
            transcendentals=heads * seq_len * seq_len,
            bytes_accessed=seq_len * width * 16 + heads * seq_len * seq_len * 4,
        ),
        name="attention_forward",
    )(queries, keys, values, query_gain, key_gain, query_scale, key_scale, cosine, sine, bias)


def attention_backward_body(
    scale,
    hidden_ref,
    w_out_ref,
    value_ref,
    q_rot_ref,
    k_rot_ref,
    probs_ref,
    query_ref,
    key_ref,
    query_gain_ref,
    key_gain_ref,
    query_scale_ref,
    key_scale_ref,
    cosine_ref,
    sine_ref,
    value_grad_ref,
    query_part_ref,
    key_part_ref,
    query_gain_grad_ref,
    key_gain_grad_ref,
    query_inner_ref,
    key_inner_ref,
):
    cosine, sine = cosine_ref[...], sine_ref[...]
    grad_mixed = dot_cols(hidden_ref[...], w_out_ref[...]).astype(bf16)
    probs = probs_ref[...]
    grad_probs = dot_cols(grad_mixed, value_ref[...])
    inner = jnp.sum(probs * grad_probs, axis=1, keepdims=True)
    grad_scores = (probs * (grad_probs - inner)).astype(bf16)
    value_grad_ref[...] = dot_rows(probs.astype(bf16), grad_mixed).astype(bf16)
    first = pl.program_id(0) == 0
    for grad_rot, raw_ref, gain_ref, scale_ref, part_ref, gain_grad_ref, inner_ref in (
        (
            dot(grad_scores, k_rot_ref[...]),
            query_ref,
            query_gain_ref,
            query_scale_ref,
            query_part_ref,
            query_gain_grad_ref,
            query_inner_ref,
        ),
        (
            dot_rows(grad_scores, q_rot_ref[...]),
            key_ref,
            key_gain_ref,
            key_scale_ref,
            key_part_ref,
            key_gain_grad_ref,
            key_inner_ref,
        ),
    ):
        grad_normed = turn(grad_rot * scale, cosine, -sine)
        raw = raw_ref[...]
        gain_grad_ref[...] = jnp.sum(raw * scale_ref[...] * grad_normed, axis=0, keepdims=True)
        weighted = grad_normed * gain_ref[...]
        part_ref[...] = weighted
        row_inner = jnp.sum(raw * weighted, axis=1, keepdims=True)

        @pl.when(first)
        def _():
            inner_ref[...] = row_inner

        @pl.when(jnp.logical_not(first))
        def _():
            inner_ref[...] += row_inner


def attention_backward(
    hidden_low,
    w_out,
    values,
    q_rot,
    k_rot,
    probs,
    queries,
    keys,
    query_gain,
    key_gain,
    query_scale,
    key_scale,
    cosine,
    sine,
    heads,
):
    seq_len, width = queries.shape
    head = width // heads
    column = pl.BlockSpec((seq_len, head), lambda h: (0, h))
    gain = pl.BlockSpec((1, head), lambda h: (0, h))

    def whole(array):
        return pl.BlockSpec(array.shape, lambda h: (0, 0))

    full = jax.ShapeDtypeStruct((seq_len, width), f32)
    line = jax.ShapeDtypeStruct((1, width), f32)
    sums = jax.ShapeDtypeStruct((seq_len, 1), f32)
    return pl.pallas_call(
        lambda *refs: attention_backward_body(head**-0.5, *refs),
        grid=(heads,),
        in_specs=[
            whole(hidden_low),
            pl.BlockSpec((head, w_out.shape[1]), lambda h: (h, 0)),
            column,
            column,
            column,
            pl.BlockSpec((None, seq_len, seq_len), lambda h: (h, 0, 0)),
            column,
            column,
            gain,
            gain,
        ]
        + [whole(a) for a in (query_scale, key_scale, cosine, sine)],
        out_specs=[column, column, column, gain, gain, whole(sums), whole(sums)],
        out_shape=[
            jax.ShapeDtypeStruct((seq_len, width), bf16),
            full,
            full,
            line,
            line,
            sums,
            sums,
        ],
        compiler_params=params(),
        cost_estimate=pl.CostEstimate(
            flops=10 * seq_len * seq_len * width + 2 * seq_len * width * w_out.shape[1],
            transcendentals=0,
            bytes_accessed=seq_len * width * 28
            + heads * seq_len * seq_len * 4
            + 2 * w_out.size
            + 2 * hidden_low.size,
        ),
        name="attention_backward",
    )(
        hidden_low,
        w_out,
        values,
        q_rot,
        k_rot,
        probs,
        queries,
        keys,
        query_gain,
        key_gain,
        query_scale,
        key_scale,
        cosine,
        sine,
    )


def projection_grads_body(
    query_part_ref,
    key_part_ref,
    query_ref,
    key_ref,
    value_grad_ref,
    query_scale_ref,
    key_scale_ref,
    query_inner_ref,
    key_inner_ref,
    query_grad_ref,
    key_grad_ref,
    stack_ref,
):
    size = query_ref.shape[1]
    for k, (part_ref, raw_ref, scale_ref, inner_ref, grad_ref) in enumerate(
        (
            (query_part_ref, query_ref, query_scale_ref, query_inner_ref, query_grad_ref),
            (key_part_ref, key_ref, key_scale_ref, key_inner_ref, key_grad_ref),
        )
    ):
        scale = scale_ref[...]
        grad = scale * part_ref[...] - raw_ref[...] * (scale * scale * scale * inner_ref[...])
        grad = grad.astype(bf16)
        grad_ref[...] = grad
        stack_ref[:, k * size : (k + 1) * size] = grad
    stack_ref[:, 2 * size :] = value_grad_ref[...]


def projection_grads(
    query_part, key_part, queries, keys, value_grad, query_scale, key_scale, inners, planes
):
    seq_len, width = queries.shape
    size = width // planes
    column = pl.BlockSpec((seq_len, size), lambda k: (0, k))
    sums = pl.BlockSpec((seq_len, 1), lambda k: (0, 0))
    grads = jax.ShapeDtypeStruct((seq_len, width), bf16)
    return pl.pallas_call(
        projection_grads_body,
        grid=(planes,),
        in_specs=[column] * 5 + [sums] * 4,
        out_specs=[
            column,
            column,
            pl.BlockSpec((None, seq_len, 3 * size), lambda k: (k, 0, 0)),
        ],
        out_shape=[grads, grads, jax.ShapeDtypeStruct((planes, seq_len, 3 * size), bf16)],
        compiler_params=params(),
        cost_estimate=pl.CostEstimate(
            flops=10 * seq_len * width, transcendentals=0, bytes_accessed=28 * seq_len * width
        ),
        name="projection_grads",
    )(query_part, key_part, queries, keys, value_grad, query_scale, key_scale, *inners)


def expert_forward_body(
    rows_ref,
    gate_own_ref,
    gate_other_ref,
    up_own_ref,
    up_other_ref,
    down_own_ref,
    down_other_ref,
    gate_act_own_ref,
    gate_act_other_ref,
    up_act_own_ref,
    up_act_other_ref,
    out_ref,
    total_ref,
):
    step = pl.program_id(0)
    last = pl.num_programs(0) - 1
    count = rows_ref.shape[0]
    size = min(256, count)
    for start in range(0, count, size):
        here = pl.ds(start, size)
        rows = rows_ref[here, :]
        total = None
        for gate_ref, up_ref, down_ref, gate_act_ref, up_act_ref in (
            (gate_own_ref, up_own_ref, down_own_ref, gate_act_own_ref, up_act_own_ref),
            (gate_other_ref, up_other_ref, down_other_ref, gate_act_other_ref, up_act_other_ref),
        ):
            gate = dot(rows, gate_ref[...])
            up = dot(rows, up_ref[...])
            gate_act_ref[here, :] = gate
            up_act_ref[here, :] = up
            inner = (gate * jax.nn.sigmoid(gate) * up).astype(bf16)
            part = dot(inner, down_ref[...])
            total = part if total is None else total + part

        @pl.when(step == 0)
        def _():
            total_ref[here, :] = total

        @pl.when((step > 0) & (step < last))
        def _():
            total_ref[here, :] += total

        @pl.when(step == last)
        def _():
            out_ref[here, :] = (total_ref[here, :] + total).astype(bf16)


def expert_forward(rows, gates, ups, downs):
    count, width = rows.shape
    units = gates[0].shape[1]
    steps = 2
    size = units // steps
    into = pl.BlockSpec((width, size), lambda k: (0, k))
    back = pl.BlockSpec((size, width), lambda k: (k, 0))
    acts = pl.BlockSpec((count, size), lambda k: (0, k))
    act = jax.ShapeDtypeStruct((count, units), f32)
    whole = pl.BlockSpec((count, width), lambda k: (0, 0))
    return pl.pallas_call(
        expert_forward_body,
        grid=(steps,),
        in_specs=[whole] + [into] * 4 + [back] * 2,
        out_specs=[acts] * 4 + [whole],
        out_shape=[act] * 4 + [jax.ShapeDtypeStruct((count, width), bf16)],
        scratch_shapes=[pltpu.VMEM((count, width), f32)],
        compiler_params=params(),
        cost_estimate=pl.CostEstimate(
            flops=12 * count * width * units,
            transcendentals=2 * count * units,
            bytes_accessed=count * width * 4 + 12 * width * units + 16 * count * units,
        ),
        name="expert_forward",
    )(rows, *gates, *ups, *downs)


def weight_parcel_body(left_ref, right_ref, extra_ref, out_ref):
    chips, height, _ = out_ref.shape
    product = dot_rows(left_ref[...], right_ref[...]).astype(bf16)
    rows = product.shape[0] // chips
    blocks = product.shape[1] // lanes
    for k in range(blocks):
        piece = product[:, k * lanes : (k + 1) * lanes].reshape(chips, rows, lanes)
        out_ref[:, k * rows : (k + 1) * rows, :] = piece
    out_ref[:, blocks * rows :, :] = extra_ref[...]


def weight_parcel(left, right, extra, steps):
    chips, extra_rows, _ = extra.shape
    tokens, width = left.shape
    columns = right.shape[1]
    rows = width // chips
    height = rows * (columns // lanes) + extra_rows
    return pl.pallas_call(
        weight_parcel_body,
        grid=(steps,),
        in_specs=[
            pl.BlockSpec((tokens, width // steps), lambda k: (0, k)),
            pl.BlockSpec((tokens, columns), lambda k: (0, 0)),
            pl.BlockSpec((chips // steps, extra_rows, lanes), lambda k: (k, 0, 0)),
        ],
        out_specs=pl.BlockSpec((chips // steps, height, lanes), lambda k: (k, 0, 0)),
        out_shape=jax.ShapeDtypeStruct((chips, height, lanes), bf16),
        compiler_params=params(),
        cost_estimate=pl.CostEstimate(
            flops=2 * tokens * width * columns,
            transcendentals=0,
            bytes_accessed=2 * (left.size + right.size + chips * height * lanes),
        ),
        name="weight_parcel",
    )(left, right, extra)


def expert_weight_grads_body(rows_ref, slot_grad_ref, inner_ref, gate_ref, up_ref, *refs):
    grads = (
        dot_rows(rows_ref[...], gate_ref[...]),
        dot_rows(rows_ref[...], up_ref[...]),
        dot_rows(inner_ref[...], slot_grad_ref[...]),
    )
    others, outs = refs[:-3], refs[-3:]
    for k, (grad, out_ref) in enumerate(zip(grads, outs)):
        if others:
            grad = grad + others[k][...].astype(f32)
        out_ref[...] = grad.astype(out_ref.dtype)


def expert_weight_grads(rows, slot_grad, inner, gate_grad, up_grad, others, kind):
    count, width = rows.shape
    units = inner.shape[1]
    steps = 4
    size = width // steps
    wide = pl.BlockSpec((count, size), lambda k: (0, k))
    narrow = pl.BlockSpec((count, units), lambda k: (0, 0))
    into = pl.BlockSpec((size, units), lambda k: (k, 0))
    back = pl.BlockSpec((units, size), lambda k: (0, k))
    return pl.pallas_call(
        expert_weight_grads_body,
        grid=(steps,),
        in_specs=[wide, wide, narrow, narrow, narrow] + [into, into, back][: len(others)],
        out_specs=[into, into, back],
        out_shape=[
            jax.ShapeDtypeStruct((width, units), kind),
            jax.ShapeDtypeStruct((width, units), kind),
            jax.ShapeDtypeStruct((units, width), kind),
        ],
        compiler_params=params(),
        cost_estimate=pl.CostEstimate(
            flops=6 * count * width * units // cheap,
            transcendentals=0,
            bytes_accessed=4 * count * width // cheap,
        ),
        name="expert_weight_grads",
    )(rows, slot_grad, inner, gate_grad, up_grad, *others)


def normed_grad_body(*refs):
    *pairs, out_ref = refs
    total = None
    for grad_ref, w_ref in zip(pairs[:3], pairs[3:]):
        part = dot_cols(grad_ref[...], w_ref[...])
        total = part if total is None else total + part
    first = pl.program_id(0) == 0

    @pl.when(first)
    def _():
        out_ref[...] = total

    @pl.when(jnp.logical_not(first))
    def _():
        out_ref[...] += total


def normed_grad_of(grads, weights, steps):
    seq_len, width = grads[0].shape
    size = width // steps
    full = weights[0].shape[0]
    return pl.pallas_call(
        normed_grad_body,
        grid=(steps,),
        in_specs=[pl.BlockSpec((seq_len, size), lambda k: (0, k))] * 3
        + [pl.BlockSpec((full, size), lambda k: (0, k))] * 3,
        out_specs=pl.BlockSpec((seq_len, full), lambda k: (0, 0)),
        out_shape=jax.ShapeDtypeStruct((seq_len, full), f32),
        compiler_params=params(),
        cost_estimate=pl.CostEstimate(
            flops=6 * seq_len * width * full // cheap,
            transcendentals=0,
            bytes_accessed=6 * width * full // cheap,
        ),
        name="normed_grad",
    )(*grads, *weights)


def local(
    residual_in,
    routes,
    segment_ids,
    gain_attn,
    w_query,
    w_key,
    w_value,
    gain_query,
    gain_key,
    w_out,
    gain_moe,
    w_router,
    w_gate,
    w_up,
    w_down,
    cotangent,
):
    core = lax.axis_index("tp")
    planes = lax.axis_size("z")
    chips = lax.axis_size(rows_of_chips)
    chip = lax.axis_index(rows_of_chips)
    own_rows, width = residual_in.shape
    seq_len, top_count = routes.shape
    local_width = w_query.shape[1]
    local_heads, head_dim = gain_query.shape
    full_width = 2 * local_width
    experts = chips
    capacity = seq_len * top_count // experts
    own_slots = capacity // 2
    score_scale = head_dim ** (-0.5)
    quarter = local_width // planes
    out_rows = width // chips

    def own_first(value):
        return jnp.where(
            core == 0, value, jnp.concatenate([value[own_rows:], value[:own_rows]], axis=0)
        )

    def other_order(value):
        return jnp.concatenate([value[own_rows:], value[:own_rows]], axis=0)

    place = own_first(jnp.arange(seq_len, dtype=jnp.int32))
    seg = own_first(segment_ids[0])
    route = own_first(routes)
    same_doc = seg[:, None] == seg[None, :]
    position = place - jnp.min(jnp.where(same_doc, place[None, :], seq_len), axis=1)
    cosine, sine = rope_angles(position, head_dim)
    cosine = jnp.concatenate([cosine, cosine], axis=1)
    sine = jnp.concatenate([-sine, sine], axis=1)
    bias = jnp.where(same_doc & (place[None, :] <= place[:, None]), 0.0, mask_fill)

    hits = jnp.any(
        route[:, :, None] == jnp.arange(experts, dtype=jnp.int32)[None, None, :], axis=1
    )
    before = (place[None, :] < place[:, None]).astype(bf16)
    rank = dot(before, hits.astype(bf16)).astype(jnp.int32)
    rank = jnp.where(hits, rank, -1)
    counts = jnp.sum(hits.astype(f32), axis=0)
    slot_number = core * own_slots + jnp.arange(own_slots, dtype=jnp.int32)
    pick = (rank.T[:, None, :] == slot_number[None, :, None]).astype(bf16)
    pick = pick.reshape(experts * own_slots, seq_len)

    cot = jnp.concatenate([cotangent, swap(cotangent)], axis=0)
    cot_slots = dot(pick, cot).astype(bf16).reshape(experts, own_slots, width)
    cot_arrived = all_to_all(cot_slots, rows_of_chips).reshape(experts * own_slots, width)

    whole_in = jnp.concatenate([residual_in, swap(residual_in)], axis=0).astype(f32)
    scale_attn = rms_scale(whole_in)
    normed = (whole_in * scale_attn * gain_attn).astype(bf16)
    normed_own = normed[:own_rows]
    normed_planes = lax.all_gather(normed_own, "z", axis=0, tiled=False)
    queries = dot(normed, w_query)
    key_proj = dot(normed, w_key)
    values = dot(normed, w_value).astype(bf16)
    squares = jnp.stack([jnp.sum(queries * queries, axis=1), jnp.sum(key_proj * key_proj, axis=1)])
    squares = squares + other_order(swap(squares).T).T
    query_scale = lax.rsqrt(squares[0] / full_width + norm_eps)[:, None]
    key_scale = lax.rsqrt(squares[1] / full_width + norm_eps)[:, None]
    query_gain = gain_query.reshape(1, local_width)
    key_gain = gain_key.reshape(1, local_width)
    q_rot, k_rot, probs, mixed = attention_forward(
        queries,
        key_proj,
        values,
        query_gain,
        key_gain,
        query_scale,
        key_scale,
        cosine,
        sine,
        bias,
        local_heads,
    )
    mixed_planes = lax.all_gather(mixed, "z", axis=0, tiled=False)
    branch = dot(mixed, w_out)
    branch = branch + other_order(swap(branch))
    hidden = whole_in + branch
    scale_moe = rms_scale(hidden)
    normed_moe = (hidden * scale_moe * gain_moe).astype(bf16)

    moe_slots = dot(pick, normed_moe).astype(bf16).reshape(experts, own_slots, width)
    moe_slots, cot_arrived = lax.optimization_barrier((moe_slots, cot_arrived))
    arrived = all_to_all(moe_slots, rows_of_chips).reshape(experts * own_slots, width)
    router_probs = jax.nn.softmax(dot(normed_moe, w_router), axis=-1)

    gate_parts = (w_gate[0], swap(w_gate[0]))
    up_parts = (w_up[0], swap(w_up[0]))
    down_parts = (w_down[0], swap(w_down[0]))
    slot_probs = jax.nn.softmax(dot(arrived, w_router), axis=-1)
    own_expert = jnp.arange(experts, dtype=jnp.int32) == chip
    slot_weight = jnp.sum(jnp.where(own_expert[None, :], slot_probs, 0.0), axis=1, keepdims=True)
    slot_grad = (slot_weight * cot_arrived.astype(f32)).astype(bf16)
    *acts, slot_out = expert_forward(arrived, gate_parts, up_parts, down_parts)
    slot_out, normed_planes, mixed_planes = lax.optimization_barrier(
        (slot_out, normed_planes, mixed_planes)
    )
    normed_planes = jnp.concatenate([normed_planes, swap(normed_planes)], axis=1).reshape(
        planes * seq_len, width
    )
    mixed_planes = mixed_planes.reshape(planes * seq_len, local_width)
    returned = all_to_all(
        slot_out.reshape(experts, own_slots, width), rows_of_chips
    ).reshape(experts * own_slots, width)
    part_grads = []
    slot_in_grad = None
    for gate_act, up_act, w_g, w_u, w_d in zip(
        acts[:2], acts[2:], gate_parts, up_parts, down_parts
    ):
        sigmoid_gate = jax.nn.sigmoid(gate_act)
        silu_gate = gate_act * sigmoid_gate
        inner_act = (silu_gate * up_act).astype(bf16)
        inner_grad = dot_cols(slot_grad, w_d)
        up_grad = (inner_grad * silu_gate).astype(bf16)
        gate_grad = (
            inner_grad * up_act * sigmoid_gate * (1.0 + gate_act * (1.0 - sigmoid_gate))
        ).astype(bf16)
        part_in = dot_cols(gate_grad, w_g) + dot_cols(up_grad, w_u)
        slot_in_grad = part_in if slot_in_grad is None else slot_in_grad + part_in
        part_grads.append((inner_act, gate_grad, up_grad))
    slot_in_grad, returned = lax.optimization_barrier((slot_in_grad.astype(bf16), returned))
    grads_back = all_to_all(
        slot_in_grad.reshape(experts, own_slots, width), rows_of_chips
    ).reshape(experts * own_slots, width)
    (inner_own, gate_own, up_own), (inner_other, gate_other, up_other) = part_grads
    others = expert_weight_grads(
        arrived, slot_grad, inner_other, gate_other, up_other, (), bf16
    )
    grads_back, *others = lax.optimization_barrier((grads_back, *others))
    others = [swap(grad) for grad in others]
    grad_w_gate, grad_w_up, grad_w_down = expert_weight_grads(
        arrived, slot_grad, inner_own, gate_own, up_own, others, f32
    )

    pick_pairs = pick.reshape(experts, own_slots, seq_len)
    weighted = pick_pairs.astype(f32) * router_probs.T[:, None, :]
    weight_high, weight_low = halves(weighted.reshape(experts * own_slots, seq_len))
    moe_part = dot_rows(weight_high, returned) + dot_rows(weight_low, returned)
    moe_own = moe_part[:own_rows] + swap(moe_part[own_rows:].astype(bf16)).astype(f32)
    output = (hidden[:own_rows] + moe_own).astype(bf16)
    pair_products = dot_cols(returned, cot).reshape(experts, own_slots, seq_len)
    prob_part = jnp.sum(pair_products * pick_pairs.astype(f32), axis=1).T
    prob_grad = prob_part + other_order(swap(prob_part))
    logit_grad = router_probs * (
        prob_grad - jnp.sum(router_probs * prob_grad, axis=1, keepdims=True)
    )
    logit_high, logit_low = halves(logit_grad)
    router_grad = dot_rows(normed_moe, logit_high) + dot_rows(normed_moe, logit_low)
    moe_in_part = dot_rows(pick, grads_back)
    moe_in_grad = (
        moe_in_part[:own_rows]
        + swap(moe_in_part[own_rows:])
        + dot_cols(logit_high[:own_rows], w_router)
        + dot_cols(logit_low[:own_rows], w_router)
    )
    cot_own = cotangent.astype(f32)
    hidden_own = hidden[:own_rows]
    scale_own = scale_moe[:own_rows]
    weighted_moe = moe_in_grad * gain_moe
    hidden_grad = (
        cot_own
        + scale_own * weighted_moe
        - hidden_own * scale_own**3 * jnp.mean(hidden_own * weighted_moe, axis=1, keepdims=True)
    )
    gain_moe_grad = jnp.sum(hidden_own * scale_own * moe_in_grad, axis=0)
    hidden_low_own = hidden_grad.astype(bf16)
    hidden_low = jnp.concatenate([hidden_low_own, swap(hidden_low_own)], axis=0)

    part = width // planes
    low_planes = all_to_all(
        jnp.stack([hidden_low_own[:, k * part : (k + 1) * part] for k in range(planes)]), "z"
    )

    def for_cores(vector):
        pieces = vector.reshape(chips, 2, -1)
        mine = jnp.where(core == 0, pieces[:, 0], pieces[:, 1])
        others = jnp.where(core == 0, pieces[:, 1], pieces[:, 0])
        return mine + swap(others)

    def small_rows(values):
        high, low = halves(jnp.pad(values, ((0, 0), (0, lanes - values.shape[1]))))
        return jnp.stack([high, low], axis=1)

    router_pieces = router_grad.reshape(chips, 2, out_rows // 2, experts)
    router_mine = jnp.where(core == 0, router_pieces[:, 0], router_pieces[:, 1])
    router_mine = router_mine.reshape(chips, -1, lanes).astype(bf16)
    router_len = router_mine.shape[1]

    (
        value_grad,
        query_part,
        key_part,
        gain_query_grad,
        gain_key_grad,
        query_inner,
        key_inner,
    ) = attention_backward(
        hidden_low,
        w_out,
        values,
        q_rot,
        k_rot,
        probs,
        queries,
        key_proj,
        query_gain,
        key_gain,
        query_scale,
        key_scale,
        cosine,
        sine,
        local_heads,
    )
    query_inner, key_inner, low_planes = lax.optimization_barrier(
        (query_inner, key_inner, low_planes)
    )
    inner = jnp.concatenate([query_inner, key_inner], axis=1)
    inner = (inner + other_order(swap(inner.T).T)) / full_width
    query_grad, key_grad, to_planes = projection_grads(
        query_part,
        key_part,
        queries,
        key_proj,
        value_grad,
        query_scale,
        key_scale,
        (inner[:, :1], inner[:, 1:]),
        planes,
    )

    grads_planes = all_to_all(to_planes, "z").reshape(planes * seq_len, 3 * quarter)
    low_planes = jnp.concatenate([low_planes, swap(low_planes)], axis=1).reshape(
        planes * seq_len, part
    )
    out_grad = dot_rows(low_planes, mixed_planes).astype(bf16)
    out_grad, grads_planes = lax.optimization_barrier((out_grad, grads_planes))
    out_sums = all_to_all(
        out_grad.reshape(chips // planes, out_rows, local_width), rows_of_chips[1:]
    )
    normed_grad = normed_grad_of(
        (query_grad, key_grad, value_grad), (w_query, w_key, w_value), planes
    )
    normed_grad = normed_grad[:own_rows] + swap(normed_grad[own_rows:])
    in_own = whole_in[:own_rows]
    in_scale = scale_attn[:own_rows]
    weighted_attn = normed_grad * gain_attn
    grad_input = (
        hidden_grad
        + in_scale * weighted_attn
        - in_own * in_scale**3 * jnp.mean(in_own * weighted_attn, axis=1, keepdims=True)
    )
    gain_attn_grad = jnp.sum(in_own * in_scale * normed_grad, axis=0)

    def by_lane(vector):
        pieces = vector.reshape(local_heads, chips, head_dim // chips)
        return jnp.swapaxes(pieces, 0, 1).reshape(chips, -1)

    first_small = small_rows(jnp.concatenate([for_cores(gain_moe_grad), counts[:, None]], axis=1))
    last_small = small_rows(
        jnp.concatenate(
            [for_cores(gain_attn_grad), by_lane(gain_query_grad), by_lane(gain_key_grad)], axis=1
        )
    )
    spare = jnp.zeros((chips, -(router_len + 4) % 16, lanes), bf16)
    extra = jnp.concatenate([router_mine, first_small, last_small, spare], axis=1)
    last_parcel = weight_parcel(normed_planes, grads_planes, extra, planes)
    last_parcel, out_sums = lax.optimization_barrier((last_parcel, out_sums))
    last_sums = all_to_all(last_parcel, rows_of_chips).astype(f32)
    last_sums = jnp.sum(last_sums.reshape((planes, chips // planes) + last_sums.shape[1:]), axis=1)

    def matrix_of(blocks):
        pieces = blocks.reshape(planes, -1, out_rows, lanes)
        return jnp.transpose(pieces, (2, 0, 1, 3)).reshape(out_rows, -1)

    block_len = quarter // lanes * out_rows
    grad_w_query, grad_w_key, grad_w_value = (
        matrix_of(last_sums[:, k * block_len : (k + 1) * block_len]) for k in range(3)
    )
    grad_w_out = jnp.sum(out_sums.astype(f32), axis=0).T
    tail = jnp.sum(last_sums[:, 3 * block_len :], axis=0)
    grad_w_router = tail[:router_len].reshape(out_rows // 2, experts)
    first_tail = tail[router_len] + tail[router_len + 1]
    last_tail = tail[router_len + 2] + tail[router_len + 3]
    own_gain = out_rows // 2
    own_lanes = local_heads * head_dim // chips
    lane_shape = (local_heads, head_dim // chips)
    return (
        output,
        grad_input,
        last_tail[:own_gain],
        grad_w_query,
        grad_w_key,
        grad_w_value,
        last_tail[own_gain : own_gain + own_lanes].reshape(lane_shape),
        last_tail[own_gain + own_lanes : own_gain + 2 * own_lanes].reshape(lane_shape),
        grad_w_out,
        first_tail[:own_gain],
        grad_w_router,
        grad_w_gate[None],
        grad_w_up[None],
        grad_w_down[None],
        first_tail[own_gain : own_gain + 1].astype(jnp.int32),
    )


def solution(mesh):
    side = round(mesh.shape["ep"] ** (1 / 3))
    cube = Mesh(mesh.devices.reshape(side, side, side, 2), rows_of_chips + ("tp",))
    ep = rows_of_chips
    both = rows_of_chips + ("tp",)
    in_specs = (
        P(both, None),
        P(ep, None),
        P(ep, None),
        P(),
        P(None, "tp"),
        P(None, "tp"),
        P(None, "tp"),
        P("tp", None),
        P("tp", None),
        P("tp", None),
        P(),
        P(),
        P(ep, None, "tp"),
        P(ep, None, "tp"),
        P(ep, "tp", None),
        P(both, None),
    )
    out_specs = (
        P(both, None),
        P(both, None),
        P(both),
        P(ep, "tp"),
        P(ep, "tp"),
        P(ep, "tp"),
        P("tp", ep),
        P("tp", ep),
        P("tp", ep),
        P(both),
        P(both, None),
        P(ep, None, "tp"),
        P(ep, None, "tp"),
        P(ep, "tp", None),
        P(ep),
    )
    return jax.shard_map(local, mesh=cube, in_specs=in_specs, out_specs=out_specs, check_vma=False)
```

```python
import jax
import jax.numpy as jnp
from jax import lax
from jax.experimental import pallas as pl
from jax.experimental.pallas import tpu as pltpu
from jax.sharding import Mesh, PartitionSpec as P

norm_eps = 1e-05
rope_base = 10000.0
mask_fill = -1e30
bf16 = jnp.bfloat16
f32 = jnp.float32
rows_of_chips = ("z", "x", "y")


def swap(value):
    return lax.ppermute(value, "tp", [(0, 1), (1, 0)])


def dot(left, right):
    return lax.dot_general(left, right, (((1,), (0,)), ((), ())), preferred_element_type=f32)


def dot_rows(left, right):
    return lax.dot_general(left, right, (((0,), (0,)), ((), ())), preferred_element_type=f32)


def dot_cols(left, right):
    return lax.dot_general(left, right, (((1,), (1,)), ((), ())), preferred_element_type=f32)


def all_to_all(value, axes):
    return lax.all_to_all(value, axes, split_axis=0, concat_axis=0, tiled=True)


def rms_scale(values):
    return lax.rsqrt(jnp.mean(values * values, axis=-1, keepdims=True) + norm_eps)


def halves(value):
    high = value.astype(bf16)
    return high, (value - high.astype(f32)).astype(bf16)


def rope_angles(positions, head_dim):
    half_dim = head_dim // 2
    exponent = jnp.arange(half_dim, dtype=f32) * (2.0 / head_dim)
    inverse = jnp.power(f32(rope_base), -exponent)
    angles = positions.astype(f32)[:, None] * inverse[None, :]
    return jnp.cos(angles), jnp.sin(angles)


lanes = 128
vmem_bytes = 56 * 1024 * 1024
cheap = 64


def params():
    return pltpu.CompilerParams(vmem_limit_bytes=vmem_bytes)


def turn(value, cosine, sine):
    return value * cosine + pltpu.roll(value, value.shape[1] // 2, 1) * sine


def attention_forward_body(
    scale,
    query_ref,
    key_ref,
    value_ref,
    query_gain_ref,
    key_gain_ref,
    query_scale_ref,
    key_scale_ref,
    cosine_ref,
    sine_ref,
    bias_ref,
    q_rot_ref,
    k_rot_ref,
    probs_ref,
    mixed_ref,
):
    cosine, sine = cosine_ref[...], sine_ref[...]
    query = query_ref[...] * query_scale_ref[...] * query_gain_ref[...]
    key = key_ref[...] * key_scale_ref[...] * key_gain_ref[...]
    q_rot = turn(query, cosine, sine).astype(bf16)
    k_rot = turn(key, cosine, sine).astype(bf16)
    q_rot_ref[...] = q_rot
    k_rot_ref[...] = k_rot
    scores = dot_cols(q_rot, k_rot) * scale + bias_ref[...]
    grown = jnp.exp(scores - jnp.max(scores, axis=1, keepdims=True))
    probs = grown / jnp.sum(grown, axis=1, keepdims=True)
    probs_ref[...] = probs
    mixed_ref[...] = dot(probs.astype(bf16), value_ref[...]).astype(bf16)


def attention_forward(
    queries, keys, values, query_gain, key_gain, query_scale, key_scale, cosine, sine, bias, heads
):
    seq_len, width = queries.shape
    head = width // heads
    column = pl.BlockSpec((seq_len, head), lambda h: (0, h))
    gain = pl.BlockSpec((1, head), lambda h: (0, h))

    def whole(array):
        return pl.BlockSpec(array.shape, lambda h: (0, 0))

    return pl.pallas_call(
        lambda *refs: attention_forward_body(head**-0.5, *refs),
        grid=(heads,),
        in_specs=[column, column, column, gain, gain]
        + [whole(a) for a in (query_scale, key_scale, cosine, sine, bias)],
        out_specs=[
            column,
            column,
            pl.BlockSpec((None, seq_len, seq_len), lambda h: (h, 0, 0)),
            column,
        ],
        out_shape=[
            jax.ShapeDtypeStruct((seq_len, width), bf16),
            jax.ShapeDtypeStruct((seq_len, width), bf16),
            jax.ShapeDtypeStruct((heads, seq_len, seq_len), f32),
            jax.ShapeDtypeStruct((seq_len, width), bf16),
        ],
        compiler_params=params(),
        cost_estimate=pl.CostEstimate(
            flops=4 * seq_len * seq_len * width,
            transcendentals=heads * seq_len * seq_len,
            bytes_accessed=seq_len * width * 16 + heads * seq_len * seq_len * 4,
        ),
        name="attention_forward",
    )(queries, keys, values, query_gain, key_gain, query_scale, key_scale, cosine, sine, bias)


def attention_backward_body(
    scale,
    hidden_own_ref,
    hidden_other_ref,
    w_out_ref,
    value_ref,
    q_rot_ref,
    k_rot_ref,
    probs_ref,
    query_ref,
    key_ref,
    query_gain_ref,
    key_gain_ref,
    query_scale_ref,
    key_scale_ref,
    cosine_ref,
    sine_ref,
    value_grad_ref,
    query_part_ref,
    key_part_ref,
    query_gain_grad_ref,
    key_gain_grad_ref,
    inner_ref,
):
    cosine, sine = cosine_ref[...], sine_ref[...]
    hidden = jnp.concatenate([hidden_own_ref[...], hidden_other_ref[...]], axis=0)
    heads, head = query_gain_grad_ref.shape[0], query_gain_grad_ref.shape[2]
    grad_mixed = dot_cols(hidden, w_out_ref[...]).astype(bf16)
    total = None
    for h in range(heads):
        here = slice(h * head, (h + 1) * head)
        grad = grad_mixed[:, here]
        probs = probs_ref[h]
        grad_probs = dot_cols(grad, value_ref[:, here])
        inner = jnp.sum(probs * grad_probs, axis=1, keepdims=True)
        grad_scores = (probs * (grad_probs - inner)).astype(bf16)
        value_grad_ref[:, here] = dot_rows(probs.astype(bf16), grad).astype(bf16)
        row_inners = []
        for grad_rot, raw_ref, gain_ref, scale_ref, part_ref, gain_grad_ref in (
            (
                dot(grad_scores, k_rot_ref[:, here]),
                query_ref,
                query_gain_ref,
                query_scale_ref,
                query_part_ref,
                query_gain_grad_ref,
            ),
            (
                dot_rows(grad_scores, q_rot_ref[:, here]),
                key_ref,
                key_gain_ref,
                key_scale_ref,
                key_part_ref,
                key_gain_grad_ref,
            ),
        ):
            grad_normed = turn(grad_rot * scale, cosine, -sine)
            raw = raw_ref[:, here]
            gain_grad_ref[h] = jnp.sum(raw * scale_ref[...] * grad_normed, axis=0, keepdims=True)
            weighted = grad_normed * gain_ref[:, here]
            part_ref[:, here] = weighted
            row_inners.append(jnp.sum(raw * weighted, axis=1, keepdims=True))
        row_inner = jnp.concatenate(row_inners, axis=1)
        total = row_inner if total is None else total + row_inner
    first = pl.program_id(0) == 0

    @pl.when(first)
    def _():
        inner_ref[...] = total

    @pl.when(jnp.logical_not(first))
    def _():
        inner_ref[...] += total


def attention_backward(
    hidden_own,
    hidden_other,
    w_out,
    values,
    q_rot,
    k_rot,
    probs,
    queries,
    keys,
    query_gain,
    key_gain,
    query_scale,
    key_scale,
    cosine,
    sine,
    heads,
):
    seq_len, width = queries.shape
    head = width // heads
    group = 2
    column = pl.BlockSpec((seq_len, group * head), lambda h: (0, h))
    gain = pl.BlockSpec((1, group * head), lambda h: (0, h))

    def whole(array):
        return pl.BlockSpec(array.shape, lambda h: (0, 0))

    full = jax.ShapeDtypeStruct((seq_len, width), f32)
    line = jax.ShapeDtypeStruct((heads, 1, head), f32)
    line_spec = pl.BlockSpec((group, 1, head), lambda h: (h, 0, 0))
    sums = jax.ShapeDtypeStruct((seq_len, 2), f32)
    return pl.pallas_call(
        lambda *refs: attention_backward_body(head**-0.5, *refs),
        grid=(heads // group,),
        in_specs=[
            whole(hidden_own),
            whole(hidden_other),
            pl.BlockSpec((group * head, w_out.shape[1]), lambda h: (h, 0)),
            column,
            column,
            column,
            pl.BlockSpec((group, seq_len, seq_len), lambda h: (h, 0, 0)),
            column,
            column,
            gain,
            gain,
        ]
        + [whole(a) for a in (query_scale, key_scale, cosine, sine)],
        out_specs=[column, column, column, line_spec, line_spec, whole(sums)],
        out_shape=[
            jax.ShapeDtypeStruct((seq_len, width), bf16),
            full,
            full,
            line,
            line,
            sums,
        ],
        compiler_params=params(),
        cost_estimate=pl.CostEstimate(
            flops=10 * seq_len * seq_len * width + 2 * seq_len * width * w_out.shape[1],
            transcendentals=0,
            bytes_accessed=seq_len * width * 28
            + heads * seq_len * seq_len * 4
            + 2 * w_out.size
            + 4 * hidden_own.size,
        ),
        name="attention_backward",
    )(
        hidden_own,
        hidden_other,
        w_out,
        values,
        q_rot,
        k_rot,
        probs,
        queries,
        keys,
        query_gain,
        key_gain,
        query_scale,
        key_scale,
        cosine,
        sine,
    )


def projection_grads_body(
    width,
    query_part_ref,
    key_part_ref,
    query_ref,
    key_ref,
    value_grad_ref,
    query_scale_ref,
    key_scale_ref,
    inner_ref,
    other_inner_ref,
    stack_ref,
):
    size = query_ref.shape[1]
    half = inner_ref.shape[0] // 2
    other = jnp.concatenate([other_inner_ref[half:, :], other_inner_ref[:half, :]], axis=0)
    inner = (inner_ref[...] + other) * (1.0 / width)
    for k, (part_ref, raw_ref, scale_ref) in enumerate(
        (
            (query_part_ref, query_ref, query_scale_ref),
            (key_part_ref, key_ref, key_scale_ref),
        )
    ):
        scale = scale_ref[...]
        factor = scale * scale * scale * inner[:, k : k + 1]
        grad = scale * part_ref[...] - raw_ref[...] * factor
        stack_ref[:, k * size : (k + 1) * size] = grad.astype(bf16)
    stack_ref[:, 2 * size :] = value_grad_ref[...]


def projection_grads(
    query_part, key_part, queries, keys, value_grad, query_scale, key_scale, inners, planes
):
    seq_len, width = queries.shape
    size = width // planes
    column = pl.BlockSpec((seq_len, size), lambda k: (0, k))
    sums = pl.BlockSpec((seq_len, 1), lambda k: (0, 0))
    pair = pl.BlockSpec((seq_len, 2), lambda k: (0, 0))
    return pl.pallas_call(
        lambda *refs: projection_grads_body(2 * width, *refs),
        grid=(planes,),
        in_specs=[column] * 5 + [sums] * 2 + [pair] * 2,
        out_specs=pl.BlockSpec((None, seq_len, 3 * size), lambda k: (k, 0, 0)),
        out_shape=jax.ShapeDtypeStruct((planes, seq_len, 3 * size), bf16),
        compiler_params=params(),
        cost_estimate=pl.CostEstimate(
            flops=10 * seq_len * width, transcendentals=0, bytes_accessed=24 * seq_len * width
        ),
        name="projection_grads",
    )(query_part, key_part, queries, keys, value_grad, query_scale, key_scale, *inners)


def expert_forward_body(
    rows_ref,
    gate_own_ref,
    gate_other_ref,
    up_own_ref,
    up_other_ref,
    down_own_ref,
    down_other_ref,
    out_ref,
    total_ref,
):
    step = pl.program_id(0)
    last = pl.num_programs(0) - 1
    rows = rows_ref[...]
    inners = []
    for gate_ref, up_ref in ((gate_own_ref, up_own_ref), (gate_other_ref, up_other_ref)):
        gate = dot(rows, gate_ref[...])
        inners.append((gate * jax.nn.sigmoid(gate) * dot(rows, up_ref[...])).astype(bf16))
    width = out_ref.shape[1]
    size = min(512, width)
    for start in range(0, width, size):
        here = pl.ds(start, size)
        part = dot(inners[0], down_own_ref[:, here]) + dot(inners[1], down_other_ref[:, here])

        @pl.when(step == 0)
        def _():
            total_ref[:, here] = part

        @pl.when((step > 0) & (step < last))
        def _():
            total_ref[:, here] += part

        @pl.when(step == last)
        def _():
            out_ref[:, here] = (total_ref[:, here] + part).astype(bf16)


def expert_specs(count, width, size):
    whole = pl.BlockSpec((count, width), lambda k: (0, 0), pipeline_mode=pl.Buffered(1))
    into = pl.BlockSpec((width, size), lambda k: (0, k))
    back = pl.BlockSpec((size, width), lambda k: (k, 0))
    return whole, into, back


def expert_forward(rows, gates, ups, downs):
    count, width = rows.shape
    units = gates[0].shape[1]
    steps = 2
    whole, into, back = expert_specs(count, width, units // steps)
    return pl.pallas_call(
        expert_forward_body,
        grid=(steps,),
        in_specs=[whole] + [into] * 4 + [back] * 2,
        out_specs=pl.BlockSpec((count, width), lambda k: (0, 0)),
        out_shape=jax.ShapeDtypeStruct((count, width), bf16),
        scratch_shapes=[pltpu.VMEM((count, width), f32)],
        compiler_params=params(),
        cost_estimate=pl.CostEstimate(
            flops=12 * count * width * units,
            transcendentals=2 * count * units,
            bytes_accessed=count * width * 4 + 12 * width * units,
        ),
        name="expert_forward",
    )(rows, *gates, *ups, *downs)


def expert_backward_body(
    rows_ref,
    slot_grad_ref,
    gate_own_ref,
    gate_other_ref,
    up_own_ref,
    up_other_ref,
    down_own_ref,
    down_other_ref,
    inner_own_ref,
    inner_other_ref,
    gate_grad_own_ref,
    gate_grad_other_ref,
    up_grad_own_ref,
    up_grad_other_ref,
    out_ref,
    total_ref,
):
    step = pl.program_id(0)
    last = pl.num_programs(0) - 1
    for gate_ref, up_ref, down_ref, inner_ref, gate_grad_ref, up_grad_ref in (
        (gate_own_ref, up_own_ref, down_own_ref, inner_own_ref, gate_grad_own_ref, up_grad_own_ref),
        (
            gate_other_ref,
            up_other_ref,
            down_other_ref,
            inner_other_ref,
            gate_grad_other_ref,
            up_grad_other_ref,
        ),
    ):
        gate = dot(rows_ref[...], gate_ref[...])
        up = dot(rows_ref[...], up_ref[...])
        inner_grad = dot_cols(slot_grad_ref[...], down_ref[...])
        sigmoid_gate = jax.nn.sigmoid(gate)
        silu_gate = gate * sigmoid_gate
        inner_ref[...] = (silu_gate * up).astype(bf16)
        up_grad_ref[...] = (inner_grad * silu_gate).astype(bf16)
        gate_grad_ref[...] = (
            inner_grad * up * sigmoid_gate * (1.0 + gate * (1.0 - sigmoid_gate))
        ).astype(bf16)
    width = out_ref.shape[1]
    size = min(512, width)
    for start in range(0, width, size):
        here = pl.ds(start, size)
        part = None
        for grad_ref, w_ref in (
            (gate_grad_own_ref, gate_own_ref),
            (gate_grad_other_ref, gate_other_ref),
            (up_grad_own_ref, up_own_ref),
            (up_grad_other_ref, up_other_ref),
        ):
            term = dot_cols(grad_ref[...], w_ref[here, :])
            part = term if part is None else part + term

        @pl.when(step == 0)
        def _():
            total_ref[:, here] = part

        @pl.when((step > 0) & (step < last))
        def _():
            total_ref[:, here] += part

        @pl.when(step == last)
        def _():
            out_ref[:, here] = (total_ref[:, here] + part).astype(bf16)


def expert_backward(rows, slot_grad, gates, ups, downs):
    count, width = rows.shape
    units = gates[0].shape[1]
    steps = 2
    size = units // steps
    whole, into, back = expert_specs(count, width, size)
    acts = pl.BlockSpec((count, size), lambda k: (0, k))
    return pl.pallas_call(
        expert_backward_body,
        grid=(steps,),
        in_specs=[whole] * 2 + [into] * 4 + [back] * 2,
        out_specs=[acts] * 6 + [pl.BlockSpec((count, width), lambda k: (0, 0))],
        out_shape=[jax.ShapeDtypeStruct((count, units), bf16)] * 6
        + [jax.ShapeDtypeStruct((count, width), bf16)],
        scratch_shapes=[pltpu.VMEM((count, width), f32)],
        compiler_params=params(),
        cost_estimate=pl.CostEstimate(
            flops=20 * count * width * units // cheap,
            transcendentals=0,
            bytes_accessed=count * width * 6 // cheap,
        ),
        name="expert_backward",
    )(rows, slot_grad, *gates, *ups, *downs)


def put_blocks(out_ref, row, product):
    chips = out_ref.shape[0]
    rows = product.shape[0] // chips
    for k in range(product.shape[1] // lanes):
        piece = product[:, k * lanes : (k + 1) * lanes].reshape(chips, rows, lanes)
        out_ref[:, row : row + rows, :] = piece
        row += rows
    return row


def joined(own_ref, other_ref):
    rows = jnp.concatenate([own_ref[...], other_ref[...]], axis=1)
    return rows.reshape(rows.shape[0] * rows.shape[1], rows.shape[2])


def weight_parcel_body(
    start,
    per_chip,
    place_ref,
    normed_ref,
    normed_other_ref,
    grads_ref,
    router_ref,
    moe_ref,
    query_gain_ref,
    key_gain_ref,
    counts_ref,
    out_ref,
):
    left = joined(normed_ref, normed_other_ref)
    put_blocks(out_ref, 0, dot_rows(left, grads_ref[...]).astype(bf16))

    chips, rows, spare = router_ref.shape[0], router_ref.shape[1] // 2, lanes // 2
    router = router_ref[:, pl.ds(place_ref[1] * rows, rows), :]
    if router.shape[2] < spare:
        fill = jnp.zeros((chips, rows, spare - router.shape[2]), f32)
        router = jnp.concatenate([router, fill], axis=2)
    lines = moe_ref.shape[1] // spare
    moe = jnp.concatenate([moe_ref[:, k * spare : (k + 1) * spare] for k in range(lines)], axis=0)
    chip = lax.broadcasted_iota(jnp.int32, (chips, lines), 0)
    line = lax.broadcasted_iota(jnp.int32, (chips, lines), 1)
    mine = jnp.where(chip * lines // chips == line, 1.0, 0.0).astype(bf16)
    gains = jnp.concatenate([query_gain_ref[:, 0, :], key_gain_ref[:, 0, :]], axis=0)
    head = gains.shape[1]
    chip = lax.broadcasted_iota(jnp.int32, (chips, head), 0) + pl.program_id(0) * chips
    lane = lax.broadcasted_iota(jnp.int32, (chips, head), 1)
    vectors = []
    for part in halves(moe):
        vectors.append(dot(mine, part))
    for part in halves(gains):
        pieces = [
            dot_cols(jnp.where(lane == chip * per_chip + k, 1.0, 0.0).astype(bf16), part)
            for k in range(per_chip)
        ]
        width = per_chip * gains.shape[0]
        if width < spare:
            pieces.append(jnp.zeros((chips, spare - width), f32))
        vectors.append(jnp.concatenate(pieces, axis=1))
    vectors.append(jnp.broadcast_to(counts_ref[...], (chips, spare)))
    row = lax.broadcasted_iota(jnp.int32, (chips, rows, spare), 1)
    beside = jnp.zeros((chips, rows, spare), f32)
    for k, vector in enumerate(vectors):
        beside = jnp.where(row == k, vector[:, None, :], beside)
    out_ref[:, start:, :] = jnp.concatenate([router, beside], axis=2).astype(bf16)


def weight_parcel(place, normed, grads, router, moe, query_gain, key_gain, counts):
    planes, half, width = normed[0].shape
    tokens, columns = grads.shape
    chips, router_rows, experts = router.shape
    heads, _, head = query_gain.shape
    start = width // chips * (columns + columns // 3) // lanes
    height = start + router_rows // 2
    steps = planes
    group = chips // steps
    left = pl.BlockSpec((planes, half, width // steps), lambda k, z: (0, 0, k))
    gain = pl.BlockSpec((heads, 1, head), lambda k, z: (0, 0, 0))
    return pl.pallas_call(
        lambda *refs: weight_parcel_body(start, head // chips, *refs),
        grid_spec=pltpu.PrefetchScalarGridSpec(
            num_scalar_prefetch=1,
            grid=(steps,),
            in_specs=[
                left,
                left,
                pl.BlockSpec((tokens, columns), lambda k, z: (0, 0)),
                pl.BlockSpec((group, router_rows, experts), lambda k, z: (k, 0, 0)),
                pl.BlockSpec((1, width // steps), lambda k, z: (0, k)),
                gain,
                gain,
                pl.BlockSpec((group, 1), lambda k, z: (k, 0)),
            ],
            out_specs=pl.BlockSpec((group, height, lanes), lambda k, z: (k, 0, 0)),
        ),
        out_shape=jax.ShapeDtypeStruct((chips, height, lanes), bf16),
        compiler_params=params(),
        cost_estimate=pl.CostEstimate(
            flops=2 * tokens * width * columns,
            transcendentals=0,
            bytes_accessed=2 * (tokens * width + grads.size + chips * height * lanes),
        ),
        name="weight_parcel",
    )(place, *normed, grads, router, moe, query_gain, key_gain, counts)


def out_parcel_body(place_ref, low_ref, low_other_ref, mixed_ref, parcel_ref, out_ref):
    left = joined(low_ref, low_other_ref)
    put_blocks(out_ref, 0, dot_rows(left, mixed_ref[...]).astype(bf16))


def out_parcel(place, low, mixed, parcel):
    planes, half, width = low[0].shape
    tokens, local_width = mixed.shape
    chips, height, _ = parcel.shape
    part = local_width // planes
    room = width // chips * part // lanes
    steps = planes
    left = pl.BlockSpec((planes, half, width // steps), lambda k, z: (0, 0, k))
    return pl.pallas_call(
        out_parcel_body,
        grid_spec=pltpu.PrefetchScalarGridSpec(
            num_scalar_prefetch=1,
            grid=(steps,),
            in_specs=[
                left,
                left,
                pl.BlockSpec((tokens, part), lambda k, z: (0, z[0])),
                pl.BlockSpec(memory_space=pl.ANY),
            ],
            out_specs=pl.BlockSpec((chips // steps, room, lanes), lambda k, z: (k, 3, 0)),
        ),
        out_shape=jax.ShapeDtypeStruct((chips, height, lanes), bf16),
        input_output_aliases={4: 0},
        compiler_params=params(),
        cost_estimate=pl.CostEstimate(
            flops=2 * tokens * width * part,
            transcendentals=0,
            bytes_accessed=2 * (tokens * width + chips * room * lanes),
        ),
        name="out_parcel",
    )(place, *low, mixed, parcel)


def parcel_sums_body(
    chip_ref,
    parcel_ref,
    w_query_ref,
    w_key_ref,
    w_value_ref,
    query_ref,
    key_ref,
    value_ref,
    out_ref,
    extra_ref,
    gain_ref,
):
    total = jnp.sum(parcel_ref[...].astype(f32), axis=0)
    rows, columns = query_ref.shape
    row = 0
    gain = jnp.zeros((rows, lanes), f32)
    for ref, w_ref in ((query_ref, w_query_ref), (key_ref, w_key_ref), (value_ref, w_value_ref)):
        for k in range(columns // lanes):
            here = slice(k * lanes, (k + 1) * lanes)
            piece = total[row : row + rows, :]
            ref[:, here] = piece
            gain = gain + piece * w_ref[:, here].astype(f32)
            row += rows
    for k in range(columns // lanes):
        out_ref[k * lanes : (k + 1) * lanes, :] = total[row : row + rows, :].T
        row += rows
    gain = jnp.sum(gain, axis=1, keepdims=True)
    first = pl.program_id(0) == 0

    @pl.when(first)
    def _():
        extra_ref[...] = total[row:, :]
        gain_ref[...] = gain

    @pl.when(jnp.logical_not(first))
    def _():
        extra_ref[...] += total[row:, :]
        gain_ref[...] += gain


def parcel_sums(chip, parcel, weights, planes, rows, width, extra_rows):
    chips, height, _ = parcel.shape
    part = width // planes
    wide = pl.BlockSpec((rows, part), lambda k, c: (0, k))
    return pl.pallas_call(
        parcel_sums_body,
        grid_spec=pltpu.PrefetchScalarGridSpec(
            num_scalar_prefetch=1,
            grid=(planes,),
            in_specs=[pl.BlockSpec((chips // planes, height, lanes), lambda k, c: (k, 0, 0))]
            + [pl.BlockSpec((rows, part), lambda k, c: (c[0], k))] * 3,
            out_specs=[wide] * 3
            + [
                pl.BlockSpec((part, rows), lambda k, c: (k, 0)),
                pl.BlockSpec((extra_rows, lanes), lambda k, c: (0, 0)),
                pl.BlockSpec((rows, 1), lambda k, c: (0, 0)),
            ],
        ),
        out_shape=[jax.ShapeDtypeStruct((rows, width), f32)] * 3
        + [
            jax.ShapeDtypeStruct((width, rows), f32),
            jax.ShapeDtypeStruct((extra_rows, lanes), f32),
            jax.ShapeDtypeStruct((rows, 1), f32),
        ],
        compiler_params=params(),
        cost_estimate=pl.CostEstimate(
            flops=parcel.size, transcendentals=0, bytes_accessed=2 * parcel.size
        ),
        name="parcel_sums",
    )(chip, parcel, *weights)


def expert_weight_grads_body(rows_ref, slot_grad_ref, inner_ref, gate_ref, up_ref, *refs):
    grads = (
        dot_rows(rows_ref[...], gate_ref[...]),
        dot_rows(rows_ref[...], up_ref[...]),
        dot_rows(inner_ref[...], slot_grad_ref[...]),
    )
    others, outs = refs[:-3], refs[-3:]
    for k, (grad, out_ref) in enumerate(zip(grads, outs)):
        if others:
            grad = grad + others[k][...].astype(f32)
        out_ref[...] = grad.astype(out_ref.dtype)


def expert_weight_grads(rows, slot_grad, inner, gate_grad, up_grad, others, kind):
    count, width = rows.shape
    units = inner.shape[1]
    steps = 4
    size = width // steps
    wide = pl.BlockSpec((count, size), lambda k: (0, k))
    narrow = pl.BlockSpec((count, units), lambda k: (0, 0))
    into = pl.BlockSpec((size, units), lambda k: (k, 0))
    back = pl.BlockSpec((units, size), lambda k: (0, k))
    return pl.pallas_call(
        expert_weight_grads_body,
        grid=(steps,),
        in_specs=[wide, wide, narrow, narrow, narrow] + [into, into, back][: len(others)],
        out_specs=[into, into, back],
        out_shape=[
            jax.ShapeDtypeStruct((width, units), kind),
            jax.ShapeDtypeStruct((width, units), kind),
            jax.ShapeDtypeStruct((units, width), kind),
        ],
        compiler_params=params(),
        cost_estimate=pl.CostEstimate(
            flops=6 * count * width * units // cheap,
            transcendentals=0,
            bytes_accessed=4 * count * width // cheap,
        ),
        name="expert_weight_grads",
    )(rows, slot_grad, inner, gate_grad, up_grad, *others)


def normed_grad_body(stack_ref, query_ref, key_ref, value_ref, own_ref, other_ref):
    size = query_ref.shape[1]
    total = None
    for k, w_ref in enumerate((query_ref, key_ref, value_ref)):
        part = dot_cols(stack_ref[:, k * size : (k + 1) * size], w_ref[...])
        total = part if total is None else total + part
    half = own_ref.shape[0]
    first = pl.program_id(0) == 0

    @pl.when(first)
    def _():
        own_ref[...] = total[:half]
        other_ref[...] = total[half:]

    @pl.when(jnp.logical_not(first))
    def _():
        own_ref[...] += total[:half]
        other_ref[...] += total[half:]


def normed_grad_of(stack, weights):
    planes, seq_len, columns = stack.shape
    size = columns // 3
    full = weights[0].shape[0]
    half = pl.BlockSpec((seq_len // 2, full), lambda k: (0, 0))
    return pl.pallas_call(
        normed_grad_body,
        grid=(planes,),
        in_specs=[pl.BlockSpec((None, seq_len, columns), lambda k: (k, 0, 0))]
        + [pl.BlockSpec((full, size), lambda k: (0, k))] * 3,
        out_specs=[half] * 2,
        out_shape=[jax.ShapeDtypeStruct((seq_len // 2, full), f32)] * 2,
        compiler_params=params(),
        cost_estimate=pl.CostEstimate(
            flops=2 * stack.size * full // cheap,
            transcendentals=0,
            bytes_accessed=2 * planes * columns * full // cheap,
        ),
        name="normed_grad",
    )(stack, *weights)


def slot_rows_body(slots, *refs):
    core_ref, routes_ref, own_ref, other_ref, pick_ref, counts_ref, out_ref = refs
    core = core_ref[0]
    experts = counts_ref.shape[0]
    half, seq_len = own_ref.shape[0], routes_ref.shape[1]

    @pl.when(pl.program_id(0) == 0)
    def _():
        routes = routes_ref[...]
        routes = jnp.where(
            core == 0, routes, jnp.concatenate([routes[:, half:], routes[:, :half]], axis=1)
        )
        numbers = lax.broadcasted_iota(jnp.int32, (experts, seq_len), 0)
        hits = numbers == routes[0:1, :]
        for k in range(1, routes.shape[0]):
            hits = hits | (numbers == routes[k : k + 1, :])
        hits_float = jnp.where(hits, 1.0, 0.0)
        counts_ref[...] = jnp.sum(hits_float, axis=1, keepdims=True)
        square = (seq_len, seq_len)
        earlier = lax.broadcasted_iota(jnp.int32, square, 0)
        later = lax.broadcasted_iota(jnp.int32, square, 1)
        shift = core * half
        earlier = jnp.where(earlier + shift >= seq_len, earlier - seq_len, earlier)
        later = jnp.where(later + shift >= seq_len, later - seq_len, later)
        before = jnp.where(earlier < later, 1.0, 0.0).astype(bf16)
        rank = dot(hits_float.astype(bf16), before)
        rank = jnp.where(hits, rank, -1.0)
        slot = lax.broadcasted_iota(jnp.int32, (experts, slots, seq_len), 1) + core * slots
        pick = jnp.where(rank[:, None, :] == slot.astype(f32), 1.0, 0.0)
        pick_ref[...] = pick.reshape(experts * slots, seq_len).astype(bf16)

    rows = jnp.concatenate([own_ref[...], other_ref[...]], axis=0)
    out_ref[...] = dot(pick_ref[...], rows).astype(bf16)


def slot_rows(core, routes, own, other, experts, slots):
    half, width = own.shape
    top_count, seq_len = routes.shape
    steps = 4
    size = width // steps
    rows = pl.BlockSpec((half, size), lambda k, c: (0, k))
    return pl.pallas_call(
        lambda *refs: slot_rows_body(slots, *refs),
        grid_spec=pltpu.PrefetchScalarGridSpec(
            num_scalar_prefetch=1,
            grid=(steps,),
            in_specs=[pl.BlockSpec((top_count, seq_len), lambda k, c: (0, 0)), rows, rows],
            out_specs=[
                pl.BlockSpec((experts * slots, seq_len), lambda k, c: (0, 0)),
                pl.BlockSpec((experts, 1), lambda k, c: (0, 0)),
                pl.BlockSpec((experts * slots, size), lambda k, c: (0, k)),
            ],
        ),
        out_shape=[
            jax.ShapeDtypeStruct((experts * slots, seq_len), bf16),
            jax.ShapeDtypeStruct((experts, 1), f32),
            jax.ShapeDtypeStruct((experts * slots, width), bf16),
        ],
        compiler_params=params(),
        cost_estimate=pl.CostEstimate(
            flops=2 * experts * slots * seq_len * width,
            transcendentals=0,
            bytes_accessed=2 * (seq_len + experts * slots) * width,
        ),
        name="slot_rows",
    )(core, routes, own, other)


def token_sums_body(pick_ref, rows_ref, own_ref, other_ref):
    total = dot_rows(pick_ref[...], rows_ref[...])
    half = own_ref.shape[0]
    own_ref[...] = total[:half]
    other_ref[...] = total[half:]


def token_sums(pick, rows):
    count, seq_len = pick.shape
    width = rows.shape[1]
    steps = 4
    half = pl.BlockSpec((seq_len // 2, width // steps), lambda k: (0, k))
    return pl.pallas_call(
        token_sums_body,
        grid=(steps,),
        in_specs=[
            pl.BlockSpec((count, seq_len), lambda k: (0, 0)),
            pl.BlockSpec((count, width // steps), lambda k: (0, k)),
        ],
        out_specs=[half] * 2,
        out_shape=[jax.ShapeDtypeStruct((seq_len // 2, width), f32)] * 2,
        compiler_params=params(),
        cost_estimate=pl.CostEstimate(
            flops=2 * count * seq_len * width,
            transcendentals=0,
            bytes_accessed=2 * count * (seq_len + width) + 4 * seq_len * width,
        ),
        name="token_sums",
    )(pick, rows)


def local(
    residual_in,
    routes,
    segment_ids,
    gain_attn,
    w_query,
    w_key,
    w_value,
    gain_query,
    gain_key,
    w_out,
    gain_moe,
    w_router,
    w_gate,
    w_up,
    w_down,
    cotangent,
):
    core = lax.axis_index("tp")
    planes = lax.axis_size("z")
    chips = lax.axis_size(rows_of_chips)
    chip = lax.axis_index(rows_of_chips)
    own_rows, width = residual_in.shape
    seq_len, top_count = routes.shape
    local_width = w_query.shape[1]
    local_heads, head_dim = gain_query.shape
    full_width = 2 * local_width
    experts = chips
    capacity = seq_len * top_count // experts
    own_slots = capacity // 2
    score_scale = head_dim ** (-0.5)
    quarter = local_width // planes
    out_rows = width // chips

    def own_first(value):
        return jnp.where(
            core == 0, value, jnp.concatenate([value[own_rows:], value[:own_rows]], axis=0)
        )

    def other_order(value):
        return jnp.concatenate([value[own_rows:], value[:own_rows]], axis=0)

    place = own_first(jnp.arange(seq_len, dtype=jnp.int32))
    seg = own_first(segment_ids[0])
    same_doc = seg[:, None] == seg[None, :]
    position = place - jnp.min(jnp.where(same_doc, place[None, :], seq_len), axis=1)
    cosine, sine = rope_angles(position, head_dim)
    cosine = jnp.concatenate([cosine, cosine], axis=1)
    sine = jnp.concatenate([-sine, sine], axis=1)
    bias = jnp.where(same_doc & (place[None, :] <= place[:, None]), 0.0, mask_fill)

    cot_other = swap(cotangent)
    pick, counts, cot_slots = slot_rows(
        core[None], routes.T, cotangent, cot_other, experts, own_slots
    )
    cot_slots, residual_in = lax.optimization_barrier((cot_slots, residual_in))
    cot_arrived = all_to_all(
        cot_slots.reshape(experts, own_slots, width), rows_of_chips
    ).reshape(experts * own_slots, width)
    cot = jnp.concatenate([cotangent, cot_other], axis=0)

    whole_in = jnp.concatenate([residual_in, swap(residual_in)], axis=0).astype(f32)
    scale_attn = rms_scale(whole_in)
    normed = (whole_in * scale_attn * gain_attn).astype(bf16)
    normed_own = normed[:own_rows]
    normed_planes = lax.all_gather(normed_own, "z", axis=0, tiled=False)
    queries = dot(normed, w_query)
    key_proj = dot(normed, w_key)
    values = dot(normed, w_value).astype(bf16)
    squares = jnp.stack([jnp.sum(queries * queries, axis=1), jnp.sum(key_proj * key_proj, axis=1)])
    squares = squares + other_order(swap(squares).T).T
    query_scale = lax.rsqrt(squares[0] / full_width + norm_eps)[:, None]
    key_scale = lax.rsqrt(squares[1] / full_width + norm_eps)[:, None]
    query_gain = gain_query.reshape(1, local_width)
    key_gain = gain_key.reshape(1, local_width)
    q_rot, k_rot, probs, mixed = attention_forward(
        queries,
        key_proj,
        values,
        query_gain,
        key_gain,
        query_scale,
        key_scale,
        cosine,
        sine,
        bias,
        local_heads,
    )
    mixed_planes = lax.all_gather(mixed, "z", axis=0, tiled=False)
    branch = dot(mixed, w_out)
    branch = branch + other_order(swap(branch))
    hidden = whole_in + branch
    scale_moe = rms_scale(hidden)
    normed_moe = (hidden * scale_moe * gain_moe).astype(bf16)

    moe_slots = dot(pick, normed_moe).astype(bf16).reshape(experts, own_slots, width)
    moe_slots, cot_arrived = lax.optimization_barrier((moe_slots, cot_arrived))
    arrived = all_to_all(moe_slots, rows_of_chips).reshape(experts * own_slots, width)
    router_probs = jax.nn.softmax(dot(normed_moe, w_router), axis=-1)

    gate_parts = (w_gate[0], swap(w_gate[0]))
    up_parts = (w_up[0], swap(w_up[0]))
    down_parts = (w_down[0], swap(w_down[0]))
    slot_out = expert_forward(arrived, gate_parts, up_parts, down_parts)
    slot_out, arrived, cot_arrived = lax.optimization_barrier((slot_out, arrived, cot_arrived))
    returned = all_to_all(
        slot_out.reshape(experts, own_slots, width), rows_of_chips
    ).reshape(experts * own_slots, width)
    slot_probs = jax.nn.softmax(dot(arrived, w_router), axis=-1)
    own_expert = jnp.arange(experts, dtype=jnp.int32) == chip
    slot_weight = jnp.sum(jnp.where(own_expert[None, :], slot_probs, 0.0), axis=1, keepdims=True)
    slot_grad = (slot_weight * cot_arrived.astype(f32)).astype(bf16)
    (
        inner_own,
        inner_other,
        gate_own,
        gate_other,
        up_own,
        up_other,
        slot_in_grad,
    ) = expert_backward(arrived, slot_grad, gate_parts, up_parts, down_parts)
    slot_in_grad, returned, normed_planes, mixed_planes = lax.optimization_barrier(
        (slot_in_grad, returned, normed_planes, mixed_planes)
    )
    grads_back = all_to_all(
        slot_in_grad.reshape(experts, own_slots, width), rows_of_chips
    ).reshape(experts * own_slots, width)
    normed_planes = (normed_planes, swap(normed_planes))
    mixed_planes = mixed_planes.reshape(planes * seq_len, local_width)
    others = expert_weight_grads(arrived, slot_grad, inner_other, gate_other, up_other, (), bf16)

    pick_pairs = pick.reshape(experts, own_slots, seq_len)
    weighted = pick_pairs.astype(f32) * router_probs.T[:, None, :]
    weight_high, weight_low = halves(weighted.reshape(experts * own_slots, seq_len))
    moe_part = dot_rows(weight_high, returned) + dot_rows(weight_low, returned)
    moe_own, moe_other = moe_part[:own_rows], moe_part[own_rows:].astype(bf16)
    pair_products = dot_cols(returned, cot).reshape(experts, own_slots, seq_len)
    prob_part = jnp.sum(pair_products * pick_pairs.astype(f32), axis=1).T
    prob_grad = prob_part + other_order(swap(prob_part))
    logit_grad = router_probs * (
        prob_grad - jnp.sum(router_probs * prob_grad, axis=1, keepdims=True)
    )
    logit_high, logit_low = halves(logit_grad)
    router_grad = dot_rows(normed_moe, logit_high) + dot_rows(normed_moe, logit_low)
    (
        grads_back,
        others,
        moe_own,
        moe_other,
        logit_high,
        logit_low,
        router_grad,
    ) = lax.optimization_barrier(
        (grads_back, others, moe_own, moe_other, logit_high, logit_low, router_grad)
    )
    moe_own = moe_own + swap(moe_other).astype(f32)
    output = (hidden[:own_rows] + moe_own).astype(bf16)
    others = [swap(grad) for grad in others]
    grad_w_gate, grad_w_up, grad_w_down = expert_weight_grads(
        arrived, slot_grad, inner_own, gate_own, up_own, others, f32
    )
    moe_in_own, moe_in_other = token_sums(pick, grads_back)
    moe_in_grad = (
        moe_in_own
        + swap(moe_in_other)
        + dot_cols(logit_high[:own_rows], w_router)
        + dot_cols(logit_low[:own_rows], w_router)
    )
    cot_own = cotangent.astype(f32)
    hidden_own = hidden[:own_rows]
    scale_own = scale_moe[:own_rows]
    weighted_moe = moe_in_grad * gain_moe
    hidden_grad = (
        cot_own
        + scale_own * weighted_moe
        - hidden_own * scale_own**3 * jnp.mean(hidden_own * weighted_moe, axis=1, keepdims=True)
    )
    gain_moe_grad = jnp.sum(hidden_own * scale_own * moe_in_grad, axis=0)
    hidden_low_own = hidden_grad.astype(bf16)
    hidden_low_other = swap(hidden_low_own)
    low_planes = lax.all_gather(hidden_low_own, "z", axis=0, tiled=False)

    value_grad, query_part, key_part, gain_query_grad, gain_key_grad, inner = attention_backward(
        hidden_low_own,
        hidden_low_other,
        w_out,
        values,
        q_rot,
        k_rot,
        probs,
        queries,
        key_proj,
        query_gain,
        key_gain,
        query_scale,
        key_scale,
        cosine,
        sine,
        local_heads,
    )
    to_planes = projection_grads(
        query_part,
        key_part,
        queries,
        key_proj,
        value_grad,
        query_scale,
        key_scale,
        (inner, swap(inner)),
        planes,
    )

    grads_planes = all_to_all(to_planes, "z").reshape(planes * seq_len, 3 * quarter)
    grads_planes, low_planes = lax.optimization_barrier((grads_planes, low_planes))
    low_planes = (low_planes, swap(low_planes))
    normed_grad, normed_grad_other = normed_grad_of(to_planes, (w_query, w_key, w_value))
    normed_grad = normed_grad + swap(normed_grad_other)
    in_own = whole_in[:own_rows]
    in_scale = scale_attn[:own_rows]
    weighted_attn = normed_grad * gain_attn
    grad_input = (
        hidden_grad
        + in_scale * weighted_attn
        - in_own * in_scale**3 * jnp.mean(in_own * weighted_attn, axis=1, keepdims=True)
    )

    gain_moe_grad = gain_moe_grad + swap(gain_moe_grad)
    place = jnp.stack([lax.axis_index("z"), core])
    last_parcel = weight_parcel(
        place,
        normed_planes,
        grads_planes,
        router_grad.reshape(chips, out_rows, experts),
        gain_moe_grad[None],
        gain_query_grad,
        gain_key_grad,
        counts,
    )
    last_parcel = out_parcel(place, low_planes, mixed_planes, last_parcel)
    last_parcel = all_to_all(last_parcel, rows_of_chips)
    grad_w_query, grad_w_key, grad_w_value, grad_w_out, tail, attn_part = parcel_sums(
        chip[None],
        last_parcel,
        (w_query, w_key, w_value),
        planes,
        out_rows,
        local_width,
        out_rows // 2,
    )
    attn_half = attn_part.reshape(2, out_rows // 2)
    attn_mine = jnp.where(core == 0, attn_half[0], attn_half[1])
    attn_sum = attn_mine + swap(jnp.where(core == 0, attn_half[1], attn_half[0]))
    own_gain = lax.dynamic_slice_in_dim(
        gain_attn, chip * out_rows + core * (out_rows // 2), out_rows // 2
    )
    spare = lanes // 2
    per_chip = head_dim // chips
    grad_w_router = tail[:, :experts]
    tail = tail[:, spare:]
    gain_place = (chip * out_rows) % spare + core * (out_rows // 2)
    gain_moe_sum = lax.dynamic_slice_in_dim(tail[0] + tail[1], gain_place, out_rows // 2)
    lane_gains = (tail[2] + tail[3])[: 2 * local_heads * per_chip]
    lane_gains = jnp.transpose(lane_gains.reshape(per_chip, 2, local_heads), (1, 2, 0))
    return (
        output,
        grad_input,
        attn_sum / own_gain,
        grad_w_query,
        grad_w_key,
        grad_w_value,
        lane_gains[0],
        lane_gains[1],
        grad_w_out,
        gain_moe_sum,
        grad_w_router,
        grad_w_gate[None],
        grad_w_up[None],
        grad_w_down[None],
        tail[4, :1].astype(jnp.int32),
    )


def solution(mesh):
    side = round(mesh.shape["ep"] ** (1 / 3))
    cube = Mesh(mesh.devices.reshape(side, side, side, 2), rows_of_chips + ("tp",))
    ep = rows_of_chips
    both = rows_of_chips + ("tp",)
    in_specs = (
        P(both, None),
        P(ep, None),
        P(ep, None),
        P(),
        P(None, "tp"),
        P(None, "tp"),
        P(None, "tp"),
        P("tp", None),
        P("tp", None),
        P("tp", None),
        P(),
        P(),
        P(ep, None, "tp"),
        P(ep, None, "tp"),
        P(ep, "tp", None),
        P(both, None),
    )
    out_specs = (
        P(both, None),
        P(both, None),
        P(both),
        P(ep, "tp"),
        P(ep, "tp"),
        P(ep, "tp"),
        P("tp", ep),
        P("tp", ep),
        P("tp", ep),
        P(both),
        P(both, None),
        P(ep, None, "tp"),
        P(ep, None, "tp"),
        P(ep, "tp", None),
        P(ep),
    )
    return jax.shard_map(local, mesh=cube, in_specs=in_specs, out_specs=out_specs, check_vma=False)
```

```python
import jax
import jax.numpy as jnp
from jax import lax
from jax.experimental import pallas as pl
from jax.experimental.pallas import tpu as pltpu
from jax.sharding import Mesh, PartitionSpec as P

norm_eps = 1e-05
rope_base = 10000.0
mask_fill = -1e30
bf16 = jnp.bfloat16
f32 = jnp.float32
rows_of_chips = ("z", "x", "y")


def swap(value):
    return lax.ppermute(value, "tp", [(0, 1), (1, 0)])


def dot(left, right):
    return lax.dot_general(left, right, (((1,), (0,)), ((), ())), preferred_element_type=f32)


def dot_rows(left, right):
    return lax.dot_general(left, right, (((0,), (0,)), ((), ())), preferred_element_type=f32)


def dot_cols(left, right):
    return lax.dot_general(left, right, (((1,), (1,)), ((), ())), preferred_element_type=f32)


def all_to_all(value, axes):
    return lax.all_to_all(value, axes, split_axis=0, concat_axis=0, tiled=True)


def rms_scale(values):
    return lax.rsqrt(jnp.mean(values * values, axis=-1, keepdims=True) + norm_eps)


def halves(value):
    high = value.astype(bf16)
    return high, (value - high.astype(f32)).astype(bf16)


def rope_angles(positions, head_dim):
    half_dim = head_dim // 2
    exponent = jnp.arange(half_dim, dtype=f32) * (2.0 / head_dim)
    inverse = jnp.power(f32(rope_base), -exponent)
    angles = positions.astype(f32)[:, None] * inverse[None, :]
    return jnp.cos(angles), jnp.sin(angles)


lanes = 128
cheap = 64


def params(megabytes):
    return pltpu.CompilerParams(vmem_limit_bytes=megabytes * 1024 * 1024)


def turn(value, cosine, sine):
    return value * cosine + pltpu.roll(value, value.shape[1] // 2, 1) * sine


def other_order(ref):
    half = ref.shape[0] // 2
    return jnp.concatenate([ref[half:, :], ref[:half, :]], axis=0)


def attention_forward_body(
    scale,
    full_width,
    query_ref,
    key_ref,
    value_ref,
    query_gain_ref,
    key_gain_ref,
    squares_ref,
    other_squares_ref,
    cosine_ref,
    sine_ref,
    bias_ref,
    q_rot_ref,
    k_rot_ref,
    probs_ref,
    mixed_ref,
    parts_ref,
    scales_ref,
):
    cosine, sine, bias = cosine_ref[...], sine_ref[...], bias_ref[...]
    head = cosine.shape[1]
    squares = squares_ref[...] + other_order(other_squares_ref)
    scales = lax.rsqrt(squares * (1.0 / full_width) + norm_eps)
    scales_ref[...] = scales
    for h in range(probs_ref.shape[0]):
        here = slice(h * head, (h + 1) * head)
        query = query_ref[:, here] * scales[:, 0:1] * query_gain_ref[:, here]
        key = key_ref[:, here] * scales[:, 1:2] * key_gain_ref[:, here]
        q_rot = turn(query, cosine, sine).astype(bf16)
        k_rot = turn(key, cosine, sine).astype(bf16)
        q_rot_ref[:, here] = q_rot
        k_rot_ref[:, here] = k_rot
        scores = dot_cols(q_rot, k_rot) * scale + bias
        grown = jnp.exp(scores - jnp.max(scores, axis=1, keepdims=True))
        probs = grown / jnp.sum(grown, axis=1, keepdims=True)
        probs_ref[h] = probs
        mixed_ref[:, here] = dot(probs.astype(bf16), value_ref[:, here]).astype(bf16)
    part = parts_ref.shape[2]
    for k in range(parts_ref.shape[0]):
        parts_ref[k] = mixed_ref[:, k * part : (k + 1) * part]


def attention_forward(
    queries, keys, values, query_gain, key_gain, squares, other, cosine, sine, bias, heads, planes
):
    seq_len, width = queries.shape
    head = width // heads
    group = min(heads, 4)
    column = pl.BlockSpec((seq_len, group * head), lambda h: (0, h))
    gain = pl.BlockSpec((1, group * head), lambda h: (0, h))

    def whole(array):
        return pl.BlockSpec(array.shape, lambda h: (0, 0))

    return pl.pallas_call(
        lambda *refs: attention_forward_body(head**-0.5, 2 * width, *refs),
        grid=(heads // group,),
        in_specs=[column, column, column, gain, gain]
        + [whole(a) for a in (squares, other, cosine, sine, bias)],
        out_specs=[
            column,
            column,
            pl.BlockSpec((group, seq_len, seq_len), lambda h: (h, 0, 0)),
            column,
            pl.BlockSpec(
                (planes * group // heads, seq_len, width // planes), lambda h: (h, 0, 0)
            ),
            whole(squares),
        ],
        out_shape=[
            jax.ShapeDtypeStruct((seq_len, width), bf16),
            jax.ShapeDtypeStruct((seq_len, width), bf16),
            jax.ShapeDtypeStruct((heads, seq_len, seq_len), f32),
            jax.ShapeDtypeStruct((seq_len, width), bf16),
            jax.ShapeDtypeStruct((planes, seq_len, width // planes), bf16),
            jax.ShapeDtypeStruct((seq_len, 2), f32),
        ],
        compiler_params=params(16),
        cost_estimate=pl.CostEstimate(
            flops=4 * seq_len * seq_len * width // cheap,
            transcendentals=0,
            bytes_accessed=seq_len * width * 16 // cheap,
        ),
        name="attention_forward",
    )(queries, keys, values, query_gain, key_gain, squares, other, cosine, sine, bias)


def attention_backward_body(
    scale,
    hidden_own_ref,
    hidden_other_ref,
    w_out_ref,
    value_ref,
    q_rot_ref,
    k_rot_ref,
    probs_ref,
    query_ref,
    key_ref,
    query_gain_ref,
    key_gain_ref,
    scales_ref,
    cosine_ref,
    sine_ref,
    value_grad_ref,
    query_part_ref,
    key_part_ref,
    query_gain_grad_ref,
    key_gain_grad_ref,
    inner_ref,
):
    cosine, sine = cosine_ref[...], sine_ref[...]
    hidden = jnp.concatenate([hidden_own_ref[...], hidden_other_ref[...]], axis=0)
    heads, head = query_gain_grad_ref.shape[0], query_gain_grad_ref.shape[2]
    grad_mixed = dot_cols(hidden, w_out_ref[...]).astype(bf16)
    total = None
    for h in range(heads):
        here = slice(h * head, (h + 1) * head)
        grad = grad_mixed[:, here]
        probs = probs_ref[h]
        grad_probs = dot_cols(grad, value_ref[:, here])
        inner = jnp.sum(probs * grad_probs, axis=1, keepdims=True)
        grad_scores = (probs * (grad_probs - inner)).astype(bf16)
        value_grad_ref[:, here] = dot_rows(probs.astype(bf16), grad).astype(bf16)
        row_inners = []
        for k, (grad_rot, raw_ref, gain_ref, part_ref, gain_grad_ref) in enumerate(
            (
                (
                    dot(grad_scores, k_rot_ref[:, here]),
                    query_ref,
                    query_gain_ref,
                    query_part_ref,
                    query_gain_grad_ref,
                ),
                (
                    dot_rows(grad_scores, q_rot_ref[:, here]),
                    key_ref,
                    key_gain_ref,
                    key_part_ref,
                    key_gain_grad_ref,
                ),
            )
        ):
            grad_normed = turn(grad_rot * scale, cosine, -sine)
            raw = raw_ref[:, here]
            gain_grad_ref[h] = jnp.sum(
                raw * scales_ref[:, k : k + 1] * grad_normed, axis=0, keepdims=True
            )
            weighted = grad_normed * gain_ref[:, here]
            part_ref[:, here] = weighted
            row_inners.append(jnp.sum(raw * weighted, axis=1, keepdims=True))
        row_inner = jnp.concatenate(row_inners, axis=1)
        total = row_inner if total is None else total + row_inner
    first = pl.program_id(0) == 0

    @pl.when(first)
    def _():
        inner_ref[...] = total

    @pl.when(jnp.logical_not(first))
    def _():
        inner_ref[...] += total


def attention_backward(
    hidden_own,
    hidden_other,
    w_out,
    values,
    q_rot,
    k_rot,
    probs,
    queries,
    keys,
    query_gain,
    key_gain,
    scales,
    cosine,
    sine,
    heads,
):
    seq_len, width = queries.shape
    head = width // heads
    group = min(heads, 4)
    column = pl.BlockSpec((seq_len, group * head), lambda h: (0, h))
    gain = pl.BlockSpec((1, group * head), lambda h: (0, h))

    def whole(array):
        return pl.BlockSpec(array.shape, lambda h: (0, 0))

    full = jax.ShapeDtypeStruct((seq_len, width), f32)
    line = jax.ShapeDtypeStruct((heads, 1, head), f32)
    line_spec = pl.BlockSpec((group, 1, head), lambda h: (h, 0, 0))
    sums = jax.ShapeDtypeStruct((seq_len, 2), f32)
    return pl.pallas_call(
        lambda *refs: attention_backward_body(head**-0.5, *refs),
        grid=(heads // group,),
        in_specs=[
            whole(hidden_own),
            whole(hidden_other),
            pl.BlockSpec((group * head, w_out.shape[1]), lambda h: (h, 0)),
            column,
            column,
            column,
            pl.BlockSpec((group, seq_len, seq_len), lambda h: (h, 0, 0)),
            column,
            column,
            gain,
            gain,
        ]
        + [whole(a) for a in (scales, cosine, sine)],
        out_specs=[column, column, column, line_spec, line_spec, whole(sums)],
        out_shape=[
            jax.ShapeDtypeStruct((seq_len, width), bf16),
            full,
            full,
            line,
            line,
            sums,
        ],
        compiler_params=params(20),
        cost_estimate=pl.CostEstimate(
            flops=10 * seq_len * seq_len * width + 2 * seq_len * width * w_out.shape[1],
            transcendentals=0,
            bytes_accessed=seq_len * width * 28
            + heads * seq_len * seq_len * 4
            + 2 * w_out.size
            + 4 * hidden_own.size,
        ),
        name="attention_backward",
    )(
        hidden_own,
        hidden_other,
        w_out,
        values,
        q_rot,
        k_rot,
        probs,
        queries,
        keys,
        query_gain,
        key_gain,
        scales,
        cosine,
        sine,
    )


def projection_grads_body(
    width,
    query_part_ref,
    key_part_ref,
    query_ref,
    key_ref,
    value_grad_ref,
    scales_ref,
    inner_ref,
    other_inner_ref,
    stack_ref,
):
    blocks, _, columns = stack_ref.shape
    size = columns // 3
    inner = (inner_ref[...] + other_order(other_inner_ref)) * (1.0 / width)
    for k, (part_ref, raw_ref) in enumerate(
        ((query_part_ref, query_ref), (key_part_ref, key_ref))
    ):
        scale = scales_ref[:, k : k + 1]
        factor = scale * scale * scale * inner[:, k : k + 1]
        for block in range(blocks):
            here = slice(block * size, (block + 1) * size)
            grad = scale * part_ref[:, here] - raw_ref[:, here] * factor
            stack_ref[block, :, k * size : (k + 1) * size] = grad.astype(bf16)
    for block in range(blocks):
        stack_ref[block, :, 2 * size :] = value_grad_ref[:, block * size : (block + 1) * size]


def projection_grads(
    query_part, key_part, queries, keys, value_grad, scales, inners, planes
):
    seq_len, width = queries.shape
    size = width // planes
    steps = 2
    column = pl.BlockSpec((seq_len, width // steps), lambda k: (0, k))
    pair = pl.BlockSpec((seq_len, 2), lambda k: (0, 0))
    return pl.pallas_call(
        lambda *refs: projection_grads_body(2 * width, *refs),
        grid=(steps,),
        in_specs=[column] * 5 + [pair] * 3,
        out_specs=pl.BlockSpec((planes // steps, seq_len, 3 * size), lambda k: (k, 0, 0)),
        out_shape=jax.ShapeDtypeStruct((planes, seq_len, 3 * size), bf16),
        compiler_params=params(10),
        cost_estimate=pl.CostEstimate(
            flops=10 * seq_len * width, transcendentals=0, bytes_accessed=24 * seq_len * width
        ),
        name="projection_grads",
    )(query_part, key_part, queries, keys, value_grad, scales, *inners)


def expert_forward_body(
    rows_hbm,
    gate_own_hbm,
    gate_other_hbm,
    up_own_hbm,
    up_other_hbm,
    down_own_hbm,
    down_other_hbm,
    out_hbm,
    rows_ref,
    gate_ref,
    up_ref,
    down_ref,
    out_ref,
    in_sems,
    out_sems,
):
    count, width = rows_ref.shape
    pieces = 2
    size = count // pieces
    copies = {}
    order = [("rows", 0), ("gate", 0), ("up", 0), ("gate", 1), ("up", 1), ("down", 0), ("down", 1)]
    order += [("rows", k) for k in range(1, pieces)]
    sources = {
        "gate": ((gate_own_hbm, gate_other_hbm), gate_ref),
        "up": ((up_own_hbm, up_other_hbm), up_ref),
        "down": ((down_own_hbm, down_other_hbm), down_ref),
    }
    for number, (name, k) in enumerate(order):
        if name == "rows":
            here = pl.ds(k * size, size)
            copy = pltpu.make_async_copy(rows_hbm.at[here], rows_ref.at[here], in_sems.at[number])
        else:
            source, target = sources[name]
            copy = pltpu.make_async_copy(source[k], target.at[k], in_sems.at[number])
        copy.start()
        copies[name, k] = copy
    outs = []
    for piece in range(pieces):
        here = pl.ds(piece * size, size)
        copies["rows", piece].wait()
        inners = []
        for k in range(2):
            if piece == 0:
                copies["gate", k].wait()
            gate = dot(rows_ref[here, :], gate_ref[k])
            if piece == 0:
                copies["up", k].wait()
            up = dot(rows_ref[here, :], up_ref[k])
            inners.append((gate * jax.nn.sigmoid(gate) * up).astype(bf16))
        if piece == 0:
            copies["down", 0].wait()
            copies["down", 1].wait()
        step = min(512, width)
        for start in range(0, width, step):
            columns = pl.ds(start, step)
            total = dot(inners[0], down_ref[0, :, columns]) + dot(
                inners[1], down_ref[1, :, columns]
            )
            out_ref[here, columns] = total.astype(bf16)
        copy = pltpu.make_async_copy(out_ref.at[here], out_hbm.at[here], out_sems.at[piece])
        copy.start()
        outs.append(copy)
    for copy in outs:
        copy.wait()


def expert_specs(count, width, size):
    whole = pl.BlockSpec((count, width), lambda k: (0, 0), pipeline_mode=pl.Buffered(1))
    into = pl.BlockSpec((width, size), lambda k: (0, k))
    back = pl.BlockSpec((size, width), lambda k: (k, 0))
    return whole, into, back


def expert_forward(rows, gates, ups, downs):
    count, width = rows.shape
    units = gates[0].shape[1]
    return pl.pallas_call(
        expert_forward_body,
        in_specs=[pl.BlockSpec(memory_space=pl.ANY)] * 7,
        out_specs=pl.BlockSpec(memory_space=pl.ANY),
        out_shape=jax.ShapeDtypeStruct((count, width), bf16),
        scratch_shapes=[
            pltpu.VMEM((count, width), bf16),
            pltpu.VMEM((2, width, units), bf16),
            pltpu.VMEM((2, width, units), bf16),
            pltpu.VMEM((2, units, width), bf16),
            pltpu.VMEM((count, width), bf16),
            pltpu.SemaphoreType.DMA((8,)),
            pltpu.SemaphoreType.DMA((2,)),
        ],
        compiler_params=params(44),
        cost_estimate=pl.CostEstimate(
            flops=12 * count * width * units // cheap,
            transcendentals=0,
            bytes_accessed=(count * width * 4 + 12 * width * units) // cheap,
        ),
        name="expert_forward",
    )(rows, *gates, *ups, *downs)


def expert_backward_body(
    rows_ref,
    slot_grad_ref,
    gate_own_ref,
    gate_other_ref,
    up_own_ref,
    up_other_ref,
    down_own_ref,
    down_other_ref,
    inner_own_ref,
    inner_other_ref,
    gate_grad_own_ref,
    gate_grad_other_ref,
    up_grad_own_ref,
    up_grad_other_ref,
    out_ref,
    total_ref,
):
    step = pl.program_id(0)
    last = pl.num_programs(0) - 1
    for gate_ref, up_ref, down_ref, inner_ref, gate_grad_ref, up_grad_ref in (
        (gate_own_ref, up_own_ref, down_own_ref, inner_own_ref, gate_grad_own_ref, up_grad_own_ref),
        (
            gate_other_ref,
            up_other_ref,
            down_other_ref,
            inner_other_ref,
            gate_grad_other_ref,
            up_grad_other_ref,
        ),
    ):
        gate = dot(rows_ref[...], gate_ref[...])
        up = dot(rows_ref[...], up_ref[...])
        inner_grad = dot_cols(slot_grad_ref[...], down_ref[...])
        sigmoid_gate = jax.nn.sigmoid(gate)
        silu_gate = gate * sigmoid_gate
        inner_ref[...] = (silu_gate * up).astype(bf16)
        up_grad_ref[...] = (inner_grad * silu_gate).astype(bf16)
        gate_grad_ref[...] = (
            inner_grad * up * sigmoid_gate * (1.0 + gate * (1.0 - sigmoid_gate))
        ).astype(bf16)
    width = out_ref.shape[1]
    size = min(512, width)
    for start in range(0, width, size):
        here = pl.ds(start, size)
        part = None
        for grad_ref, w_ref in (
            (gate_grad_own_ref, gate_own_ref),
            (gate_grad_other_ref, gate_other_ref),
            (up_grad_own_ref, up_own_ref),
            (up_grad_other_ref, up_other_ref),
        ):
            term = dot_cols(grad_ref[...], w_ref[here, :])
            part = term if part is None else part + term

        @pl.when(step == 0)
        def _():
            total_ref[:, here] = part

        @pl.when((step > 0) & (step < last))
        def _():
            total_ref[:, here] += part

        @pl.when(step == last)
        def _():
            out_ref[:, here] = (total_ref[:, here] + part).astype(bf16)


def expert_backward(rows, slot_grad, gates, ups, downs):
    count, width = rows.shape
    units = gates[0].shape[1]
    steps = 2
    size = units // steps
    whole, into, back = expert_specs(count, width, size)
    acts = pl.BlockSpec((count, size), lambda k: (0, k))
    return pl.pallas_call(
        expert_backward_body,
        grid=(steps,),
        in_specs=[whole] * 2 + [into] * 4 + [back] * 2,
        out_specs=[acts] * 6 + [pl.BlockSpec((count, width), lambda k: (0, 0))],
        out_shape=[jax.ShapeDtypeStruct((count, units), bf16)] * 6
        + [jax.ShapeDtypeStruct((count, width), bf16)],
        scratch_shapes=[pltpu.VMEM((count, width), f32)],
        compiler_params=params(56),
        cost_estimate=pl.CostEstimate(
            flops=20 * count * width * units // cheap,
            transcendentals=0,
            bytes_accessed=count * width * 6 // cheap,
        ),
        name="expert_backward",
    )(rows, slot_grad, *gates, *ups, *downs)


def put_blocks(out_ref, row, product):
    chips = out_ref.shape[0]
    rows = product.shape[0] // chips
    for k in range(product.shape[1] // lanes):
        piece = product[:, k * lanes : (k + 1) * lanes].reshape(chips, rows, lanes)
        out_ref[:, row : row + rows, :] = piece
        row += rows
    return row


def joined(own_ref, other_ref):
    rows = jnp.concatenate([own_ref[...], other_ref[...]], axis=1)
    return rows.reshape(rows.shape[0] * rows.shape[1], rows.shape[2])


def weight_parcel_body(
    start,
    per_chip,
    place_ref,
    normed_ref,
    normed_other_ref,
    grads_ref,
    router_ref,
    moe_ref,
    moe_other_ref,
    query_gain_ref,
    key_gain_ref,
    counts_ref,
    out_ref,
):
    left = joined(normed_ref, normed_other_ref)
    put_blocks(out_ref, 0, dot_rows(left, grads_ref[...]).astype(bf16))

    chips, rows, spare = router_ref.shape[0], router_ref.shape[1] // 2, lanes // 2
    core = place_ref[1]
    router = router_ref[:, pl.ds(core * rows, rows), :]
    if router.shape[2] < spare:
        fill = jnp.zeros((chips, rows, spare - router.shape[2]), f32)
        router = jnp.concatenate([router, fill], axis=2)
    moe = moe_ref[...] + moe_other_ref[...]
    span = 2 * rows
    moe = jnp.concatenate([moe[:, k * span : (k + 1) * span] for k in range(chips)], axis=0)
    moe = jnp.where(core == 0, moe[:, :rows], moe[:, rows:])
    heads, head = query_gain_ref.shape[0], query_gain_ref.shape[2]
    chip = lax.broadcasted_iota(jnp.int32, (chips, heads, head), 0) + pl.program_id(0) * chips
    lane = lax.broadcasted_iota(jnp.int32, (chips, heads, head), 2)
    mine = lane // per_chip == chip
    feature = lax.broadcasted_iota(jnp.int32, (head, spare), 0) % per_chip
    column = lax.broadcasted_iota(jnp.int32, (head, spare), 1)
    first_row = lax.broadcasted_iota(jnp.int32, (chips, heads, spare), 1) == 0
    used = 2 * per_chip + rows + 1
    blocks = []
    for part in range(2):
        block = jnp.zeros((chips * heads, spare), f32)
        for k, gain_ref in enumerate((query_gain_ref, key_gain_ref)):
            values = halves(gain_ref[:, 0, :])[part].astype(f32)
            values = jnp.where(mine, values[None], 0.0).reshape(chips * heads, head).astype(bf16)
            target = jnp.where(column == feature + k * per_chip, 1.0, 0.0).astype(bf16)
            block = block + dot(values, target)
        moe_part = halves(moe)[part].astype(f32)
        count = counts_ref[...] if part == 0 else jnp.zeros((chips, 1), f32)
        vector = jnp.concatenate(
            [jnp.zeros((chips, 2 * per_chip), f32), moe_part, count]
            + [jnp.zeros((chips, spare - used), f32)] * (used < spare),
            axis=1,
        )
        block = block.reshape(chips, heads, spare)
        blocks.append(block + jnp.where(first_row, vector[:, None, :], 0.0))
        if heads < rows // 2:
            blocks.append(jnp.zeros((chips, rows // 2 - heads, spare), f32))
    beside = jnp.concatenate(blocks, axis=1)
    out_ref[:, start:, :] = jnp.concatenate([router, beside], axis=2).astype(bf16)


def weight_parcel(place, normed, grads, router, moe, query_gain, key_gain, counts):
    planes, half, width = normed[0].shape
    tokens, columns = grads.shape
    chips, router_rows, experts = router.shape
    heads, _, head = query_gain.shape
    start = width // chips * (columns + columns // 3) // lanes
    height = start + router_rows // 2
    steps = planes
    group = chips // steps
    left = pl.BlockSpec((planes, half, width // steps), lambda k, z: (0, 0, k))
    gain = pl.BlockSpec((heads, 1, head), lambda k, z: (0, 0, 0))
    return pl.pallas_call(
        lambda *refs: weight_parcel_body(start, head // chips, *refs),
        grid_spec=pltpu.PrefetchScalarGridSpec(
            num_scalar_prefetch=1,
            grid=(steps,),
            in_specs=[
                left,
                left,
                pl.BlockSpec((tokens, columns), lambda k, z: (0, 0)),
                pl.BlockSpec((group, router_rows, experts), lambda k, z: (k, 0, 0)),
                pl.BlockSpec((1, width // steps), lambda k, z: (0, k)),
                pl.BlockSpec((1, width // steps), lambda k, z: (0, k)),
                gain,
                gain,
                pl.BlockSpec((group, 1), lambda k, z: (k, 0)),
            ],
            out_specs=pl.BlockSpec((group, height, lanes), lambda k, z: (k, 0, 0)),
        ),
        out_shape=jax.ShapeDtypeStruct((chips, height, lanes), bf16),
        compiler_params=params(18),
        cost_estimate=pl.CostEstimate(
            flops=2 * tokens * width * columns,
            transcendentals=0,
            bytes_accessed=2 * (tokens * width + grads.size + chips * height * lanes),
        ),
        name="weight_parcel",
    )(place, *normed, grads, router, *moe, query_gain, key_gain, counts)


def out_parcel_body(place_ref, low_ref, low_other_ref, *refs):
    *mixed_refs, parcel_ref, out_ref = refs
    planes = len(mixed_refs)
    total = None
    for shift, mixed_ref in enumerate(mixed_refs):
        source = (place_ref[0] + planes - shift) % planes
        left = jnp.concatenate([low_ref[source], low_other_ref[source]], axis=0)
        part = dot_rows(left, mixed_ref[...])
        total = part if total is None else total + part
    put_blocks(out_ref, 0, total.astype(bf16))


def out_parcel(place, low, mixed, parcel):
    planes, half, width = low[0].shape
    tokens, part = mixed[0].shape
    chips, height, _ = parcel.shape
    room = width // chips * part // lanes
    steps = planes
    left = pl.BlockSpec((planes, half, width // steps), lambda k, z: (0, 0, k))
    return pl.pallas_call(
        out_parcel_body,
        grid_spec=pltpu.PrefetchScalarGridSpec(
            num_scalar_prefetch=1,
            grid=(steps,),
            in_specs=[left, left]
            + [pl.BlockSpec((tokens, part), lambda k, z: (0, 0))] * planes
            + [pl.BlockSpec(memory_space=pl.ANY)],
            out_specs=pl.BlockSpec((chips // steps, room, lanes), lambda k, z: (k, 3, 0)),
        ),
        out_shape=jax.ShapeDtypeStruct((chips, height, lanes), bf16),
        input_output_aliases={3 + planes: 0},
        compiler_params=params(14),
        cost_estimate=pl.CostEstimate(
            flops=2 * tokens * width * part // cheap,
            transcendentals=0,
            bytes_accessed=2 * (tokens * width + chips * room * lanes) // cheap,
        ),
        name="out_parcel",
    )(place, *low, *mixed, parcel)


def parcel_sums_body(
    per_chip,
    place_ref,
    parcel_ref,
    w_query_ref,
    w_key_ref,
    w_value_ref,
    own_gain_ref,
    query_ref,
    key_ref,
    value_ref,
    out_ref,
    router_ref,
    query_gain_ref,
    key_gain_ref,
    moe_ref,
    count_ref,
    attn_ref,
    attn_other_ref,
    extra_ref,
    gain_ref,
):
    total = jnp.sum(parcel_ref[...].astype(f32), axis=0)
    rows, columns = query_ref.shape
    row = 0
    gain = jnp.zeros((rows, lanes), f32)
    weights = (w_query_ref, w_key_ref, w_value_ref, None)
    for ref, w_ref in zip((query_ref, key_ref, value_ref, out_ref), weights):
        for k in range(columns // lanes):
            here = slice(k * lanes, (k + 1) * lanes)
            piece = total[row : row + rows, :]
            ref[:, here] = piece
            if w_ref is not None:
                gain = gain + piece * w_ref[:, here].astype(f32)
            row += rows
    step = pl.program_id(0)

    @pl.when(step == 0)
    def _():
        extra_ref[...] = total[row:, :]
        gain_ref[...] = gain

    @pl.when(step > 0)
    def _():
        extra_ref[...] += total[row:, :]
        gain_ref[...] += gain

    @pl.when(step == pl.num_programs(0) - 1)
    def _():
        half = rows // 2
        heads = query_gain_ref.shape[0]
        spare = lanes // 2
        router_ref[...] = extra_ref[:, : router_ref.shape[1]]
        sums = extra_ref[0:heads, spare:] + extra_ref[half // 2 : half // 2 + heads, spare:]
        query_gain_ref[...] = sums[:, :per_chip]
        key_gain_ref[...] = sums[:, per_chip : 2 * per_chip]
        moe_ref[...] = sums[0:1, 2 * per_chip : 2 * per_chip + half]
        count_ref[...] = sums[0:1, 2 * per_chip + half : 2 * per_chip + half + 1].astype(jnp.int32)
        attn = jnp.sum(gain_ref[...].T, axis=0, keepdims=True) / own_gain_ref[...]
        first = place_ref[1] == 0
        attn_ref[...] = jnp.where(first, attn[:, :half], attn[:, half:])
        attn_other_ref[...] = jnp.where(first, attn[:, half:], attn[:, :half])


def parcel_sums(place, parcel, weights, own_gain, planes, rows, width, heads, per_chip, experts):
    chips, height, _ = parcel.shape
    part = width // planes
    half = rows // 2
    wide = pl.BlockSpec((rows, part), lambda k, c: (0, k))

    def whole(shape):
        return pl.BlockSpec(shape, lambda k, c: (0, 0))

    small = [(half, experts), (heads, per_chip), (heads, per_chip), (1, half), (1, 1)]
    small += [(1, half), (1, half)]
    kinds = [f32] * 4 + [jnp.int32] + [f32] * 2
    return pl.pallas_call(
        lambda *refs: parcel_sums_body(per_chip, *refs),
        grid_spec=pltpu.PrefetchScalarGridSpec(
            num_scalar_prefetch=1,
            grid=(planes,),
            in_specs=[pl.BlockSpec((chips // planes, height, lanes), lambda k, c: (k, 0, 0))]
            + [pl.BlockSpec((rows, part), lambda k, c: (c[2], k))] * 3
            + [whole((1, rows))],
            out_specs=[wide] * 4 + [whole(shape) for shape in small],
            scratch_shapes=[pltpu.VMEM((half, lanes), f32), pltpu.VMEM((rows, lanes), f32)],
        ),
        out_shape=[jax.ShapeDtypeStruct((rows, width), f32)] * 4
        + [jax.ShapeDtypeStruct(shape, kind) for shape, kind in zip(small, kinds)],
        compiler_params=params(14),
        cost_estimate=pl.CostEstimate(
            flops=parcel.size, transcendentals=0, bytes_accessed=2 * parcel.size
        ),
        name="parcel_sums",
    )(place, parcel, *weights, own_gain)


def expert_weight_grads_body(rows_ref, slot_grad_ref, inner_ref, gate_ref, up_ref, *refs):
    grads = (
        dot_rows(rows_ref[...], gate_ref[...]),
        dot_rows(rows_ref[...], up_ref[...]),
        dot_rows(inner_ref[...], slot_grad_ref[...]),
    )
    others, outs = refs[:-3], refs[-3:]
    for k, (grad, out_ref) in enumerate(zip(grads, outs)):
        if others:
            grad = grad + others[k][...].astype(f32)
        out_ref[...] = grad.astype(out_ref.dtype)


def expert_weight_grads(rows, slot_grad, inner, gate_grad, up_grad, others, kind):
    count, width = rows.shape
    units = inner.shape[1]
    steps = 4
    size = width // steps
    wide = pl.BlockSpec((count, size), lambda k: (0, k))
    narrow = pl.BlockSpec((count, units), lambda k: (0, 0))
    into = pl.BlockSpec((size, units), lambda k: (k, 0))
    back = pl.BlockSpec((units, size), lambda k: (0, k))
    return pl.pallas_call(
        expert_weight_grads_body,
        grid=(steps,),
        in_specs=[wide, wide, narrow, narrow, narrow] + [into, into, back][: len(others)],
        out_specs=[into, into, back],
        out_shape=[
            jax.ShapeDtypeStruct((width, units), kind),
            jax.ShapeDtypeStruct((width, units), kind),
            jax.ShapeDtypeStruct((units, width), kind),
        ],
        compiler_params=params(30),
        cost_estimate=pl.CostEstimate(
            flops=6 * count * width * units // cheap,
            transcendentals=0,
            bytes_accessed=4 * count * width // cheap,
        ),
        name="expert_weight_grads",
    )(rows, slot_grad, inner, gate_grad, up_grad, *others)


def normed_grad_body(stack_ref, query_ref, key_ref, value_ref, own_ref, other_ref):
    size = query_ref.shape[1]
    total = None
    for k, w_ref in enumerate((query_ref, key_ref, value_ref)):
        part = dot_cols(stack_ref[:, k * size : (k + 1) * size], w_ref[...])
        total = part if total is None else total + part
    half = own_ref.shape[0]
    first = pl.program_id(0) == 0

    @pl.when(first)
    def _():
        own_ref[...] = total[:half]
        other_ref[...] = total[half:]

    @pl.when(jnp.logical_not(first))
    def _():
        own_ref[...] += total[:half]
        other_ref[...] += total[half:]


def normed_grad_of(stack, weights):
    planes, seq_len, columns = stack.shape
    size = columns // 3
    full = weights[0].shape[0]
    half = pl.BlockSpec((seq_len // 2, full), lambda k: (0, 0))
    return pl.pallas_call(
        normed_grad_body,
        grid=(planes,),
        in_specs=[pl.BlockSpec((None, seq_len, columns), lambda k: (k, 0, 0))]
        + [pl.BlockSpec((full, size), lambda k: (0, k))] * 3,
        out_specs=[half] * 2,
        out_shape=[jax.ShapeDtypeStruct((seq_len // 2, full), f32)] * 2,
        compiler_params=params(20),
        cost_estimate=pl.CostEstimate(
            flops=2 * stack.size * full // cheap,
            transcendentals=0,
            bytes_accessed=2 * planes * columns * full // cheap,
        ),
        name="normed_grad",
    )(stack, *weights)


def slot_rows_body(
    slots, place_ref, routes_ref, own_ref, other_ref, pick_ref, pick_back_ref, counts_ref, out_ref
):
    core = place_ref[1]
    experts = counts_ref.shape[0]
    half, seq_len = own_ref.shape[0], routes_ref.shape[0]

    @pl.when(pl.program_id(0) == 0)
    def _():
        routes = routes_ref[...]
        routes = jnp.where(
            core == 0, routes, jnp.concatenate([routes[half:, :], routes[:half, :]], axis=0)
        )
        numbers = lax.broadcasted_iota(jnp.int32, (seq_len, experts), 1)
        hits = numbers == routes[:, 0:1]
        for k in range(1, routes.shape[1]):
            hits = hits | (numbers == routes[:, k : k + 1])
        square = (seq_len, seq_len)
        shift = core * half
        place = lax.broadcasted_iota(jnp.int32, square, 0) + shift
        earlier = lax.broadcasted_iota(jnp.int32, square, 1) + shift
        place = jnp.where(place >= seq_len, place - seq_len, place)
        earlier = jnp.where(earlier >= seq_len, earlier - seq_len, earlier)
        before = jnp.where(earlier < place, 1.0, 0.0).astype(bf16)
        rank = dot(before, jnp.where(hits, 1.0, 0.0).astype(bf16))
        rank = jnp.where(hits, rank, -1.0)
        wide = (experts, experts * slots)
        spread = lax.broadcasted_iota(jnp.int32, wide, 1) // slots
        spread = spread == lax.broadcasted_iota(jnp.int32, wide, 0)
        spread_rank = dot(rank.astype(bf16), jnp.where(spread, 1.0, 0.0).astype(bf16))
        slot = lax.broadcasted_iota(jnp.int32, spread_rank.shape, 1) % slots + core * slots
        pick_back_ref[...] = jnp.where(spread_rank == slot.astype(f32), 1.0, 0.0).astype(bf16)
        rank = rank.T
        counts_ref[...] = jnp.sum(jnp.where(rank >= 0.0, 1.0, 0.0), axis=1, keepdims=True)
        slot = lax.broadcasted_iota(jnp.int32, (experts, slots, seq_len), 1) + core * slots
        pick = jnp.where(rank[:, None, :] == slot.astype(f32), 1.0, 0.0)
        pick_ref[...] = pick.reshape(experts * slots, seq_len).astype(bf16)

    rows = jnp.concatenate([own_ref[...], other_ref[...]], axis=0)
    out_ref[...] = dot(pick_ref[...], rows).astype(bf16)


def slot_rows(place, routes, own, other, experts, slots, columns):
    half = own.shape[0]
    seq_len, top_count = routes.shape
    steps = 2
    size = columns // steps
    rows = pl.BlockSpec((half, size), lambda k, c: (0, k))

    def whole(*shape):
        return pl.BlockSpec(shape, lambda k, c: (0, 0))

    return pl.pallas_call(
        lambda *refs: slot_rows_body(slots, *refs),
        grid_spec=pltpu.PrefetchScalarGridSpec(
            num_scalar_prefetch=1,
            grid=(steps,),
            in_specs=[whole(seq_len, top_count), rows, rows],
            out_specs=[
                whole(experts * slots, seq_len),
                whole(seq_len, experts * slots),
                whole(experts, 1),
                pl.BlockSpec((experts * slots, size), lambda k, c: (0, k)),
            ],
        ),
        out_shape=[
            jax.ShapeDtypeStruct((experts * slots, seq_len), bf16),
            jax.ShapeDtypeStruct((seq_len, experts * slots), bf16),
            jax.ShapeDtypeStruct((experts, 1), f32),
            jax.ShapeDtypeStruct((experts * slots, columns), bf16),
        ],
        compiler_params=params(20),
        cost_estimate=pl.CostEstimate(
            flops=2 * experts * slots * seq_len * columns,
            transcendentals=0,
            bytes_accessed=2 * (seq_len + experts * slots) * columns,
        ),
        name="slot_rows",
    )(place, routes, own, other)


def token_sums_body(pick_ref, rows_ref, own_ref, other_ref):
    total = dot(pick_ref[...], rows_ref[...])
    half = own_ref.shape[0]
    own_ref[...] = total[:half]
    other_ref[...] = total[half:]


def token_sums(pick_back, rows):
    seq_len, count = pick_back.shape
    width = rows.shape[1]
    steps = 2
    half = pl.BlockSpec((seq_len // 2, width // steps), lambda k: (0, k))
    return pl.pallas_call(
        token_sums_body,
        grid=(steps,),
        in_specs=[
            pl.BlockSpec((seq_len, count), lambda k: (0, 0)),
            pl.BlockSpec((count, width // steps), lambda k: (0, k)),
        ],
        out_specs=[half] * 2,
        out_shape=[jax.ShapeDtypeStruct((seq_len // 2, width), f32)] * 2,
        compiler_params=params(16),
        cost_estimate=pl.CostEstimate(
            flops=2 * count * seq_len * width,
            transcendentals=0,
            bytes_accessed=2 * count * (seq_len + width) + 4 * seq_len * width,
        ),
        name="token_sums",
    )(pick_back, rows)


def hidden_grad_body(
    own_ref,
    other_ref,
    logit_high_ref,
    logit_low_ref,
    w_router_ref,
    gain_ref,
    hidden_ref,
    scale_ref,
    cot_ref,
    grad_ref,
    low_ref,
    gain_grad_ref,
):
    w_router = w_router_ref[...]
    moe_in = own_ref[...] + other_ref[...]
    moe_in = moe_in + dot_cols(logit_high_ref[...], w_router)
    moe_in = moe_in + dot_cols(logit_low_ref[...], w_router)
    hidden, scale = hidden_ref[...], scale_ref[...]
    gain_grad_ref[...] = jnp.sum(hidden * scale * moe_in, axis=0, keepdims=True)
    weighted = moe_in * gain_ref[...]
    inner = jnp.mean(hidden * weighted, axis=1, keepdims=True)
    grad = cot_ref[...].astype(f32) + scale * weighted
    grad = grad - hidden * (scale * scale * scale * inner)
    grad_ref[...] = grad
    low_ref[...] = grad.astype(bf16)


def hidden_grad_of(own, other, logit_high, logit_low, w_router, gain, hidden, scale, cot):
    rows, width = own.shape
    return pl.pallas_call(
        hidden_grad_body,
        out_shape=[
            jax.ShapeDtypeStruct((rows, width), f32),
            jax.ShapeDtypeStruct((rows, width), bf16),
            jax.ShapeDtypeStruct((1, width), f32),
        ],
        compiler_params=params(16),
        cost_estimate=pl.CostEstimate(
            flops=20 * rows * width, transcendentals=0, bytes_accessed=20 * rows * width
        ),
        name="hidden_grad",
    )(own, other, logit_high, logit_low, w_router, gain, hidden, scale, cot)


def router_grad_body(normed_ref, high_ref, low_ref, out_ref):
    normed = normed_ref[...]
    out_ref[...] = dot_rows(normed, high_ref[...]) + dot_rows(normed, low_ref[...])


def router_grad_of(normed, high, low):
    return pl.pallas_call(
        router_grad_body,
        out_shape=jax.ShapeDtypeStruct((normed.shape[1], high.shape[1]), f32),
        compiler_params=params(10),
        cost_estimate=pl.CostEstimate(
            flops=1 << 20, transcendentals=0, bytes_accessed=normed.size
        ),
        name="router_grad",
    )(normed, high, low)


def projections_body(
    own_ref,
    other_ref,
    gain_ref,
    w_query_ref,
    w_key_ref,
    w_value_ref,
    normed_own_ref,
    normed_other_ref,
    scale_ref,
    query_ref,
    key_ref,
    value_ref,
    squares_ref,
    normed_ref,
):
    half = own_ref.shape[0]
    step = pl.program_id(0)

    @pl.when(step == 0)
    def _():
        for k, (ref, out_ref) in enumerate(
            ((own_ref, normed_own_ref), (other_ref, normed_other_ref))
        ):
            rows = ref[...].astype(f32)
            scale = rms_scale(rows)
            normed = (rows * scale * gain_ref[...]).astype(bf16)
            out_ref[...] = normed
            normed_ref[k * half : (k + 1) * half, :] = normed
            if k == 0:
                scale_ref[...] = scale

    normed = normed_ref[...]
    query = dot(normed, w_query_ref[...])
    key = dot(normed, w_key_ref[...])
    query_ref[...] = query
    key_ref[...] = key
    value_ref[...] = dot(normed, w_value_ref[...]).astype(bf16)
    squares = jnp.concatenate(
        [jnp.sum(v * v, axis=1, keepdims=True) for v in (query, key)], axis=1
    )

    @pl.when(step == 0)
    def _():
        squares_ref[...] = squares

    @pl.when(step > 0)
    def _():
        squares_ref[...] += squares


def projections(own, other, gain, weights):
    half, width = own.shape
    local_width = weights[0].shape[1]
    steps = 4
    size = local_width // steps

    def whole(*shape):
        return pl.BlockSpec(shape, lambda k: (0, 0))

    column = pl.BlockSpec((2 * half, size), lambda k: (0, k))
    return pl.pallas_call(
        projections_body,
        grid=(steps,),
        in_specs=[whole(half, width), whole(half, width), whole(1, width)]
        + [pl.BlockSpec((width, size), lambda k: (0, k))] * 3,
        out_specs=[whole(half, width)] * 2
        + [whole(half, 1), column, column, column, whole(2 * half, 2)],
        out_shape=[jax.ShapeDtypeStruct((half, width), bf16)] * 2
        + [jax.ShapeDtypeStruct((half, 1), f32)]
        + [jax.ShapeDtypeStruct((2 * half, local_width), kind) for kind in (f32, f32, bf16)]
        + [jax.ShapeDtypeStruct((2 * half, 2), f32)],
        scratch_shapes=[pltpu.VMEM((2 * half, width), bf16)],
        compiler_params=params(22),
        cost_estimate=pl.CostEstimate(
            flops=1 << 20, transcendentals=0, bytes_accessed=width * local_width // cheap
        ),
        name="projections",
    )(own, other, gain, *weights)


def branch_body(mixed_ref, w_ref, own_ref, other_ref):
    total = dot(mixed_ref[...], w_ref[...])
    half = own_ref.shape[0]
    own_ref[...] = total[:half]
    other_ref[...] = total[half:]


def branch_of(mixed, w_out):
    seq_len, local_width = mixed.shape
    width = w_out.shape[1]
    steps = 4
    half = pl.BlockSpec((seq_len // 2, width // steps), lambda k: (0, k))
    return pl.pallas_call(
        branch_body,
        grid=(steps,),
        in_specs=[
            pl.BlockSpec((seq_len, local_width), lambda k: (0, 0)),
            pl.BlockSpec((local_width, width // steps), lambda k: (0, k)),
        ],
        out_specs=[half] * 2,
        out_shape=[jax.ShapeDtypeStruct((seq_len // 2, width), f32)] * 2,
        compiler_params=params(12),
        cost_estimate=pl.CostEstimate(
            flops=1 << 20, transcendentals=0, bytes_accessed=width * local_width // cheap
        ),
        name="branch",
    )(mixed, w_out)


def moe_rows_body(
    own_ref,
    other_ref,
    branch_own_ref,
    branch_other_ref,
    got_own_ref,
    got_other_ref,
    gain_ref,
    w_router_ref,
    pick_ref,
    hidden_ref,
    scale_ref,
    normed_ref,
    probs_ref,
    out_ref,
):
    half = own_ref.shape[0]
    step = pl.program_id(0)

    @pl.when(step == 0)
    def _():
        for k, (ref, branch_ref, got_ref) in enumerate(
            ((own_ref, branch_own_ref, got_own_ref), (other_ref, branch_other_ref, got_other_ref))
        ):
            hidden = ref[...].astype(f32) + (branch_ref[...] + got_ref[...])
            scale = rms_scale(hidden)
            normed_ref[k * half : (k + 1) * half, :] = (hidden * scale * gain_ref[...]).astype(bf16)
            if k == 0:
                hidden_ref[...] = hidden
                scale_ref[...] = scale
        logits = dot(normed_ref[...], w_router_ref[...])
        grown = jnp.exp(logits - jnp.max(logits, axis=1, keepdims=True))
        probs_ref[...] = grown / jnp.sum(grown, axis=1, keepdims=True)

    size = out_ref.shape[1]
    columns = pl.ds(pl.multiple_of(step * size, size), size)
    out_ref[...] = dot(pick_ref[...], normed_ref[:, columns]).astype(bf16)


def moe_rows(own, other, branch, got, gain, w_router, pick):
    half, width = own.shape
    count, seq_len = pick.shape
    experts = w_router.shape[1]
    steps = 4

    def whole(*shape):
        return pl.BlockSpec(shape, lambda k: (0, 0), pipeline_mode=pl.Buffered(1))

    def kept(*shape):
        return pl.BlockSpec(shape, lambda k: (0, 0))

    return pl.pallas_call(
        moe_rows_body,
        grid=(steps,),
        in_specs=[whole(half, width)] * 6
        + [whole(1, width), whole(width, experts), whole(count, seq_len)],
        out_specs=[
            kept(half, width),
            kept(half, 1),
            kept(seq_len, width),
            kept(seq_len, experts),
            pl.BlockSpec((count, width // steps), lambda k: (0, k)),
        ],
        out_shape=[
            jax.ShapeDtypeStruct((half, width), f32),
            jax.ShapeDtypeStruct((half, 1), f32),
            jax.ShapeDtypeStruct((seq_len, width), bf16),
            jax.ShapeDtypeStruct((seq_len, experts), f32),
            jax.ShapeDtypeStruct((count, width), bf16),
        ],
        compiler_params=params(24),
        cost_estimate=pl.CostEstimate(
            flops=1 << 20, transcendentals=0, bytes_accessed=width * count // cheap
        ),
        name="moe_rows",
    )(own, other, *branch, *got, gain, w_router, pick)


def local(
    residual_in,
    routes,
    segment_ids,
    gain_attn,
    w_query,
    w_key,
    w_value,
    gain_query,
    gain_key,
    w_out,
    gain_moe,
    w_router,
    w_gate,
    w_up,
    w_down,
    cotangent,
):
    core = lax.axis_index("tp")
    planes = lax.axis_size("z")
    chips = lax.axis_size(rows_of_chips)
    chip = lax.axis_index(rows_of_chips)
    own_rows, width = residual_in.shape
    seq_len, top_count = routes.shape
    local_width = w_query.shape[1]
    local_heads, head_dim = gain_query.shape
    experts = chips
    capacity = seq_len * top_count // experts
    own_slots = capacity // 2
    quarter = local_width // planes
    out_rows = width // chips

    def own_first(value):
        return jnp.where(
            core == 0, value, jnp.concatenate([value[own_rows:], value[:own_rows]], axis=0)
        )

    first_columns = width * 5 // 8
    numbers = jnp.stack([lax.axis_index("z"), core, chip])
    cot_other = swap(cotangent)
    pick, pick_back, counts, cot_slots = slot_rows(
        numbers, routes, cotangent, cot_other, experts, own_slots, first_columns
    )
    cot_slots, residual_in, segment_ids = lax.optimization_barrier(
        (cot_slots, residual_in, segment_ids)
    )
    cot_first = all_to_all(
        cot_slots.reshape(experts, own_slots, first_columns), rows_of_chips
    ).reshape(experts * own_slots, first_columns)
    cot = jnp.concatenate([cotangent, cot_other], axis=0)

    place = own_first(jnp.arange(seq_len, dtype=jnp.int32))
    seg = own_first(segment_ids[0])
    same_doc = seg[:, None] == seg[None, :]
    position = place - jnp.min(jnp.where(same_doc, place[None, :], seq_len), axis=1)
    cosine, sine = rope_angles(position, head_dim)
    cosine = jnp.concatenate([cosine, cosine], axis=1)
    sine = jnp.concatenate([-sine, sine], axis=1)
    bias = jnp.where(same_doc & (place[None, :] <= place[:, None]), 0.0, mask_fill)

    other_in = swap(residual_in)
    normed_own, normed_other, scale_attn, queries, key_proj, values, squares = projections(
        residual_in, other_in, gain_attn[None], (w_query, w_key, w_value)
    )
    normed_planes = lax.all_gather(normed_own, "z", axis=0, tiled=False)
    query_gain = gain_query.reshape(1, local_width)
    key_gain = gain_key.reshape(1, local_width)
    q_rot, k_rot, probs, mixed, mixed_parts, scales = attention_forward(
        queries,
        key_proj,
        values,
        query_gain,
        key_gain,
        squares,
        swap(squares),
        cosine,
        sine,
        bias,
        local_heads,
        planes,
    )
    branch = branch_of(mixed, w_out)
    hidden_own, scale_moe, normed_moe, router_probs, moe_slots = moe_rows(
        residual_in,
        other_in,
        branch,
        (swap(branch[1]), swap(branch[0])),
        gain_moe[None],
        w_router,
        pick,
    )

    moe_slots, cot_first = lax.optimization_barrier((moe_slots, cot_first))
    arrived = all_to_all(
        moe_slots.reshape(experts, own_slots, width), rows_of_chips
    ).reshape(experts * own_slots, width)
    cot_slots = dot(pick, cot[:, first_columns:]).astype(bf16)
    arrived, cot_slots, normed_planes = lax.optimization_barrier(
        (arrived, cot_slots, normed_planes)
    )
    cot_rest = all_to_all(
        cot_slots.reshape(experts, own_slots, width - first_columns), rows_of_chips
    ).reshape(experts * own_slots, width - first_columns)

    gate_parts = (w_gate[0], swap(w_gate[0]))
    up_parts = (w_up[0], swap(w_up[0]))
    down_parts = (w_down[0], swap(w_down[0]))
    slot_out = expert_forward(arrived, gate_parts, up_parts, down_parts)
    slot_out, arrived, cot_rest = lax.optimization_barrier((slot_out, arrived, cot_rest))
    cot_arrived = jnp.concatenate([cot_first, cot_rest], axis=1)
    returned = all_to_all(
        slot_out.reshape(experts, own_slots, width), rows_of_chips
    ).reshape(experts * own_slots, width)
    slot_probs = jax.nn.softmax(dot(arrived, w_router), axis=-1)
    own_expert = jnp.arange(experts, dtype=jnp.int32) == chip
    slot_weight = jnp.sum(jnp.where(own_expert[None, :], slot_probs, 0.0), axis=1, keepdims=True)
    slot_grad = (slot_weight * cot_arrived.astype(f32)).astype(bf16)
    (
        inner_own,
        inner_other,
        gate_own,
        gate_other,
        up_own,
        up_other,
        slot_in_grad,
    ) = expert_backward(arrived, slot_grad, gate_parts, up_parts, down_parts)
    slot_in_grad, returned = lax.optimization_barrier((slot_in_grad, returned))
    grads_back = all_to_all(
        slot_in_grad.reshape(experts, own_slots, width), rows_of_chips
    ).reshape(experts * own_slots, width)
    normed_planes = (normed_planes, swap(normed_planes))
    plane = lax.axis_index("z")
    mixed_planes = [lax.dynamic_index_in_dim(mixed_parts, plane, 0, keepdims=False)]
    for shift in range(1, planes):
        part = lax.dynamic_index_in_dim(mixed_parts, (plane + shift) % planes, 0, keepdims=False)
        mixed_planes.append(
            lax.ppermute(part, "z", [(k, (k + shift) % planes) for k in range(planes)])
        )
    others = expert_weight_grads(arrived, slot_grad, inner_other, gate_other, up_other, (), bf16)

    pick_pairs = pick.reshape(experts, own_slots, seq_len)
    weighted = pick_pairs.astype(f32) * router_probs.T[:, None, :]
    weight_high, weight_low = halves(weighted.reshape(experts * own_slots, seq_len))
    moe_part = dot_rows(weight_high, returned) + dot_rows(weight_low, returned)
    moe_own, moe_other = moe_part[:own_rows], moe_part[own_rows:].astype(bf16)
    pair_products = dot_cols(returned, cot).reshape(experts, own_slots, seq_len)
    prob_part = jnp.sum(pair_products * pick_pairs.astype(f32), axis=1).T
    other_part = swap(prob_part)
    prob_grad = prob_part + jnp.concatenate([other_part[own_rows:], other_part[:own_rows]], axis=0)
    logit_grad = router_probs * (
        prob_grad - jnp.sum(router_probs * prob_grad, axis=1, keepdims=True)
    )
    logit_high, logit_low = halves(logit_grad)
    router_grad = router_grad_of(normed_moe, logit_high, logit_low)
    (
        grads_back,
        others,
        moe_own,
        moe_other,
        logit_high,
        logit_low,
        router_grad,
        mixed_planes,
    ) = lax.optimization_barrier(
        (
            grads_back,
            others,
            moe_own,
            moe_other,
            logit_high,
            logit_low,
            router_grad,
            mixed_planes,
        )
    )
    moe_own = moe_own + swap(moe_other).astype(f32)
    output = (hidden_own + moe_own).astype(bf16)
    others = [swap(grad) for grad in others]
    grad_w_gate, grad_w_up, grad_w_down = expert_weight_grads(
        arrived, slot_grad, inner_own, gate_own, up_own, others, f32
    )
    moe_in_own, moe_in_other = token_sums(pick_back, grads_back)
    hidden_grad, hidden_low_own, gain_moe_grad = hidden_grad_of(
        moe_in_own,
        swap(moe_in_other),
        logit_high[:own_rows],
        logit_low[:own_rows],
        w_router,
        gain_moe[None],
        hidden_own,
        scale_moe,
        cotangent,
    )
    hidden_low_other = swap(hidden_low_own)
    low_planes = lax.all_gather(hidden_low_own, "z", axis=0, tiled=False)

    value_grad, query_part, key_part, gain_query_grad, gain_key_grad, inner = attention_backward(
        hidden_low_own,
        hidden_low_other,
        w_out,
        values,
        q_rot,
        k_rot,
        probs,
        queries,
        key_proj,
        query_gain,
        key_gain,
        scales,
        cosine,
        sine,
        local_heads,
    )
    inner_other, gain_moe_other = lax.optimization_barrier((swap(inner), swap(gain_moe_grad)))
    to_planes = projection_grads(
        query_part,
        key_part,
        queries,
        key_proj,
        value_grad,
        scales,
        (inner, inner_other),
        planes,
    )

    grads_planes = all_to_all(to_planes, "z").reshape(planes * seq_len, 3 * quarter)
    grads_planes, low_planes = lax.optimization_barrier((grads_planes, low_planes))
    low_planes = (low_planes, swap(low_planes))
    normed_grad, normed_grad_other = normed_grad_of(to_planes, (w_query, w_key, w_value))
    normed_grad = normed_grad + swap(normed_grad_other)
    in_own = residual_in.astype(f32)
    in_scale = scale_attn
    weighted_attn = normed_grad * gain_attn
    grad_input = (
        hidden_grad
        + in_scale * weighted_attn
        - in_own * in_scale**3 * jnp.mean(in_own * weighted_attn, axis=1, keepdims=True)
    )

    parcel = weight_parcel(
        numbers,
        normed_planes,
        grads_planes,
        router_grad.reshape(chips, out_rows, experts),
        (gain_moe_grad, gain_moe_other),
        gain_query_grad,
        gain_key_grad,
        counts,
    )
    parcel = out_parcel(numbers, low_planes, mixed_planes, parcel)
    parcel = all_to_all(parcel, rows_of_chips)
    per_chip = head_dim // chips
    own_gain = lax.dynamic_slice_in_dim(gain_attn, chip * out_rows, out_rows)[None]
    (
        grad_w_query,
        grad_w_key,
        grad_w_value,
        grad_w_out,
        grad_w_router,
        grad_gain_query,
        grad_gain_key,
        grad_gain_moe,
        count,
        attn_own,
        attn_other,
    ) = parcel_sums(
        numbers,
        parcel,
        (w_query, w_key, w_value),
        own_gain,
        planes,
        out_rows,
        local_width,
        local_heads,
        per_chip,
        experts,
    )
    return (
        output,
        grad_input,
        (attn_own + swap(attn_other))[0],
        grad_w_query,
        grad_w_key,
        grad_w_value,
        grad_gain_query,
        grad_gain_key,
        grad_w_out.T,
        grad_gain_moe[0],
        grad_w_router,
        grad_w_gate[None],
        grad_w_up[None],
        grad_w_down[None],
        count[0],
    )


def solution(mesh):
    side = round(mesh.shape["ep"] ** (1 / 3))
    cube = Mesh(mesh.devices.reshape(side, side, side, 2), rows_of_chips + ("tp",))
    ep = rows_of_chips
    both = rows_of_chips + ("tp",)
    in_specs = (
        P(both, None),
        P(ep, None),
        P(ep, None),
        P(),
        P(None, "tp"),
        P(None, "tp"),
        P(None, "tp"),
        P("tp", None),
        P("tp", None),
        P("tp", None),
        P(),
        P(),
        P(ep, None, "tp"),
        P(ep, None, "tp"),
        P(ep, "tp", None),
        P(both, None),
    )
    out_specs = (
        P(both, None),
        P(both, None),
        P(both),
        P(ep, "tp"),
        P(ep, "tp"),
        P(ep, "tp"),
        P("tp", ep),
        P("tp", ep),
        P("tp", ep),
        P(both),
        P(both, None),
        P(ep, None, "tp"),
        P(ep, None, "tp"),
        P(ep, "tp", None),
        P(ep),
    )
    return jax.shard_map(local, mesh=cube, in_specs=in_specs, out_specs=out_specs, check_vma=False)
```

```python
import jax
import jax.numpy as jnp
from jax import lax
from jax.experimental import pallas as pl
from jax.experimental.pallas import tpu as pltpu
from jax.sharding import Mesh, PartitionSpec as P

norm_eps = 1e-05
rope_base = 10000.0
mask_fill = -1e30
bf16 = jnp.bfloat16
f32 = jnp.float32
rows_of_chips = ("z", "x", "y")


def swap(value):
    return lax.ppermute(value, "tp", [(0, 1), (1, 0)])


def dot(left, right):
    return lax.dot_general(left, right, (((1,), (0,)), ((), ())), preferred_element_type=f32)


def dot_rows(left, right):
    return lax.dot_general(left, right, (((0,), (0,)), ((), ())), preferred_element_type=f32)


def dot_cols(left, right):
    return lax.dot_general(left, right, (((1,), (1,)), ((), ())), preferred_element_type=f32)


def all_to_all(value, axes):
    return lax.all_to_all(value, axes, split_axis=0, concat_axis=0, tiled=True)


def rms_scale(values):
    return lax.rsqrt(jnp.mean(values * values, axis=-1, keepdims=True) + norm_eps)


def halves(value):
    high = value.astype(bf16)
    return high, (value - high.astype(f32)).astype(bf16)


def rope_angles(positions, head_dim):
    half_dim = head_dim // 2
    exponent = jnp.arange(half_dim, dtype=f32) * (2.0 / head_dim)
    inverse = jnp.power(f32(rope_base), -exponent)
    angles = positions.astype(f32)[:, None] * inverse[None, :]
    return jnp.cos(angles), jnp.sin(angles)


lanes = 128
cheap = 64


def in_hbm(*arrays):
    return [pltpu.with_memory_space_constraint(array, pltpu.HBM) for array in arrays]


def params(megabytes):
    return pltpu.CompilerParams(vmem_limit_bytes=megabytes * 1024 * 1024)


def turn(value, cosine, sine):
    return value * cosine + pltpu.roll(value, value.shape[1] // 2, 1) * sine


def other_order(ref):
    half = ref.shape[0] // 2
    return jnp.concatenate([ref[half:, :], ref[:half, :]], axis=0)


def attention_forward_body(
    scale,
    full_width,
    query_ref,
    key_ref,
    value_ref,
    query_gain_ref,
    key_gain_ref,
    squares_ref,
    other_squares_ref,
    cosine_ref,
    sine_ref,
    bias_ref,
    q_rot_ref,
    k_rot_ref,
    probs_ref,
    mixed_ref,
    parts_ref,
    scales_ref,
):
    cosine, sine, bias = cosine_ref[...], sine_ref[...], bias_ref[...]
    head = cosine.shape[1]
    squares = squares_ref[...] + other_order(other_squares_ref)
    scales = lax.rsqrt(squares * (1.0 / full_width) + norm_eps)
    scales_ref[...] = scales
    for h in range(probs_ref.shape[0]):
        here = slice(h * head, (h + 1) * head)
        query = query_ref[:, here] * scales[:, 0:1] * query_gain_ref[:, here]
        key = key_ref[:, here] * scales[:, 1:2] * key_gain_ref[:, here]
        q_rot = turn(query, cosine, sine).astype(bf16)
        k_rot = turn(key, cosine, sine).astype(bf16)
        q_rot_ref[:, here] = q_rot
        k_rot_ref[:, here] = k_rot
        scores = dot_cols(q_rot, k_rot) * scale + bias
        grown = jnp.exp(scores - jnp.max(scores, axis=1, keepdims=True))
        probs = grown / jnp.sum(grown, axis=1, keepdims=True)
        probs_ref[h] = probs
        mixed_ref[:, here] = dot(probs.astype(bf16), value_ref[:, here]).astype(bf16)
    part = parts_ref.shape[2]
    for k in range(parts_ref.shape[0]):
        parts_ref[k] = mixed_ref[:, k * part : (k + 1) * part]


def attention_forward(
    queries, keys, values, query_gain, key_gain, squares, other, cosine, sine, bias, heads, planes
):
    seq_len, width = queries.shape
    head = width // heads
    group = min(heads, 4)
    column = pl.BlockSpec((seq_len, group * head), lambda h: (0, h))
    gain = pl.BlockSpec((1, group * head), lambda h: (0, h))

    def whole(array):
        return pl.BlockSpec(array.shape, lambda h: (0, 0))

    return pl.pallas_call(
        lambda *refs: attention_forward_body(head**-0.5, 2 * width, *refs),
        grid=(heads // group,),
        in_specs=[column, column, column, gain, gain]
        + [whole(a) for a in (squares, other, cosine, sine, bias)],
        out_specs=[
            column,
            column,
            pl.BlockSpec((group, seq_len, seq_len), lambda h: (h, 0, 0)),
            column,
            pl.BlockSpec(
                (planes * group // heads, seq_len, width // planes), lambda h: (h, 0, 0)
            ),
            whole(squares),
        ],
        out_shape=[
            jax.ShapeDtypeStruct((seq_len, width), bf16),
            jax.ShapeDtypeStruct((seq_len, width), bf16),
            jax.ShapeDtypeStruct((heads, seq_len, seq_len), f32),
            jax.ShapeDtypeStruct((seq_len, width), bf16),
            jax.ShapeDtypeStruct((planes, seq_len, width // planes), bf16),
            jax.ShapeDtypeStruct((seq_len, 2), f32),
        ],
        compiler_params=params(16),
        cost_estimate=pl.CostEstimate(
            flops=4 * seq_len * seq_len * width // cheap,
            transcendentals=0,
            bytes_accessed=seq_len * width * 16 // cheap,
        ),
        name="attention_forward",
    )(queries, keys, values, query_gain, key_gain, squares, other, cosine, sine, bias)


def attention_backward_body(
    scale,
    hidden_own_ref,
    hidden_other_ref,
    w_out_ref,
    value_ref,
    q_rot_ref,
    k_rot_ref,
    probs_ref,
    query_ref,
    key_ref,
    query_gain_ref,
    key_gain_ref,
    scales_ref,
    cosine_ref,
    sine_ref,
    value_grad_ref,
    query_part_ref,
    key_part_ref,
    query_gain_grad_ref,
    key_gain_grad_ref,
    inner_ref,
):
    cosine, sine = cosine_ref[...], sine_ref[...]
    hidden = jnp.concatenate([hidden_own_ref[...], hidden_other_ref[...]], axis=0)
    heads, head = query_gain_grad_ref.shape[0], query_gain_grad_ref.shape[2]
    grad_mixed = dot_cols(hidden, w_out_ref[...]).astype(bf16)
    total = None
    for h in range(heads):
        here = slice(h * head, (h + 1) * head)
        grad = grad_mixed[:, here]
        probs = probs_ref[h]
        grad_probs = dot_cols(grad, value_ref[:, here])
        inner = jnp.sum(probs * grad_probs, axis=1, keepdims=True)
        grad_scores = (probs * (grad_probs - inner)).astype(bf16)
        value_grad_ref[:, here] = dot_rows(probs.astype(bf16), grad).astype(bf16)
        row_inners = []
        for k, (grad_rot, raw_ref, gain_ref, part_ref, gain_grad_ref) in enumerate(
            (
                (
                    dot(grad_scores, k_rot_ref[:, here]),
                    query_ref,
                    query_gain_ref,
                    query_part_ref,
                    query_gain_grad_ref,
                ),
                (
                    dot_rows(grad_scores, q_rot_ref[:, here]),
                    key_ref,
                    key_gain_ref,
                    key_part_ref,
                    key_gain_grad_ref,
                ),
            )
        ):
            grad_normed = turn(grad_rot * scale, cosine, -sine)
            raw = raw_ref[:, here]
            gain_grad_ref[h] = jnp.sum(
                raw * scales_ref[:, k : k + 1] * grad_normed, axis=0, keepdims=True
            )
            weighted = grad_normed * gain_ref[:, here]
            part_ref[:, here] = weighted
            row_inners.append(jnp.sum(raw * weighted, axis=1, keepdims=True))
        row_inner = jnp.concatenate(row_inners, axis=1)
        total = row_inner if total is None else total + row_inner
    first = pl.program_id(0) == 0

    @pl.when(first)
    def _():
        inner_ref[...] = total

    @pl.when(jnp.logical_not(first))
    def _():
        inner_ref[...] += total


def attention_backward(
    hidden_own,
    hidden_other,
    w_out,
    values,
    q_rot,
    k_rot,
    probs,
    queries,
    keys,
    query_gain,
    key_gain,
    scales,
    cosine,
    sine,
    heads,
):
    seq_len, width = queries.shape
    head = width // heads
    group = min(heads, 4)
    column = pl.BlockSpec((seq_len, group * head), lambda h: (0, h))
    gain = pl.BlockSpec((1, group * head), lambda h: (0, h))

    def whole(array):
        return pl.BlockSpec(array.shape, lambda h: (0, 0))

    full = jax.ShapeDtypeStruct((seq_len, width), f32)
    line = jax.ShapeDtypeStruct((heads, 1, head), f32)
    line_spec = pl.BlockSpec((group, 1, head), lambda h: (h, 0, 0))
    sums = jax.ShapeDtypeStruct((seq_len, 2), f32)
    return pl.pallas_call(
        lambda *refs: attention_backward_body(head**-0.5, *refs),
        grid=(heads // group,),
        in_specs=[
            whole(hidden_own),
            whole(hidden_other),
            pl.BlockSpec((group * head, w_out.shape[1]), lambda h: (h, 0)),
            column,
            column,
            column,
            pl.BlockSpec((group, seq_len, seq_len), lambda h: (h, 0, 0)),
            column,
            column,
            gain,
            gain,
        ]
        + [whole(a) for a in (scales, cosine, sine)],
        out_specs=[column, column, column, line_spec, line_spec, whole(sums)],
        out_shape=[
            jax.ShapeDtypeStruct((seq_len, width), bf16),
            full,
            full,
            line,
            line,
            sums,
        ],
        compiler_params=params(20),
        cost_estimate=pl.CostEstimate(
            flops=10 * seq_len * seq_len * width + 2 * seq_len * width * w_out.shape[1],
            transcendentals=0,
            bytes_accessed=seq_len * width * 28
            + heads * seq_len * seq_len * 4
            + 2 * w_out.size
            + 4 * hidden_own.size,
        ),
        name="attention_backward",
    )(
        *in_hbm(hidden_own, hidden_other, w_out, values, q_rot, k_rot, probs, queries, keys),
        query_gain,
        key_gain,
        scales,
        cosine,
        sine,
    )


def projection_grads_body(
    width,
    query_part_ref,
    key_part_ref,
    query_ref,
    key_ref,
    value_grad_ref,
    scales_ref,
    inner_ref,
    other_inner_ref,
    stack_ref,
):
    blocks, _, columns = stack_ref.shape
    size = columns // 3
    inner = (inner_ref[...] + other_order(other_inner_ref)) * (1.0 / width)
    for k, (part_ref, raw_ref) in enumerate(
        ((query_part_ref, query_ref), (key_part_ref, key_ref))
    ):
        scale = scales_ref[:, k : k + 1]
        factor = scale * scale * scale * inner[:, k : k + 1]
        for block in range(blocks):
            here = slice(block * size, (block + 1) * size)
            grad = scale * part_ref[:, here] - raw_ref[:, here] * factor
            stack_ref[block, :, k * size : (k + 1) * size] = grad.astype(bf16)
    for block in range(blocks):
        stack_ref[block, :, 2 * size :] = value_grad_ref[:, block * size : (block + 1) * size]


def projection_grads(
    query_part, key_part, queries, keys, value_grad, scales, inners, planes
):
    seq_len, width = queries.shape
    size = width // planes
    steps = 2
    column = pl.BlockSpec((seq_len, width // steps), lambda k: (0, k))
    pair = pl.BlockSpec((seq_len, 2), lambda k: (0, 0))
    return pl.pallas_call(
        lambda *refs: projection_grads_body(2 * width, *refs),
        grid=(steps,),
        in_specs=[column] * 5 + [pair] * 3,
        out_specs=pl.BlockSpec((planes // steps, seq_len, 3 * size), lambda k: (k, 0, 0)),
        out_shape=jax.ShapeDtypeStruct((planes, seq_len, 3 * size), bf16),
        compiler_params=params(10),
        cost_estimate=pl.CostEstimate(
            flops=10 * seq_len * width, transcendentals=0, bytes_accessed=24 * seq_len * width
        ),
        name="projection_grads",
    )(query_part, key_part, queries, keys, value_grad, scales, *inners)


def expert_forward_body(
    rows_hbm,
    gate_own_hbm,
    gate_other_hbm,
    up_own_hbm,
    up_other_hbm,
    down_own_hbm,
    down_other_hbm,
    out_hbm,
    rows_ref,
    gate_ref,
    up_ref,
    down_ref,
    out_ref,
    in_sems,
    out_sems,
):
    count, width = rows_ref.shape
    pieces = 2
    size = count // pieces
    copies = {}
    order = [("rows", 0), ("gate", 0), ("up", 0), ("gate", 1), ("up", 1), ("down", 0), ("down", 1)]
    order += [("rows", k) for k in range(1, pieces)]
    sources = {
        "gate": ((gate_own_hbm, gate_other_hbm), gate_ref),
        "up": ((up_own_hbm, up_other_hbm), up_ref),
        "down": ((down_own_hbm, down_other_hbm), down_ref),
    }
    for number, (name, k) in enumerate(order):
        if name == "rows":
            here = pl.ds(k * size, size)
            copy = pltpu.make_async_copy(rows_hbm.at[here], rows_ref.at[here], in_sems.at[number])
        else:
            source, target = sources[name]
            copy = pltpu.make_async_copy(source[k], target.at[k], in_sems.at[number])
        copy.start()
        copies[name, k] = copy
    outs = []
    for piece in range(pieces):
        here = pl.ds(piece * size, size)
        copies["rows", piece].wait()
        inners = []
        for k in range(2):
            if piece == 0:
                copies["gate", k].wait()
            gate = dot(rows_ref[here, :], gate_ref[k])
            if piece == 0:
                copies["up", k].wait()
            up = dot(rows_ref[here, :], up_ref[k])
            inners.append((gate * jax.nn.sigmoid(gate) * up).astype(bf16))
        if piece == 0:
            copies["down", 0].wait()
            copies["down", 1].wait()
        step = min(512, width)
        for start in range(0, width, step):
            columns = pl.ds(start, step)
            total = dot(inners[0], down_ref[0, :, columns]) + dot(
                inners[1], down_ref[1, :, columns]
            )
            out_ref[here, columns] = total.astype(bf16)
        copy = pltpu.make_async_copy(out_ref.at[here], out_hbm.at[here], out_sems.at[piece])
        copy.start()
        outs.append(copy)
    for copy in outs:
        copy.wait()


def expert_specs(count, width, size):
    whole = pl.BlockSpec((count, width), lambda k: (0, 0), pipeline_mode=pl.Buffered(1))
    into = pl.BlockSpec((width, size), lambda k: (0, k))
    back = pl.BlockSpec((size, width), lambda k: (k, 0))
    return whole, into, back


def expert_forward(rows, gates, ups, downs):
    count, width = rows.shape
    units = gates[0].shape[1]
    return pl.pallas_call(
        expert_forward_body,
        in_specs=[pl.BlockSpec(memory_space=pl.ANY)] * 7,
        out_specs=pl.BlockSpec(memory_space=pl.ANY),
        out_shape=pltpu.HBM((count, width), bf16),
        scratch_shapes=[
            pltpu.VMEM((count, width), bf16),
            pltpu.VMEM((2, width, units), bf16),
            pltpu.VMEM((2, width, units), bf16),
            pltpu.VMEM((2, units, width), bf16),
            pltpu.VMEM((count, width), bf16),
            pltpu.SemaphoreType.DMA((8,)),
            pltpu.SemaphoreType.DMA((2,)),
        ],
        compiler_params=params(44),
        cost_estimate=pl.CostEstimate(
            flops=12 * count * width * units // cheap,
            transcendentals=0,
            bytes_accessed=(count * width * 4 + 12 * width * units) // cheap,
        ),
        name="expert_forward",
    )(*in_hbm(rows, *gates, *ups, *downs))


def expert_backward_body(
    rows_ref,
    slot_grad_ref,
    gate_own_ref,
    gate_other_ref,
    up_own_ref,
    up_other_ref,
    down_own_ref,
    down_other_ref,
    inner_own_ref,
    inner_other_ref,
    gate_grad_own_ref,
    gate_grad_other_ref,
    up_grad_own_ref,
    up_grad_other_ref,
    out_ref,
    total_ref,
):
    step = pl.program_id(0)
    last = pl.num_programs(0) - 1
    for gate_ref, up_ref, down_ref, inner_ref, gate_grad_ref, up_grad_ref in (
        (gate_own_ref, up_own_ref, down_own_ref, inner_own_ref, gate_grad_own_ref, up_grad_own_ref),
        (
            gate_other_ref,
            up_other_ref,
            down_other_ref,
            inner_other_ref,
            gate_grad_other_ref,
            up_grad_other_ref,
        ),
    ):
        gate = dot(rows_ref[...], gate_ref[...])
        up = dot(rows_ref[...], up_ref[...])
        inner_grad = dot_cols(slot_grad_ref[...], down_ref[...])
        sigmoid_gate = jax.nn.sigmoid(gate)
        silu_gate = gate * sigmoid_gate
        inner_ref[...] = (silu_gate * up).astype(bf16)
        up_grad_ref[...] = (inner_grad * silu_gate).astype(bf16)
        gate_grad_ref[...] = (
            inner_grad * up * sigmoid_gate * (1.0 + gate * (1.0 - sigmoid_gate))
        ).astype(bf16)
    width = out_ref.shape[1]
    size = min(512, width)
    for start in range(0, width, size):
        here = pl.ds(start, size)
        part = None
        for grad_ref, w_ref in (
            (gate_grad_own_ref, gate_own_ref),
            (gate_grad_other_ref, gate_other_ref),
            (up_grad_own_ref, up_own_ref),
            (up_grad_other_ref, up_other_ref),
        ):
            term = dot_cols(grad_ref[...], w_ref[here, :])
            part = term if part is None else part + term

        @pl.when(step == 0)
        def _():
            total_ref[:, here] = part

        @pl.when((step > 0) & (step < last))
        def _():
            total_ref[:, here] += part

        @pl.when(step == last)
        def _():
            out_ref[:, here] = (total_ref[:, here] + part).astype(bf16)


def expert_backward(rows, slot_grad, gates, ups, downs):
    count, width = rows.shape
    units = gates[0].shape[1]
    steps = 2
    size = units // steps
    whole, into, back = expert_specs(count, width, size)
    acts = pl.BlockSpec((count, size), lambda k: (0, k))
    return pl.pallas_call(
        expert_backward_body,
        grid=(steps,),
        in_specs=[whole] * 2 + [into] * 4 + [back] * 2,
        out_specs=[acts] * 6 + [pl.BlockSpec((count, width), lambda k: (0, 0))],
        out_shape=[jax.ShapeDtypeStruct((count, units), bf16)] * 6
        + [jax.ShapeDtypeStruct((count, width), bf16)],
        scratch_shapes=[pltpu.VMEM((count, width), f32)],
        compiler_params=params(56),
        cost_estimate=pl.CostEstimate(
            flops=20 * count * width * units // cheap,
            transcendentals=0,
            bytes_accessed=count * width * 6 // cheap,
        ),
        name="expert_backward",
    )(rows, slot_grad, *gates, *ups, *downs)


def put_blocks(out_ref, row, product):
    chips = out_ref.shape[0]
    rows = product.shape[0] // chips
    for k in range(product.shape[1] // lanes):
        piece = product[:, k * lanes : (k + 1) * lanes].reshape(chips, rows, lanes)
        out_ref[:, row : row + rows, :] = piece
        row += rows
    return row


def joined(own_ref, other_ref):
    rows = jnp.concatenate([own_ref[...], other_ref[...]], axis=1)
    return rows.reshape(rows.shape[0] * rows.shape[1], rows.shape[2])


def weight_parcel_body(
    start,
    per_chip,
    place_ref,
    normed_ref,
    normed_other_ref,
    grads_ref,
    router_ref,
    moe_ref,
    moe_other_ref,
    query_gain_ref,
    key_gain_ref,
    counts_ref,
    out_ref,
):
    left = joined(normed_ref, normed_other_ref)
    put_blocks(out_ref, 0, dot_rows(left, grads_ref[...]).astype(bf16))

    chips, rows, spare = router_ref.shape[0], router_ref.shape[1] // 2, lanes // 2
    core = place_ref[1]
    router = router_ref[:, pl.ds(core * rows, rows), :]
    if router.shape[2] < spare:
        fill = jnp.zeros((chips, rows, spare - router.shape[2]), f32)
        router = jnp.concatenate([router, fill], axis=2)
    moe = moe_ref[...] + moe_other_ref[...]
    span = 2 * rows
    moe = jnp.concatenate([moe[:, k * span : (k + 1) * span] for k in range(chips)], axis=0)
    moe = jnp.where(core == 0, moe[:, :rows], moe[:, rows:])
    heads, head = query_gain_ref.shape[0], query_gain_ref.shape[2]
    chip = lax.broadcasted_iota(jnp.int32, (chips, heads, head), 0) + pl.program_id(0) * chips
    lane = lax.broadcasted_iota(jnp.int32, (chips, heads, head), 2)
    mine = lane // per_chip == chip
    feature = lax.broadcasted_iota(jnp.int32, (head, spare), 0) % per_chip
    column = lax.broadcasted_iota(jnp.int32, (head, spare), 1)
    first_row = lax.broadcasted_iota(jnp.int32, (chips, heads, spare), 1) == 0
    used = 2 * per_chip + rows + 1
    blocks = []
    for part in range(2):
        block = jnp.zeros((chips * heads, spare), f32)
        for k, gain_ref in enumerate((query_gain_ref, key_gain_ref)):
            values = halves(gain_ref[:, 0, :])[part].astype(f32)
            values = jnp.where(mine, values[None], 0.0).reshape(chips * heads, head).astype(bf16)
            target = jnp.where(column == feature + k * per_chip, 1.0, 0.0).astype(bf16)
            block = block + dot(values, target)
        moe_part = halves(moe)[part].astype(f32)
        count = counts_ref[...] if part == 0 else jnp.zeros((chips, 1), f32)
        vector = jnp.concatenate(
            [jnp.zeros((chips, 2 * per_chip), f32), moe_part, count]
            + [jnp.zeros((chips, spare - used), f32)] * (used < spare),
            axis=1,
        )
        block = block.reshape(chips, heads, spare)
        blocks.append(block + jnp.where(first_row, vector[:, None, :], 0.0))
        if heads < rows // 2:
            blocks.append(jnp.zeros((chips, rows // 2 - heads, spare), f32))
    beside = jnp.concatenate(blocks, axis=1)
    out_ref[:, start:, :] = jnp.concatenate([router, beside], axis=2).astype(bf16)


def weight_parcel(place, normed, grads, router, moe, query_gain, key_gain, counts):
    planes, half, width = normed[0].shape
    tokens, columns = grads.shape
    chips, router_rows, experts = router.shape
    heads, _, head = query_gain.shape
    start = width // chips * (columns + columns // 3) // lanes
    height = start + router_rows // 2
    steps = planes
    group = chips // steps
    left = pl.BlockSpec((planes, half, width // steps), lambda k, z: (0, 0, k))
    gain = pl.BlockSpec((heads, 1, head), lambda k, z: (0, 0, 0))
    return pl.pallas_call(
        lambda *refs: weight_parcel_body(start, head // chips, *refs),
        grid_spec=pltpu.PrefetchScalarGridSpec(
            num_scalar_prefetch=1,
            grid=(steps,),
            in_specs=[
                left,
                left,
                pl.BlockSpec((tokens, columns), lambda k, z: (0, 0)),
                pl.BlockSpec((group, router_rows, experts), lambda k, z: (k, 0, 0)),
                pl.BlockSpec((1, width // steps), lambda k, z: (0, k)),
                pl.BlockSpec((1, width // steps), lambda k, z: (0, k)),
                gain,
                gain,
                pl.BlockSpec((group, 1), lambda k, z: (k, 0)),
            ],
            out_specs=pl.BlockSpec((group, height, lanes), lambda k, z: (k, 0, 0)),
        ),
        out_shape=pltpu.HBM((chips, height, lanes), bf16),
        compiler_params=params(18),
        cost_estimate=pl.CostEstimate(
            flops=2 * tokens * width * columns,
            transcendentals=0,
            bytes_accessed=2 * (tokens * width + grads.size + chips * height * lanes),
        ),
        name="weight_parcel",
    )(place, *in_hbm(*normed, grads, router), *moe, query_gain, key_gain, counts)


def out_parcel_body(place_ref, low_ref, low_other_ref, *refs):
    *mixed_refs, parcel_ref, out_ref = refs
    planes = len(mixed_refs)
    total = None
    for shift, mixed_ref in enumerate(mixed_refs):
        source = (place_ref[0] + planes - shift) % planes
        left = jnp.concatenate([low_ref[source], low_other_ref[source]], axis=0)
        part = dot_rows(left, mixed_ref[...])
        total = part if total is None else total + part
    put_blocks(out_ref, 0, total.astype(bf16))


def out_parcel(place, low, mixed, parcel):
    planes, half, width = low[0].shape
    tokens, part = mixed[0].shape
    chips, height, _ = parcel.shape
    room = width // chips * part // lanes
    steps = planes
    left = pl.BlockSpec((planes, half, width // steps), lambda k, z: (0, 0, k))
    return pl.pallas_call(
        out_parcel_body,
        grid_spec=pltpu.PrefetchScalarGridSpec(
            num_scalar_prefetch=1,
            grid=(steps,),
            in_specs=[left, left]
            + [pl.BlockSpec((tokens, part), lambda k, z: (0, 0))] * planes
            + [pl.BlockSpec(memory_space=pl.ANY)],
            out_specs=pl.BlockSpec((chips // steps, room, lanes), lambda k, z: (k, 3, 0)),
        ),
        out_shape=pltpu.HBM((chips, height, lanes), bf16),
        input_output_aliases={3 + planes: 0},
        compiler_params=params(14),
        cost_estimate=pl.CostEstimate(
            flops=2 * tokens * width * part // cheap,
            transcendentals=0,
            bytes_accessed=2 * (tokens * width + chips * room * lanes) // cheap,
        ),
        name="out_parcel",
    )(place, *in_hbm(*low), *mixed, *in_hbm(parcel))


def parcel_sums_body(
    per_chip,
    place_ref,
    parcel_ref,
    w_query_ref,
    w_key_ref,
    w_value_ref,
    own_gain_ref,
    query_ref,
    key_ref,
    value_ref,
    out_ref,
    router_ref,
    query_gain_ref,
    key_gain_ref,
    moe_ref,
    count_ref,
    attn_ref,
    attn_other_ref,
    extra_ref,
    gain_ref,
):
    total = jnp.sum(parcel_ref[...].astype(f32), axis=0)
    rows, columns = query_ref.shape
    row = 0
    gain = jnp.zeros((rows, lanes), f32)
    weights = (w_query_ref, w_key_ref, w_value_ref, None)
    for ref, w_ref in zip((query_ref, key_ref, value_ref, out_ref), weights):
        for k in range(columns // lanes):
            here = slice(k * lanes, (k + 1) * lanes)
            piece = total[row : row + rows, :]
            ref[:, here] = piece
            if w_ref is not None:
                gain = gain + piece * w_ref[:, here].astype(f32)
            row += rows
    step = pl.program_id(0)

    @pl.when(step == 0)
    def _():
        extra_ref[...] = total[row:, :]
        gain_ref[...] = gain

    @pl.when(step > 0)
    def _():
        extra_ref[...] += total[row:, :]
        gain_ref[...] += gain

    @pl.when(step == pl.num_programs(0) - 1)
    def _():
        half = rows // 2
        heads = query_gain_ref.shape[0]
        spare = lanes // 2
        router_ref[...] = extra_ref[:, : router_ref.shape[1]]
        sums = extra_ref[0:heads, spare:] + extra_ref[half // 2 : half // 2 + heads, spare:]
        query_gain_ref[...] = sums[:, :per_chip]
        key_gain_ref[...] = sums[:, per_chip : 2 * per_chip]
        moe_ref[...] = sums[0:1, 2 * per_chip : 2 * per_chip + half]
        count_ref[...] = sums[0:1, 2 * per_chip + half : 2 * per_chip + half + 1].astype(jnp.int32)
        attn = jnp.sum(gain_ref[...].T, axis=0, keepdims=True) / own_gain_ref[...]
        first = place_ref[1] == 0
        attn_ref[...] = jnp.where(first, attn[:, :half], attn[:, half:])
        attn_other_ref[...] = jnp.where(first, attn[:, half:], attn[:, :half])


def parcel_sums(place, parcel, weights, own_gain, planes, rows, width, heads, per_chip, experts):
    chips, height, _ = parcel.shape
    part = width // planes
    half = rows // 2
    wide = pl.BlockSpec((rows, part), lambda k, c: (0, k))

    def whole(shape):
        return pl.BlockSpec(shape, lambda k, c: (0, 0))

    small = [(half, experts), (heads, per_chip), (heads, per_chip), (1, half), (1, 1)]
    small += [(1, half), (1, half)]
    kinds = [f32] * 4 + [jnp.int32] + [f32] * 2
    return pl.pallas_call(
        lambda *refs: parcel_sums_body(per_chip, *refs),
        grid_spec=pltpu.PrefetchScalarGridSpec(
            num_scalar_prefetch=1,
            grid=(planes,),
            in_specs=[pl.BlockSpec((chips // planes, height, lanes), lambda k, c: (k, 0, 0))]
            + [pl.BlockSpec((rows, part), lambda k, c: (c[2], k))] * 3
            + [whole((1, rows))],
            out_specs=[wide] * 4 + [whole(shape) for shape in small],
            scratch_shapes=[pltpu.VMEM((half, lanes), f32), pltpu.VMEM((rows, lanes), f32)],
        ),
        out_shape=[jax.ShapeDtypeStruct((rows, width), f32)] * 4
        + [jax.ShapeDtypeStruct(shape, kind) for shape, kind in zip(small, kinds)],
        compiler_params=params(14),
        cost_estimate=pl.CostEstimate(
            flops=parcel.size, transcendentals=0, bytes_accessed=2 * parcel.size
        ),
        name="parcel_sums",
    )(place, parcel, *in_hbm(*weights), own_gain)


def expert_weight_grads_body(rows_ref, slot_grad_ref, inner_ref, gate_ref, up_ref, *refs):
    grads = (
        dot_rows(rows_ref[...], gate_ref[...]),
        dot_rows(rows_ref[...], up_ref[...]),
        dot_rows(inner_ref[...], slot_grad_ref[...]),
    )
    others, outs = refs[:-3], refs[-3:]
    for k, (grad, out_ref) in enumerate(zip(grads, outs)):
        if others:
            grad = grad + others[k][...].astype(f32)
        out_ref[...] = grad.astype(out_ref.dtype)


def expert_weight_grads(rows, slot_grad, inner, gate_grad, up_grad, others, kind):
    count, width = rows.shape
    units = inner.shape[1]
    steps = 4
    size = width // steps
    wide = pl.BlockSpec((count, size), lambda k: (0, k))
    narrow = pl.BlockSpec((count, units), lambda k: (0, 0))
    into = pl.BlockSpec((size, units), lambda k: (k, 0))
    back = pl.BlockSpec((units, size), lambda k: (0, k))
    return pl.pallas_call(
        expert_weight_grads_body,
        grid=(steps,),
        in_specs=[wide, wide, narrow, narrow, narrow] + [into, into, back][: len(others)],
        out_specs=[into, into, back],
        out_shape=[
            jax.ShapeDtypeStruct((width, units), kind),
            jax.ShapeDtypeStruct((width, units), kind),
            jax.ShapeDtypeStruct((units, width), kind),
        ],
        compiler_params=params(30),
        cost_estimate=pl.CostEstimate(
            flops=6 * count * width * units // cheap,
            transcendentals=0,
            bytes_accessed=4 * count * width // cheap,
        ),
        name="expert_weight_grads",
    )(*in_hbm(rows, slot_grad, inner, gate_grad, up_grad, *others))


def normed_grad_body(stack_ref, query_ref, key_ref, value_ref, own_ref, other_ref):
    size = query_ref.shape[1]
    total = None
    for k, w_ref in enumerate((query_ref, key_ref, value_ref)):
        part = dot_cols(stack_ref[:, k * size : (k + 1) * size], w_ref[...])
        total = part if total is None else total + part
    half = own_ref.shape[0]
    first = pl.program_id(0) == 0

    @pl.when(first)
    def _():
        own_ref[...] = total[:half]
        other_ref[...] = total[half:]

    @pl.when(jnp.logical_not(first))
    def _():
        own_ref[...] += total[:half]
        other_ref[...] += total[half:]


def normed_grad_of(stack, weights):
    planes, seq_len, columns = stack.shape
    size = columns // 3
    full = weights[0].shape[0]
    half = pl.BlockSpec((seq_len // 2, full), lambda k: (0, 0))
    return pl.pallas_call(
        normed_grad_body,
        grid=(planes,),
        in_specs=[pl.BlockSpec((None, seq_len, columns), lambda k: (k, 0, 0))]
        + [pl.BlockSpec((full, size), lambda k: (0, k))] * 3,
        out_specs=[half] * 2,
        out_shape=[jax.ShapeDtypeStruct((seq_len // 2, full), f32)] * 2,
        compiler_params=params(20),
        cost_estimate=pl.CostEstimate(
            flops=2 * stack.size * full // cheap,
            transcendentals=0,
            bytes_accessed=2 * planes * columns * full // cheap,
        ),
        name="normed_grad",
    )(stack, *in_hbm(*weights))


def slot_rows_body(
    slots, place_ref, routes_ref, own_ref, other_ref, pick_ref, pick_back_ref, counts_ref, out_ref
):
    core = place_ref[1]
    experts = counts_ref.shape[0]
    half, seq_len = own_ref.shape[0], routes_ref.shape[0]

    @pl.when(pl.program_id(0) == 0)
    def _():
        routes = routes_ref[...]
        routes = jnp.where(
            core == 0, routes, jnp.concatenate([routes[half:, :], routes[:half, :]], axis=0)
        )
        numbers = lax.broadcasted_iota(jnp.int32, (seq_len, experts), 1)
        hits = numbers == routes[:, 0:1]
        for k in range(1, routes.shape[1]):
            hits = hits | (numbers == routes[:, k : k + 1])
        square = (seq_len, seq_len)
        shift = core * half
        place = lax.broadcasted_iota(jnp.int32, square, 0) + shift
        earlier = lax.broadcasted_iota(jnp.int32, square, 1) + shift
        place = jnp.where(place >= seq_len, place - seq_len, place)
        earlier = jnp.where(earlier >= seq_len, earlier - seq_len, earlier)
        before = jnp.where(earlier < place, 1.0, 0.0).astype(bf16)
        rank = dot(before, jnp.where(hits, 1.0, 0.0).astype(bf16))
        rank = jnp.where(hits, rank, -1.0)
        wide = (experts, experts * slots)
        spread = lax.broadcasted_iota(jnp.int32, wide, 1) // slots
        spread = spread == lax.broadcasted_iota(jnp.int32, wide, 0)
        spread_rank = dot(rank.astype(bf16), jnp.where(spread, 1.0, 0.0).astype(bf16))
        slot = lax.broadcasted_iota(jnp.int32, spread_rank.shape, 1) % slots + core * slots
        pick_back_ref[...] = jnp.where(spread_rank == slot.astype(f32), 1.0, 0.0).astype(bf16)
        rank = rank.T
        counts_ref[...] = jnp.sum(jnp.where(rank >= 0.0, 1.0, 0.0), axis=1, keepdims=True)
        slot = lax.broadcasted_iota(jnp.int32, (experts, slots, seq_len), 1) + core * slots
        pick = jnp.where(rank[:, None, :] == slot.astype(f32), 1.0, 0.0)
        pick_ref[...] = pick.reshape(experts * slots, seq_len).astype(bf16)

    rows = jnp.concatenate([own_ref[...], other_ref[...]], axis=0)
    out_ref[...] = dot(pick_ref[...], rows).astype(bf16)


def slot_rows(place, routes, own, other, experts, slots, columns):
    half = own.shape[0]
    seq_len, top_count = routes.shape
    steps = 2
    size = columns // steps
    rows = pl.BlockSpec((half, size), lambda k, c: (0, k))

    def whole(*shape):
        return pl.BlockSpec(shape, lambda k, c: (0, 0))

    return pl.pallas_call(
        lambda *refs: slot_rows_body(slots, *refs),
        grid_spec=pltpu.PrefetchScalarGridSpec(
            num_scalar_prefetch=1,
            grid=(steps,),
            in_specs=[whole(seq_len, top_count), rows, rows],
            out_specs=[
                whole(experts * slots, seq_len),
                whole(seq_len, experts * slots),
                whole(experts, 1),
                pl.BlockSpec((experts * slots, size), lambda k, c: (0, k)),
            ],
        ),
        out_shape=[
            jax.ShapeDtypeStruct((experts * slots, seq_len), bf16),
            jax.ShapeDtypeStruct((seq_len, experts * slots), bf16),
            jax.ShapeDtypeStruct((experts, 1), f32),
            pltpu.HBM((experts * slots, columns), bf16),
        ],
        compiler_params=params(20),
        cost_estimate=pl.CostEstimate(
            flops=2 * experts * slots * seq_len * columns,
            transcendentals=0,
            bytes_accessed=2 * (seq_len + experts * slots) * columns,
        ),
        name="slot_rows",
    )(place, routes, *in_hbm(own, other))


def token_sums_body(pick_ref, rows_ref, own_ref, other_ref):
    total = dot(pick_ref[...], rows_ref[...])
    half = own_ref.shape[0]
    own_ref[...] = total[:half]
    other_ref[...] = total[half:]


def token_sums(pick_back, rows):
    seq_len, count = pick_back.shape
    width = rows.shape[1]
    steps = 2
    half = pl.BlockSpec((seq_len // 2, width // steps), lambda k: (0, k))
    return pl.pallas_call(
        token_sums_body,
        grid=(steps,),
        in_specs=[
            pl.BlockSpec((seq_len, count), lambda k: (0, 0)),
            pl.BlockSpec((count, width // steps), lambda k: (0, k)),
        ],
        out_specs=[half] * 2,
        out_shape=[jax.ShapeDtypeStruct((seq_len // 2, width), f32)] * 2,
        compiler_params=params(16),
        cost_estimate=pl.CostEstimate(
            flops=2 * count * seq_len * width,
            transcendentals=0,
            bytes_accessed=2 * count * (seq_len + width) + 4 * seq_len * width,
        ),
        name="token_sums",
    )(*in_hbm(pick_back, rows))


def hidden_grad_body(
    own_ref,
    other_ref,
    logit_high_ref,
    logit_low_ref,
    w_router_ref,
    gain_ref,
    hidden_ref,
    scale_ref,
    cot_ref,
    grad_ref,
    low_ref,
    gain_grad_ref,
):
    w_router = w_router_ref[...]
    moe_in = own_ref[...] + other_ref[...]
    moe_in = moe_in + dot(logit_high_ref[...], w_router)
    moe_in = moe_in + dot(logit_low_ref[...], w_router)
    hidden, scale = hidden_ref[...], scale_ref[...]
    gain_grad_ref[...] = jnp.sum(hidden * scale * moe_in, axis=0, keepdims=True)
    weighted = moe_in * gain_ref[...]
    inner = jnp.mean(hidden * weighted, axis=1, keepdims=True)
    grad = cot_ref[...].astype(f32) + scale * weighted
    grad = grad - hidden * (scale * scale * scale * inner)
    grad_ref[...] = grad
    low_ref[...] = grad.astype(bf16)


def hidden_grad_of(own, other, logit_high, logit_low, w_router, gain, hidden, scale, cot):
    rows, width = own.shape
    return pl.pallas_call(
        hidden_grad_body,
        out_shape=[
            pltpu.HBM((rows, width), f32),
            pltpu.HBM((rows, width), bf16),
            jax.ShapeDtypeStruct((1, width), f32),
        ],
        compiler_params=params(16),
        cost_estimate=pl.CostEstimate(
            flops=20 * rows * width, transcendentals=0, bytes_accessed=20 * rows * width
        ),
        name="hidden_grad",
    )(own, other, logit_high, logit_low, w_router, gain, hidden, scale, cot)


def router_grad_body(normed_ref, high_ref, low_ref, out_ref):
    normed = normed_ref[...]
    out_ref[...] = dot_rows(normed, high_ref[...]) + dot_rows(normed, low_ref[...])


def router_grad_of(normed, high, low):
    return pl.pallas_call(
        router_grad_body,
        out_shape=jax.ShapeDtypeStruct((normed.shape[1], high.shape[1]), f32),
        compiler_params=params(10),
        cost_estimate=pl.CostEstimate(
            flops=1 << 20, transcendentals=0, bytes_accessed=normed.size
        ),
        name="router_grad",
    )(normed, high, low)


def projections_body(
    own_ref,
    other_ref,
    gain_ref,
    w_query_ref,
    w_key_ref,
    w_value_ref,
    normed_own_ref,
    normed_other_ref,
    scale_ref,
    query_ref,
    key_ref,
    value_ref,
    squares_ref,
    normed_ref,
):
    half = own_ref.shape[0]
    step = pl.program_id(0)

    @pl.when(step == 0)
    def _():
        for k, (ref, out_ref) in enumerate(
            ((own_ref, normed_own_ref), (other_ref, normed_other_ref))
        ):
            rows = ref[...].astype(f32)
            scale = rms_scale(rows)
            normed = (rows * scale * gain_ref[...]).astype(bf16)
            out_ref[...] = normed
            normed_ref[k * half : (k + 1) * half, :] = normed
            if k == 0:
                scale_ref[...] = scale

    normed = normed_ref[...]
    query = dot(normed, w_query_ref[...])
    key = dot(normed, w_key_ref[...])
    query_ref[...] = query
    key_ref[...] = key
    value_ref[...] = dot(normed, w_value_ref[...]).astype(bf16)
    squares = jnp.concatenate(
        [jnp.sum(v * v, axis=1, keepdims=True) for v in (query, key)], axis=1
    )

    @pl.when(step == 0)
    def _():
        squares_ref[...] = squares

    @pl.when(step > 0)
    def _():
        squares_ref[...] += squares


def projections(own, other, gain, weights):
    half, width = own.shape
    local_width = weights[0].shape[1]
    steps = 4
    size = local_width // steps

    def whole(*shape):
        return pl.BlockSpec(shape, lambda k: (0, 0))

    column = pl.BlockSpec((2 * half, size), lambda k: (0, k))
    return pl.pallas_call(
        projections_body,
        grid=(steps,),
        in_specs=[whole(half, width), whole(half, width), whole(1, width)]
        + [pl.BlockSpec((width, size), lambda k: (0, k))] * 3,
        out_specs=[whole(half, width)] * 2
        + [whole(half, 1), column, column, column, whole(2 * half, 2)],
        out_shape=[jax.ShapeDtypeStruct((half, width), bf16)] * 2
        + [jax.ShapeDtypeStruct((half, 1), f32)]
        + [jax.ShapeDtypeStruct((2 * half, local_width), kind) for kind in (f32, f32, bf16)]
        + [jax.ShapeDtypeStruct((2 * half, 2), f32)],
        scratch_shapes=[pltpu.VMEM((2 * half, width), bf16)],
        compiler_params=params(22),
        cost_estimate=pl.CostEstimate(
            flops=1 << 20, transcendentals=0, bytes_accessed=width * local_width // cheap
        ),
        name="projections",
    )(*in_hbm(own, other), gain, *in_hbm(*weights))


def branch_body(mixed_ref, w_ref, own_ref, other_ref):
    total = dot(mixed_ref[...], w_ref[...])
    half = own_ref.shape[0]
    own_ref[...] = total[:half]
    other_ref[...] = total[half:]


def branch_of(mixed, w_out):
    seq_len, local_width = mixed.shape
    width = w_out.shape[1]
    steps = 4
    half = pl.BlockSpec((seq_len // 2, width // steps), lambda k: (0, k))
    return pl.pallas_call(
        branch_body,
        grid=(steps,),
        in_specs=[
            pl.BlockSpec((seq_len, local_width), lambda k: (0, 0)),
            pl.BlockSpec((local_width, width // steps), lambda k: (0, k)),
        ],
        out_specs=[half] * 2,
        out_shape=[jax.ShapeDtypeStruct((seq_len // 2, width), f32)] * 2,
        compiler_params=params(12),
        cost_estimate=pl.CostEstimate(
            flops=1 << 20, transcendentals=0, bytes_accessed=width * local_width // cheap
        ),
        name="branch",
    )(mixed, *in_hbm(w_out))


def moe_rows_body(
    own_ref,
    other_ref,
    branch_own_ref,
    branch_other_ref,
    got_own_ref,
    got_other_ref,
    gain_ref,
    w_router_ref,
    pick_ref,
    hidden_ref,
    scale_ref,
    normed_ref,
    probs_ref,
    out_ref,
):
    half = own_ref.shape[0]
    step = pl.program_id(0)

    @pl.when(step == 0)
    def _():
        for k, (ref, branch_ref, got_ref) in enumerate(
            ((own_ref, branch_own_ref, got_own_ref), (other_ref, branch_other_ref, got_other_ref))
        ):
            hidden = ref[...].astype(f32) + (branch_ref[...] + got_ref[...])
            scale = rms_scale(hidden)
            normed_ref[k * half : (k + 1) * half, :] = (hidden * scale * gain_ref[...]).astype(bf16)
            if k == 0:
                hidden_ref[...] = hidden
                scale_ref[...] = scale
        logits = dot_cols(normed_ref[...], w_router_ref[...])
        grown = jnp.exp(logits - jnp.max(logits, axis=1, keepdims=True))
        probs_ref[...] = grown / jnp.sum(grown, axis=1, keepdims=True)

    size = out_ref.shape[1]
    columns = pl.ds(pl.multiple_of(step * size, size), size)
    out_ref[...] = dot(pick_ref[...], normed_ref[:, columns]).astype(bf16)


def moe_rows(own, other, branch, got, gain, w_router, pick):
    half, width = own.shape
    count, seq_len = pick.shape
    experts = w_router.shape[0]
    steps = 4

    def whole(*shape):
        return pl.BlockSpec(shape, lambda k: (0, 0), pipeline_mode=pl.Buffered(1))

    def kept(*shape):
        return pl.BlockSpec(shape, lambda k: (0, 0))

    return pl.pallas_call(
        moe_rows_body,
        grid=(steps,),
        in_specs=[whole(half, width)] * 6
        + [whole(1, width), whole(experts, width), whole(count, seq_len)],
        out_specs=[
            kept(half, width),
            kept(half, 1),
            kept(seq_len, width),
            kept(seq_len, experts),
            pl.BlockSpec((count, width // steps), lambda k: (0, k)),
        ],
        out_shape=[
            pltpu.HBM((half, width), f32),
            jax.ShapeDtypeStruct((half, 1), f32),
            pltpu.HBM((seq_len, width), bf16),
            jax.ShapeDtypeStruct((seq_len, experts), f32),
            pltpu.HBM((count, width), bf16),
        ],
        compiler_params=params(24),
        cost_estimate=pl.CostEstimate(
            flops=1 << 20, transcendentals=0, bytes_accessed=width * count // cheap
        ),
        name="moe_rows",
    )(*in_hbm(own, other), *branch, *got, gain, *in_hbm(w_router, pick))


def local(
    residual_in,
    routes,
    segment_ids,
    gain_attn,
    w_query,
    w_key,
    w_value,
    gain_query,
    gain_key,
    w_out,
    gain_moe,
    w_router,
    w_gate,
    w_up,
    w_down,
    cotangent,
):
    core = lax.axis_index("tp")
    planes = lax.axis_size("z")
    chips = lax.axis_size(rows_of_chips)
    chip = lax.axis_index(rows_of_chips)
    own_rows, width = residual_in.shape
    seq_len, top_count = routes.shape
    local_width = w_query.shape[1]
    local_heads, head_dim = gain_query.shape
    experts = chips
    capacity = seq_len * top_count // experts
    own_slots = capacity // 2
    quarter = local_width // planes
    out_rows = width // chips

    def own_first(value):
        return jnp.where(
            core == 0, value, jnp.concatenate([value[own_rows:], value[:own_rows]], axis=0)
        )

    first_columns = width * 5 // 8
    numbers = jnp.stack([lax.axis_index("z"), core, chip])
    cot_other = swap(cotangent)
    pick, pick_back, counts, cot_slots = slot_rows(
        numbers, routes, cotangent, cot_other, experts, own_slots, first_columns
    )
    cot_slots, residual_in, segment_ids = lax.optimization_barrier(
        (cot_slots, residual_in, segment_ids)
    )
    cot_first = all_to_all(
        cot_slots.reshape(experts, own_slots, first_columns), rows_of_chips
    ).reshape(experts * own_slots, first_columns)
    cot = jnp.concatenate([cotangent, cot_other], axis=0)

    place = own_first(jnp.arange(seq_len, dtype=jnp.int32))
    seg = own_first(segment_ids[0])
    same_doc = seg[:, None] == seg[None, :]
    position = place - jnp.min(jnp.where(same_doc, place[None, :], seq_len), axis=1)
    cosine, sine = rope_angles(position, head_dim)
    cosine = jnp.concatenate([cosine, cosine], axis=1)
    sine = jnp.concatenate([-sine, sine], axis=1)
    bias = jnp.where(same_doc & (place[None, :] <= place[:, None]), 0.0, mask_fill)

    other_in = swap(residual_in)
    normed_own, normed_other, scale_attn, queries, key_proj, values, squares = projections(
        residual_in, other_in, gain_attn[None], (w_query, w_key, w_value)
    )
    normed_planes = lax.all_gather(normed_own, "z", axis=0, tiled=False)
    query_gain = gain_query.reshape(1, local_width)
    key_gain = gain_key.reshape(1, local_width)
    q_rot, k_rot, probs, mixed, mixed_parts, scales = attention_forward(
        queries,
        key_proj,
        values,
        query_gain,
        key_gain,
        squares,
        swap(squares),
        cosine,
        sine,
        bias,
        local_heads,
        planes,
    )
    branch = branch_of(mixed, w_out)
    hidden_own, scale_moe, normed_moe, router_probs, moe_slots = moe_rows(
        residual_in,
        other_in,
        branch,
        (swap(branch[1]), swap(branch[0])),
        gain_moe[None],
        w_router.T,
        pick,
    )

    moe_slots, cot_first = lax.optimization_barrier((moe_slots, cot_first))
    arrived = all_to_all(
        moe_slots.reshape(experts, own_slots, width), rows_of_chips
    ).reshape(experts * own_slots, width)
    cot_slots = dot(pick, cot[:, first_columns:]).astype(bf16)
    arrived, cot_slots = lax.optimization_barrier((arrived, cot_slots))
    cot_rest = all_to_all(
        cot_slots.reshape(experts, own_slots, width - first_columns), rows_of_chips
    ).reshape(experts * own_slots, width - first_columns)

    gate_parts = (w_gate[0], swap(w_gate[0]))
    up_parts = (w_up[0], swap(w_up[0]))
    down_parts = (w_down[0], swap(w_down[0]))
    slot_out = expert_forward(arrived, gate_parts, up_parts, down_parts)
    slot_out, arrived, cot_rest, normed_planes = lax.optimization_barrier(
        (slot_out, arrived, cot_rest, normed_planes)
    )
    cot_arrived = jnp.concatenate([cot_first, cot_rest], axis=1)
    returned = all_to_all(
        slot_out.reshape(experts, own_slots, width), rows_of_chips
    ).reshape(experts * own_slots, width)
    slot_probs = jax.nn.softmax(dot(arrived, w_router), axis=-1)
    own_expert = jnp.arange(experts, dtype=jnp.int32) == chip
    slot_weight = jnp.sum(jnp.where(own_expert[None, :], slot_probs, 0.0), axis=1, keepdims=True)
    slot_grad = (slot_weight * cot_arrived.astype(f32)).astype(bf16)
    (
        inner_own,
        inner_other,
        gate_own,
        gate_other,
        up_own,
        up_other,
        slot_in_grad,
    ) = expert_backward(arrived, slot_grad, gate_parts, up_parts, down_parts)
    slot_in_grad, returned = lax.optimization_barrier((slot_in_grad, returned))
    grads_back = all_to_all(
        slot_in_grad.reshape(experts, own_slots, width), rows_of_chips
    ).reshape(experts * own_slots, width)
    normed_planes = (normed_planes, swap(normed_planes))
    plane = lax.axis_index("z")
    mixed_planes = [lax.dynamic_index_in_dim(mixed_parts, plane, 0, keepdims=False)]
    for shift in range(1, planes):
        part = lax.dynamic_index_in_dim(mixed_parts, (plane + shift) % planes, 0, keepdims=False)
        mixed_planes.append(
            lax.ppermute(part, "z", [(k, (k + shift) % planes) for k in range(planes)])
        )
    others = expert_weight_grads(arrived, slot_grad, inner_other, gate_other, up_other, (), bf16)

    pick_pairs = pick.reshape(experts, own_slots, seq_len)
    weighted = pick_pairs.astype(f32) * router_probs.T[:, None, :]
    weight_high, weight_low = halves(weighted.reshape(experts * own_slots, seq_len))
    moe_part = dot_rows(weight_high, returned) + dot_rows(weight_low, returned)
    moe_own, moe_other = moe_part[:own_rows], moe_part[own_rows:].astype(bf16)
    pair_products = dot_cols(returned, cot).reshape(experts, own_slots, seq_len)
    prob_part = jnp.sum(pair_products * pick_pairs.astype(f32), axis=1).T
    other_part = swap(prob_part)
    prob_grad = prob_part + jnp.concatenate([other_part[own_rows:], other_part[:own_rows]], axis=0)
    logit_grad = router_probs * (
        prob_grad - jnp.sum(router_probs * prob_grad, axis=1, keepdims=True)
    )
    logit_high, logit_low = halves(logit_grad)
    router_grad = router_grad_of(normed_moe, logit_high, logit_low)
    (
        grads_back,
        others,
        moe_own,
        moe_other,
        logit_high,
        logit_low,
        router_grad,
        mixed_planes,
    ) = lax.optimization_barrier(
        (
            grads_back,
            others,
            moe_own,
            moe_other,
            logit_high,
            logit_low,
            router_grad,
            mixed_planes,
        )
    )
    moe_own = moe_own + swap(moe_other).astype(f32)
    output = (hidden_own + moe_own).astype(bf16)
    others = [swap(grad) for grad in others]
    grad_w_gate, grad_w_up, grad_w_down = expert_weight_grads(
        arrived, slot_grad, inner_own, gate_own, up_own, others, f32
    )
    moe_in_own, moe_in_other = token_sums(pick_back, grads_back)
    hidden_grad, hidden_low_own, gain_moe_grad = hidden_grad_of(
        moe_in_own,
        swap(moe_in_other),
        logit_high[:own_rows],
        logit_low[:own_rows],
        w_router.T,
        gain_moe[None],
        hidden_own,
        scale_moe,
        cotangent,
    )
    hidden_low_other = swap(hidden_low_own)
    low_planes = lax.all_gather(hidden_low_own, "z", axis=0, tiled=False)

    value_grad, query_part, key_part, gain_query_grad, gain_key_grad, inner = attention_backward(
        hidden_low_own,
        hidden_low_other,
        w_out,
        values,
        q_rot,
        k_rot,
        probs,
        queries,
        key_proj,
        query_gain,
        key_gain,
        scales,
        cosine,
        sine,
        local_heads,
    )
    inner_other, gain_moe_other = lax.optimization_barrier((swap(inner), swap(gain_moe_grad)))
    to_planes = projection_grads(
        query_part,
        key_part,
        queries,
        key_proj,
        value_grad,
        scales,
        (inner, inner_other),
        planes,
    )

    grads_planes = all_to_all(to_planes, "z").reshape(planes * seq_len, 3 * quarter)
    grads_planes, low_planes = lax.optimization_barrier((grads_planes, low_planes))
    low_planes = (low_planes, swap(low_planes))
    normed_grad, normed_grad_other = normed_grad_of(to_planes, (w_query, w_key, w_value))
    normed_grad = normed_grad + swap(normed_grad_other)
    in_own = residual_in.astype(f32)
    in_scale = scale_attn
    weighted_attn = normed_grad * gain_attn
    grad_input = (
        hidden_grad
        + in_scale * weighted_attn
        - in_own * in_scale**3 * jnp.mean(in_own * weighted_attn, axis=1, keepdims=True)
    )

    parcel = weight_parcel(
        numbers,
        normed_planes,
        grads_planes,
        router_grad.reshape(chips, out_rows, experts),
        (gain_moe_grad, gain_moe_other),
        gain_query_grad,
        gain_key_grad,
        counts,
    )
    parcel = out_parcel(numbers, low_planes, mixed_planes, parcel)
    parcel = all_to_all(parcel, rows_of_chips)
    per_chip = head_dim // chips
    own_gain = lax.dynamic_slice_in_dim(gain_attn, chip * out_rows, out_rows)[None]
    (
        grad_w_query,
        grad_w_key,
        grad_w_value,
        grad_w_out,
        grad_w_router,
        grad_gain_query,
        grad_gain_key,
        grad_gain_moe,
        count,
        attn_own,
        attn_other,
    ) = parcel_sums(
        numbers,
        parcel,
        (w_query, w_key, w_value),
        own_gain,
        planes,
        out_rows,
        local_width,
        local_heads,
        per_chip,
        experts,
    )
    return (
        output,
        grad_input,
        (attn_own + swap(attn_other))[0],
        grad_w_query,
        grad_w_key,
        grad_w_value,
        grad_gain_query,
        grad_gain_key,
        grad_w_out.T,
        grad_gain_moe[0],
        grad_w_router,
        grad_w_gate[None],
        grad_w_up[None],
        grad_w_down[None],
        count[0],
    )


def solution(mesh):
    side = round(mesh.shape["ep"] ** (1 / 3))
    cube = Mesh(mesh.devices.reshape(side, side, side, 2), rows_of_chips + ("tp",))
    ep = rows_of_chips
    both = rows_of_chips + ("tp",)
    in_specs = (
        P(both, None),
        P(ep, None),
        P(ep, None),
        P(),
        P(None, "tp"),
        P(None, "tp"),
        P(None, "tp"),
        P("tp", None),
        P("tp", None),
        P("tp", None),
        P(),
        P(),
        P(ep, None, "tp"),
        P(ep, None, "tp"),
        P(ep, "tp", None),
        P(both, None),
    )
    out_specs = (
        P(both, None),
        P(both, None),
        P(both),
        P(ep, "tp"),
        P(ep, "tp"),
        P(ep, "tp"),
        P("tp", ep),
        P("tp", ep),
        P("tp", ep),
        P(both),
        P(both, None),
        P(ep, None, "tp"),
        P(ep, None, "tp"),
        P(ep, "tp", None),
        P(ep),
    )
    return jax.shard_map(local, mesh=cube, in_specs=in_specs, out_specs=out_specs, check_vma=False)
```

```python
import jax
import jax.numpy as jnp
from jax import lax
from jax.experimental import pallas as pl
from jax.experimental.pallas import tpu as pltpu
from jax.sharding import Mesh, PartitionSpec as P

norm_eps = 1e-05
rope_base = 10000.0
mask_fill = -1e30
bf16 = jnp.bfloat16
f32 = jnp.float32
rows_of_chips = ("z", "x", "y")


def swap(value):
    return lax.ppermute(value, "tp", [(0, 1), (1, 0)])


def dot(left, right):
    return lax.dot_general(left, right, (((1,), (0,)), ((), ())), preferred_element_type=f32)


def dot_rows(left, right):
    return lax.dot_general(left, right, (((0,), (0,)), ((), ())), preferred_element_type=f32)


def dot_cols(left, right):
    return lax.dot_general(left, right, (((1,), (1,)), ((), ())), preferred_element_type=f32)


def all_to_all(value, axes):
    return lax.all_to_all(value, axes, split_axis=0, concat_axis=0, tiled=True)


def rms_scale(values):
    return lax.rsqrt(jnp.mean(values * values, axis=-1, keepdims=True) + norm_eps)


def halves(value):
    high = value.astype(bf16)
    return high, (value - high.astype(f32)).astype(bf16)


def rope_angles(positions, head_dim):
    half_dim = head_dim // 2
    exponent = jnp.arange(half_dim, dtype=f32) * (2.0 / head_dim)
    inverse = jnp.power(f32(rope_base), -exponent)
    angles = positions.astype(f32)[:, None] * inverse[None, :]
    return jnp.cos(angles), jnp.sin(angles)


lanes = 128
cheap = 64


def in_hbm(*arrays):
    return [pltpu.with_memory_space_constraint(array, pltpu.HBM) for array in arrays]


def params(megabytes):
    return pltpu.CompilerParams(vmem_limit_bytes=megabytes * 1024 * 1024)


def turn(value, cosine, sine):
    return value * cosine + pltpu.roll(value, value.shape[1] // 2, 1) * sine


def other_order(ref):
    half = ref.shape[0] // 2
    return jnp.concatenate([ref[half:, :], ref[:half, :]], axis=0)


def attention_forward_body(
    scale,
    full_width,
    query_ref,
    key_ref,
    value_ref,
    query_gain_ref,
    key_gain_ref,
    squares_ref,
    other_squares_ref,
    cosine_ref,
    sine_ref,
    bias_ref,
    q_rot_ref,
    k_rot_ref,
    probs_ref,
    mixed_ref,
    parts_ref,
    scales_ref,
):
    cosine, sine, bias = cosine_ref[...], sine_ref[...], bias_ref[...]
    head = cosine.shape[1]
    squares = squares_ref[...] + other_order(other_squares_ref)
    scales = lax.rsqrt(squares * (1.0 / full_width) + norm_eps)
    scales_ref[...] = scales
    for h in range(probs_ref.shape[0]):
        here = slice(h * head, (h + 1) * head)
        query = query_ref[:, here] * scales[:, 0:1] * query_gain_ref[:, here]
        key = key_ref[:, here] * scales[:, 1:2] * key_gain_ref[:, here]
        q_rot = turn(query, cosine, sine).astype(bf16)
        k_rot = turn(key, cosine, sine).astype(bf16)
        q_rot_ref[:, here] = q_rot
        k_rot_ref[:, here] = k_rot
        scores = dot_cols(q_rot, k_rot) * scale + bias
        grown = jnp.exp(scores - jnp.max(scores, axis=1, keepdims=True))
        probs = grown / jnp.sum(grown, axis=1, keepdims=True)
        probs_ref[h] = probs
        mixed_ref[:, here] = dot(probs.astype(bf16), value_ref[:, here]).astype(bf16)
    part = parts_ref.shape[2]
    for k in range(parts_ref.shape[0]):
        parts_ref[k] = mixed_ref[:, k * part : (k + 1) * part]


def attention_forward(
    queries, keys, values, query_gain, key_gain, squares, other, cosine, sine, bias, heads, planes
):
    seq_len, width = queries.shape
    head = width // heads
    group = min(heads, 4)
    column = pl.BlockSpec((seq_len, group * head), lambda h: (0, h))
    gain = pl.BlockSpec((1, group * head), lambda h: (0, h))

    def whole(array):
        return pl.BlockSpec(array.shape, lambda h: (0, 0))

    return pl.pallas_call(
        lambda *refs: attention_forward_body(head**-0.5, 2 * width, *refs),
        grid=(heads // group,),
        in_specs=[column, column, column, gain, gain]
        + [whole(a) for a in (squares, other, cosine, sine, bias)],
        out_specs=[
            column,
            column,
            pl.BlockSpec((group, seq_len, seq_len), lambda h: (h, 0, 0)),
            column,
            pl.BlockSpec(
                (planes * group // heads, seq_len, width // planes), lambda h: (h, 0, 0)
            ),
            whole(squares),
        ],
        out_shape=[
            jax.ShapeDtypeStruct((seq_len, width), bf16),
            jax.ShapeDtypeStruct((seq_len, width), bf16),
            jax.ShapeDtypeStruct((heads, seq_len, seq_len), f32),
            jax.ShapeDtypeStruct((seq_len, width), bf16),
            jax.ShapeDtypeStruct((planes, seq_len, width // planes), bf16),
            jax.ShapeDtypeStruct((seq_len, 2), f32),
        ],
        compiler_params=params(16),
        cost_estimate=pl.CostEstimate(
            flops=4 * seq_len * seq_len * width // cheap,
            transcendentals=0,
            bytes_accessed=seq_len * width * 16 // cheap,
        ),
        name="attention_forward",
    )(queries, keys, values, query_gain, key_gain, squares, other, cosine, sine, bias)


def attention_backward_body(
    scale,
    hidden_own_ref,
    hidden_other_ref,
    w_out_ref,
    value_ref,
    q_rot_ref,
    k_rot_ref,
    probs_ref,
    query_ref,
    key_ref,
    query_gain_ref,
    key_gain_ref,
    scales_ref,
    cosine_ref,
    sine_ref,
    value_grad_ref,
    query_part_ref,
    key_part_ref,
    query_gain_grad_ref,
    key_gain_grad_ref,
    inner_ref,
):
    cosine, sine = cosine_ref[...], sine_ref[...]
    hidden = jnp.concatenate([hidden_own_ref[...], hidden_other_ref[...]], axis=0)
    heads, head = query_gain_grad_ref.shape[0], query_gain_grad_ref.shape[2]
    grad_mixed = dot_cols(hidden, w_out_ref[...]).astype(bf16)
    total = None
    for h in range(heads):
        here = slice(h * head, (h + 1) * head)
        grad = grad_mixed[:, here]
        probs = probs_ref[h]
        grad_probs = dot_cols(grad, value_ref[:, here])
        inner = jnp.sum(probs * grad_probs, axis=1, keepdims=True)
        grad_scores = (probs * (grad_probs - inner)).astype(bf16)
        value_grad_ref[:, here] = dot_rows(probs.astype(bf16), grad).astype(bf16)
        row_inners = []
        for k, (grad_rot, raw_ref, gain_ref, part_ref, gain_grad_ref) in enumerate(
            (
                (
                    dot(grad_scores, k_rot_ref[:, here]),
                    query_ref,
                    query_gain_ref,
                    query_part_ref,
                    query_gain_grad_ref,
                ),
                (
                    dot_rows(grad_scores, q_rot_ref[:, here]),
                    key_ref,
                    key_gain_ref,
                    key_part_ref,
                    key_gain_grad_ref,
                ),
            )
        ):
            grad_normed = turn(grad_rot * scale, cosine, -sine)
            raw = raw_ref[:, here]
            gain_grad_ref[h] = jnp.sum(
                raw * scales_ref[:, k : k + 1] * grad_normed, axis=0, keepdims=True
            )
            weighted = grad_normed * gain_ref[:, here]
            part_ref[:, here] = weighted
            row_inners.append(jnp.sum(raw * weighted, axis=1, keepdims=True))
        row_inner = jnp.concatenate(row_inners, axis=1)
        total = row_inner if total is None else total + row_inner
    first = pl.program_id(0) == 0

    @pl.when(first)
    def _():
        inner_ref[...] = total

    @pl.when(jnp.logical_not(first))
    def _():
        inner_ref[...] += total


def attention_backward(
    hidden_own,
    hidden_other,
    w_out,
    values,
    q_rot,
    k_rot,
    probs,
    queries,
    keys,
    query_gain,
    key_gain,
    scales,
    cosine,
    sine,
    heads,
):
    seq_len, width = queries.shape
    head = width // heads
    group = min(heads, 4)
    column = pl.BlockSpec((seq_len, group * head), lambda h: (0, h))
    gain = pl.BlockSpec((1, group * head), lambda h: (0, h))

    def whole(array):
        return pl.BlockSpec(array.shape, lambda h: (0, 0))

    full = jax.ShapeDtypeStruct((seq_len, width), f32)
    line = jax.ShapeDtypeStruct((heads, 1, head), f32)
    line_spec = pl.BlockSpec((group, 1, head), lambda h: (h, 0, 0))
    sums = jax.ShapeDtypeStruct((seq_len, 2), f32)
    return pl.pallas_call(
        lambda *refs: attention_backward_body(head**-0.5, *refs),
        grid=(heads // group,),
        in_specs=[
            whole(hidden_own),
            whole(hidden_other),
            pl.BlockSpec((group * head, w_out.shape[1]), lambda h: (h, 0)),
            column,
            column,
            column,
            pl.BlockSpec((group, seq_len, seq_len), lambda h: (h, 0, 0)),
            column,
            column,
            gain,
            gain,
        ]
        + [whole(a) for a in (scales, cosine, sine)],
        out_specs=[column, column, column, line_spec, line_spec, whole(sums)],
        out_shape=[
            jax.ShapeDtypeStruct((seq_len, width), bf16),
            full,
            full,
            line,
            line,
            sums,
        ],
        compiler_params=params(20),
        cost_estimate=pl.CostEstimate(
            flops=10 * seq_len * seq_len * width + 2 * seq_len * width * w_out.shape[1],
            transcendentals=0,
            bytes_accessed=seq_len * width * 28
            + heads * seq_len * seq_len * 4
            + 2 * w_out.size
            + 4 * hidden_own.size,
        ),
        name="attention_backward",
    )(
        *in_hbm(hidden_own, hidden_other, w_out, values, q_rot, k_rot, probs, queries, keys),
        query_gain,
        key_gain,
        scales,
        cosine,
        sine,
    )


def projection_grads_body(
    width,
    query_part_ref,
    key_part_ref,
    query_ref,
    key_ref,
    value_grad_ref,
    scales_ref,
    inner_ref,
    other_inner_ref,
    stack_ref,
):
    blocks, _, columns = stack_ref.shape
    size = columns // 3
    inner = (inner_ref[...] + other_order(other_inner_ref)) * (1.0 / width)
    for k, (part_ref, raw_ref) in enumerate(
        ((query_part_ref, query_ref), (key_part_ref, key_ref))
    ):
        scale = scales_ref[:, k : k + 1]
        factor = scale * scale * scale * inner[:, k : k + 1]
        for block in range(blocks):
            here = slice(block * size, (block + 1) * size)
            grad = scale * part_ref[:, here] - raw_ref[:, here] * factor
            stack_ref[block, :, k * size : (k + 1) * size] = grad.astype(bf16)
    for block in range(blocks):
        stack_ref[block, :, 2 * size :] = value_grad_ref[:, block * size : (block + 1) * size]


def projection_grads(
    query_part, key_part, queries, keys, value_grad, scales, inners, planes
):
    seq_len, width = queries.shape
    size = width // planes
    steps = 2
    column = pl.BlockSpec((seq_len, width // steps), lambda k: (0, k))
    pair = pl.BlockSpec((seq_len, 2), lambda k: (0, 0))
    return pl.pallas_call(
        lambda *refs: projection_grads_body(2 * width, *refs),
        grid=(steps,),
        in_specs=[column] * 5 + [pair] * 3,
        out_specs=pl.BlockSpec((planes // steps, seq_len, 3 * size), lambda k: (k, 0, 0)),
        out_shape=jax.ShapeDtypeStruct((planes, seq_len, 3 * size), bf16),
        compiler_params=params(10),
        cost_estimate=pl.CostEstimate(
            flops=10 * seq_len * width, transcendentals=0, bytes_accessed=24 * seq_len * width
        ),
        name="projection_grads",
    )(query_part, key_part, queries, keys, value_grad, scales, *inners)


def expert_forward_body(
    rows_hbm,
    gate_own_hbm,
    gate_other_hbm,
    up_own_hbm,
    up_other_hbm,
    down_own_hbm,
    down_other_hbm,
    out_hbm,
    rows_ref,
    gate_ref,
    up_ref,
    down_ref,
    out_ref,
    in_sems,
    out_sems,
):
    count, width = rows_ref.shape
    pieces = 2
    size = count // pieces
    copies = {}
    order = [("rows", 0), ("gate", 0), ("up", 0), ("gate", 1), ("up", 1), ("down", 0), ("down", 1)]
    order += [("rows", k) for k in range(1, pieces)]
    sources = {
        "gate": ((gate_own_hbm, gate_other_hbm), gate_ref),
        "up": ((up_own_hbm, up_other_hbm), up_ref),
        "down": ((down_own_hbm, down_other_hbm), down_ref),
    }
    for number, (name, k) in enumerate(order):
        if name == "rows":
            here = pl.ds(k * size, size)
            copy = pltpu.make_async_copy(rows_hbm.at[here], rows_ref.at[here], in_sems.at[number])
        else:
            source, target = sources[name]
            copy = pltpu.make_async_copy(source[k], target.at[k], in_sems.at[number])
        copy.start()
        copies[name, k] = copy
    outs = []
    for piece in range(pieces):
        here = pl.ds(piece * size, size)
        copies["rows", piece].wait()
        inners = []
        for k in range(2):
            if piece == 0:
                copies["gate", k].wait()
            gate = dot(rows_ref[here, :], gate_ref[k])
            if piece == 0:
                copies["up", k].wait()
            up = dot(rows_ref[here, :], up_ref[k])
            inners.append((gate * jax.nn.sigmoid(gate) * up).astype(bf16))
        if piece == 0:
            copies["down", 0].wait()
            copies["down", 1].wait()
        step = min(512, width)
        for start in range(0, width, step):
            columns = pl.ds(start, step)
            total = dot(inners[0], down_ref[0, :, columns]) + dot(
                inners[1], down_ref[1, :, columns]
            )
            out_ref[here, columns] = total.astype(bf16)
        copy = pltpu.make_async_copy(out_ref.at[here], out_hbm.at[here], out_sems.at[piece])
        copy.start()
        outs.append(copy)
    for copy in outs:
        copy.wait()


def expert_specs(count, width, size):
    whole = pl.BlockSpec((count, width), lambda k: (0, 0), pipeline_mode=pl.Buffered(1))
    into = pl.BlockSpec((width, size), lambda k: (0, k))
    back = pl.BlockSpec((size, width), lambda k: (k, 0))
    return whole, into, back


def expert_forward(rows, gates, ups, downs):
    count, width = rows.shape
    units = gates[0].shape[1]
    return pl.pallas_call(
        expert_forward_body,
        in_specs=[pl.BlockSpec(memory_space=pl.ANY)] * 7,
        out_specs=pl.BlockSpec(memory_space=pl.ANY),
        out_shape=pltpu.HBM((count, width), bf16),
        scratch_shapes=[
            pltpu.VMEM((count, width), bf16),
            pltpu.VMEM((2, width, units), bf16),
            pltpu.VMEM((2, width, units), bf16),
            pltpu.VMEM((2, units, width), bf16),
            pltpu.VMEM((count, width), bf16),
            pltpu.SemaphoreType.DMA((8,)),
            pltpu.SemaphoreType.DMA((2,)),
        ],
        compiler_params=params(44),
        cost_estimate=pl.CostEstimate(
            flops=12 * count * width * units // cheap,
            transcendentals=0,
            bytes_accessed=(count * width * 4 + 12 * width * units) // cheap,
        ),
        name="expert_forward",
    )(*in_hbm(rows, *gates, *ups, *downs))


def expert_backward_body(
    rows_ref,
    slot_grad_ref,
    gate_own_ref,
    gate_other_ref,
    up_own_ref,
    up_other_ref,
    down_own_ref,
    down_other_ref,
    inner_own_ref,
    inner_other_ref,
    gate_grad_own_ref,
    gate_grad_other_ref,
    up_grad_own_ref,
    up_grad_other_ref,
    out_ref,
    total_ref,
):
    step = pl.program_id(0)
    last = pl.num_programs(0) - 1
    for gate_ref, up_ref, down_ref, inner_ref, gate_grad_ref, up_grad_ref in (
        (gate_own_ref, up_own_ref, down_own_ref, inner_own_ref, gate_grad_own_ref, up_grad_own_ref),
        (
            gate_other_ref,
            up_other_ref,
            down_other_ref,
            inner_other_ref,
            gate_grad_other_ref,
            up_grad_other_ref,
        ),
    ):
        gate = dot(rows_ref[...], gate_ref[...])
        up = dot(rows_ref[...], up_ref[...])
        inner_grad = dot_cols(slot_grad_ref[...], down_ref[...])
        sigmoid_gate = jax.nn.sigmoid(gate)
        silu_gate = gate * sigmoid_gate
        inner_ref[...] = (silu_gate * up).astype(bf16)
        up_grad_ref[...] = (inner_grad * silu_gate).astype(bf16)
        gate_grad_ref[...] = (
            inner_grad * up * sigmoid_gate * (1.0 + gate * (1.0 - sigmoid_gate))
        ).astype(bf16)
    width = out_ref.shape[1]
    size = min(512, width)
    for start in range(0, width, size):
        here = pl.ds(start, size)
        part = None
        for grad_ref, w_ref in (
            (gate_grad_own_ref, gate_own_ref),
            (gate_grad_other_ref, gate_other_ref),
            (up_grad_own_ref, up_own_ref),
            (up_grad_other_ref, up_other_ref),
        ):
            term = dot_cols(grad_ref[...], w_ref[here, :])
            part = term if part is None else part + term

        @pl.when(step == 0)
        def _():
            total_ref[:, here] = part

        @pl.when((step > 0) & (step < last))
        def _():
            total_ref[:, here] += part

        @pl.when(step == last)
        def _():
            out_ref[:, here] = (total_ref[:, here] + part).astype(bf16)


def expert_backward(rows, slot_grad, gates, ups, downs):
    count, width = rows.shape
    units = gates[0].shape[1]
    steps = 2
    size = units // steps
    whole, into, back = expert_specs(count, width, size)
    acts = pl.BlockSpec((count, size), lambda k: (0, k))
    return pl.pallas_call(
        expert_backward_body,
        grid=(steps,),
        in_specs=[whole] * 2 + [into] * 4 + [back] * 2,
        out_specs=[acts] * 6 + [pl.BlockSpec((count, width), lambda k: (0, 0))],
        out_shape=[jax.ShapeDtypeStruct((count, units), bf16)] * 6
        + [jax.ShapeDtypeStruct((count, width), bf16)],
        scratch_shapes=[pltpu.VMEM((count, width), f32)],
        compiler_params=params(56),
        cost_estimate=pl.CostEstimate(
            flops=20 * count * width * units // cheap,
            transcendentals=0,
            bytes_accessed=count * width * 6 // cheap,
        ),
        name="expert_backward",
    )(rows, slot_grad, *gates, *ups, *downs)


def put_blocks(out_ref, row, product):
    chips = out_ref.shape[0]
    rows = product.shape[0] // chips
    for k in range(product.shape[1] // lanes):
        piece = product[:, k * lanes : (k + 1) * lanes].reshape(chips, rows, lanes)
        out_ref[:, row : row + rows, :] = piece
        row += rows
    return row


def joined(own_ref, other_ref):
    rows = jnp.concatenate([own_ref[...], other_ref[...]], axis=1)
    return rows.reshape(rows.shape[0] * rows.shape[1], rows.shape[2])


def weight_parcel_body(
    normed_ref, normed_other_ref, grads_ref, parcel_hbm, out_hbm, block_ref, sems
):
    step = pl.program_id(0)
    slot = step % 2
    group, rows = block_ref.shape[1], block_ref.shape[2]

    def copy(at):
        here = out_hbm.at[pl.ds(step * group, group), pl.ds(0, rows)]
        return pltpu.make_async_copy(block_ref.at[at], here, sems.at[at])

    @pl.when(step >= 2)
    def _():
        copy(slot).wait()

    left = joined(normed_ref, normed_other_ref)
    put_blocks(block_ref.at[slot], 0, dot_rows(left, grads_ref[...]).astype(bf16))
    copy(slot).start()

    @pl.when(step == pl.num_programs(0) - 1)
    def _():
        copy(1 - slot).wait()
        copy(slot).wait()


def weight_parcel(normed, grads, parcel):
    planes, half, width = normed[0].shape
    tokens, columns = grads.shape
    chips, height, _ = parcel.shape
    rows = width // chips * columns // lanes
    steps = planes
    left = pl.BlockSpec((planes, half, width // steps), lambda k: (0, 0, k))
    return pl.pallas_call(
        weight_parcel_body,
        grid=(steps,),
        in_specs=[
            left,
            left,
            pl.BlockSpec((tokens, columns), lambda k: (0, 0)),
            pl.BlockSpec(memory_space=pl.ANY),
        ],
        out_specs=pl.BlockSpec(memory_space=pl.ANY),
        out_shape=pltpu.HBM((chips, height, lanes), bf16),
        input_output_aliases={3: 0},
        scratch_shapes=[
            pltpu.VMEM((2, chips // steps, rows, lanes), bf16),
            pltpu.SemaphoreType.DMA((2,)),
        ],
        compiler_params=params(18),
        cost_estimate=pl.CostEstimate(
            flops=2 * tokens * width * columns,
            transcendentals=0,
            bytes_accessed=2 * (tokens * width + grads.size + chips * height * lanes),
        ),
        name="weight_parcel",
    )(*in_hbm(*normed, grads, parcel))


def out_parcel_body(
    start,
    per_chip,
    line,
    place_ref,
    low_ref,
    *refs,
):
    low_other_refs, mixed_refs, refs = refs[:line], refs[line : 2 * line], refs[2 * line :]
    router_ref, moe_ref, moe_other_ref, query_gain_ref, key_gain_ref, counts_ref = refs[:6]
    out_hbm, block_ref, sems = refs[6:]
    step = pl.program_id(0)
    slot = step % 2
    group = block_ref.shape[1]

    def copy(at):
        here = out_hbm.at[pl.ds(step * group, group), pl.ds(start, block_ref.shape[2])]
        return pltpu.make_async_copy(block_ref.at[at], here, sems.at[at])

    @pl.when(step >= 2)
    def _():
        copy(slot).wait()

    total = None
    for shift, mixed_ref in enumerate(mixed_refs):
        source = (place_ref[3] + line - shift) % line
        other = low_other_refs[0][...]
        for k in range(1, line):
            other = jnp.where(source == k, low_other_refs[k][...], other)
        left = jnp.concatenate([low_ref[source], other], axis=0)
        part = dot_rows(left, mixed_ref[...])
        total = part if total is None else total + part
    row = put_blocks(block_ref.at[slot], 0, total.astype(bf16))

    chips, rows, spare = router_ref.shape[0], router_ref.shape[1] // 2, lanes // 2
    core = place_ref[1]
    router = router_ref[:, pl.ds(core * rows, rows), :]
    if router.shape[2] < spare:
        fill = jnp.zeros((chips, rows, spare - router.shape[2]), f32)
        router = jnp.concatenate([router, fill], axis=2)
    moe = moe_ref[...] + moe_other_ref[...]
    span = 2 * rows
    moe = jnp.concatenate([moe[:, k * span : (k + 1) * span] for k in range(chips)], axis=0)
    moe = jnp.where(core == 0, moe[:, :rows], moe[:, rows:])
    heads, head = query_gain_ref.shape[0], query_gain_ref.shape[2]
    chip = lax.broadcasted_iota(jnp.int32, (chips, heads, head), 0) + step * chips
    lane = lax.broadcasted_iota(jnp.int32, (chips, heads, head), 2)
    mine = lane // per_chip == chip
    feature = lax.broadcasted_iota(jnp.int32, (head, spare), 0) % per_chip
    column = lax.broadcasted_iota(jnp.int32, (head, spare), 1)
    first_row = lax.broadcasted_iota(jnp.int32, (chips, heads, spare), 1) == 0
    used = 2 * per_chip + rows + 1
    blocks = []
    for part in range(2):
        block = jnp.zeros((chips * heads, spare), f32)
        for k, gain_ref in enumerate((query_gain_ref, key_gain_ref)):
            values = halves(gain_ref[:, 0, :])[part].astype(f32)
            values = jnp.where(mine, values[None], 0.0).reshape(chips * heads, head).astype(bf16)
            target = jnp.where(column == feature + k * per_chip, 1.0, 0.0).astype(bf16)
            block = block + dot(values, target)
        moe_part = halves(moe)[part].astype(f32)
        count = counts_ref[...] if part == 0 else jnp.zeros((chips, 1), f32)
        vector = jnp.concatenate(
            [jnp.zeros((chips, 2 * per_chip), f32), moe_part, count]
            + [jnp.zeros((chips, spare - used), f32)] * (used < spare),
            axis=1,
        )
        block = block.reshape(chips, heads, spare)
        blocks.append(block + jnp.where(first_row, vector[:, None, :], 0.0))
        if heads < rows // 2:
            blocks.append(jnp.zeros((chips, rows // 2 - heads, spare), f32))
    beside = jnp.concatenate(blocks, axis=1)
    small = jnp.concatenate([router, beside], axis=2).astype(bf16)
    block_ref[slot, :, row:, :] = small
    copy(slot).start()

    @pl.when(step == pl.num_programs(0) - 1)
    def _():
        copy(1 - slot).wait()
        copy(slot).wait()


def out_parcel(place, low, low_other, mixed, router, moe, query_gain, key_gain, counts):
    line, half, width = low.shape
    tokens, part = mixed[0].shape
    chips, router_rows, experts = router.shape
    heads, _, head = query_gain.shape
    room = width // chips * part // lanes
    small_rows = router_rows // 2
    height = 4 * room + small_rows
    steps = line
    group = chips // steps
    gain = pl.BlockSpec((heads, 1, head), lambda k, z: (0, 0, 0))
    vector = pl.BlockSpec((1, width // steps), lambda k, z: (0, k))
    return pl.pallas_call(
        lambda *refs: out_parcel_body(3 * room, head // chips, line, *refs),
        grid_spec=pltpu.PrefetchScalarGridSpec(
            num_scalar_prefetch=1,
            grid=(steps,),
            in_specs=[pl.BlockSpec((line, half, width // steps), lambda k, z: (0, 0, k))]
            + [pl.BlockSpec((half, width // steps), lambda k, z: (0, k))] * line
            + [pl.BlockSpec((tokens, part), lambda k, z: (0, 0))] * line
            + [pl.BlockSpec((group, router_rows, experts), lambda k, z: (k, 0, 0))]
            + [vector, vector, gain, gain, pl.BlockSpec((group, 1), lambda k, z: (k, 0))],
            out_specs=pl.BlockSpec(memory_space=pl.ANY),
            scratch_shapes=[
                pltpu.VMEM((2, group, room + small_rows, lanes), bf16),
                pltpu.SemaphoreType.DMA((2,)),
            ],
        ),
        out_shape=pltpu.HBM((chips, height, lanes), bf16),
        compiler_params=params(18),
        cost_estimate=pl.CostEstimate(
            flops=2 * tokens * width * part // cheap,
            transcendentals=0,
            bytes_accessed=2 * (tokens * width + chips * room * lanes) // cheap,
        ),
        name="out_parcel",
    )(
        place,
        *in_hbm(low),
        *low_other,
        *mixed,
        *in_hbm(router),
        *moe,
        query_gain,
        key_gain,
        counts,
    )


def parcel_sums_body(
    per_chip,
    place_ref,
    parcel_ref,
    w_query_ref,
    w_key_ref,
    w_value_ref,
    own_gain_ref,
    query_ref,
    key_ref,
    value_ref,
    out_ref,
    router_ref,
    query_gain_ref,
    key_gain_ref,
    moe_ref,
    count_ref,
    attn_ref,
    attn_other_ref,
    extra_ref,
    gain_ref,
):
    rows, columns = query_ref.shape
    step = pl.program_id(0)
    blocks = columns // lanes
    row = 3 * blocks * rows
    total = jnp.sum(parcel_ref[:, :row, :].astype(f32), axis=0)
    gain = jnp.zeros((rows, lanes), f32)
    for number, (ref, w_ref) in enumerate(
        ((query_ref, w_query_ref), (key_ref, w_key_ref), (value_ref, w_value_ref))
    ):
        for k in range(blocks):
            here = slice(k * lanes, (k + 1) * lanes)
            first_row = (number * blocks + k) * rows
            piece = total[first_row : first_row + rows, :]
            ref[:, here] = piece
            gain = gain + piece * w_ref[:, here].astype(f32)

    @pl.when(step == 0)
    def _():
        out_ref[...] = jnp.zeros_like(out_ref)
        extra_ref[...] = jnp.zeros_like(extra_ref)
        gain_ref[...] = jnp.zeros_like(gain_ref)

    gain_ref[...] += gain
    extra_ref[...] += jnp.sum(parcel_ref[:, row + blocks * rows :, :].astype(f32), axis=0)
    line = pl.num_programs(0)
    group = parcel_ref.shape[0] // line
    for x in range(line):
        part = parcel_ref[x * group : (x + 1) * group, row : row + blocks * rows, :]
        part = jnp.sum(part.astype(f32), axis=0)
        for k in range(blocks):
            here = slice(x * columns + k * lanes, x * columns + (k + 1) * lanes)
            out_ref[:, here] += part[k * rows : (k + 1) * rows, :]

    @pl.when(step == pl.num_programs(0) - 1)
    def _():
        half = rows // 2
        heads = query_gain_ref.shape[1]
        router_ref[...] = extra_ref[:, : router_ref.shape[1]]
        sums = extra_ref[0:heads, :] + extra_ref[half // 2 : half // 2 + heads, :]
        first_lane = lanes // 2 + 2 * per_chip
        moe_ref[...] = sums[0:1, first_lane : first_lane + half]
        count_ref[...] = sums[0:1, first_lane + half : first_lane + half + 1].astype(jnp.int32)
        sums = sums.T
        query_gain_ref[...] = sums[lanes // 2 : lanes // 2 + per_chip, :]
        key_gain_ref[...] = sums[lanes // 2 + per_chip : first_lane, :]
        attn = jnp.sum(gain_ref[...].T, axis=0, keepdims=True) / own_gain_ref[...]
        first = place_ref[1] == 0
        attn_ref[...] = jnp.where(first, attn[:, :half], attn[:, half:])
        attn_other_ref[...] = jnp.where(first, attn[:, half:], attn[:, :half])


def parcel_sums(place, parcel, weights, own_gain, planes, rows, width, heads, per_chip, experts):
    chips, height, _ = parcel.shape
    part = width // planes
    half = rows // 2
    wide = pl.BlockSpec((rows, part), lambda k, c: (0, k))

    def whole(shape):
        return pl.BlockSpec(shape, lambda k, c: (0, 0))

    small = [(half, experts), (per_chip, heads), (per_chip, heads), (1, half), (1, 1)]
    small += [(1, half), (1, half)]
    kinds = [f32] * 4 + [jnp.int32] + [f32] * 2
    return pl.pallas_call(
        lambda *refs: parcel_sums_body(per_chip, *refs),
        grid_spec=pltpu.PrefetchScalarGridSpec(
            num_scalar_prefetch=1,
            grid=(planes,),
            in_specs=[pl.BlockSpec((chips // planes, height, lanes), lambda k, c: (k, 0, 0))]
            + [pl.BlockSpec((rows, part), lambda k, c: (c[2], k))] * 3
            + [whole((1, rows))],
            out_specs=[wide] * 3 + [whole((rows, width))] + [whole(shape) for shape in small],
            scratch_shapes=[pltpu.VMEM((half, lanes), f32), pltpu.VMEM((rows, lanes), f32)],
        ),
        out_shape=[jax.ShapeDtypeStruct((rows, width), f32)] * 4
        + [jax.ShapeDtypeStruct(shape, kind) for shape, kind in zip(small, kinds)],
        compiler_params=params(14),
        cost_estimate=pl.CostEstimate(
            flops=parcel.size, transcendentals=0, bytes_accessed=2 * parcel.size
        ),
        name="parcel_sums",
    )(place, parcel, *in_hbm(*weights), own_gain)


def expert_weight_grads_body(rows_ref, slot_grad_ref, inner_ref, gate_ref, up_ref, *refs):
    grads = (
        dot_rows(rows_ref[...], gate_ref[...]),
        dot_rows(rows_ref[...], up_ref[...]),
        dot_rows(inner_ref[...], slot_grad_ref[...]),
    )
    others, outs = refs[:-3], refs[-3:]
    for k, (grad, out_ref) in enumerate(zip(grads, outs)):
        if others:
            grad = grad + others[k][...].astype(f32)
        out_ref[...] = grad.astype(out_ref.dtype)


def expert_weight_grads(rows, slot_grad, inner, gate_grad, up_grad, others, kind):
    count, width = rows.shape
    units = inner.shape[1]
    steps = 4
    size = width // steps
    wide = pl.BlockSpec((count, size), lambda k: (0, k))
    narrow = pl.BlockSpec((count, units), lambda k: (0, 0))
    into = pl.BlockSpec((size, units), lambda k: (k, 0))
    back = pl.BlockSpec((units, size), lambda k: (0, k))
    return pl.pallas_call(
        expert_weight_grads_body,
        grid=(steps,),
        in_specs=[wide, wide, narrow, narrow, narrow] + [into, into, back][: len(others)],
        out_specs=[into, into, back],
        out_shape=[
            jax.ShapeDtypeStruct((width, units), kind),
            jax.ShapeDtypeStruct((width, units), kind),
            jax.ShapeDtypeStruct((units, width), kind),
        ],
        compiler_params=params(30),
        cost_estimate=pl.CostEstimate(
            flops=6 * count * width * units // cheap,
            transcendentals=0,
            bytes_accessed=4 * count * width // cheap,
        ),
        name="expert_weight_grads",
    )(*in_hbm(rows, slot_grad, inner, gate_grad, up_grad, *others))


def normed_grad_body(stack_ref, query_ref, key_ref, value_ref, own_ref, other_ref):
    size = query_ref.shape[1]
    total = None
    for k, w_ref in enumerate((query_ref, key_ref, value_ref)):
        part = dot_cols(stack_ref[:, k * size : (k + 1) * size], w_ref[...])
        total = part if total is None else total + part
    half = own_ref.shape[0]
    first = pl.program_id(0) == 0

    @pl.when(first)
    def _():
        own_ref[...] = total[:half]
        other_ref[...] = total[half:]

    @pl.when(jnp.logical_not(first))
    def _():
        own_ref[...] += total[:half]
        other_ref[...] += total[half:]


def normed_grad_of(stack, weights):
    planes, seq_len, columns = stack.shape
    size = columns // 3
    full = weights[0].shape[0]
    half = pl.BlockSpec((seq_len // 2, full), lambda k: (0, 0))
    return pl.pallas_call(
        normed_grad_body,
        grid=(planes,),
        in_specs=[pl.BlockSpec((None, seq_len, columns), lambda k: (k, 0, 0))]
        + [pl.BlockSpec((full, size), lambda k: (0, k))] * 3,
        out_specs=[half] * 2,
        out_shape=[jax.ShapeDtypeStruct((seq_len // 2, full), f32)] * 2,
        compiler_params=params(20),
        cost_estimate=pl.CostEstimate(
            flops=2 * stack.size * full // cheap,
            transcendentals=0,
            bytes_accessed=2 * planes * columns * full // cheap,
        ),
        name="normed_grad",
    )(stack, *in_hbm(*weights))


def slot_rows_body(
    slots, place_ref, routes_ref, own_ref, other_ref, pick_ref, pick_back_ref, counts_ref, out_ref
):
    core = place_ref[1]
    experts = counts_ref.shape[0]
    half, seq_len = own_ref.shape[0], routes_ref.shape[1]

    @pl.when(pl.program_id(0) == 0)
    def _():
        routes = routes_ref[...]
        routes = jnp.where(
            core == 0, routes, jnp.concatenate([routes[:, half:], routes[:, :half]], axis=1)
        )
        numbers = lax.broadcasted_iota(jnp.int32, (experts, seq_len), 0)
        hits = numbers == routes[0:1, :]
        for k in range(1, routes.shape[0]):
            hits = hits | (numbers == routes[k : k + 1, :])
        hits_float = jnp.where(hits, 1.0, 0.0)
        counts_ref[...] = jnp.sum(hits_float, axis=1, keepdims=True)
        square = (seq_len, seq_len)
        shift = core * half
        earlier = lax.broadcasted_iota(jnp.int32, square, 0) + shift
        place = lax.broadcasted_iota(jnp.int32, square, 1) + shift
        earlier = jnp.where(earlier >= seq_len, earlier - seq_len, earlier)
        place = jnp.where(place >= seq_len, place - seq_len, place)
        before = jnp.where(earlier < place, 1.0, 0.0).astype(bf16)
        rank = jnp.where(hits, dot(hits_float.astype(bf16), before), -1.0)
        slot = lax.broadcasted_iota(jnp.int32, (experts, slots, seq_len), 1) + core * slots
        pick = jnp.where(rank[:, None, :] == slot.astype(f32), 1.0, 0.0)
        pick_ref[...] = pick.reshape(experts * slots, seq_len).astype(bf16)
        wide = (experts, experts * slots)
        spread = lax.broadcasted_iota(jnp.int32, wide, 1) // slots
        spread = spread == lax.broadcasted_iota(jnp.int32, wide, 0)
        spread_rank = dot(rank.T.astype(bf16), jnp.where(spread, 1.0, 0.0).astype(bf16))
        slot = lax.broadcasted_iota(jnp.int32, spread_rank.shape, 1) % slots + core * slots
        pick_back_ref[...] = jnp.where(spread_rank == slot.astype(f32), 1.0, 0.0).astype(bf16)

    rows = jnp.concatenate([own_ref[...], other_ref[...]], axis=0)
    out_ref[...] = dot(pick_ref[...], rows).astype(bf16)


def slot_rows(place, routes, own, other, experts, slots, columns):
    half = own.shape[0]
    top_count, seq_len = routes.shape
    steps = 2
    size = columns // steps
    rows = pl.BlockSpec((half, size), lambda k, c: (0, k))

    def whole(*shape):
        return pl.BlockSpec(shape, lambda k, c: (0, 0))

    return pl.pallas_call(
        lambda *refs: slot_rows_body(slots, *refs),
        grid_spec=pltpu.PrefetchScalarGridSpec(
            num_scalar_prefetch=1,
            grid=(steps,),
            in_specs=[whole(top_count, seq_len), rows, rows],
            out_specs=[
                whole(experts * slots, seq_len),
                whole(seq_len, experts * slots),
                whole(experts, 1),
                pl.BlockSpec((experts * slots, size), lambda k, c: (0, k)),
            ],
        ),
        out_shape=[
            pltpu.HBM((experts * slots, seq_len), bf16),
            pltpu.HBM((seq_len, experts * slots), bf16),
            pltpu.HBM((experts, 1), f32),
            pltpu.HBM((experts * slots, columns), bf16),
        ],
        compiler_params=params(20),
        cost_estimate=pl.CostEstimate(
            flops=2 * experts * slots * seq_len * columns,
            transcendentals=0,
            bytes_accessed=2 * (seq_len + experts * slots) * columns,
        ),
        name="slot_rows",
    )(place, routes, *in_hbm(own), other)


def token_sums_body(pick_ref, rows_ref, own_ref, other_ref):
    total = dot(pick_ref[...], rows_ref[...])
    half = own_ref.shape[0]
    own_ref[...] = total[:half]
    other_ref[...] = total[half:].astype(bf16)


def token_sums(pick_back, rows):
    seq_len, count = pick_back.shape
    width = rows.shape[1]
    steps = 2
    half = pl.BlockSpec((seq_len // 2, width // steps), lambda k: (0, k))
    return pl.pallas_call(
        token_sums_body,
        grid=(steps,),
        in_specs=[
            pl.BlockSpec((seq_len, count), lambda k: (0, 0)),
            pl.BlockSpec((count, width // steps), lambda k: (0, k)),
        ],
        out_specs=[half] * 2,
        out_shape=[jax.ShapeDtypeStruct((seq_len // 2, width), kind) for kind in (f32, bf16)],
        compiler_params=params(16),
        cost_estimate=pl.CostEstimate(
            flops=2 * count * seq_len * width,
            transcendentals=0,
            bytes_accessed=2 * count * (seq_len + width) + 4 * seq_len * width,
        ),
        name="token_sums",
    )(*in_hbm(pick_back, rows))


def hidden_grad_body(
    own_ref,
    other_ref,
    logit_high_ref,
    logit_low_ref,
    w_router_ref,
    gain_ref,
    hidden_ref,
    scale_ref,
    cot_ref,
    grad_ref,
    low_ref,
    gain_grad_ref,
):
    w_router = w_router_ref[...]
    moe_in = own_ref[...] + other_ref[...].astype(f32)
    moe_in = moe_in + dot(logit_high_ref[...], w_router)
    moe_in = moe_in + dot(logit_low_ref[...], w_router)
    hidden, scale = hidden_ref[...], scale_ref[...]
    gain_grad_ref[...] = jnp.sum(hidden * scale * moe_in, axis=0, keepdims=True)
    weighted = moe_in * gain_ref[...]
    inner = jnp.mean(hidden * weighted, axis=1, keepdims=True)
    grad = cot_ref[...].astype(f32) + scale * weighted
    grad = grad - hidden * (scale * scale * scale * inner)
    grad_ref[...] = grad
    low_ref[...] = grad.astype(bf16)


def hidden_grad_of(own, other, logit_high, logit_low, w_router, gain, hidden, scale, cot):
    rows, width = own.shape
    return pl.pallas_call(
        hidden_grad_body,
        out_shape=[
            pltpu.HBM((rows, width), f32),
            pltpu.HBM((rows, width), bf16),
            jax.ShapeDtypeStruct((1, width), f32),
        ],
        compiler_params=params(16),
        cost_estimate=pl.CostEstimate(
            flops=20 * rows * width, transcendentals=0, bytes_accessed=20 * rows * width
        ),
        name="hidden_grad",
    )(own, other, logit_high, logit_low, w_router, gain, hidden, scale, cot)


def router_grad_body(normed_ref, high_ref, low_ref, out_ref):
    normed = normed_ref[...]
    out_ref[...] = dot_rows(normed, high_ref[...]) + dot_rows(normed, low_ref[...])


def router_grad_of(normed, high, low):
    return pl.pallas_call(
        router_grad_body,
        out_shape=jax.ShapeDtypeStruct((normed.shape[1], high.shape[1]), f32),
        compiler_params=params(10),
        cost_estimate=pl.CostEstimate(
            flops=1 << 20, transcendentals=0, bytes_accessed=normed.size
        ),
        name="router_grad",
    )(normed, high, low)


def projections_body(
    own_ref,
    other_ref,
    gain_ref,
    w_query_ref,
    w_key_ref,
    w_value_ref,
    normed_own_ref,
    normed_other_ref,
    scale_ref,
    query_ref,
    key_ref,
    value_ref,
    squares_ref,
    normed_ref,
):
    half = own_ref.shape[0]
    step = pl.program_id(0)

    @pl.when(step == 0)
    def _():
        for k, (ref, out_ref) in enumerate(
            ((own_ref, normed_own_ref), (other_ref, normed_other_ref))
        ):
            rows = ref[...].astype(f32)
            scale = rms_scale(rows)
            normed = (rows * scale * gain_ref[...]).astype(bf16)
            out_ref[...] = normed
            normed_ref[k * half : (k + 1) * half, :] = normed
            if k == 0:
                scale_ref[...] = scale

    normed = normed_ref[...]
    query = dot(normed, w_query_ref[...])
    key = dot(normed, w_key_ref[...])
    query_ref[...] = query
    key_ref[...] = key
    value_ref[...] = dot(normed, w_value_ref[...]).astype(bf16)
    squares = jnp.concatenate(
        [jnp.sum(v * v, axis=1, keepdims=True) for v in (query, key)], axis=1
    )

    @pl.when(step == 0)
    def _():
        squares_ref[...] = squares

    @pl.when(step > 0)
    def _():
        squares_ref[...] += squares


def projections(own, other, gain, weights):
    half, width = own.shape
    local_width = weights[0].shape[1]
    steps = 4
    size = local_width // steps

    def whole(*shape):
        return pl.BlockSpec(shape, lambda k: (0, 0))

    column = pl.BlockSpec((2 * half, size), lambda k: (0, k))
    return pl.pallas_call(
        projections_body,
        grid=(steps,),
        in_specs=[whole(half, width), whole(half, width), whole(1, width)]
        + [pl.BlockSpec((width, size), lambda k: (0, k))] * 3,
        out_specs=[whole(half, width)] * 2
        + [whole(half, 1), column, column, column, whole(2 * half, 2)],
        out_shape=[jax.ShapeDtypeStruct((half, width), bf16)] * 2
        + [jax.ShapeDtypeStruct((half, 1), f32)]
        + [jax.ShapeDtypeStruct((2 * half, local_width), kind) for kind in (f32, f32, bf16)]
        + [jax.ShapeDtypeStruct((2 * half, 2), f32)],
        scratch_shapes=[pltpu.VMEM((2 * half, width), bf16)],
        compiler_params=params(22),
        cost_estimate=pl.CostEstimate(
            flops=1 << 20, transcendentals=0, bytes_accessed=width * local_width // cheap
        ),
        name="projections",
    )(*in_hbm(own, other), gain, *in_hbm(*weights))


def branch_body(mixed_ref, w_ref, own_ref, other_ref):
    total = dot(mixed_ref[...], w_ref[...])
    half = own_ref.shape[0]
    own_ref[...] = total[:half]
    other_ref[...] = total[half:]


def branch_of(mixed, w_out):
    seq_len, local_width = mixed.shape
    width = w_out.shape[1]
    steps = 4
    half = pl.BlockSpec((seq_len // 2, width // steps), lambda k: (0, k))
    return pl.pallas_call(
        branch_body,
        grid=(steps,),
        in_specs=[
            pl.BlockSpec((seq_len, local_width), lambda k: (0, 0)),
            pl.BlockSpec((local_width, width // steps), lambda k: (0, k)),
        ],
        out_specs=[half] * 2,
        out_shape=[jax.ShapeDtypeStruct((seq_len // 2, width), f32)] * 2,
        compiler_params=params(12),
        cost_estimate=pl.CostEstimate(
            flops=1 << 20, transcendentals=0, bytes_accessed=width * local_width // cheap
        ),
        name="branch",
    )(mixed, *in_hbm(w_out))


def moe_rows_body(
    own_ref,
    other_ref,
    branch_own_ref,
    branch_other_ref,
    got_own_ref,
    got_other_ref,
    gain_ref,
    w_router_ref,
    pick_ref,
    hidden_ref,
    scale_ref,
    normed_ref,
    probs_ref,
    out_ref,
):
    half = own_ref.shape[0]
    step = pl.program_id(0)

    @pl.when(step == 0)
    def _():
        for k, (ref, branch_ref, got_ref) in enumerate(
            ((own_ref, branch_own_ref, got_own_ref), (other_ref, branch_other_ref, got_other_ref))
        ):
            hidden = ref[...].astype(f32) + (branch_ref[...] + got_ref[...])
            scale = rms_scale(hidden)
            normed_ref[k * half : (k + 1) * half, :] = (hidden * scale * gain_ref[...]).astype(bf16)
            if k == 0:
                hidden_ref[...] = hidden
                scale_ref[...] = scale
        logits = dot_cols(normed_ref[...], w_router_ref[...])
        grown = jnp.exp(logits - jnp.max(logits, axis=1, keepdims=True))
        probs_ref[...] = grown / jnp.sum(grown, axis=1, keepdims=True)

    size = out_ref.shape[1]
    columns = pl.ds(pl.multiple_of(step * size, size), size)
    out_ref[...] = dot(pick_ref[...], normed_ref[:, columns]).astype(bf16)


def moe_rows(own, other, branch, got, gain, w_router, pick):
    half, width = own.shape
    count, seq_len = pick.shape
    experts = w_router.shape[0]
    steps = 4

    def whole(*shape):
        return pl.BlockSpec(shape, lambda k: (0, 0), pipeline_mode=pl.Buffered(1))

    def kept(*shape):
        return pl.BlockSpec(shape, lambda k: (0, 0))

    return pl.pallas_call(
        moe_rows_body,
        grid=(steps,),
        in_specs=[whole(half, width)] * 6
        + [whole(1, width), whole(experts, width), whole(count, seq_len)],
        out_specs=[
            kept(half, width),
            kept(half, 1),
            kept(seq_len, width),
            kept(seq_len, experts),
            pl.BlockSpec((count, width // steps), lambda k: (0, k)),
        ],
        out_shape=[
            pltpu.HBM((half, width), f32),
            jax.ShapeDtypeStruct((half, 1), f32),
            pltpu.HBM((seq_len, width), bf16),
            jax.ShapeDtypeStruct((seq_len, experts), f32),
            pltpu.HBM((count, width), bf16),
        ],
        compiler_params=params(24),
        cost_estimate=pl.CostEstimate(
            flops=1 << 20, transcendentals=0, bytes_accessed=width * count // cheap
        ),
        name="moe_rows",
    )(*in_hbm(own, other), *branch, *got, gain, *in_hbm(w_router, pick))


def local(
    residual_in,
    routes,
    segment_ids,
    gain_attn,
    w_query,
    w_key,
    w_value,
    gain_query,
    gain_key,
    w_out,
    gain_moe,
    w_router,
    w_gate,
    w_up,
    w_down,
    cotangent,
):
    core = lax.axis_index("tp")
    planes = lax.axis_size("z")
    chips = lax.axis_size(rows_of_chips)
    chip = lax.axis_index(rows_of_chips)
    own_rows, width = residual_in.shape
    seq_len, top_count = routes.shape
    local_width = w_query.shape[1]
    local_heads, head_dim = gain_query.shape
    experts = chips
    capacity = seq_len * top_count // experts
    own_slots = capacity // 2
    quarter = local_width // planes
    out_rows = width // chips

    def own_first(value):
        return jnp.where(
            core == 0, value, jnp.concatenate([value[own_rows:], value[:own_rows]], axis=0)
        )

    first_columns = width * 5 // 8
    numbers = jnp.stack([lax.axis_index("z"), core, chip, lax.axis_index("x")])
    cot_other = swap(cotangent)
    pick, pick_back, counts, cot_slots = slot_rows(
        numbers, routes.T, cotangent, cot_other, experts, own_slots, first_columns
    )
    cot_slots, residual_in, segment_ids = lax.optimization_barrier(
        (cot_slots, residual_in, segment_ids)
    )
    cot_first = all_to_all(
        cot_slots.reshape(experts, own_slots, first_columns), rows_of_chips
    ).reshape(experts * own_slots, first_columns)
    cot = jnp.concatenate([cotangent, cot_other], axis=0)

    place = own_first(jnp.arange(seq_len, dtype=jnp.int32))
    seg = own_first(segment_ids[0])
    same_doc = seg[:, None] == seg[None, :]
    position = place - jnp.min(jnp.where(same_doc, place[None, :], seq_len), axis=1)
    cosine, sine = rope_angles(position, head_dim)
    cosine = jnp.concatenate([cosine, cosine], axis=1)
    sine = jnp.concatenate([-sine, sine], axis=1)
    bias = jnp.where(same_doc & (place[None, :] <= place[:, None]), 0.0, mask_fill)

    other_in = swap(residual_in)
    normed_own, normed_other, scale_attn, queries, key_proj, values, squares = projections(
        residual_in, other_in, gain_attn[None], (w_query, w_key, w_value)
    )
    normed_planes = lax.all_gather(normed_own, "z", axis=0, tiled=False)
    query_gain = gain_query.reshape(1, local_width)
    key_gain = gain_key.reshape(1, local_width)
    q_rot, k_rot, probs, mixed, mixed_parts, scales = attention_forward(
        queries,
        key_proj,
        values,
        query_gain,
        key_gain,
        squares,
        swap(squares),
        cosine,
        sine,
        bias,
        local_heads,
        planes,
    )
    branch = branch_of(mixed, w_out)
    hidden_own, scale_moe, normed_moe, router_probs, moe_slots = moe_rows(
        residual_in,
        other_in,
        branch,
        (swap(branch[1]), swap(branch[0])),
        gain_moe[None],
        w_router.T,
        pick,
    )

    moe_slots, cot_first = lax.optimization_barrier((moe_slots, cot_first))
    arrived = all_to_all(
        moe_slots.reshape(experts, own_slots, width), rows_of_chips
    ).reshape(experts * own_slots, width)
    cot_slots = dot(pick, cot[:, first_columns:]).astype(bf16)
    arrived, cot_slots = lax.optimization_barrier((arrived, cot_slots))
    cot_rest = all_to_all(
        cot_slots.reshape(experts, own_slots, width - first_columns), rows_of_chips
    ).reshape(experts * own_slots, width - first_columns)

    gate_parts = (w_gate[0], swap(w_gate[0]))
    up_parts = (w_up[0], swap(w_up[0]))
    down_parts = (w_down[0], swap(w_down[0]))
    slot_out = expert_forward(arrived, gate_parts, up_parts, down_parts)
    slot_out, arrived, cot_rest, normed_planes = lax.optimization_barrier(
        (slot_out, arrived, cot_rest, normed_planes)
    )
    cot_arrived = jnp.concatenate([cot_first, cot_rest], axis=1)
    returned = all_to_all(
        slot_out.reshape(experts, own_slots, width), rows_of_chips
    ).reshape(experts * own_slots, width)
    slot_probs = jax.nn.softmax(dot(arrived, w_router), axis=-1)
    own_expert = jnp.arange(experts, dtype=jnp.int32) == chip
    slot_weight = jnp.sum(jnp.where(own_expert[None, :], slot_probs, 0.0), axis=1, keepdims=True)
    slot_grad = (slot_weight * cot_arrived.astype(f32)).astype(bf16)
    (
        inner_own,
        inner_other,
        gate_own,
        gate_other,
        up_own,
        up_other,
        slot_in_grad,
    ) = expert_backward(arrived, slot_grad, gate_parts, up_parts, down_parts)
    slot_in_grad, returned = lax.optimization_barrier((slot_in_grad, returned))
    grads_back = all_to_all(
        slot_in_grad.reshape(experts, own_slots, width), rows_of_chips
    ).reshape(experts * own_slots, width)
    normed_planes = (normed_planes, swap(normed_planes))
    number = lax.axis_index("x")
    line = lax.axis_size("x")
    mixed_line = [lax.dynamic_index_in_dim(mixed_parts, number, 0, keepdims=False)]
    for shift in range(1, line):
        part = lax.dynamic_index_in_dim(mixed_parts, (number + shift) % line, 0, keepdims=False)
        mixed_line.append(lax.ppermute(part, "x", [(k, (k + shift) % line) for k in range(line)]))
    others = expert_weight_grads(arrived, slot_grad, inner_other, gate_other, up_other, (), bf16)

    pick_pairs = pick.reshape(experts, own_slots, seq_len)
    weighted = pick_pairs.astype(f32) * router_probs.T[:, None, :]
    weight_high, weight_low = halves(weighted.reshape(experts * own_slots, seq_len))
    moe_part = dot_rows(weight_high, returned) + dot_rows(weight_low, returned)
    moe_own, moe_other = moe_part[:own_rows], moe_part[own_rows:].astype(bf16)
    pair_products = dot_cols(returned, cot).reshape(experts, own_slots, seq_len)
    prob_part = jnp.sum(pair_products * pick_pairs.astype(f32), axis=1).T
    other_part = swap(prob_part)
    prob_grad = prob_part + jnp.concatenate([other_part[own_rows:], other_part[:own_rows]], axis=0)
    logit_grad = router_probs * (
        prob_grad - jnp.sum(router_probs * prob_grad, axis=1, keepdims=True)
    )
    logit_high, logit_low = halves(logit_grad)
    router_grad = router_grad_of(normed_moe, logit_high, logit_low)
    (
        grads_back,
        others,
        moe_own,
        moe_other,
        logit_high,
        logit_low,
        router_grad,
        mixed_line,
    ) = lax.optimization_barrier(
        (
            grads_back,
            others,
            moe_own,
            moe_other,
            logit_high,
            logit_low,
            router_grad,
            mixed_line,
        )
    )
    moe_own = moe_own + swap(moe_other).astype(f32)
    output = (hidden_own + moe_own).astype(bf16)
    others = [swap(grad) for grad in others]
    grad_w_gate, grad_w_up, grad_w_down = expert_weight_grads(
        arrived, slot_grad, inner_own, gate_own, up_own, others, f32
    )
    moe_in_own, moe_in_other = token_sums(pick_back, grads_back)
    hidden_grad, hidden_low_own, gain_moe_grad = hidden_grad_of(
        moe_in_own,
        swap(moe_in_other),
        logit_high[:own_rows],
        logit_low[:own_rows],
        w_router.T,
        gain_moe[None],
        hidden_own,
        scale_moe,
        cotangent,
    )
    hidden_low_other = swap(hidden_low_own)
    low_line = lax.all_gather(hidden_low_own, "x", axis=0, tiled=False)

    value_grad, query_part, key_part, gain_query_grad, gain_key_grad, inner = attention_backward(
        hidden_low_own,
        hidden_low_other,
        w_out,
        values,
        q_rot,
        k_rot,
        probs,
        queries,
        key_proj,
        query_gain,
        key_gain,
        scales,
        cosine,
        sine,
        local_heads,
    )
    inner_other, gain_moe_other = lax.optimization_barrier((swap(inner), swap(gain_moe_grad)))
    to_planes = projection_grads(
        query_part,
        key_part,
        queries,
        key_proj,
        value_grad,
        scales,
        (inner, inner_other),
        planes,
    )

    grads_planes = all_to_all(to_planes, "z").reshape(planes * seq_len, 3 * quarter)
    low_line, _ = lax.optimization_barrier((low_line, to_planes))
    parcel = out_parcel(
        numbers,
        low_line,
        [swap(low_line[k]) for k in range(line)],
        mixed_line,
        router_grad.reshape(chips, out_rows, experts),
        (gain_moe_grad, gain_moe_other),
        gain_query_grad,
        gain_key_grad,
        counts,
    )
    normed_grad, normed_grad_other = normed_grad_of(to_planes, (w_query, w_key, w_value))
    normed_grad = normed_grad + swap(normed_grad_other)
    in_own = residual_in.astype(f32)
    in_scale = scale_attn
    weighted_attn = normed_grad * gain_attn
    grad_input = (
        hidden_grad
        + in_scale * weighted_attn
        - in_own * in_scale**3 * jnp.mean(in_own * weighted_attn, axis=1, keepdims=True)
    )

    grads_planes, parcel = lax.optimization_barrier((grads_planes, parcel))
    parcel = weight_parcel(normed_planes, grads_planes, parcel)
    parcel = all_to_all(parcel, rows_of_chips)
    per_chip = head_dim // chips
    own_gain = lax.dynamic_slice_in_dim(gain_attn, chip * out_rows, out_rows)[None]
    (
        grad_w_query,
        grad_w_key,
        grad_w_value,
        grad_w_out,
        grad_w_router,
        grad_gain_query,
        grad_gain_key,
        grad_gain_moe,
        count,
        attn_own,
        attn_other,
    ) = parcel_sums(
        numbers,
        parcel,
        (w_query, w_key, w_value),
        own_gain,
        planes,
        out_rows,
        local_width,
        local_heads,
        per_chip,
        experts,
    )
    return (
        output,
        grad_input,
        (attn_own + swap(attn_other))[0],
        grad_w_query,
        grad_w_key,
        grad_w_value,
        grad_gain_query.T,
        grad_gain_key.T,
        grad_w_out.T,
        grad_gain_moe[0],
        grad_w_router,
        grad_w_gate[None],
        grad_w_up[None],
        grad_w_down[None],
        count[0],
    )


def solution(mesh):
    side = round(mesh.shape["ep"] ** (1 / 3))
    cube = Mesh(mesh.devices.reshape(side, side, side, 2), rows_of_chips + ("tp",))
    ep = rows_of_chips
    both = rows_of_chips + ("tp",)
    in_specs = (
        P(both, None),
        P(ep, None),
        P(ep, None),
        P(),
        P(None, "tp"),
        P(None, "tp"),
        P(None, "tp"),
        P("tp", None),
        P("tp", None),
        P("tp", None),
        P(),
        P(),
        P(ep, None, "tp"),
        P(ep, None, "tp"),
        P(ep, "tp", None),
        P(both, None),
    )
    out_specs = (
        P(both, None),
        P(both, None),
        P(both),
        P(ep, "tp"),
        P(ep, "tp"),
        P(ep, "tp"),
        P("tp", ep),
        P("tp", ep),
        P("tp", ep),
        P(both),
        P(both, None),
        P(ep, None, "tp"),
        P(ep, None, "tp"),
        P(ep, "tp", None),
        P(ep),
    )
    return jax.shard_map(local, mesh=cube, in_specs=in_specs, out_specs=out_specs, check_vma=False)
```

```python
import jax
import jax.numpy as jnp
from jax import lax
from jax.experimental import pallas as pl
from jax.experimental.pallas import tpu as pltpu
from jax.sharding import Mesh, PartitionSpec as P

norm_eps = 1e-05
rope_base = 10000.0
mask_fill = -1e30
bf16 = jnp.bfloat16
f32 = jnp.float32
rows_of_chips = ("z", "x", "y")


def swap(value):
    return lax.ppermute(value, "tp", [(0, 1), (1, 0)])


def dot(left, right):
    return lax.dot_general(left, right, (((1,), (0,)), ((), ())), preferred_element_type=f32)


def dot_rows(left, right):
    return lax.dot_general(left, right, (((0,), (0,)), ((), ())), preferred_element_type=f32)


def dot_cols(left, right):
    return lax.dot_general(left, right, (((1,), (1,)), ((), ())), preferred_element_type=f32)


def all_to_all(value, axes):
    return lax.all_to_all(value, axes, split_axis=0, concat_axis=0, tiled=True)


def rms_scale(values):
    return lax.rsqrt(jnp.mean(values * values, axis=-1, keepdims=True) + norm_eps)


def halves(value):
    high = value.astype(bf16)
    return high, (value - high.astype(f32)).astype(bf16)


def rope_angles(positions, head_dim):
    half_dim = head_dim // 2
    exponent = jnp.arange(half_dim, dtype=f32) * (2.0 / head_dim)
    inverse = jnp.power(f32(rope_base), -exponent)
    angles = positions.astype(f32)[:, None] * inverse[None, :]
    return jnp.cos(angles), jnp.sin(angles)


lanes = 128
cheap = 64


def in_hbm(*arrays):
    return [pltpu.with_memory_space_constraint(array, pltpu.HBM) for array in arrays]


def params(megabytes):
    return pltpu.CompilerParams(vmem_limit_bytes=megabytes * 1024 * 1024)


def turn(value, cosine, sine):
    return value * cosine + pltpu.roll(value, value.shape[1] // 2, 1) * sine


def other_order(ref):
    half = ref.shape[0] // 2
    return jnp.concatenate([ref[half:, :], ref[:half, :]], axis=0)


def attention_forward_body(
    scale,
    full_width,
    query_ref,
    key_ref,
    value_ref,
    query_gain_ref,
    key_gain_ref,
    squares_ref,
    other_squares_ref,
    cosine_ref,
    sine_ref,
    bias_ref,
    q_rot_ref,
    k_rot_ref,
    probs_ref,
    mixed_ref,
    parts_ref,
    scales_ref,
):
    cosine, sine, bias = cosine_ref[...], sine_ref[...], bias_ref[...]
    head = cosine.shape[1]
    squares = squares_ref[...] + other_order(other_squares_ref)
    scales = lax.rsqrt(squares * (1.0 / full_width) + norm_eps)
    scales_ref[...] = scales
    for h in range(probs_ref.shape[0]):
        here = slice(h * head, (h + 1) * head)
        query = query_ref[:, here] * scales[:, 0:1] * query_gain_ref[:, here]
        key = key_ref[:, here] * scales[:, 1:2] * key_gain_ref[:, here]
        q_rot = turn(query, cosine, sine).astype(bf16)
        k_rot = turn(key, cosine, sine).astype(bf16)
        q_rot_ref[:, here] = q_rot
        k_rot_ref[:, here] = k_rot
        scores = dot_cols(q_rot, k_rot) * scale + bias
        grown = jnp.exp(scores - jnp.max(scores, axis=1, keepdims=True))
        probs = grown / jnp.sum(grown, axis=1, keepdims=True)
        probs_ref[h] = probs
        mixed_ref[:, here] = dot(probs.astype(bf16), value_ref[:, here]).astype(bf16)
    part = parts_ref.shape[2]
    for k in range(parts_ref.shape[0]):
        parts_ref[k] = mixed_ref[:, k * part : (k + 1) * part]


def attention_forward(
    queries, keys, values, query_gain, key_gain, squares, other, cosine, sine, bias, heads, planes
):
    seq_len, width = queries.shape
    head = width // heads
    group = min(heads, 4)
    column = pl.BlockSpec((seq_len, group * head), lambda h: (0, h))
    gain = pl.BlockSpec((1, group * head), lambda h: (0, h))

    def whole(array):
        return pl.BlockSpec(array.shape, lambda h: (0, 0))

    return pl.pallas_call(
        lambda *refs: attention_forward_body(head**-0.5, 2 * width, *refs),
        grid=(heads // group,),
        in_specs=[column, column, column, gain, gain]
        + [whole(a) for a in (squares, other, cosine, sine, bias)],
        out_specs=[
            column,
            column,
            pl.BlockSpec((group, seq_len, seq_len), lambda h: (h, 0, 0)),
            column,
            pl.BlockSpec(
                (planes * group // heads, seq_len, width // planes), lambda h: (h, 0, 0)
            ),
            whole(squares),
        ],
        out_shape=[
            jax.ShapeDtypeStruct((seq_len, width), bf16),
            jax.ShapeDtypeStruct((seq_len, width), bf16),
            jax.ShapeDtypeStruct((heads, seq_len, seq_len), f32),
            jax.ShapeDtypeStruct((seq_len, width), bf16),
            jax.ShapeDtypeStruct((planes, seq_len, width // planes), bf16),
            jax.ShapeDtypeStruct((seq_len, 2), f32),
        ],
        compiler_params=params(16),
        cost_estimate=pl.CostEstimate(
            flops=4 * seq_len * seq_len * width // cheap,
            transcendentals=0,
            bytes_accessed=seq_len * width * 16 // cheap,
        ),
        name="attention_forward",
    )(queries, keys, values, query_gain, key_gain, squares, other, cosine, sine, bias)


def attention_backward_body(
    scale,
    hidden_own_ref,
    hidden_other_ref,
    w_out_ref,
    value_ref,
    q_rot_ref,
    k_rot_ref,
    probs_ref,
    query_ref,
    key_ref,
    query_gain_ref,
    key_gain_ref,
    scales_ref,
    cosine_ref,
    sine_ref,
    value_grad_ref,
    query_part_ref,
    key_part_ref,
    query_gain_grad_ref,
    key_gain_grad_ref,
    inner_ref,
):
    cosine, sine = cosine_ref[...], sine_ref[...]
    hidden = jnp.concatenate([hidden_own_ref[...], hidden_other_ref[...]], axis=0)
    heads, head = query_gain_grad_ref.shape[0], query_gain_grad_ref.shape[2]
    grad_mixed = dot_cols(hidden, w_out_ref[...]).astype(bf16)
    total = None
    for h in range(heads):
        here = slice(h * head, (h + 1) * head)
        grad = grad_mixed[:, here]
        probs = probs_ref[h]
        grad_probs = dot_cols(grad, value_ref[:, here])
        inner = jnp.sum(probs * grad_probs, axis=1, keepdims=True)
        grad_scores = (probs * (grad_probs - inner)).astype(bf16)
        value_grad_ref[:, here] = dot_rows(probs.astype(bf16), grad).astype(bf16)
        row_inners = []
        for k, (grad_rot, raw_ref, gain_ref, part_ref, gain_grad_ref) in enumerate(
            (
                (
                    dot(grad_scores, k_rot_ref[:, here]),
                    query_ref,
                    query_gain_ref,
                    query_part_ref,
                    query_gain_grad_ref,
                ),
                (
                    dot_rows(grad_scores, q_rot_ref[:, here]),
                    key_ref,
                    key_gain_ref,
                    key_part_ref,
                    key_gain_grad_ref,
                ),
            )
        ):
            grad_normed = turn(grad_rot * scale, cosine, -sine)
            raw = raw_ref[:, here]
            gain_grad_ref[h] = jnp.sum(
                raw * scales_ref[:, k : k + 1] * grad_normed, axis=0, keepdims=True
            )
            weighted = grad_normed * gain_ref[:, here]
            part_ref[:, here] = weighted
            row_inners.append(jnp.sum(raw * weighted, axis=1, keepdims=True))
        row_inner = jnp.concatenate(row_inners, axis=1)
        total = row_inner if total is None else total + row_inner
    first = pl.program_id(0) == 0

    @pl.when(first)
    def _():
        inner_ref[...] = total

    @pl.when(jnp.logical_not(first))
    def _():
        inner_ref[...] += total


def attention_backward(
    hidden_own,
    hidden_other,
    w_out,
    values,
    q_rot,
    k_rot,
    probs,
    queries,
    keys,
    query_gain,
    key_gain,
    scales,
    cosine,
    sine,
    heads,
):
    seq_len, width = queries.shape
    head = width // heads
    group = min(heads, 4)
    column = pl.BlockSpec((seq_len, group * head), lambda h: (0, h))
    gain = pl.BlockSpec((1, group * head), lambda h: (0, h))

    def whole(array):
        return pl.BlockSpec(array.shape, lambda h: (0, 0))

    full = jax.ShapeDtypeStruct((seq_len, width), f32)
    line = jax.ShapeDtypeStruct((heads, 1, head), f32)
    line_spec = pl.BlockSpec((group, 1, head), lambda h: (h, 0, 0))
    sums = jax.ShapeDtypeStruct((seq_len, 2), f32)
    return pl.pallas_call(
        lambda *refs: attention_backward_body(head**-0.5, *refs),
        grid=(heads // group,),
        in_specs=[
            whole(hidden_own),
            whole(hidden_other),
            pl.BlockSpec((group * head, w_out.shape[1]), lambda h: (h, 0)),
            column,
            column,
            column,
            pl.BlockSpec((group, seq_len, seq_len), lambda h: (h, 0, 0)),
            column,
            column,
            gain,
            gain,
        ]
        + [whole(a) for a in (scales, cosine, sine)],
        out_specs=[column, column, column, line_spec, line_spec, whole(sums)],
        out_shape=[
            jax.ShapeDtypeStruct((seq_len, width), bf16),
            full,
            full,
            line,
            line,
            sums,
        ],
        compiler_params=params(20),
        cost_estimate=pl.CostEstimate(
            flops=10 * seq_len * seq_len * width + 2 * seq_len * width * w_out.shape[1],
            transcendentals=0,
            bytes_accessed=seq_len * width * 28
            + heads * seq_len * seq_len * 4
            + 2 * w_out.size
            + 4 * hidden_own.size,
        ),
        name="attention_backward",
    )(
        hidden_own,
        hidden_other,
        *in_hbm(w_out, values, q_rot, k_rot, probs, queries, keys),
        query_gain,
        key_gain,
        scales,
        cosine,
        sine,
    )


def projection_grads_body(
    width,
    query_part_ref,
    key_part_ref,
    query_ref,
    key_ref,
    value_grad_ref,
    scales_ref,
    inner_ref,
    other_inner_ref,
    stack_ref,
):
    blocks, _, columns = stack_ref.shape
    size = columns // 3
    inner = (inner_ref[...] + other_order(other_inner_ref)) * (1.0 / width)
    for k, (part_ref, raw_ref) in enumerate(
        ((query_part_ref, query_ref), (key_part_ref, key_ref))
    ):
        scale = scales_ref[:, k : k + 1]
        factor = scale * scale * scale * inner[:, k : k + 1]
        for block in range(blocks):
            here = slice(block * size, (block + 1) * size)
            grad = scale * part_ref[:, here] - raw_ref[:, here] * factor
            stack_ref[block, :, k * size : (k + 1) * size] = grad.astype(bf16)
    for block in range(blocks):
        stack_ref[block, :, 2 * size :] = value_grad_ref[:, block * size : (block + 1) * size]


def projection_grads(
    query_part, key_part, queries, keys, value_grad, scales, inners, planes
):
    seq_len, width = queries.shape
    size = width // planes
    steps = 2
    column = pl.BlockSpec((seq_len, width // steps), lambda k: (0, k))
    pair = pl.BlockSpec((seq_len, 2), lambda k: (0, 0))
    return pl.pallas_call(
        lambda *refs: projection_grads_body(2 * width, *refs),
        grid=(steps,),
        in_specs=[column] * 5 + [pair] * 3,
        out_specs=pl.BlockSpec((planes // steps, seq_len, 3 * size), lambda k: (k, 0, 0)),
        out_shape=jax.ShapeDtypeStruct((planes, seq_len, 3 * size), bf16),
        compiler_params=params(10),
        cost_estimate=pl.CostEstimate(
            flops=10 * seq_len * width, transcendentals=0, bytes_accessed=24 * seq_len * width
        ),
        name="projection_grads",
    )(query_part, key_part, queries, keys, value_grad, scales, *inners)


def expert_forward_body(
    rows_hbm,
    gate_own_hbm,
    gate_other_hbm,
    up_own_hbm,
    up_other_hbm,
    down_own_hbm,
    down_other_hbm,
    out_hbm,
    rows_ref,
    gate_ref,
    up_ref,
    down_ref,
    out_ref,
    in_sems,
    out_sems,
):
    count, width = rows_ref.shape
    pieces = 2
    size = count // pieces
    copies = {}
    order = [("rows", 0), ("gate", 0), ("up", 0), ("gate", 1), ("up", 1), ("down", 0), ("down", 1)]
    order += [("rows", k) for k in range(1, pieces)]
    sources = {
        "gate": ((gate_own_hbm, gate_other_hbm), gate_ref),
        "up": ((up_own_hbm, up_other_hbm), up_ref),
        "down": ((down_own_hbm, down_other_hbm), down_ref),
    }
    for number, (name, k) in enumerate(order):
        if name == "rows":
            here = pl.ds(k * size, size)
            copy = pltpu.make_async_copy(rows_hbm.at[here], rows_ref.at[here], in_sems.at[number])
        else:
            source, target = sources[name]
            copy = pltpu.make_async_copy(source[k], target.at[k], in_sems.at[number])
        copy.start()
        copies[name, k] = copy
    outs = []
    for piece in range(pieces):
        here = pl.ds(piece * size, size)
        copies["rows", piece].wait()
        inners = []
        for k in range(2):
            if piece == 0:
                copies["gate", k].wait()
            gate = dot(rows_ref[here, :], gate_ref[k])
            if piece == 0:
                copies["up", k].wait()
            up = dot(rows_ref[here, :], up_ref[k])
            inners.append((gate * jax.nn.sigmoid(gate) * up).astype(bf16))
        if piece == 0:
            copies["down", 0].wait()
            copies["down", 1].wait()
        step = min(512, width)
        for start in range(0, width, step):
            columns = pl.ds(start, step)
            total = dot(inners[0], down_ref[0, :, columns]) + dot(
                inners[1], down_ref[1, :, columns]
            )
            out_ref[here, columns] = total.astype(bf16)
        copy = pltpu.make_async_copy(out_ref.at[here], out_hbm.at[here], out_sems.at[piece])
        copy.start()
        outs.append(copy)
    for copy in outs:
        copy.wait()


def expert_specs(count, width, size):
    whole = pl.BlockSpec((count, width), lambda k: (0, 0), pipeline_mode=pl.Buffered(1))
    into = pl.BlockSpec((width, size), lambda k: (0, k))
    back = pl.BlockSpec((size, width), lambda k: (k, 0))
    return whole, into, back


def expert_forward(rows, gates, ups, downs):
    count, width = rows.shape
    units = gates[0].shape[1]
    return pl.pallas_call(
        expert_forward_body,
        in_specs=[pl.BlockSpec(memory_space=pl.ANY)] * 7,
        out_specs=pl.BlockSpec(memory_space=pl.ANY),
        out_shape=pltpu.HBM((count, width), bf16),
        scratch_shapes=[
            pltpu.VMEM((count, width), bf16),
            pltpu.VMEM((2, width, units), bf16),
            pltpu.VMEM((2, width, units), bf16),
            pltpu.VMEM((2, units, width), bf16),
            pltpu.VMEM((count, width), bf16),
            pltpu.SemaphoreType.DMA((8,)),
            pltpu.SemaphoreType.DMA((2,)),
        ],
        compiler_params=params(44),
        cost_estimate=pl.CostEstimate(
            flops=12 * count * width * units // cheap,
            transcendentals=0,
            bytes_accessed=(count * width * 4 + 12 * width * units) // cheap,
        ),
        name="expert_forward",
    )(*in_hbm(rows, *gates, *ups, *downs))


def expert_backward_body(
    rows_ref,
    slot_grad_ref,
    gate_own_ref,
    gate_other_ref,
    up_own_ref,
    up_other_ref,
    down_own_ref,
    down_other_ref,
    inner_own_ref,
    inner_other_ref,
    gate_grad_own_ref,
    gate_grad_other_ref,
    up_grad_own_ref,
    up_grad_other_ref,
    out_ref,
    total_ref,
):
    step = pl.program_id(0)
    last = pl.num_programs(0) - 1
    for gate_ref, up_ref, down_ref, inner_ref, gate_grad_ref, up_grad_ref in (
        (gate_own_ref, up_own_ref, down_own_ref, inner_own_ref, gate_grad_own_ref, up_grad_own_ref),
        (
            gate_other_ref,
            up_other_ref,
            down_other_ref,
            inner_other_ref,
            gate_grad_other_ref,
            up_grad_other_ref,
        ),
    ):
        gate = dot(rows_ref[...], gate_ref[...])
        up = dot(rows_ref[...], up_ref[...])
        inner_grad = dot_cols(slot_grad_ref[...], down_ref[...])
        sigmoid_gate = jax.nn.sigmoid(gate)
        silu_gate = gate * sigmoid_gate
        inner_ref[...] = (silu_gate * up).astype(bf16)
        up_grad_ref[...] = (inner_grad * silu_gate).astype(bf16)
        gate_grad_ref[...] = (
            inner_grad * up * sigmoid_gate * (1.0 + gate * (1.0 - sigmoid_gate))
        ).astype(bf16)
    width = out_ref.shape[1]
    size = min(512, width)
    for start in range(0, width, size):
        here = pl.ds(start, size)
        part = None
        for grad_ref, w_ref in (
            (gate_grad_own_ref, gate_own_ref),
            (gate_grad_other_ref, gate_other_ref),
            (up_grad_own_ref, up_own_ref),
            (up_grad_other_ref, up_other_ref),
        ):
            term = dot_cols(grad_ref[...], w_ref[here, :])
            part = term if part is None else part + term

        @pl.when(step == 0)
        def _():
            total_ref[:, here] = part

        @pl.when((step > 0) & (step < last))
        def _():
            total_ref[:, here] += part

        @pl.when(step == last)
        def _():
            out_ref[:, here] = (total_ref[:, here] + part).astype(bf16)


def expert_backward(rows, slot_grad, gates, ups, downs):
    count, width = rows.shape
    units = gates[0].shape[1]
    steps = 2
    size = units // steps
    whole, into, back = expert_specs(count, width, size)
    acts = pl.BlockSpec((count, size), lambda k: (0, k))
    return pl.pallas_call(
        expert_backward_body,
        grid=(steps,),
        in_specs=[whole] * 2 + [into] * 4 + [back] * 2,
        out_specs=[acts] * 6 + [pl.BlockSpec((count, width), lambda k: (0, 0))],
        out_shape=[jax.ShapeDtypeStruct((count, units), bf16)] * 6
        + [jax.ShapeDtypeStruct((count, width), bf16)],
        scratch_shapes=[pltpu.VMEM((count, width), f32)],
        compiler_params=params(56),
        cost_estimate=pl.CostEstimate(
            flops=20 * count * width * units // cheap,
            transcendentals=0,
            bytes_accessed=count * width * 6 // cheap,
        ),
        name="expert_backward",
    )(rows, slot_grad, *gates, *ups, *downs)


def put_blocks(out_ref, row, product):
    chips = out_ref.shape[0]
    rows = product.shape[0] // chips
    for k in range(product.shape[1] // lanes):
        piece = product[:, k * lanes : (k + 1) * lanes].reshape(chips, rows, lanes)
        out_ref[:, row : row + rows, :] = piece
        row += rows
    return row


def joined(own_ref, other_ref):
    rows = jnp.concatenate([own_ref[...], other_ref[...]], axis=1)
    return rows.reshape(rows.shape[0] * rows.shape[1], rows.shape[2])


def weight_parcel_body(
    normed_ref, normed_other_ref, grads_ref, parcel_hbm, out_hbm, block_ref, sems
):
    step = pl.program_id(0)
    slot = step % 2
    group, rows = block_ref.shape[1], block_ref.shape[2]

    def copy(at):
        here = out_hbm.at[pl.ds(step * group, group), pl.ds(0, rows)]
        return pltpu.make_async_copy(block_ref.at[at], here, sems.at[at])

    @pl.when(step >= 2)
    def _():
        copy(slot).wait()

    left = joined(normed_ref, normed_other_ref)
    put_blocks(block_ref.at[slot], 0, dot_rows(left, grads_ref[...]).astype(bf16))
    copy(slot).start()

    @pl.when(step == pl.num_programs(0) - 1)
    def _():
        copy(1 - slot).wait()
        copy(slot).wait()


def weight_parcel(normed, grads, parcel):
    planes, half, width = normed[0].shape
    tokens, columns = grads.shape
    chips, height, _ = parcel.shape
    rows = width // chips * columns // lanes
    steps = planes
    left = pl.BlockSpec((planes, half, width // steps), lambda k: (0, 0, k))
    return pl.pallas_call(
        weight_parcel_body,
        grid=(steps,),
        in_specs=[
            left,
            left,
            pl.BlockSpec((tokens, columns), lambda k: (0, 0)),
            pl.BlockSpec(memory_space=pl.ANY),
        ],
        out_specs=pl.BlockSpec(memory_space=pl.ANY),
        out_shape=pltpu.HBM((chips, height, lanes), bf16),
        input_output_aliases={3: 0},
        scratch_shapes=[
            pltpu.VMEM((2, chips // steps, rows, lanes), bf16),
            pltpu.SemaphoreType.DMA((2,)),
        ],
        compiler_params=params(18),
        cost_estimate=pl.CostEstimate(
            flops=2 * tokens * width * columns,
            transcendentals=0,
            bytes_accessed=2 * (tokens * width + grads.size + chips * height * lanes),
        ),
        name="weight_parcel",
    )(*in_hbm(*normed, grads, parcel))


def out_parcel_body(
    start,
    per_chip,
    line,
    place_ref,
    low_ref,
    *refs,
):
    low_other_refs, mixed_refs, refs = refs[:line], refs[line : 2 * line], refs[2 * line :]
    router_ref, moe_ref, moe_other_ref, query_gain_ref, key_gain_ref, counts_ref = refs[:6]
    out_hbm, block_ref, sems = refs[6:]
    step = pl.program_id(0)
    slot = step % 2
    group = block_ref.shape[1]

    def copy(at):
        here = out_hbm.at[pl.ds(step * group, group), pl.ds(start, block_ref.shape[2])]
        return pltpu.make_async_copy(block_ref.at[at], here, sems.at[at])

    @pl.when(step >= 2)
    def _():
        copy(slot).wait()

    total = None
    for shift, mixed_ref in enumerate(mixed_refs):
        source = (place_ref[3] + line - shift) % line
        other = low_other_refs[0][...]
        for k in range(1, line):
            other = jnp.where(source == k, low_other_refs[k][...], other)
        left = jnp.concatenate([low_ref[source], other], axis=0)
        part = dot_rows(left, mixed_ref[...])
        total = part if total is None else total + part
    row = put_blocks(block_ref.at[slot], 0, total.astype(bf16))

    chips, rows, spare = router_ref.shape[0], router_ref.shape[1] // 2, lanes // 2
    core = place_ref[1]
    router = router_ref[:, pl.ds(core * rows, rows), :]
    if router.shape[2] < spare:
        fill = jnp.zeros((chips, rows, spare - router.shape[2]), f32)
        router = jnp.concatenate([router, fill], axis=2)
    moe = moe_ref[...] + moe_other_ref[...]
    span = 2 * rows
    moe = jnp.concatenate([moe[:, k * span : (k + 1) * span] for k in range(chips)], axis=0)
    moe = jnp.where(core == 0, moe[:, :rows], moe[:, rows:])
    heads, head = query_gain_ref.shape[0], query_gain_ref.shape[2]
    chip = lax.broadcasted_iota(jnp.int32, (chips, heads, head), 0) + step * chips
    lane = lax.broadcasted_iota(jnp.int32, (chips, heads, head), 2)
    mine = lane // per_chip == chip
    feature = lax.broadcasted_iota(jnp.int32, (head, spare), 0) % per_chip
    column = lax.broadcasted_iota(jnp.int32, (head, spare), 1)
    first_row = lax.broadcasted_iota(jnp.int32, (chips, heads, spare), 1) == 0
    used = 2 * per_chip + rows + 1
    blocks = []
    for part in range(2):
        block = jnp.zeros((chips * heads, spare), f32)
        for k, gain_ref in enumerate((query_gain_ref, key_gain_ref)):
            values = halves(gain_ref[:, 0, :])[part].astype(f32)
            values = jnp.where(mine, values[None], 0.0).reshape(chips * heads, head).astype(bf16)
            target = jnp.where(column == feature + k * per_chip, 1.0, 0.0).astype(bf16)
            block = block + dot(values, target)
        moe_part = halves(moe)[part].astype(f32)
        count = counts_ref[...] if part == 0 else jnp.zeros((chips, 1), f32)
        vector = jnp.concatenate(
            [jnp.zeros((chips, 2 * per_chip), f32), moe_part, count]
            + [jnp.zeros((chips, spare - used), f32)] * (used < spare),
            axis=1,
        )
        block = block.reshape(chips, heads, spare)
        blocks.append(block + jnp.where(first_row, vector[:, None, :], 0.0))
        if heads < rows // 2:
            blocks.append(jnp.zeros((chips, rows // 2 - heads, spare), f32))
    beside = jnp.concatenate(blocks, axis=1)
    small = jnp.concatenate([router, beside], axis=2).astype(bf16)
    block_ref[slot, :, row:, :] = small
    copy(slot).start()

    @pl.when(step == pl.num_programs(0) - 1)
    def _():
        copy(1 - slot).wait()
        copy(slot).wait()


def out_parcel(place, low, low_other, mixed, router, moe, query_gain, key_gain, counts):
    line, half, width = low.shape
    tokens, part = mixed[0].shape
    chips, router_rows, experts = router.shape
    heads, _, head = query_gain.shape
    room = width // chips * part // lanes
    small_rows = router_rows // 2
    height = 4 * room + small_rows
    steps = line
    group = chips // steps
    gain = pl.BlockSpec((heads, 1, head), lambda k, z: (0, 0, 0))
    vector = pl.BlockSpec((1, width // steps), lambda k, z: (0, k))
    return pl.pallas_call(
        lambda *refs: out_parcel_body(3 * room, head // chips, line, *refs),
        grid_spec=pltpu.PrefetchScalarGridSpec(
            num_scalar_prefetch=1,
            grid=(steps,),
            in_specs=[pl.BlockSpec((line, half, width // steps), lambda k, z: (0, 0, k))]
            + [pl.BlockSpec((half, width // steps), lambda k, z: (0, k))] * line
            + [pl.BlockSpec((tokens, part), lambda k, z: (0, 0))] * line
            + [pl.BlockSpec((group, router_rows, experts), lambda k, z: (k, 0, 0))]
            + [vector, vector, gain, gain, pl.BlockSpec((group, 1), lambda k, z: (k, 0))],
            out_specs=pl.BlockSpec(memory_space=pl.ANY),
            scratch_shapes=[
                pltpu.VMEM((2, group, room + small_rows, lanes), bf16),
                pltpu.SemaphoreType.DMA((2,)),
            ],
        ),
        out_shape=pltpu.HBM((chips, height, lanes), bf16),
        compiler_params=params(18),
        cost_estimate=pl.CostEstimate(
            flops=2 * tokens * width * part // cheap,
            transcendentals=0,
            bytes_accessed=2 * (tokens * width + chips * room * lanes) // cheap,
        ),
        name="out_parcel",
    )(
        place,
        *in_hbm(low),
        *low_other,
        *mixed,
        *in_hbm(router),
        *moe,
        query_gain,
        key_gain,
        counts,
    )


def parcel_sums_body(
    per_chip,
    place_ref,
    parcel_ref,
    w_query_ref,
    w_key_ref,
    w_value_ref,
    own_gain_ref,
    query_ref,
    key_ref,
    value_ref,
    out_ref,
    router_ref,
    query_gain_ref,
    key_gain_ref,
    moe_ref,
    count_ref,
    attn_ref,
    attn_other_ref,
    extra_ref,
    gain_ref,
):
    rows, columns = query_ref.shape
    step = pl.program_id(0)
    blocks = columns // lanes
    row = 3 * blocks * rows
    total = jnp.sum(parcel_ref[:, :row, :].astype(f32), axis=0)
    gain = jnp.zeros((rows, lanes), f32)
    for number, (ref, w_ref) in enumerate(
        ((query_ref, w_query_ref), (key_ref, w_key_ref), (value_ref, w_value_ref))
    ):
        for k in range(blocks):
            here = slice(k * lanes, (k + 1) * lanes)
            first_row = (number * blocks + k) * rows
            piece = total[first_row : first_row + rows, :]
            ref[:, here] = piece
            gain = gain + piece * w_ref[:, here].astype(f32)

    @pl.when(step == 0)
    def _():
        out_ref[...] = jnp.zeros_like(out_ref)
        extra_ref[...] = jnp.zeros_like(extra_ref)
        gain_ref[...] = jnp.zeros_like(gain_ref)

    gain_ref[...] += gain
    extra_ref[...] += jnp.sum(parcel_ref[:, row + blocks * rows :, :].astype(f32), axis=0)
    line = pl.num_programs(0)
    group = parcel_ref.shape[0] // line
    for x in range(line):
        part = parcel_ref[x * group : (x + 1) * group, row : row + blocks * rows, :]
        part = jnp.sum(part.astype(f32), axis=0)
        for k in range(blocks):
            here = slice(x * columns + k * lanes, x * columns + (k + 1) * lanes)
            out_ref[:, here] += part[k * rows : (k + 1) * rows, :]

    @pl.when(step == pl.num_programs(0) - 1)
    def _():
        half = rows // 2
        heads = query_gain_ref.shape[1]
        router_ref[...] = extra_ref[:, : router_ref.shape[1]]
        sums = extra_ref[0:heads, :] + extra_ref[half // 2 : half // 2 + heads, :]
        first_lane = lanes // 2 + 2 * per_chip
        moe_ref[...] = sums[0:1, first_lane : first_lane + half]
        count_ref[...] = sums[0:1, first_lane + half : first_lane + half + 1].astype(jnp.int32)
        sums = sums.T
        query_gain_ref[...] = sums[lanes // 2 : lanes // 2 + per_chip, :]
        key_gain_ref[...] = sums[lanes // 2 + per_chip : first_lane, :]
        attn = jnp.sum(gain_ref[...].T, axis=0, keepdims=True) / own_gain_ref[...]
        first = place_ref[1] == 0
        attn_ref[...] = jnp.where(first, attn[:, :half], attn[:, half:])
        attn_other_ref[...] = jnp.where(first, attn[:, half:], attn[:, :half])


def parcel_sums(place, parcel, weights, own_gain, planes, rows, width, heads, per_chip, experts):
    chips, height, _ = parcel.shape
    part = width // planes
    half = rows // 2
    wide = pl.BlockSpec((rows, part), lambda k, c: (0, k))

    def whole(shape):
        return pl.BlockSpec(shape, lambda k, c: (0, 0))

    small = [(half, experts), (per_chip, heads), (per_chip, heads), (1, half), (1, 1)]
    small += [(1, half), (1, half)]
    kinds = [f32] * 4 + [jnp.int32] + [f32] * 2
    return pl.pallas_call(
        lambda *refs: parcel_sums_body(per_chip, *refs),
        grid_spec=pltpu.PrefetchScalarGridSpec(
            num_scalar_prefetch=1,
            grid=(planes,),
            in_specs=[pl.BlockSpec((chips // planes, height, lanes), lambda k, c: (k, 0, 0))]
            + [pl.BlockSpec((rows, part), lambda k, c: (c[2], k))] * 3
            + [whole((1, rows))],
            out_specs=[wide] * 3 + [whole((rows, width))] + [whole(shape) for shape in small],
            scratch_shapes=[pltpu.VMEM((half, lanes), f32), pltpu.VMEM((rows, lanes), f32)],
        ),
        out_shape=[jax.ShapeDtypeStruct((rows, width), f32)] * 4
        + [jax.ShapeDtypeStruct(shape, kind) for shape, kind in zip(small, kinds)],
        compiler_params=params(14),
        cost_estimate=pl.CostEstimate(
            flops=parcel.size, transcendentals=0, bytes_accessed=2 * parcel.size
        ),
        name="parcel_sums",
    )(place, parcel, *in_hbm(*weights), own_gain)


def expert_weight_grads_body(rows_ref, slot_grad_ref, inner_ref, gate_ref, up_ref, *refs):
    grads = (
        dot_rows(rows_ref[...], gate_ref[...]),
        dot_rows(rows_ref[...], up_ref[...]),
        dot_rows(inner_ref[...], slot_grad_ref[...]),
    )
    others, outs = refs[:-3], refs[-3:]
    for k, (grad, out_ref) in enumerate(zip(grads, outs)):
        if others:
            grad = grad + others[k][...].astype(f32)
        out_ref[...] = grad.astype(out_ref.dtype)


def expert_weight_grads(rows, slot_grad, inner, gate_grad, up_grad, others, kind):
    count, width = rows.shape
    units = inner.shape[1]
    steps = 4
    size = width // steps
    wide = pl.BlockSpec((count, size), lambda k: (0, k))
    narrow = pl.BlockSpec((count, units), lambda k: (0, 0))
    into = pl.BlockSpec((size, units), lambda k: (k, 0))
    back = pl.BlockSpec((units, size), lambda k: (0, k))
    return pl.pallas_call(
        expert_weight_grads_body,
        grid=(steps,),
        in_specs=[wide, wide, narrow, narrow, narrow] + [into, into, back][: len(others)],
        out_specs=[into, into, back],
        out_shape=[
            jax.ShapeDtypeStruct((width, units), kind),
            jax.ShapeDtypeStruct((width, units), kind),
            jax.ShapeDtypeStruct((units, width), kind),
        ],
        compiler_params=params(30),
        cost_estimate=pl.CostEstimate(
            flops=6 * count * width * units // cheap,
            transcendentals=0,
            bytes_accessed=4 * count * width // cheap,
        ),
        name="expert_weight_grads",
    )(*in_hbm(rows, slot_grad, inner, gate_grad, up_grad, *others))


def normed_grad_body(stack_ref, query_ref, key_ref, value_ref, own_ref, other_ref):
    size = query_ref.shape[1]
    total = None
    for k, w_ref in enumerate((query_ref, key_ref, value_ref)):
        part = dot_cols(stack_ref[:, k * size : (k + 1) * size], w_ref[...])
        total = part if total is None else total + part
    half = own_ref.shape[0]
    first = pl.program_id(0) == 0

    @pl.when(first)
    def _():
        own_ref[...] = total[:half]
        other_ref[...] = total[half:]

    @pl.when(jnp.logical_not(first))
    def _():
        own_ref[...] += total[:half]
        other_ref[...] += total[half:]


def normed_grad_of(stack, weights):
    planes, seq_len, columns = stack.shape
    size = columns // 3
    full = weights[0].shape[0]
    half = pl.BlockSpec((seq_len // 2, full), lambda k: (0, 0))
    return pl.pallas_call(
        normed_grad_body,
        grid=(planes,),
        in_specs=[pl.BlockSpec((None, seq_len, columns), lambda k: (k, 0, 0))]
        + [pl.BlockSpec((full, size), lambda k: (0, k))] * 3,
        out_specs=[half] * 2,
        out_shape=[jax.ShapeDtypeStruct((seq_len // 2, full), f32)] * 2,
        compiler_params=params(20),
        cost_estimate=pl.CostEstimate(
            flops=2 * stack.size * full // cheap,
            transcendentals=0,
            bytes_accessed=2 * planes * columns * full // cheap,
        ),
        name="normed_grad",
    )(stack, *in_hbm(*weights))


def slot_rows_body(
    slots, place_ref, routes_ref, own_ref, other_ref, pick_ref, pick_back_ref, counts_ref, out_ref
):
    core = place_ref[1]
    experts = counts_ref.shape[0]
    half, seq_len = own_ref.shape[0], routes_ref.shape[1]

    @pl.when(pl.program_id(0) == 0)
    def _():
        routes = routes_ref[...]
        routes = jnp.where(
            core == 0, routes, jnp.concatenate([routes[:, half:], routes[:, :half]], axis=1)
        )
        numbers = lax.broadcasted_iota(jnp.int32, (experts, seq_len), 0)
        hits = numbers == routes[0:1, :]
        for k in range(1, routes.shape[0]):
            hits = hits | (numbers == routes[k : k + 1, :])
        hits_float = jnp.where(hits, 1.0, 0.0)
        counts_ref[...] = jnp.sum(hits_float, axis=1, keepdims=True)
        square = (seq_len, seq_len)
        shift = core * half
        earlier = lax.broadcasted_iota(jnp.int32, square, 0) + shift
        place = lax.broadcasted_iota(jnp.int32, square, 1) + shift
        earlier = jnp.where(earlier >= seq_len, earlier - seq_len, earlier)
        place = jnp.where(place >= seq_len, place - seq_len, place)
        before = jnp.where(earlier < place, 1.0, 0.0).astype(bf16)
        rank = jnp.where(hits, dot(hits_float.astype(bf16), before), -1.0)
        slot = lax.broadcasted_iota(jnp.int32, (experts, slots, seq_len), 1) + core * slots
        pick = jnp.where(rank[:, None, :] == slot.astype(f32), 1.0, 0.0)
        pick_ref[...] = pick.reshape(experts * slots, seq_len).astype(bf16)
        wide = (experts, experts * slots)
        spread = lax.broadcasted_iota(jnp.int32, wide, 1) // slots
        spread = spread == lax.broadcasted_iota(jnp.int32, wide, 0)
        spread_rank = dot(rank.T.astype(bf16), jnp.where(spread, 1.0, 0.0).astype(bf16))
        slot = lax.broadcasted_iota(jnp.int32, spread_rank.shape, 1) % slots + core * slots
        pick_back_ref[...] = jnp.where(spread_rank == slot.astype(f32), 1.0, 0.0).astype(bf16)

    rows = jnp.concatenate([own_ref[...], other_ref[...]], axis=0)
    out_ref[...] = dot(pick_ref[...], rows).astype(bf16)


def slot_rows(place, routes, own, other, experts, slots, columns):
    half = own.shape[0]
    top_count, seq_len = routes.shape
    steps = 2
    size = columns // steps
    rows = pl.BlockSpec((half, size), lambda k, c: (0, k))

    def whole(*shape):
        return pl.BlockSpec(shape, lambda k, c: (0, 0))

    return pl.pallas_call(
        lambda *refs: slot_rows_body(slots, *refs),
        grid_spec=pltpu.PrefetchScalarGridSpec(
            num_scalar_prefetch=1,
            grid=(steps,),
            in_specs=[whole(top_count, seq_len), rows, rows],
            out_specs=[
                whole(experts * slots, seq_len),
                whole(seq_len, experts * slots),
                whole(experts, 1),
                pl.BlockSpec((experts * slots, size), lambda k, c: (0, k)),
            ],
        ),
        out_shape=[
            pltpu.HBM((experts * slots, seq_len), bf16),
            pltpu.HBM((seq_len, experts * slots), bf16),
            pltpu.HBM((experts, 1), f32),
            pltpu.HBM((experts * slots, columns), bf16),
        ],
        compiler_params=params(20),
        cost_estimate=pl.CostEstimate(
            flops=2 * experts * slots * seq_len * columns,
            transcendentals=0,
            bytes_accessed=2 * (seq_len + experts * slots) * columns,
        ),
        name="slot_rows",
    )(place, routes, *in_hbm(own), other)


def token_sums_body(pick_ref, rows_ref, own_ref, other_ref):
    total = dot(pick_ref[...], rows_ref[...])
    half = own_ref.shape[0]
    own_ref[...] = total[:half]
    other_ref[...] = total[half:].astype(bf16)


def token_sums(pick_back, rows):
    seq_len, count = pick_back.shape
    width = rows.shape[1]
    steps = 2
    half = pl.BlockSpec((seq_len // 2, width // steps), lambda k: (0, k))
    return pl.pallas_call(
        token_sums_body,
        grid=(steps,),
        in_specs=[
            pl.BlockSpec((seq_len, count), lambda k: (0, 0)),
            pl.BlockSpec((count, width // steps), lambda k: (0, k)),
        ],
        out_specs=[half] * 2,
        out_shape=[jax.ShapeDtypeStruct((seq_len // 2, width), kind) for kind in (f32, bf16)],
        compiler_params=params(16),
        cost_estimate=pl.CostEstimate(
            flops=2 * count * seq_len * width,
            transcendentals=0,
            bytes_accessed=2 * count * (seq_len + width) + 4 * seq_len * width,
        ),
        name="token_sums",
    )(*in_hbm(pick_back, rows))


def hidden_grad_body(
    own_ref,
    other_ref,
    logit_high_ref,
    logit_low_ref,
    w_router_ref,
    gain_ref,
    hidden_ref,
    scale_ref,
    cot_ref,
    grad_ref,
    low_ref,
    gain_grad_ref,
):
    w_router = w_router_ref[...]
    moe_in = own_ref[...] + other_ref[...].astype(f32)
    moe_in = moe_in + dot(logit_high_ref[...], w_router)
    moe_in = moe_in + dot(logit_low_ref[...], w_router)
    hidden, scale = hidden_ref[...], scale_ref[...]
    gain_grad_ref[...] = jnp.sum(hidden * scale * moe_in, axis=0, keepdims=True)
    weighted = moe_in * gain_ref[...]
    inner = jnp.mean(hidden * weighted, axis=1, keepdims=True)
    grad = cot_ref[...].astype(f32) + scale * weighted
    grad = grad - hidden * (scale * scale * scale * inner)
    grad_ref[...] = grad
    low_ref[...] = grad.astype(bf16)


def hidden_grad_of(own, other, logit_high, logit_low, w_router, gain, hidden, scale, cot):
    rows, width = own.shape
    return pl.pallas_call(
        hidden_grad_body,
        out_shape=[
            pltpu.HBM((rows, width), f32),
            pltpu.HBM((rows, width), bf16),
            jax.ShapeDtypeStruct((1, width), f32),
        ],
        compiler_params=params(16),
        cost_estimate=pl.CostEstimate(
            flops=20 * rows * width, transcendentals=0, bytes_accessed=20 * rows * width
        ),
        name="hidden_grad",
    )(own, other, logit_high, logit_low, w_router, gain, hidden, scale, cot)


def router_grad_body(normed_ref, high_ref, low_ref, out_ref):
    normed = normed_ref[...]
    out_ref[...] = dot_rows(normed, high_ref[...]) + dot_rows(normed, low_ref[...])


def router_grad_of(normed, high, low):
    return pl.pallas_call(
        router_grad_body,
        out_shape=jax.ShapeDtypeStruct((normed.shape[1], high.shape[1]), f32),
        compiler_params=params(10),
        cost_estimate=pl.CostEstimate(
            flops=1 << 20, transcendentals=0, bytes_accessed=normed.size
        ),
        name="router_grad",
    )(normed, high, low)


def projections_body(
    own_ref,
    other_ref,
    gain_ref,
    w_query_ref,
    w_key_ref,
    w_value_ref,
    normed_own_ref,
    normed_other_ref,
    scale_ref,
    query_ref,
    key_ref,
    value_ref,
    squares_ref,
    normed_ref,
):
    half = own_ref.shape[0]
    step = pl.program_id(0)

    @pl.when(step == 0)
    def _():
        for k, (ref, out_ref) in enumerate(
            ((own_ref, normed_own_ref), (other_ref, normed_other_ref))
        ):
            rows = ref[...].astype(f32)
            scale = rms_scale(rows)
            normed = (rows * scale * gain_ref[...]).astype(bf16)
            out_ref[...] = normed
            normed_ref[k * half : (k + 1) * half, :] = normed
            if k == 0:
                scale_ref[...] = scale

    normed = normed_ref[...]
    query = dot(normed, w_query_ref[...])
    key = dot(normed, w_key_ref[...])
    query_ref[...] = query
    key_ref[...] = key
    value_ref[...] = dot(normed, w_value_ref[...]).astype(bf16)
    squares = jnp.concatenate(
        [jnp.sum(v * v, axis=1, keepdims=True) for v in (query, key)], axis=1
    )

    @pl.when(step == 0)
    def _():
        squares_ref[...] = squares

    @pl.when(step > 0)
    def _():
        squares_ref[...] += squares


def projections(own, other, gain, weights):
    half, width = own.shape
    local_width = weights[0].shape[1]
    steps = 4
    size = local_width // steps

    def whole(*shape):
        return pl.BlockSpec(shape, lambda k: (0, 0))

    column = pl.BlockSpec((2 * half, size), lambda k: (0, k))
    return pl.pallas_call(
        projections_body,
        grid=(steps,),
        in_specs=[whole(half, width), whole(half, width), whole(1, width)]
        + [pl.BlockSpec((width, size), lambda k: (0, k))] * 3,
        out_specs=[whole(half, width)] * 2
        + [whole(half, 1), column, column, column, whole(2 * half, 2)],
        out_shape=[jax.ShapeDtypeStruct((half, width), bf16)] * 2
        + [jax.ShapeDtypeStruct((half, 1), f32)]
        + [jax.ShapeDtypeStruct((2 * half, local_width), kind) for kind in (f32, f32, bf16)]
        + [jax.ShapeDtypeStruct((2 * half, 2), f32)],
        scratch_shapes=[pltpu.VMEM((2 * half, width), bf16)],
        compiler_params=params(22),
        cost_estimate=pl.CostEstimate(
            flops=1 << 20, transcendentals=0, bytes_accessed=width * local_width // cheap
        ),
        name="projections",
    )(*in_hbm(own, other), gain, *in_hbm(*weights))


def branch_body(mixed_ref, w_ref, own_ref, other_ref):
    total = dot(mixed_ref[...], w_ref[...])
    half = own_ref.shape[0]
    own_ref[...] = total[:half]
    other_ref[...] = total[half:]


def branch_of(mixed, w_out):
    seq_len, local_width = mixed.shape
    width = w_out.shape[1]
    steps = 4
    half = pl.BlockSpec((seq_len // 2, width // steps), lambda k: (0, k))
    return pl.pallas_call(
        branch_body,
        grid=(steps,),
        in_specs=[
            pl.BlockSpec((seq_len, local_width), lambda k: (0, 0)),
            pl.BlockSpec((local_width, width // steps), lambda k: (0, k)),
        ],
        out_specs=[half] * 2,
        out_shape=[jax.ShapeDtypeStruct((seq_len // 2, width), f32)] * 2,
        compiler_params=params(12),
        cost_estimate=pl.CostEstimate(
            flops=1 << 20, transcendentals=0, bytes_accessed=width * local_width // cheap
        ),
        name="branch",
    )(mixed, *in_hbm(w_out))


def moe_rows_body(
    own_ref,
    other_ref,
    branch_own_ref,
    branch_other_ref,
    got_own_ref,
    got_other_ref,
    gain_ref,
    w_router_ref,
    pick_ref,
    hidden_ref,
    scale_ref,
    normed_ref,
    probs_ref,
    out_ref,
):
    half = own_ref.shape[0]
    step = pl.program_id(0)

    @pl.when(step == 0)
    def _():
        for k, (ref, branch_ref, got_ref) in enumerate(
            ((own_ref, branch_own_ref, got_own_ref), (other_ref, branch_other_ref, got_other_ref))
        ):
            hidden = ref[...].astype(f32) + (branch_ref[...] + got_ref[...])
            scale = rms_scale(hidden)
            normed_ref[k * half : (k + 1) * half, :] = (hidden * scale * gain_ref[...]).astype(bf16)
            if k == 0:
                hidden_ref[...] = hidden
                scale_ref[...] = scale
        logits = dot_cols(normed_ref[...], w_router_ref[...])
        grown = jnp.exp(logits - jnp.max(logits, axis=1, keepdims=True))
        probs_ref[...] = grown / jnp.sum(grown, axis=1, keepdims=True)

    size = out_ref.shape[1]
    columns = pl.ds(pl.multiple_of(step * size, size), size)
    out_ref[...] = dot(pick_ref[...], normed_ref[:, columns]).astype(bf16)


def moe_rows(own, other, branch, got, gain, w_router, pick):
    half, width = own.shape
    count, seq_len = pick.shape
    experts = w_router.shape[0]
    steps = 4

    def whole(*shape):
        return pl.BlockSpec(shape, lambda k: (0, 0), pipeline_mode=pl.Buffered(1))

    def kept(*shape):
        return pl.BlockSpec(shape, lambda k: (0, 0))

    return pl.pallas_call(
        moe_rows_body,
        grid=(steps,),
        in_specs=[whole(half, width)] * 6
        + [whole(1, width), whole(experts, width), whole(count, seq_len)],
        out_specs=[
            kept(half, width),
            kept(half, 1),
            kept(seq_len, width),
            kept(seq_len, experts),
            pl.BlockSpec((count, width // steps), lambda k: (0, k)),
        ],
        out_shape=[
            pltpu.HBM((half, width), f32),
            jax.ShapeDtypeStruct((half, 1), f32),
            pltpu.HBM((seq_len, width), bf16),
            jax.ShapeDtypeStruct((seq_len, experts), f32),
            pltpu.HBM((count, width), bf16),
        ],
        compiler_params=params(24),
        cost_estimate=pl.CostEstimate(
            flops=1 << 20, transcendentals=0, bytes_accessed=width * count // cheap
        ),
        name="moe_rows",
    )(*in_hbm(own, other), *branch, *got, gain, *in_hbm(w_router, pick))


def local(
    residual_in,
    routes,
    segment_ids,
    gain_attn,
    w_query,
    w_key,
    w_value,
    gain_query,
    gain_key,
    w_out,
    gain_moe,
    w_router,
    w_gate,
    w_up,
    w_down,
    cotangent,
):
    core = lax.axis_index("tp")
    planes = lax.axis_size("z")
    chips = lax.axis_size(rows_of_chips)
    chip = lax.axis_index(rows_of_chips)
    own_rows, width = residual_in.shape
    seq_len, top_count = routes.shape
    local_width = w_query.shape[1]
    local_heads, head_dim = gain_query.shape
    experts = chips
    capacity = seq_len * top_count // experts
    own_slots = capacity // 2
    quarter = local_width // planes
    out_rows = width // chips

    def own_first(value):
        return jnp.where(
            core == 0, value, jnp.concatenate([value[own_rows:], value[:own_rows]], axis=0)
        )

    first_columns = width * 5 // 8
    numbers = jnp.stack([lax.axis_index("z"), core, chip, lax.axis_index("x")])
    cot_other = swap(cotangent)
    pick, pick_back, counts, cot_slots = slot_rows(
        numbers, routes.T, cotangent, cot_other, experts, own_slots, first_columns
    )
    cot_slots, residual_in, segment_ids = lax.optimization_barrier(
        (cot_slots, residual_in, segment_ids)
    )
    cot_first = all_to_all(
        cot_slots.reshape(experts, own_slots, first_columns), rows_of_chips
    ).reshape(experts * own_slots, first_columns)
    cot = jnp.concatenate([cotangent, cot_other], axis=0)

    place = own_first(jnp.arange(seq_len, dtype=jnp.int32))
    seg = own_first(segment_ids[0])
    same_doc = seg[:, None] == seg[None, :]
    position = place - jnp.min(jnp.where(same_doc, place[None, :], seq_len), axis=1)
    cosine, sine = rope_angles(position, head_dim)
    cosine = jnp.concatenate([cosine, cosine], axis=1)
    sine = jnp.concatenate([-sine, sine], axis=1)
    bias = jnp.where(same_doc & (place[None, :] <= place[:, None]), 0.0, mask_fill)

    other_in = swap(residual_in)
    normed_own, normed_other, scale_attn, queries, key_proj, values, squares = projections(
        residual_in, other_in, gain_attn[None], (w_query, w_key, w_value)
    )
    normed_planes = lax.all_gather(normed_own, "z", axis=0, tiled=False)
    query_gain = gain_query.reshape(1, local_width)
    key_gain = gain_key.reshape(1, local_width)
    q_rot, k_rot, probs, mixed, mixed_parts, scales = attention_forward(
        queries,
        key_proj,
        values,
        query_gain,
        key_gain,
        squares,
        swap(squares),
        cosine,
        sine,
        bias,
        local_heads,
        planes,
    )
    branch = branch_of(mixed, w_out)
    hidden_own, scale_moe, normed_moe, router_probs, moe_slots = moe_rows(
        residual_in,
        other_in,
        branch,
        (swap(branch[1]), swap(branch[0])),
        gain_moe[None],
        w_router.T,
        pick,
    )

    moe_slots, cot_first = lax.optimization_barrier((moe_slots, cot_first))
    arrived = all_to_all(
        moe_slots.reshape(experts, own_slots, width), rows_of_chips
    ).reshape(experts * own_slots, width)
    cot_slots = dot(pick, cot[:, first_columns:]).astype(bf16)
    arrived, cot_slots = lax.optimization_barrier((arrived, cot_slots))
    cot_rest = all_to_all(
        cot_slots.reshape(experts, own_slots, width - first_columns), rows_of_chips
    ).reshape(experts * own_slots, width - first_columns)

    gate_parts = (w_gate[0], swap(w_gate[0]))
    up_parts = (w_up[0], swap(w_up[0]))
    down_parts = (w_down[0], swap(w_down[0]))
    slot_out = expert_forward(arrived, gate_parts, up_parts, down_parts)
    slot_out, arrived, cot_rest, normed_planes = lax.optimization_barrier(
        (slot_out, arrived, cot_rest, normed_planes)
    )
    cot_arrived = jnp.concatenate([cot_first, cot_rest], axis=1)
    returned = all_to_all(
        slot_out.reshape(experts, own_slots, width), rows_of_chips
    ).reshape(experts * own_slots, width)
    slot_probs = jax.nn.softmax(dot(arrived, w_router), axis=-1)
    own_expert = jnp.arange(experts, dtype=jnp.int32) == chip
    slot_weight = jnp.sum(jnp.where(own_expert[None, :], slot_probs, 0.0), axis=1, keepdims=True)
    slot_grad = (slot_weight * cot_arrived.astype(f32)).astype(bf16)
    (
        inner_own,
        inner_other,
        gate_own,
        gate_other,
        up_own,
        up_other,
        slot_in_grad,
    ) = expert_backward(arrived, slot_grad, gate_parts, up_parts, down_parts)
    slot_in_grad, returned = lax.optimization_barrier((slot_in_grad, returned))
    grads_back = all_to_all(
        slot_in_grad.reshape(experts, own_slots, width), rows_of_chips
    ).reshape(experts * own_slots, width)
    normed_planes = (normed_planes, swap(normed_planes))
    number = lax.axis_index("x")
    line = lax.axis_size("x")
    mixed_line = [lax.dynamic_index_in_dim(mixed_parts, number, 0, keepdims=False)]
    for shift in range(1, line):
        part = lax.dynamic_index_in_dim(mixed_parts, (number + shift) % line, 0, keepdims=False)
        mixed_line.append(lax.ppermute(part, "x", [(k, (k + shift) % line) for k in range(line)]))
    others = expert_weight_grads(arrived, slot_grad, inner_other, gate_other, up_other, (), bf16)

    pick_pairs = pick.reshape(experts, own_slots, seq_len)
    weighted = pick_pairs.astype(f32) * router_probs.T[:, None, :]
    weight_high, weight_low = halves(weighted.reshape(experts * own_slots, seq_len))
    moe_part = dot_rows(weight_high, returned) + dot_rows(weight_low, returned)
    moe_own, moe_other = moe_part[:own_rows], moe_part[own_rows:].astype(bf16)
    pair_products = dot_cols(returned, cot).reshape(experts, own_slots, seq_len)
    prob_part = jnp.sum(pair_products * pick_pairs.astype(f32), axis=1).T
    other_part = swap(prob_part)
    prob_grad = prob_part + jnp.concatenate([other_part[own_rows:], other_part[:own_rows]], axis=0)
    logit_grad = router_probs * (
        prob_grad - jnp.sum(router_probs * prob_grad, axis=1, keepdims=True)
    )
    logit_high, logit_low = halves(logit_grad)
    router_grad = router_grad_of(normed_moe, logit_high, logit_low)
    (
        grads_back,
        others,
        moe_own,
        moe_other,
        logit_high,
        logit_low,
        router_grad,
        mixed_line,
        normed_planes,
    ) = lax.optimization_barrier(
        (
            grads_back,
            others,
            moe_own,
            moe_other,
            logit_high,
            logit_low,
            router_grad,
            mixed_line,
            normed_planes,
        )
    )
    moe_own = moe_own + swap(moe_other).astype(f32)
    output = (hidden_own + moe_own).astype(bf16)
    others = [swap(grad) for grad in others]
    grad_w_gate, grad_w_up, grad_w_down = expert_weight_grads(
        arrived, slot_grad, inner_own, gate_own, up_own, others, f32
    )
    moe_in_own, moe_in_other = token_sums(pick_back, grads_back)
    hidden_grad, hidden_low_own, gain_moe_grad = hidden_grad_of(
        moe_in_own,
        swap(moe_in_other),
        logit_high[:own_rows],
        logit_low[:own_rows],
        w_router.T,
        gain_moe[None],
        hidden_own,
        scale_moe,
        cotangent,
    )
    hidden_low_other = swap(hidden_low_own)
    low_line = lax.all_gather(hidden_low_own, "x", axis=0, tiled=False)

    value_grad, query_part, key_part, gain_query_grad, gain_key_grad, inner = attention_backward(
        hidden_low_own,
        hidden_low_other,
        w_out,
        values,
        q_rot,
        k_rot,
        probs,
        queries,
        key_proj,
        query_gain,
        key_gain,
        scales,
        cosine,
        sine,
        local_heads,
    )
    inner_other, gain_moe_other = lax.optimization_barrier((swap(inner), swap(gain_moe_grad)))
    to_planes = projection_grads(
        query_part,
        key_part,
        queries,
        key_proj,
        value_grad,
        scales,
        (inner, inner_other),
        planes,
    )

    grads_planes = all_to_all(to_planes, "z").reshape(planes * seq_len, 3 * quarter)
    low_line, _ = lax.optimization_barrier((low_line, to_planes))
    parcel = out_parcel(
        numbers,
        low_line,
        [swap(low_line[k]) for k in range(line)],
        mixed_line,
        router_grad.reshape(chips, out_rows, experts),
        (gain_moe_grad, gain_moe_other),
        gain_query_grad,
        gain_key_grad,
        counts,
    )
    normed_grad, normed_grad_other = normed_grad_of(to_planes, (w_query, w_key, w_value))
    normed_grad = normed_grad + swap(normed_grad_other)
    in_own = residual_in.astype(f32)
    in_scale = scale_attn
    weighted_attn = normed_grad * gain_attn
    grad_input = (
        hidden_grad
        + in_scale * weighted_attn
        - in_own * in_scale**3 * jnp.mean(in_own * weighted_attn, axis=1, keepdims=True)
    )

    grads_planes, parcel = lax.optimization_barrier((grads_planes, parcel))
    parcel = weight_parcel(normed_planes, grads_planes, parcel)
    parcel, *done = lax.optimization_barrier(
        (
            all_to_all(parcel, rows_of_chips),
            output,
            grad_input,
            grad_w_gate,
            grad_w_up,
            grad_w_down,
        )
    )
    output, grad_input, grad_w_gate, grad_w_up, grad_w_down = done
    per_chip = head_dim // chips
    own_gain = lax.dynamic_slice_in_dim(gain_attn, chip * out_rows, out_rows)[None]
    (
        grad_w_query,
        grad_w_key,
        grad_w_value,
        grad_w_out,
        grad_w_router,
        grad_gain_query,
        grad_gain_key,
        grad_gain_moe,
        count,
        attn_own,
        attn_other,
    ) = parcel_sums(
        numbers,
        parcel,
        (w_query, w_key, w_value),
        own_gain,
        planes,
        out_rows,
        local_width,
        local_heads,
        per_chip,
        experts,
    )
    return (
        output,
        grad_input,
        (attn_own + swap(attn_other))[0],
        grad_w_query,
        grad_w_key,
        grad_w_value,
        grad_gain_query.T,
        grad_gain_key.T,
        grad_w_out.T,
        grad_gain_moe[0],
        grad_w_router,
        grad_w_gate[None],
        grad_w_up[None],
        grad_w_down[None],
        count[0],
    )


def solution(mesh):
    side = round(mesh.shape["ep"] ** (1 / 3))
    cube = Mesh(mesh.devices.reshape(side, side, side, 2), rows_of_chips + ("tp",))
    ep = rows_of_chips
    both = rows_of_chips + ("tp",)
    in_specs = (
        P(both, None),
        P(ep, None),
        P(ep, None),
        P(),
        P(None, "tp"),
        P(None, "tp"),
        P(None, "tp"),
        P("tp", None),
        P("tp", None),
        P("tp", None),
        P(),
        P(),
        P(ep, None, "tp"),
        P(ep, None, "tp"),
        P(ep, "tp", None),
        P(both, None),
    )
    out_specs = (
        P(both, None),
        P(both, None),
        P(both),
        P(ep, "tp"),
        P(ep, "tp"),
        P(ep, "tp"),
        P("tp", ep),
        P("tp", ep),
        P("tp", ep),
        P(both),
        P(both, None),
        P(ep, None, "tp"),
        P(ep, None, "tp"),
        P(ep, "tp", None),
        P(ep),
    )
    return jax.shard_map(local, mesh=cube, in_specs=in_specs, out_specs=out_specs, check_vma=False)
```

```python
import jax
import jax.numpy as jnp
from jax import lax
from jax.experimental import pallas as pl
from jax.experimental.pallas import tpu as pltpu
from jax.sharding import Mesh, PartitionSpec as P

norm_eps = 1e-05
rope_base = 10000.0
mask_fill = -1e30
bf16 = jnp.bfloat16
f32 = jnp.float32
rows_of_chips = ("z", "x", "y")


def swap(value):
    return lax.ppermute(value, "tp", [(0, 1), (1, 0)])


def dot(left, right):
    return lax.dot_general(left, right, (((1,), (0,)), ((), ())), preferred_element_type=f32)


def dot_rows(left, right):
    return lax.dot_general(left, right, (((0,), (0,)), ((), ())), preferred_element_type=f32)


def dot_cols(left, right):
    return lax.dot_general(left, right, (((1,), (1,)), ((), ())), preferred_element_type=f32)


def all_to_all(value, axes):
    return lax.all_to_all(value, axes, split_axis=0, concat_axis=0, tiled=True)


def rms_scale(values):
    return lax.rsqrt(jnp.mean(values * values, axis=-1, keepdims=True) + norm_eps)


def halves(value):
    high = value.astype(bf16)
    return high, (value - high.astype(f32)).astype(bf16)


def rope_angles(positions, head_dim):
    half_dim = head_dim // 2
    exponent = jnp.arange(half_dim, dtype=f32) * (2.0 / head_dim)
    inverse = jnp.power(f32(rope_base), -exponent)
    angles = positions.astype(f32)[:, None] * inverse[None, :]
    return jnp.cos(angles), jnp.sin(angles)


lanes = 128
cheap = 64


def in_hbm(*arrays):
    return [pltpu.with_memory_space_constraint(array, pltpu.HBM) for array in arrays]


def params(megabytes):
    return pltpu.CompilerParams(vmem_limit_bytes=megabytes * 1024 * 1024)


def turn(value, cosine, sine):
    return value * cosine + pltpu.roll(value, value.shape[1] // 2, 1) * sine


def other_order(ref):
    half = ref.shape[0] // 2
    return jnp.concatenate([ref[half:, :], ref[:half, :]], axis=0)


def attention_forward_body(
    scale,
    full_width,
    query_ref,
    key_ref,
    value_ref,
    query_gain_ref,
    key_gain_ref,
    squares_ref,
    other_squares_ref,
    cosine_ref,
    sine_ref,
    bias_ref,
    q_rot_ref,
    k_rot_ref,
    probs_ref,
    mixed_ref,
    parts_ref,
    scales_ref,
):
    cosine, sine, bias = cosine_ref[...], sine_ref[...], bias_ref[...]
    head = cosine.shape[1]
    squares = squares_ref[...] + other_order(other_squares_ref)
    scales = lax.rsqrt(squares * (1.0 / full_width) + norm_eps)
    scales_ref[...] = scales
    for h in range(probs_ref.shape[0]):
        here = slice(h * head, (h + 1) * head)
        query = query_ref[:, here] * scales[:, 0:1] * query_gain_ref[:, here]
        key = key_ref[:, here] * scales[:, 1:2] * key_gain_ref[:, here]
        q_rot = turn(query, cosine, sine).astype(bf16)
        k_rot = turn(key, cosine, sine).astype(bf16)
        q_rot_ref[:, here] = q_rot
        k_rot_ref[:, here] = k_rot
        scores = dot_cols(q_rot, k_rot) * scale + bias
        grown = jnp.exp(scores - jnp.max(scores, axis=1, keepdims=True))
        probs = grown / jnp.sum(grown, axis=1, keepdims=True)
        probs_ref[h] = probs
        mixed_ref[:, here] = dot(probs.astype(bf16), value_ref[:, here]).astype(bf16)
    part = parts_ref.shape[2]
    for k in range(parts_ref.shape[0]):
        parts_ref[k] = mixed_ref[:, k * part : (k + 1) * part]


def attention_forward(
    queries, keys, values, query_gain, key_gain, squares, other, cosine, sine, bias, heads, planes
):
    seq_len, width = queries.shape
    head = width // heads
    group = min(heads, 4)
    column = pl.BlockSpec((seq_len, group * head), lambda h: (0, h))
    gain = pl.BlockSpec((1, group * head), lambda h: (0, h))

    def whole(array):
        return pl.BlockSpec(array.shape, lambda h: (0, 0))

    return pl.pallas_call(
        lambda *refs: attention_forward_body(head**-0.5, 2 * width, *refs),
        grid=(heads // group,),
        in_specs=[column, column, column, gain, gain]
        + [whole(a) for a in (squares, other, cosine, sine, bias)],
        out_specs=[
            column,
            column,
            pl.BlockSpec((group, seq_len, seq_len), lambda h: (h, 0, 0)),
            column,
            pl.BlockSpec(
                (planes * group // heads, seq_len, width // planes), lambda h: (h, 0, 0)
            ),
            whole(squares),
        ],
        out_shape=[
            jax.ShapeDtypeStruct((seq_len, width), bf16),
            jax.ShapeDtypeStruct((seq_len, width), bf16),
            jax.ShapeDtypeStruct((heads, seq_len, seq_len), f32),
            jax.ShapeDtypeStruct((seq_len, width), bf16),
            jax.ShapeDtypeStruct((planes, seq_len, width // planes), bf16),
            jax.ShapeDtypeStruct((seq_len, 2), f32),
        ],
        compiler_params=params(16),
        cost_estimate=pl.CostEstimate(
            flops=4 * seq_len * seq_len * width // cheap,
            transcendentals=0,
            bytes_accessed=seq_len * width * 16 // cheap,
        ),
        name="attention_forward",
    )(queries, keys, values, query_gain, key_gain, squares, other, cosine, sine, bias)


def attention_backward_body(
    scale,
    hidden_own_ref,
    hidden_other_ref,
    w_out_ref,
    value_ref,
    q_rot_ref,
    k_rot_ref,
    probs_ref,
    query_ref,
    key_ref,
    query_gain_ref,
    key_gain_ref,
    scales_ref,
    cosine_ref,
    sine_ref,
    value_grad_ref,
    query_part_ref,
    key_part_ref,
    query_gain_grad_ref,
    key_gain_grad_ref,
    inner_ref,
):
    cosine, sine = cosine_ref[...], sine_ref[...]
    hidden = jnp.concatenate([hidden_own_ref[...], hidden_other_ref[...]], axis=0)
    heads, head = query_gain_grad_ref.shape[0], query_gain_grad_ref.shape[2]
    grad_mixed = dot_cols(hidden, w_out_ref[...]).astype(bf16)
    total = None
    for h in range(heads):
        here = slice(h * head, (h + 1) * head)
        grad = grad_mixed[:, here]
        probs = probs_ref[h]
        grad_probs = dot_cols(grad, value_ref[:, here])
        inner = jnp.sum(probs * grad_probs, axis=1, keepdims=True)
        grad_scores = (probs * (grad_probs - inner)).astype(bf16)
        value_grad_ref[:, here] = dot_rows(probs.astype(bf16), grad).astype(bf16)
        row_inners = []
        for k, (grad_rot, raw_ref, gain_ref, part_ref, gain_grad_ref) in enumerate(
            (
                (
                    dot(grad_scores, k_rot_ref[:, here]),
                    query_ref,
                    query_gain_ref,
                    query_part_ref,
                    query_gain_grad_ref,
                ),
                (
                    dot_rows(grad_scores, q_rot_ref[:, here]),
                    key_ref,
                    key_gain_ref,
                    key_part_ref,
                    key_gain_grad_ref,
                ),
            )
        ):
            grad_normed = turn(grad_rot * scale, cosine, -sine)
            raw = raw_ref[:, here]
            gain_grad_ref[h] = jnp.sum(
                raw * scales_ref[:, k : k + 1] * grad_normed, axis=0, keepdims=True
            )
            weighted = grad_normed * gain_ref[:, here]
            part_ref[:, here] = weighted
            row_inners.append(jnp.sum(raw * weighted, axis=1, keepdims=True))
        row_inner = jnp.concatenate(row_inners, axis=1)
        total = row_inner if total is None else total + row_inner
    first = pl.program_id(0) == 0

    @pl.when(first)
    def _():
        inner_ref[...] = total

    @pl.when(jnp.logical_not(first))
    def _():
        inner_ref[...] += total


def attention_backward(
    hidden_own,
    hidden_other,
    w_out,
    values,
    q_rot,
    k_rot,
    probs,
    queries,
    keys,
    query_gain,
    key_gain,
    scales,
    cosine,
    sine,
    heads,
):
    seq_len, width = queries.shape
    head = width // heads
    group = min(heads, 4)
    column = pl.BlockSpec((seq_len, group * head), lambda h: (0, h))
    gain = pl.BlockSpec((1, group * head), lambda h: (0, h))

    def whole(array):
        return pl.BlockSpec(array.shape, lambda h: (0, 0))

    full = jax.ShapeDtypeStruct((seq_len, width), f32)
    line = jax.ShapeDtypeStruct((heads, 1, head), f32)
    line_spec = pl.BlockSpec((group, 1, head), lambda h: (h, 0, 0))
    sums = jax.ShapeDtypeStruct((seq_len, 2), f32)
    return pl.pallas_call(
        lambda *refs: attention_backward_body(head**-0.5, *refs),
        grid=(heads // group,),
        in_specs=[
            whole(hidden_own),
            whole(hidden_other),
            pl.BlockSpec((group * head, w_out.shape[1]), lambda h: (h, 0)),
            column,
            column,
            column,
            pl.BlockSpec((group, seq_len, seq_len), lambda h: (h, 0, 0)),
            column,
            column,
            gain,
            gain,
        ]
        + [whole(a) for a in (scales, cosine, sine)],
        out_specs=[column, column, column, line_spec, line_spec, whole(sums)],
        out_shape=[
            jax.ShapeDtypeStruct((seq_len, width), bf16),
            full,
            full,
            line,
            line,
            sums,
        ],
        compiler_params=params(20),
        cost_estimate=pl.CostEstimate(
            flops=10 * seq_len * seq_len * width + 2 * seq_len * width * w_out.shape[1],
            transcendentals=0,
            bytes_accessed=seq_len * width * 28
            + heads * seq_len * seq_len * 4
            + 2 * w_out.size
            + 4 * hidden_own.size,
        ),
        name="attention_backward",
    )(
        *in_hbm(hidden_own),
        hidden_other,
        *in_hbm(w_out, values, q_rot, k_rot, probs, queries, keys),
        query_gain,
        key_gain,
        scales,
        cosine,
        sine,
    )


def projection_grads_body(
    width,
    query_part_ref,
    key_part_ref,
    query_ref,
    key_ref,
    value_grad_ref,
    scales_ref,
    inner_ref,
    other_inner_ref,
    stack_ref,
):
    blocks, _, columns = stack_ref.shape
    size = columns // 3
    inner = (inner_ref[...] + other_order(other_inner_ref)) * (1.0 / width)
    for k, (part_ref, raw_ref) in enumerate(
        ((query_part_ref, query_ref), (key_part_ref, key_ref))
    ):
        scale = scales_ref[:, k : k + 1]
        factor = scale * scale * scale * inner[:, k : k + 1]
        for block in range(blocks):
            here = slice(block * size, (block + 1) * size)
            grad = scale * part_ref[:, here] - raw_ref[:, here] * factor
            stack_ref[block, :, k * size : (k + 1) * size] = grad.astype(bf16)
    for block in range(blocks):
        stack_ref[block, :, 2 * size :] = value_grad_ref[:, block * size : (block + 1) * size]


def projection_grads(
    query_part, key_part, queries, keys, value_grad, scales, inners, planes
):
    seq_len, width = queries.shape
    size = width // planes
    steps = 2
    column = pl.BlockSpec((seq_len, width // steps), lambda k: (0, k))
    pair = pl.BlockSpec((seq_len, 2), lambda k: (0, 0))
    return pl.pallas_call(
        lambda *refs: projection_grads_body(2 * width, *refs),
        grid=(steps,),
        in_specs=[column] * 5 + [pair] * 3,
        out_specs=pl.BlockSpec((planes // steps, seq_len, 3 * size), lambda k: (k, 0, 0)),
        out_shape=jax.ShapeDtypeStruct((planes, seq_len, 3 * size), bf16),
        compiler_params=params(10),
        cost_estimate=pl.CostEstimate(
            flops=10 * seq_len * width, transcendentals=0, bytes_accessed=24 * seq_len * width
        ),
        name="projection_grads",
    )(query_part, key_part, queries, keys, value_grad, scales, *inners)


def expert_forward_body(
    rows_hbm,
    gate_own_hbm,
    gate_other_hbm,
    up_own_hbm,
    up_other_hbm,
    down_own_hbm,
    down_other_hbm,
    out_hbm,
    rows_ref,
    gate_ref,
    up_ref,
    down_ref,
    out_ref,
    in_sems,
    out_sems,
):
    count, width = rows_ref.shape
    pieces = 2
    size = count // pieces
    copies = {}
    order = [("rows", 0), ("gate", 0), ("up", 0), ("gate", 1), ("up", 1), ("down", 0), ("down", 1)]
    order += [("rows", k) for k in range(1, pieces)]
    sources = {
        "gate": ((gate_own_hbm, gate_other_hbm), gate_ref),
        "up": ((up_own_hbm, up_other_hbm), up_ref),
        "down": ((down_own_hbm, down_other_hbm), down_ref),
    }
    for number, (name, k) in enumerate(order):
        if name == "rows":
            here = pl.ds(k * size, size)
            copy = pltpu.make_async_copy(rows_hbm.at[here], rows_ref.at[here], in_sems.at[number])
        else:
            source, target = sources[name]
            copy = pltpu.make_async_copy(source[k], target.at[k], in_sems.at[number])
        copy.start()
        copies[name, k] = copy
    outs = []
    for piece in range(pieces):
        here = pl.ds(piece * size, size)
        copies["rows", piece].wait()
        inners = []
        for k in range(2):
            if piece == 0:
                copies["gate", k].wait()
            gate = dot(rows_ref[here, :], gate_ref[k])
            if piece == 0:
                copies["up", k].wait()
            up = dot(rows_ref[here, :], up_ref[k])
            inners.append((gate * jax.nn.sigmoid(gate) * up).astype(bf16))
        if piece == 0:
            copies["down", 0].wait()
            copies["down", 1].wait()
        step = min(512, width)
        for start in range(0, width, step):
            columns = pl.ds(start, step)
            total = dot(inners[0], down_ref[0, :, columns]) + dot(
                inners[1], down_ref[1, :, columns]
            )
            out_ref[here, columns] = total.astype(bf16)
        copy = pltpu.make_async_copy(out_ref.at[here], out_hbm.at[here], out_sems.at[piece])
        copy.start()
        outs.append(copy)
    for copy in outs:
        copy.wait()


def expert_specs(count, width, size):
    whole = pl.BlockSpec((count, width), lambda k: (0, 0), pipeline_mode=pl.Buffered(1))
    into = pl.BlockSpec((width, size), lambda k: (0, k))
    back = pl.BlockSpec((size, width), lambda k: (k, 0))
    return whole, into, back


def expert_forward(rows, gates, ups, downs):
    count, width = rows.shape
    units = gates[0].shape[1]
    return pl.pallas_call(
        expert_forward_body,
        in_specs=[pl.BlockSpec(memory_space=pl.ANY)] * 7,
        out_specs=pl.BlockSpec(memory_space=pl.ANY),
        out_shape=pltpu.HBM((count, width), bf16),
        scratch_shapes=[
            pltpu.VMEM((count, width), bf16),
            pltpu.VMEM((2, width, units), bf16),
            pltpu.VMEM((2, width, units), bf16),
            pltpu.VMEM((2, units, width), bf16),
            pltpu.VMEM((count, width), bf16),
            pltpu.SemaphoreType.DMA((8,)),
            pltpu.SemaphoreType.DMA((2,)),
        ],
        compiler_params=params(44),
        cost_estimate=pl.CostEstimate(
            flops=12 * count * width * units // cheap,
            transcendentals=0,
            bytes_accessed=(count * width * 4 + 12 * width * units) // cheap,
        ),
        name="expert_forward",
    )(*in_hbm(rows, *gates, *ups, *downs))


def expert_backward_body(
    rows_ref,
    slot_grad_ref,
    gate_own_ref,
    gate_other_ref,
    up_own_ref,
    up_other_ref,
    down_own_ref,
    down_other_ref,
    inner_own_ref,
    inner_other_ref,
    gate_grad_own_ref,
    gate_grad_other_ref,
    up_grad_own_ref,
    up_grad_other_ref,
    out_ref,
    total_ref,
):
    step = pl.program_id(0)
    last = pl.num_programs(0) - 1
    for gate_ref, up_ref, down_ref, inner_ref, gate_grad_ref, up_grad_ref in (
        (gate_own_ref, up_own_ref, down_own_ref, inner_own_ref, gate_grad_own_ref, up_grad_own_ref),
        (
            gate_other_ref,
            up_other_ref,
            down_other_ref,
            inner_other_ref,
            gate_grad_other_ref,
            up_grad_other_ref,
        ),
    ):
        gate = dot(rows_ref[...], gate_ref[...])
        up = dot(rows_ref[...], up_ref[...])
        inner_grad = dot_cols(slot_grad_ref[...], down_ref[...])
        sigmoid_gate = jax.nn.sigmoid(gate)
        silu_gate = gate * sigmoid_gate
        inner_ref[...] = (silu_gate * up).astype(bf16)
        up_grad_ref[...] = (inner_grad * silu_gate).astype(bf16)
        gate_grad_ref[...] = (
            inner_grad * up * sigmoid_gate * (1.0 + gate * (1.0 - sigmoid_gate))
        ).astype(bf16)
    width = out_ref.shape[1]
    size = min(512, width)
    for start in range(0, width, size):
        here = pl.ds(start, size)
        part = None
        for grad_ref, w_ref in (
            (gate_grad_own_ref, gate_own_ref),
            (gate_grad_other_ref, gate_other_ref),
            (up_grad_own_ref, up_own_ref),
            (up_grad_other_ref, up_other_ref),
        ):
            term = dot_cols(grad_ref[...], w_ref[here, :])
            part = term if part is None else part + term

        @pl.when(step == 0)
        def _():
            total_ref[:, here] = part

        @pl.when((step > 0) & (step < last))
        def _():
            total_ref[:, here] += part

        @pl.when(step == last)
        def _():
            out_ref[:, here] = (total_ref[:, here] + part).astype(bf16)


def expert_backward(rows, slot_grad, gates, ups, downs):
    count, width = rows.shape
    units = gates[0].shape[1]
    steps = 2
    size = units // steps
    whole, into, back = expert_specs(count, width, size)
    acts = pl.BlockSpec((count, size), lambda k: (0, k))
    return pl.pallas_call(
        expert_backward_body,
        grid=(steps,),
        in_specs=[whole] * 2 + [into] * 4 + [back] * 2,
        out_specs=[acts] * 6 + [pl.BlockSpec((count, width), lambda k: (0, 0))],
        out_shape=[jax.ShapeDtypeStruct((count, units), bf16)] * 6
        + [jax.ShapeDtypeStruct((count, width), bf16)],
        scratch_shapes=[pltpu.VMEM((count, width), f32)],
        compiler_params=params(56),
        cost_estimate=pl.CostEstimate(
            flops=20 * count * width * units // cheap,
            transcendentals=0,
            bytes_accessed=count * width * 6 // cheap,
        ),
        name="expert_backward",
    )(rows, slot_grad, *gates, *ups, *downs)


def put_blocks(out_ref, row, product):
    chips = out_ref.shape[0]
    rows = product.shape[0] // chips
    for k in range(product.shape[1] // lanes):
        piece = product[:, k * lanes : (k + 1) * lanes].reshape(chips, rows, lanes)
        out_ref[:, row : row + rows, :] = piece
        row += rows
    return row


def joined(own_ref, other_ref):
    rows = jnp.concatenate([own_ref[...], other_ref[...]], axis=1)
    return rows.reshape(rows.shape[0] * rows.shape[1], rows.shape[2])


def columns_first_body(own_ref, other_ref, out_ref):
    out_ref[...] = joined(own_ref, other_ref).T


def columns_first(own, other):
    planes, half, width = own.shape
    steps = planes
    left = pl.BlockSpec((planes, half, width // steps), lambda k: (0, 0, k))
    tokens = 2 * planes * half
    return pl.pallas_call(
        columns_first_body,
        grid=(steps,),
        in_specs=[left, left],
        out_specs=pl.BlockSpec((width // steps, tokens), lambda k: (k, 0)),
        out_shape=pltpu.HBM((width, tokens), bf16),
        compiler_params=params(16),
        cost_estimate=pl.CostEstimate(
            flops=1 << 16, transcendentals=0, bytes_accessed=2 * tokens * width // cheap
        ),
        name="columns_first",
    )(*in_hbm(own, other))


def weight_parcel_body(normed_ref, grads_ref, parcel_hbm, out_hbm, block_ref, sems):
    step = pl.program_id(0)
    slot = step % 2
    group, rows = block_ref.shape[1], block_ref.shape[2]

    def copy(at):
        here = out_hbm.at[pl.ds(step * group, group), pl.ds(0, rows)]
        return pltpu.make_async_copy(block_ref.at[at], here, sems.at[at])

    @pl.when(step >= 2)
    def _():
        copy(slot).wait()

    put_blocks(block_ref.at[slot], 0, dot(normed_ref[...], grads_ref[...]).astype(bf16))
    copy(slot).start()

    @pl.when(step == pl.num_programs(0) - 1)
    def _():
        copy(1 - slot).wait()
        copy(slot).wait()


def weight_parcel(normed, grads, parcel):
    width, tokens = normed.shape
    columns = grads.shape[1]
    chips, height, _ = parcel.shape
    rows = width // chips * columns // lanes
    steps = 4
    return pl.pallas_call(
        weight_parcel_body,
        grid=(steps,),
        in_specs=[
            pl.BlockSpec((width // steps, tokens), lambda k: (k, 0)),
            pl.BlockSpec((tokens, columns), lambda k: (0, 0)),
            pl.BlockSpec(memory_space=pl.ANY),
        ],
        out_specs=pl.BlockSpec(memory_space=pl.ANY),
        out_shape=pltpu.HBM((chips, height, lanes), bf16),
        input_output_aliases={2: 0},
        scratch_shapes=[
            pltpu.VMEM((2, chips // steps, rows, lanes), bf16),
            pltpu.SemaphoreType.DMA((2,)),
        ],
        compiler_params=params(18),
        cost_estimate=pl.CostEstimate(
            flops=2 * tokens * width * columns,
            transcendentals=0,
            bytes_accessed=2 * (tokens * width + grads.size + chips * height * lanes),
        ),
        name="weight_parcel",
    )(*in_hbm(normed, grads, parcel))


def out_parcel_body(
    start,
    per_chip,
    line,
    place_ref,
    low_ref,
    *refs,
):
    low_other_refs, mixed_refs, refs = refs[:line], refs[line : 2 * line], refs[2 * line :]
    router_ref, moe_ref, moe_other_ref, query_gain_ref, key_gain_ref, counts_ref = refs[:6]
    out_hbm, block_ref, sems = refs[6:]
    step = pl.program_id(0)
    slot = step % 2
    group = block_ref.shape[1]

    def copy(at):
        here = out_hbm.at[pl.ds(step * group, group), pl.ds(start, block_ref.shape[2])]
        return pltpu.make_async_copy(block_ref.at[at], here, sems.at[at])

    @pl.when(step >= 2)
    def _():
        copy(slot).wait()

    total = None
    for shift, mixed_ref in enumerate(mixed_refs):
        source = (place_ref[3] + line - shift) % line
        other = low_other_refs[0][...]
        for k in range(1, line):
            other = jnp.where(source == k, low_other_refs[k][...], other)
        left = jnp.concatenate([low_ref[source], other], axis=0)
        part = dot_rows(left, mixed_ref[...])
        total = part if total is None else total + part
    row = put_blocks(block_ref.at[slot], 0, total.astype(bf16))

    chips, rows, spare = router_ref.shape[0], router_ref.shape[1] // 2, lanes // 2
    core = place_ref[1]
    router = router_ref[:, pl.ds(core * rows, rows), :]
    if router.shape[2] < spare:
        fill = jnp.zeros((chips, rows, spare - router.shape[2]), f32)
        router = jnp.concatenate([router, fill], axis=2)
    moe = moe_ref[...] + moe_other_ref[...]
    span = 2 * rows
    moe = jnp.concatenate([moe[:, k * span : (k + 1) * span] for k in range(chips)], axis=0)
    moe = jnp.where(core == 0, moe[:, :rows], moe[:, rows:])
    heads, head = query_gain_ref.shape[0], query_gain_ref.shape[2]
    chip = lax.broadcasted_iota(jnp.int32, (chips, heads, head), 0) + step * chips
    lane = lax.broadcasted_iota(jnp.int32, (chips, heads, head), 2)
    mine = lane // per_chip == chip
    feature = lax.broadcasted_iota(jnp.int32, (head, spare), 0) % per_chip
    column = lax.broadcasted_iota(jnp.int32, (head, spare), 1)
    first_row = lax.broadcasted_iota(jnp.int32, (chips, heads, spare), 1) == 0
    used = 2 * per_chip + rows + 1
    blocks = []
    for part in range(2):
        block = jnp.zeros((chips * heads, spare), f32)
        for k, gain_ref in enumerate((query_gain_ref, key_gain_ref)):
            values = halves(gain_ref[:, 0, :])[part].astype(f32)
            values = jnp.where(mine, values[None], 0.0).reshape(chips * heads, head).astype(bf16)
            target = jnp.where(column == feature + k * per_chip, 1.0, 0.0).astype(bf16)
            block = block + dot(values, target)
        moe_part = halves(moe)[part].astype(f32)
        count = counts_ref[...] if part == 0 else jnp.zeros((chips, 1), f32)
        vector = jnp.concatenate(
            [jnp.zeros((chips, 2 * per_chip), f32), moe_part, count]
            + [jnp.zeros((chips, spare - used), f32)] * (used < spare),
            axis=1,
        )
        block = block.reshape(chips, heads, spare)
        blocks.append(block + jnp.where(first_row, vector[:, None, :], 0.0))
        if heads < rows // 2:
            blocks.append(jnp.zeros((chips, rows // 2 - heads, spare), f32))
    beside = jnp.concatenate(blocks, axis=1)
    small = jnp.concatenate([router, beside], axis=2).astype(bf16)
    block_ref[slot, :, row:, :] = small
    copy(slot).start()

    @pl.when(step == pl.num_programs(0) - 1)
    def _():
        copy(1 - slot).wait()
        copy(slot).wait()


def out_parcel(place, low, low_other, mixed, router, moe, query_gain, key_gain, counts):
    line, half, width = low.shape
    tokens, part = mixed[0].shape
    chips, router_rows, experts = router.shape
    heads, _, head = query_gain.shape
    room = width // chips * part // lanes
    small_rows = router_rows // 2
    height = 4 * room + small_rows
    steps = line
    group = chips // steps
    gain = pl.BlockSpec((heads, 1, head), lambda k, z: (0, 0, 0))
    vector = pl.BlockSpec((1, width // steps), lambda k, z: (0, k))
    return pl.pallas_call(
        lambda *refs: out_parcel_body(3 * room, head // chips, line, *refs),
        grid_spec=pltpu.PrefetchScalarGridSpec(
            num_scalar_prefetch=1,
            grid=(steps,),
            in_specs=[pl.BlockSpec((line, half, width // steps), lambda k, z: (0, 0, k))]
            + [pl.BlockSpec((half, width // steps), lambda k, z: (0, k))] * line
            + [pl.BlockSpec((tokens, part), lambda k, z: (0, 0))] * line
            + [pl.BlockSpec((group, router_rows, experts), lambda k, z: (k, 0, 0))]
            + [vector, vector, gain, gain, pl.BlockSpec((group, 1), lambda k, z: (k, 0))],
            out_specs=pl.BlockSpec(memory_space=pl.ANY),
            scratch_shapes=[
                pltpu.VMEM((2, group, room + small_rows, lanes), bf16),
                pltpu.SemaphoreType.DMA((2,)),
            ],
        ),
        out_shape=pltpu.HBM((chips, height, lanes), bf16),
        compiler_params=params(18),
        cost_estimate=pl.CostEstimate(
            flops=2 * tokens * width * part // cheap,
            transcendentals=0,
            bytes_accessed=2 * (tokens * width + chips * room * lanes) // cheap,
        ),
        name="out_parcel",
    )(
        place,
        *in_hbm(low),
        *low_other,
        *mixed,
        *in_hbm(router),
        *moe,
        query_gain,
        key_gain,
        counts,
    )


def parcel_sums_body(
    per_chip,
    place_ref,
    parcel_ref,
    w_query_ref,
    w_key_ref,
    w_value_ref,
    own_gain_ref,
    query_ref,
    key_ref,
    value_ref,
    out_ref,
    router_ref,
    query_gain_ref,
    key_gain_ref,
    moe_ref,
    count_ref,
    attn_ref,
    attn_other_ref,
    extra_ref,
    gain_ref,
):
    rows, width = query_ref.shape
    step = pl.program_id(0)
    line = pl.num_programs(0)
    columns = width // line
    blocks = columns // lanes
    row = 3 * blocks * rows
    total = jnp.sum(parcel_ref[:, :row, :].astype(f32), axis=0)
    gain = jnp.zeros((rows, lanes), f32)
    for number, (ref, w_ref) in enumerate(
        ((query_ref, w_query_ref), (key_ref, w_key_ref), (value_ref, w_value_ref))
    ):
        for k in range(blocks):
            here = pl.ds(pl.multiple_of(step * columns + k * lanes, lanes), lanes)
            first_row = (number * blocks + k) * rows
            piece = total[first_row : first_row + rows, :]
            ref[:, here] = piece
            gain = gain + piece * w_ref[:, here].astype(f32)

    @pl.when(step == 0)
    def _():
        out_ref[...] = jnp.zeros_like(out_ref)
        extra_ref[...] = jnp.zeros_like(extra_ref)
        gain_ref[...] = jnp.zeros_like(gain_ref)

    gain_ref[...] += gain
    extra_ref[...] += jnp.sum(parcel_ref[:, row + blocks * rows :, :].astype(f32), axis=0)
    group = parcel_ref.shape[0] * columns // width
    for x in range(width // columns):
        part = parcel_ref[x * group : (x + 1) * group, row : row + blocks * rows, :]
        part = jnp.sum(part.astype(f32), axis=0)
        for k in range(blocks):
            here = slice(x * columns + k * lanes, x * columns + (k + 1) * lanes)
            out_ref[:, here] += part[k * rows : (k + 1) * rows, :]

    @pl.when(step == pl.num_programs(0) - 1)
    def _():
        half = rows // 2
        heads = query_gain_ref.shape[1]
        router_ref[...] = extra_ref[:, : router_ref.shape[1]]
        sums = extra_ref[0:heads, :] + extra_ref[half // 2 : half // 2 + heads, :]
        first_lane = lanes // 2 + 2 * per_chip
        moe_ref[...] = sums[0:1, first_lane : first_lane + half]
        count_ref[...] = sums[0:1, first_lane + half : first_lane + half + 1].astype(jnp.int32)
        sums = sums.T
        query_gain_ref[...] = sums[lanes // 2 : lanes // 2 + per_chip, :]
        key_gain_ref[...] = sums[lanes // 2 + per_chip : first_lane, :]
        attn = jnp.sum(gain_ref[...].T, axis=0, keepdims=True) / own_gain_ref[...]
        first = place_ref[1] == 0
        attn_ref[...] = jnp.where(first, attn[:, :half], attn[:, half:])
        attn_other_ref[...] = jnp.where(first, attn[:, half:], attn[:, :half])


def parcel_sums(place, parcel, weights, own_gain, planes, rows, width, heads, per_chip, experts):
    chips, height, _ = parcel.shape
    half = rows // 2

    def whole(shape):
        return pl.BlockSpec(shape, lambda k, c: (0, 0))

    small = [(half, experts), (per_chip, heads), (per_chip, heads), (1, half), (1, 1)]
    small += [(1, half), (1, half)]
    kinds = [f32] * 4 + [jnp.int32] + [f32] * 2
    return pl.pallas_call(
        lambda *refs: parcel_sums_body(per_chip, *refs),
        grid_spec=pltpu.PrefetchScalarGridSpec(
            num_scalar_prefetch=1,
            grid=(planes,),
            in_specs=[pl.BlockSpec((chips // planes, height, lanes), lambda k, c: (k, 0, 0))]
            + [pl.BlockSpec((rows, width), lambda k, c: (c[2], 0))] * 3
            + [whole((1, rows))],
            out_specs=[whole((rows, width))] * 4 + [whole(shape) for shape in small],
            scratch_shapes=[pltpu.VMEM((half, lanes), f32), pltpu.VMEM((rows, lanes), f32)],
        ),
        out_shape=[jax.ShapeDtypeStruct((rows, width), f32)] * 4
        + [jax.ShapeDtypeStruct(shape, kind) for shape, kind in zip(small, kinds)],
        compiler_params=params(14),
        cost_estimate=pl.CostEstimate(
            flops=parcel.size, transcendentals=0, bytes_accessed=2 * parcel.size
        ),
        name="parcel_sums",
    )(place, parcel, *in_hbm(*weights), own_gain)


def expert_weight_grads_body(rows_ref, slot_grad_ref, inner_ref, gate_ref, up_ref, *refs):
    grads = (
        dot_rows(rows_ref[...], gate_ref[...]),
        dot_rows(rows_ref[...], up_ref[...]),
        dot_rows(inner_ref[...], slot_grad_ref[...]),
    )
    others, outs = refs[:-3], refs[-3:]
    for k, (grad, out_ref) in enumerate(zip(grads, outs)):
        if others:
            grad = grad + others[k][...].astype(f32)
        out_ref[...] = grad.astype(out_ref.dtype)


def expert_weight_grads(rows, slot_grad, inner, gate_grad, up_grad, others, kind):
    count, width = rows.shape
    units = inner.shape[1]
    steps = 4
    size = width // steps
    wide = pl.BlockSpec((count, size), lambda k: (0, k))
    narrow = pl.BlockSpec((count, units), lambda k: (0, 0))
    into = pl.BlockSpec((size, units), lambda k: (k, 0))
    back = pl.BlockSpec((units, size), lambda k: (0, k))
    return pl.pallas_call(
        expert_weight_grads_body,
        grid=(steps,),
        in_specs=[wide, wide, narrow, narrow, narrow] + [into, into, back][: len(others)],
        out_specs=[into, into, back],
        out_shape=[
            jax.ShapeDtypeStruct((width, units), kind),
            jax.ShapeDtypeStruct((width, units), kind),
            jax.ShapeDtypeStruct((units, width), kind),
        ],
        compiler_params=params(30),
        cost_estimate=pl.CostEstimate(
            flops=6 * count * width * units // cheap,
            transcendentals=0,
            bytes_accessed=4 * count * width // cheap,
        ),
        name="expert_weight_grads",
    )(*in_hbm(rows, slot_grad, inner, gate_grad, up_grad, *others))


def normed_grad_body(stack_ref, query_ref, key_ref, value_ref, own_ref, other_ref):
    size = query_ref.shape[1]
    total = None
    for k, w_ref in enumerate((query_ref, key_ref, value_ref)):
        part = dot_cols(stack_ref[:, k * size : (k + 1) * size], w_ref[...])
        total = part if total is None else total + part
    half = own_ref.shape[0]
    first = pl.program_id(0) == 0

    @pl.when(first)
    def _():
        own_ref[...] = total[:half]
        other_ref[...] = total[half:]

    @pl.when(jnp.logical_not(first))
    def _():
        own_ref[...] += total[:half]
        other_ref[...] += total[half:]


def normed_grad_of(stack, weights):
    planes, seq_len, columns = stack.shape
    size = columns // 3
    full = weights[0].shape[0]
    half = pl.BlockSpec((seq_len // 2, full), lambda k: (0, 0))
    return pl.pallas_call(
        normed_grad_body,
        grid=(planes,),
        in_specs=[pl.BlockSpec((None, seq_len, columns), lambda k: (k, 0, 0))]
        + [pl.BlockSpec((full, size), lambda k: (0, k))] * 3,
        out_specs=[half] * 2,
        out_shape=[jax.ShapeDtypeStruct((seq_len // 2, full), f32)] * 2,
        compiler_params=params(20),
        cost_estimate=pl.CostEstimate(
            flops=2 * stack.size * full // cheap,
            transcendentals=0,
            bytes_accessed=2 * planes * columns * full // cheap,
        ),
        name="normed_grad",
    )(stack, *in_hbm(*weights))


def slot_rows_body(
    slots, place_ref, routes_ref, own_ref, other_ref, pick_ref, pick_back_ref, counts_ref, out_ref
):
    core = place_ref[1]
    experts = counts_ref.shape[0]
    half, seq_len = own_ref.shape[0], routes_ref.shape[1]

    @pl.when(pl.program_id(0) == 0)
    def _():
        routes = routes_ref[...]
        routes = jnp.where(
            core == 0, routes, jnp.concatenate([routes[:, half:], routes[:, :half]], axis=1)
        )
        numbers = lax.broadcasted_iota(jnp.int32, (experts, seq_len), 0)
        hits = numbers == routes[0:1, :]
        for k in range(1, routes.shape[0]):
            hits = hits | (numbers == routes[k : k + 1, :])
        hits_float = jnp.where(hits, 1.0, 0.0)
        counts_ref[...] = jnp.sum(hits_float, axis=1, keepdims=True)
        square = (seq_len, seq_len)
        shift = core * half
        earlier = lax.broadcasted_iota(jnp.int32, square, 0) + shift
        place = lax.broadcasted_iota(jnp.int32, square, 1) + shift
        earlier = jnp.where(earlier >= seq_len, earlier - seq_len, earlier)
        place = jnp.where(place >= seq_len, place - seq_len, place)
        before = jnp.where(earlier < place, 1.0, 0.0).astype(bf16)
        rank = jnp.where(hits, dot(hits_float.astype(bf16), before), -1.0)
        slot = lax.broadcasted_iota(jnp.int32, (experts, slots, seq_len), 1) + core * slots
        pick = jnp.where(rank[:, None, :] == slot.astype(f32), 1.0, 0.0)
        pick_ref[...] = pick.reshape(experts * slots, seq_len).astype(bf16)
        wide = (experts, experts * slots)
        spread = lax.broadcasted_iota(jnp.int32, wide, 1) // slots
        spread = spread == lax.broadcasted_iota(jnp.int32, wide, 0)
        spread_rank = dot(rank.T.astype(bf16), jnp.where(spread, 1.0, 0.0).astype(bf16))
        slot = lax.broadcasted_iota(jnp.int32, spread_rank.shape, 1) % slots + core * slots
        pick_back_ref[...] = jnp.where(spread_rank == slot.astype(f32), 1.0, 0.0).astype(bf16)

    rows = jnp.concatenate([own_ref[...], other_ref[...]], axis=0)
    out_ref[...] = dot(pick_ref[...], rows).astype(bf16)


def slot_rows(place, routes, own, other, experts, slots, columns):
    half = own.shape[0]
    top_count, seq_len = routes.shape
    steps = 2
    size = columns // steps
    rows = pl.BlockSpec((half, size), lambda k, c: (0, k))

    def whole(*shape):
        return pl.BlockSpec(shape, lambda k, c: (0, 0))

    return pl.pallas_call(
        lambda *refs: slot_rows_body(slots, *refs),
        grid_spec=pltpu.PrefetchScalarGridSpec(
            num_scalar_prefetch=1,
            grid=(steps,),
            in_specs=[whole(top_count, seq_len), rows, rows],
            out_specs=[
                whole(experts * slots, seq_len),
                whole(seq_len, experts * slots),
                whole(experts, 1),
                pl.BlockSpec((experts * slots, size), lambda k, c: (0, k)),
            ],
        ),
        out_shape=[
            pltpu.HBM((experts * slots, seq_len), bf16),
            pltpu.HBM((seq_len, experts * slots), bf16),
            pltpu.HBM((experts, 1), f32),
            pltpu.HBM((experts * slots, columns), bf16),
        ],
        compiler_params=params(20),
        cost_estimate=pl.CostEstimate(
            flops=2 * experts * slots * seq_len * columns,
            transcendentals=0,
            bytes_accessed=2 * (seq_len + experts * slots) * columns,
        ),
        name="slot_rows",
    )(place, routes, *in_hbm(own), other)


def token_sums_body(pick_ref, rows_ref, out_ref):
    out_ref[...] = dot(pick_ref[...], rows_ref[...]).astype(out_ref.dtype)


def token_sums(pick_back, rows, part, kind):
    seq_len, count = pick_back.shape
    half, width = seq_len // 2, rows.shape[1]
    steps = 2
    return pl.pallas_call(
        token_sums_body,
        grid=(steps,),
        in_specs=[
            pl.BlockSpec((half, count), lambda k: (part, 0)),
            pl.BlockSpec((count, width // steps), lambda k: (0, k)),
        ],
        out_specs=pl.BlockSpec((half, width // steps), lambda k: (0, k)),
        out_shape=jax.ShapeDtypeStruct((half, width), kind),
        compiler_params=params(16),
        cost_estimate=pl.CostEstimate(
            flops=2 * count * half * width,
            transcendentals=0,
            bytes_accessed=2 * count * (half + width) + 4 * half * width,
        ),
        name="token_sums",
    )(*in_hbm(pick_back, rows))


def hidden_grad_body(
    own_ref,
    other_ref,
    logit_high_ref,
    logit_low_ref,
    w_router_ref,
    gain_ref,
    hidden_ref,
    scale_ref,
    cot_ref,
    grad_ref,
    low_ref,
    gain_grad_ref,
):
    w_router = w_router_ref[...]
    moe_in = own_ref[...] + other_ref[...].astype(f32)
    moe_in = moe_in + dot(logit_high_ref[...], w_router)
    moe_in = moe_in + dot(logit_low_ref[...], w_router)
    hidden, scale = hidden_ref[...], scale_ref[...]
    gain_grad_ref[...] = jnp.sum(hidden * scale * moe_in, axis=0, keepdims=True)
    weighted = moe_in * gain_ref[...]
    inner = jnp.mean(hidden * weighted, axis=1, keepdims=True)
    grad = cot_ref[...].astype(f32) + scale * weighted
    grad = grad - hidden * (scale * scale * scale * inner)
    grad_ref[...] = grad
    low_ref[...] = grad.astype(bf16)


def hidden_grad_of(own, other, logit_high, logit_low, w_router, gain, hidden, scale, cot):
    rows, width = own.shape
    return pl.pallas_call(
        hidden_grad_body,
        out_shape=[
            pltpu.HBM((rows, width), f32),
            pltpu.HBM((rows, width), bf16),
            jax.ShapeDtypeStruct((1, width), f32),
        ],
        compiler_params=params(16),
        cost_estimate=pl.CostEstimate(
            flops=20 * rows * width, transcendentals=0, bytes_accessed=20 * rows * width
        ),
        name="hidden_grad",
    )(own, other, logit_high, logit_low, w_router, gain, hidden, scale, cot)


def router_grad_body(normed_ref, high_ref, low_ref, out_ref):
    normed = normed_ref[...]
    out_ref[...] = dot_rows(normed, high_ref[...]) + dot_rows(normed, low_ref[...])


def router_grad_of(normed, high, low):
    return pl.pallas_call(
        router_grad_body,
        out_shape=jax.ShapeDtypeStruct((normed.shape[1], high.shape[1]), f32),
        compiler_params=params(10),
        cost_estimate=pl.CostEstimate(
            flops=1 << 20, transcendentals=0, bytes_accessed=normed.size
        ),
        name="router_grad",
    )(normed, high, low)


def projections_body(
    own_ref,
    other_ref,
    gain_ref,
    w_query_ref,
    w_key_ref,
    w_value_ref,
    normed_own_ref,
    normed_other_ref,
    scale_ref,
    query_ref,
    key_ref,
    value_ref,
    squares_ref,
    normed_ref,
):
    half = own_ref.shape[0]
    step = pl.program_id(0)

    @pl.when(step == 0)
    def _():
        for k, (ref, out_ref) in enumerate(
            ((own_ref, normed_own_ref), (other_ref, normed_other_ref))
        ):
            rows = ref[...].astype(f32)
            scale = rms_scale(rows)
            normed = (rows * scale * gain_ref[...]).astype(bf16)
            out_ref[...] = normed
            normed_ref[k * half : (k + 1) * half, :] = normed
            if k == 0:
                scale_ref[...] = scale

    normed = normed_ref[...]
    query = dot(normed, w_query_ref[...])
    key = dot(normed, w_key_ref[...])
    query_ref[...] = query
    key_ref[...] = key
    value_ref[...] = dot(normed, w_value_ref[...]).astype(bf16)
    squares = jnp.concatenate(
        [jnp.sum(v * v, axis=1, keepdims=True) for v in (query, key)], axis=1
    )

    @pl.when(step == 0)
    def _():
        squares_ref[...] = squares

    @pl.when(step > 0)
    def _():
        squares_ref[...] += squares


def projections(own, other, gain, weights):
    half, width = own.shape
    local_width = weights[0].shape[1]
    steps = 4
    size = local_width // steps

    def whole(*shape):
        return pl.BlockSpec(shape, lambda k: (0, 0))

    column = pl.BlockSpec((2 * half, size), lambda k: (0, k))
    return pl.pallas_call(
        projections_body,
        grid=(steps,),
        in_specs=[whole(half, width), whole(half, width), whole(1, width)]
        + [pl.BlockSpec((width, size), lambda k: (0, k))] * 3,
        out_specs=[whole(half, width)] * 2
        + [whole(half, 1), column, column, column, whole(2 * half, 2)],
        out_shape=[jax.ShapeDtypeStruct((half, width), bf16)] * 2
        + [jax.ShapeDtypeStruct((half, 1), f32)]
        + [jax.ShapeDtypeStruct((2 * half, local_width), kind) for kind in (f32, f32, bf16)]
        + [jax.ShapeDtypeStruct((2 * half, 2), f32)],
        scratch_shapes=[pltpu.VMEM((2 * half, width), bf16)],
        compiler_params=params(22),
        cost_estimate=pl.CostEstimate(
            flops=1 << 20, transcendentals=0, bytes_accessed=width * local_width // cheap
        ),
        name="projections",
    )(*in_hbm(own, other), gain, *in_hbm(*weights))


def branch_body(mixed_ref, w_ref, own_ref, other_ref):
    total = dot(mixed_ref[...], w_ref[...])
    half = own_ref.shape[0]
    own_ref[...] = total[:half]
    other_ref[...] = total[half:]


def branch_of(mixed, w_out):
    seq_len, local_width = mixed.shape
    width = w_out.shape[1]
    steps = 4
    half = pl.BlockSpec((seq_len // 2, width // steps), lambda k: (0, k))
    return pl.pallas_call(
        branch_body,
        grid=(steps,),
        in_specs=[
            pl.BlockSpec((seq_len, local_width), lambda k: (0, 0)),
            pl.BlockSpec((local_width, width // steps), lambda k: (0, k)),
        ],
        out_specs=[half] * 2,
        out_shape=[jax.ShapeDtypeStruct((seq_len // 2, width), f32)] * 2,
        compiler_params=params(12),
        cost_estimate=pl.CostEstimate(
            flops=1 << 20, transcendentals=0, bytes_accessed=width * local_width // cheap
        ),
        name="branch",
    )(mixed, *in_hbm(w_out))


def moe_rows_body(
    own_ref,
    other_ref,
    branch_own_ref,
    branch_other_ref,
    got_own_ref,
    got_other_ref,
    gain_ref,
    w_router_ref,
    pick_ref,
    hidden_ref,
    scale_ref,
    normed_ref,
    probs_ref,
    out_ref,
):
    half = own_ref.shape[0]
    step = pl.program_id(0)

    @pl.when(step == 0)
    def _():
        for k, (ref, branch_ref, got_ref) in enumerate(
            ((own_ref, branch_own_ref, got_own_ref), (other_ref, branch_other_ref, got_other_ref))
        ):
            hidden = ref[...].astype(f32) + (branch_ref[...] + got_ref[...])
            scale = rms_scale(hidden)
            normed_ref[k * half : (k + 1) * half, :] = (hidden * scale * gain_ref[...]).astype(bf16)
            if k == 0:
                hidden_ref[...] = hidden
                scale_ref[...] = scale
        logits = dot_cols(normed_ref[...], w_router_ref[...])
        grown = jnp.exp(logits - jnp.max(logits, axis=1, keepdims=True))
        probs_ref[...] = grown / jnp.sum(grown, axis=1, keepdims=True)

    size = out_ref.shape[1]
    columns = pl.ds(pl.multiple_of(step * size, size), size)
    out_ref[...] = dot(pick_ref[...], normed_ref[:, columns]).astype(bf16)


def moe_rows(own, other, branch, got, gain, w_router, pick):
    half, width = own.shape
    count, seq_len = pick.shape
    experts = w_router.shape[0]
    steps = 4

    def whole(*shape):
        return pl.BlockSpec(shape, lambda k: (0, 0), pipeline_mode=pl.Buffered(1))

    def kept(*shape):
        return pl.BlockSpec(shape, lambda k: (0, 0))

    return pl.pallas_call(
        moe_rows_body,
        grid=(steps,),
        in_specs=[whole(half, width)] * 6
        + [whole(1, width), whole(experts, width), whole(count, seq_len)],
        out_specs=[
            kept(half, width),
            kept(half, 1),
            kept(seq_len, width),
            kept(seq_len, experts),
            pl.BlockSpec((count, width // steps), lambda k: (0, k)),
        ],
        out_shape=[
            pltpu.HBM((half, width), f32),
            jax.ShapeDtypeStruct((half, 1), f32),
            pltpu.HBM((seq_len, width), bf16),
            jax.ShapeDtypeStruct((seq_len, experts), f32),
            pltpu.HBM((count, width), bf16),
        ],
        compiler_params=params(24),
        cost_estimate=pl.CostEstimate(
            flops=1 << 20, transcendentals=0, bytes_accessed=width * count // cheap
        ),
        name="moe_rows",
    )(*in_hbm(own, other), *branch, *got, gain, *in_hbm(w_router, pick))


def local(
    residual_in,
    routes,
    segment_ids,
    gain_attn,
    w_query,
    w_key,
    w_value,
    gain_query,
    gain_key,
    w_out,
    gain_moe,
    w_router,
    w_gate,
    w_up,
    w_down,
    cotangent,
):
    core = lax.axis_index("tp")
    planes = lax.axis_size("z")
    chips = lax.axis_size(rows_of_chips)
    chip = lax.axis_index(rows_of_chips)
    own_rows, width = residual_in.shape
    seq_len, top_count = routes.shape
    local_width = w_query.shape[1]
    local_heads, head_dim = gain_query.shape
    experts = chips
    capacity = seq_len * top_count // experts
    own_slots = capacity // 2
    quarter = local_width // planes
    out_rows = width // chips

    def own_first(value):
        return jnp.where(
            core == 0, value, jnp.concatenate([value[own_rows:], value[:own_rows]], axis=0)
        )

    first_columns = width * 5 // 8
    numbers = jnp.stack([lax.axis_index("z"), core, chip, lax.axis_index("x")])
    cot_other = swap(cotangent)
    pick, pick_back, counts, cot_slots = slot_rows(
        numbers, routes.T, cotangent, cot_other, experts, own_slots, first_columns
    )
    cot_slots, residual_in, segment_ids = lax.optimization_barrier(
        (cot_slots, residual_in, segment_ids)
    )
    cot_first = all_to_all(
        cot_slots.reshape(experts, own_slots, first_columns), rows_of_chips
    ).reshape(experts * own_slots, first_columns)
    cot = jnp.concatenate([cotangent, cot_other], axis=0)

    place = own_first(jnp.arange(seq_len, dtype=jnp.int32))
    seg = own_first(segment_ids[0])
    same_doc = seg[:, None] == seg[None, :]
    position = place - jnp.min(jnp.where(same_doc, place[None, :], seq_len), axis=1)
    cosine, sine = rope_angles(position, head_dim)
    cosine = jnp.concatenate([cosine, cosine], axis=1)
    sine = jnp.concatenate([-sine, sine], axis=1)
    bias = jnp.where(same_doc & (place[None, :] <= place[:, None]), 0.0, mask_fill)

    other_in = swap(residual_in)
    normed_own, normed_other, scale_attn, queries, key_proj, values, squares = projections(
        residual_in, other_in, gain_attn[None], (w_query, w_key, w_value)
    )
    normed_planes = lax.all_gather(normed_own, "z", axis=0, tiled=False)
    query_gain = gain_query.reshape(1, local_width)
    key_gain = gain_key.reshape(1, local_width)
    q_rot, k_rot, probs, mixed, mixed_parts, scales = attention_forward(
        queries,
        key_proj,
        values,
        query_gain,
        key_gain,
        squares,
        swap(squares),
        cosine,
        sine,
        bias,
        local_heads,
        planes,
    )
    branch = branch_of(mixed, w_out)
    hidden_own, scale_moe, normed_moe, router_probs, moe_slots = moe_rows(
        residual_in,
        other_in,
        branch,
        (swap(branch[1]), swap(branch[0])),
        gain_moe[None],
        w_router.T,
        pick,
    )

    moe_slots, cot_first = lax.optimization_barrier((moe_slots, cot_first))
    arrived = all_to_all(
        moe_slots.reshape(experts, own_slots, width), rows_of_chips
    ).reshape(experts * own_slots, width)
    cot_slots = dot(pick, cot[:, first_columns:]).astype(bf16)
    arrived, cot_slots = lax.optimization_barrier((arrived, cot_slots))
    cot_rest = all_to_all(
        cot_slots.reshape(experts, own_slots, width - first_columns), rows_of_chips
    ).reshape(experts * own_slots, width - first_columns)

    gate_parts = (w_gate[0], swap(w_gate[0]))
    up_parts = (w_up[0], swap(w_up[0]))
    down_parts = (w_down[0], swap(w_down[0]))
    slot_out = expert_forward(arrived, gate_parts, up_parts, down_parts)
    slot_out, arrived, cot_rest, normed_planes = lax.optimization_barrier(
        (slot_out, arrived, cot_rest, normed_planes)
    )
    cot_arrived = jnp.concatenate([cot_first, cot_rest], axis=1)
    returned = all_to_all(
        slot_out.reshape(experts, own_slots, width), rows_of_chips
    ).reshape(experts * own_slots, width)
    slot_probs = jax.nn.softmax(dot(arrived, w_router), axis=-1)
    own_expert = jnp.arange(experts, dtype=jnp.int32) == chip
    slot_weight = jnp.sum(jnp.where(own_expert[None, :], slot_probs, 0.0), axis=1, keepdims=True)
    slot_grad = (slot_weight * cot_arrived.astype(f32)).astype(bf16)
    (
        inner_own,
        inner_other,
        gate_own,
        gate_other,
        up_own,
        up_other,
        slot_in_grad,
    ) = expert_backward(arrived, slot_grad, gate_parts, up_parts, down_parts)
    slot_in_grad, returned = lax.optimization_barrier((slot_in_grad, returned))
    grads_back = all_to_all(
        slot_in_grad.reshape(experts, own_slots, width), rows_of_chips
    ).reshape(experts * own_slots, width)
    normed_planes = columns_first(normed_planes, swap(normed_planes))
    number = lax.axis_index("x")
    line = lax.axis_size("x")
    mixed_line = [lax.dynamic_index_in_dim(mixed_parts, number, 0, keepdims=False)]
    for shift in range(1, line):
        part = lax.dynamic_index_in_dim(mixed_parts, (number + shift) % line, 0, keepdims=False)
        mixed_line.append(lax.ppermute(part, "x", [(k, (k + shift) % line) for k in range(line)]))
    others = expert_weight_grads(arrived, slot_grad, inner_other, gate_other, up_other, (), bf16)

    pick_pairs = pick.reshape(experts, own_slots, seq_len)
    weighted = pick_pairs.astype(f32) * router_probs.T[:, None, :]
    weight_high, weight_low = halves(weighted.reshape(experts * own_slots, seq_len))
    moe_part = dot_rows(weight_high, returned) + dot_rows(weight_low, returned)
    moe_own, moe_other = moe_part[:own_rows], moe_part[own_rows:].astype(bf16)
    pair_products = dot_cols(returned, cot).reshape(experts, own_slots, seq_len)
    prob_part = jnp.sum(pair_products * pick_pairs.astype(f32), axis=1).T
    other_part = swap(prob_part)
    prob_grad = prob_part + jnp.concatenate([other_part[own_rows:], other_part[:own_rows]], axis=0)
    logit_grad = router_probs * (
        prob_grad - jnp.sum(router_probs * prob_grad, axis=1, keepdims=True)
    )
    logit_high, logit_low = halves(logit_grad)
    router_grad = router_grad_of(normed_moe, logit_high, logit_low)
    (
        grads_back,
        others,
        moe_own,
        moe_other,
        logit_high,
        logit_low,
        router_grad,
        mixed_line,
        normed_planes,
    ) = lax.optimization_barrier(
        (
            grads_back,
            others,
            moe_own,
            moe_other,
            logit_high,
            logit_low,
            router_grad,
            mixed_line,
            normed_planes,
        )
    )
    moe_own = moe_own + swap(moe_other).astype(f32)
    output = (hidden_own + moe_own).astype(bf16)
    others = [swap(grad) for grad in others]
    grad_w_gate, grad_w_up, grad_w_down = expert_weight_grads(
        arrived, slot_grad, inner_own, gate_own, up_own, others, f32
    )
    moe_in_other = token_sums(pick_back, grads_back, 1, bf16)
    moe_in_own = token_sums(pick_back, grads_back, 0, f32)
    hidden_grad, hidden_low_own, gain_moe_grad = hidden_grad_of(
        moe_in_own,
        swap(moe_in_other),
        logit_high[:own_rows],
        logit_low[:own_rows],
        w_router.T,
        gain_moe[None],
        hidden_own,
        scale_moe,
        cotangent,
    )
    hidden_low_other = swap(hidden_low_own)
    low_line = lax.all_gather(hidden_low_own, "x", axis=0, tiled=False)

    value_grad, query_part, key_part, gain_query_grad, gain_key_grad, inner = attention_backward(
        hidden_low_own,
        hidden_low_other,
        w_out,
        values,
        q_rot,
        k_rot,
        probs,
        queries,
        key_proj,
        query_gain,
        key_gain,
        scales,
        cosine,
        sine,
        local_heads,
    )
    inner_other, gain_moe_other = lax.optimization_barrier((swap(inner), swap(gain_moe_grad)))
    to_planes = projection_grads(
        query_part,
        key_part,
        queries,
        key_proj,
        value_grad,
        scales,
        (inner, inner_other),
        planes,
    )

    grads_planes = all_to_all(to_planes, "z").reshape(planes * seq_len, 3 * quarter)
    low_line, _ = lax.optimization_barrier((low_line, to_planes))
    parcel = out_parcel(
        numbers,
        low_line,
        [swap(low_line[k]) for k in range(line)],
        mixed_line,
        router_grad.reshape(chips, out_rows, experts),
        (gain_moe_grad, gain_moe_other),
        gain_query_grad,
        gain_key_grad,
        counts,
    )
    normed_grad, normed_grad_other = normed_grad_of(to_planes, (w_query, w_key, w_value))
    normed_grad = normed_grad + swap(normed_grad_other)
    in_own = residual_in.astype(f32)
    in_scale = scale_attn
    weighted_attn = normed_grad * gain_attn
    grad_input = (
        hidden_grad
        + in_scale * weighted_attn
        - in_own * in_scale**3 * jnp.mean(in_own * weighted_attn, axis=1, keepdims=True)
    )

    grads_planes, parcel = lax.optimization_barrier((grads_planes, parcel))
    parcel = weight_parcel(normed_planes, grads_planes, parcel)
    parcel, *done = lax.optimization_barrier(
        (
            all_to_all(parcel, rows_of_chips),
            output,
            grad_input,
            grad_w_gate,
            grad_w_up,
            grad_w_down,
        )
    )
    output, grad_input, grad_w_gate, grad_w_up, grad_w_down = done
    per_chip = head_dim // chips
    own_gain = lax.dynamic_slice_in_dim(gain_attn, chip * out_rows, out_rows)[None]
    (
        grad_w_query,
        grad_w_key,
        grad_w_value,
        grad_w_out,
        grad_w_router,
        grad_gain_query,
        grad_gain_key,
        grad_gain_moe,
        count,
        attn_own,
        attn_other,
    ) = parcel_sums(
        numbers,
        parcel,
        (w_query, w_key, w_value),
        own_gain,
        planes,
        out_rows,
        local_width,
        local_heads,
        per_chip,
        experts,
    )
    return (
        output,
        grad_input,
        (attn_own + swap(attn_other))[0],
        grad_w_query,
        grad_w_key,
        grad_w_value,
        grad_gain_query.T,
        grad_gain_key.T,
        grad_w_out.T,
        grad_gain_moe[0],
        grad_w_router,
        grad_w_gate[None],
        grad_w_up[None],
        grad_w_down[None],
        count[0],
    )


def solution(mesh):
    side = round(mesh.shape["ep"] ** (1 / 3))
    cube = Mesh(mesh.devices.reshape(side, side, side, 2), rows_of_chips + ("tp",))
    ep = rows_of_chips
    both = rows_of_chips + ("tp",)
    in_specs = (
        P(both, None),
        P(ep, None),
        P(ep, None),
        P(),
        P(None, "tp"),
        P(None, "tp"),
        P(None, "tp"),
        P("tp", None),
        P("tp", None),
        P("tp", None),
        P(),
        P(),
        P(ep, None, "tp"),
        P(ep, None, "tp"),
        P(ep, "tp", None),
        P(both, None),
    )
    out_specs = (
        P(both, None),
        P(both, None),
        P(both),
        P(ep, "tp"),
        P(ep, "tp"),
        P(ep, "tp"),
        P("tp", ep),
        P("tp", ep),
        P("tp", ep),
        P(both),
        P(both, None),
        P(ep, None, "tp"),
        P(ep, None, "tp"),
        P(ep, "tp", None),
        P(ep),
    )
    return jax.shard_map(local, mesh=cube, in_specs=in_specs, out_specs=out_specs, check_vma=False)
```

```python
import jax
import jax.numpy as jnp
from jax import lax
from jax.experimental import pallas as pl
from jax.experimental.pallas import tpu as pltpu
from jax.sharding import Mesh, PartitionSpec as P

norm_eps = 1e-05
rope_base = 10000.0
mask_fill = -1e30
bf16 = jnp.bfloat16
f32 = jnp.float32
rows_of_chips = ("z", "x", "y")


def swap(value):
    return lax.ppermute(value, "tp", [(0, 1), (1, 0)])


def dot(left, right):
    return lax.dot_general(left, right, (((1,), (0,)), ((), ())), preferred_element_type=f32)


def dot_rows(left, right):
    return lax.dot_general(left, right, (((0,), (0,)), ((), ())), preferred_element_type=f32)


def dot_cols(left, right):
    return lax.dot_general(left, right, (((1,), (1,)), ((), ())), preferred_element_type=f32)


def all_to_all(value, axes):
    return lax.all_to_all(value, axes, split_axis=0, concat_axis=0, tiled=True)


def rms_scale(values):
    return lax.rsqrt(jnp.mean(values * values, axis=-1, keepdims=True) + norm_eps)


def halves(value):
    high = value.astype(bf16)
    return high, (value - high.astype(f32)).astype(bf16)


def rope_angles(positions, head_dim):
    half_dim = head_dim // 2
    exponent = jnp.arange(half_dim, dtype=f32) * (2.0 / head_dim)
    inverse = jnp.power(f32(rope_base), -exponent)
    angles = positions.astype(f32)[:, None] * inverse[None, :]
    return jnp.cos(angles), jnp.sin(angles)


lanes = 128
cheap = 64


def in_hbm(*arrays):
    return [pltpu.with_memory_space_constraint(array, pltpu.HBM) for array in arrays]


def params(megabytes):
    return pltpu.CompilerParams(vmem_limit_bytes=megabytes * 1024 * 1024)


def turn(value, cosine, sine):
    return value * cosine + pltpu.roll(value, value.shape[1] // 2, 1) * sine


def other_order(ref):
    half = ref.shape[0] // 2
    return jnp.concatenate([ref[half:, :], ref[:half, :]], axis=0)


def attention_forward_body(
    scale,
    full_width,
    query_ref,
    key_ref,
    value_ref,
    query_gain_ref,
    key_gain_ref,
    squares_ref,
    other_squares_ref,
    cosine_ref,
    sine_ref,
    bias_ref,
    q_rot_ref,
    k_rot_ref,
    probs_ref,
    mixed_ref,
    parts_ref,
    scales_ref,
):
    cosine, sine, bias = cosine_ref[...], sine_ref[...], bias_ref[...]
    head = cosine.shape[1]
    squares = squares_ref[...] + other_order(other_squares_ref)
    scales = lax.rsqrt(squares * (1.0 / full_width) + norm_eps)
    scales_ref[...] = scales
    for h in range(probs_ref.shape[0]):
        here = slice(h * head, (h + 1) * head)
        query = query_ref[:, here] * scales[:, 0:1] * query_gain_ref[:, here]
        key = key_ref[:, here] * scales[:, 1:2] * key_gain_ref[:, here]
        q_rot = turn(query, cosine, sine).astype(bf16)
        k_rot = turn(key, cosine, sine).astype(bf16)
        q_rot_ref[:, here] = q_rot
        k_rot_ref[:, here] = k_rot
        scores = dot_cols(q_rot, k_rot) * scale + bias
        grown = jnp.exp(scores - jnp.max(scores, axis=1, keepdims=True))
        probs = grown / jnp.sum(grown, axis=1, keepdims=True)
        probs_ref[h] = probs
        mixed_ref[:, here] = dot(probs.astype(bf16), value_ref[:, here]).astype(bf16)
    part = parts_ref.shape[2]
    for k in range(parts_ref.shape[0]):
        parts_ref[k] = mixed_ref[:, k * part : (k + 1) * part]


def attention_forward(
    queries, keys, values, query_gain, key_gain, squares, other, cosine, sine, bias, heads, planes
):
    seq_len, width = queries.shape
    head = width // heads
    group = min(heads, 4)
    column = pl.BlockSpec((seq_len, group * head), lambda h: (0, h))
    gain = pl.BlockSpec((1, group * head), lambda h: (0, h))

    def whole(array):
        return pl.BlockSpec(array.shape, lambda h: (0, 0))

    return pl.pallas_call(
        lambda *refs: attention_forward_body(head**-0.5, 2 * width, *refs),
        grid=(heads // group,),
        in_specs=[column, column, column, gain, gain]
        + [whole(a) for a in (squares, other, cosine, sine, bias)],
        out_specs=[
            column,
            column,
            pl.BlockSpec((group, seq_len, seq_len), lambda h: (h, 0, 0)),
            column,
            pl.BlockSpec(
                (planes * group // heads, seq_len, width // planes), lambda h: (h, 0, 0)
            ),
            whole(squares),
        ],
        out_shape=[
            jax.ShapeDtypeStruct((seq_len, width), bf16),
            jax.ShapeDtypeStruct((seq_len, width), bf16),
            jax.ShapeDtypeStruct((heads, seq_len, seq_len), f32),
            jax.ShapeDtypeStruct((seq_len, width), bf16),
            jax.ShapeDtypeStruct((planes, seq_len, width // planes), bf16),
            jax.ShapeDtypeStruct((seq_len, 2), f32),
        ],
        compiler_params=params(16),
        cost_estimate=pl.CostEstimate(
            flops=4 * seq_len * seq_len * width // cheap,
            transcendentals=0,
            bytes_accessed=seq_len * width * 16 // cheap,
        ),
        name="attention_forward",
    )(queries, keys, values, query_gain, key_gain, squares, other, cosine, sine, bias)


def attention_backward_body(
    scale,
    hidden_own_ref,
    hidden_other_ref,
    w_out_ref,
    value_ref,
    q_rot_ref,
    k_rot_ref,
    probs_ref,
    query_ref,
    key_ref,
    query_gain_ref,
    key_gain_ref,
    scales_ref,
    cosine_ref,
    sine_ref,
    value_grad_ref,
    query_part_ref,
    key_part_ref,
    query_gain_grad_ref,
    key_gain_grad_ref,
    inner_ref,
):
    cosine, sine = cosine_ref[...], sine_ref[...]
    hidden = jnp.concatenate([hidden_own_ref[...], hidden_other_ref[...]], axis=0)
    heads, head = query_gain_grad_ref.shape[0], query_gain_grad_ref.shape[2]
    grad_mixed = dot_cols(hidden, w_out_ref[...]).astype(bf16)
    total = None
    for h in range(heads):
        here = slice(h * head, (h + 1) * head)
        grad = grad_mixed[:, here]
        probs = probs_ref[h]
        grad_probs = dot_cols(grad, value_ref[:, here])
        inner = jnp.sum(probs * grad_probs, axis=1, keepdims=True)
        grad_scores = (probs * (grad_probs - inner)).astype(bf16)
        value_grad_ref[:, here] = dot_rows(probs.astype(bf16), grad).astype(bf16)
        row_inners = []
        for k, (grad_rot, raw_ref, gain_ref, part_ref, gain_grad_ref) in enumerate(
            (
                (
                    dot(grad_scores, k_rot_ref[:, here]),
                    query_ref,
                    query_gain_ref,
                    query_part_ref,
                    query_gain_grad_ref,
                ),
                (
                    dot_rows(grad_scores, q_rot_ref[:, here]),
                    key_ref,
                    key_gain_ref,
                    key_part_ref,
                    key_gain_grad_ref,
                ),
            )
        ):
            grad_normed = turn(grad_rot * scale, cosine, -sine)
            raw = raw_ref[:, here]
            gain_grad_ref[h] = jnp.sum(
                raw * scales_ref[:, k : k + 1] * grad_normed, axis=0, keepdims=True
            )
            weighted = grad_normed * gain_ref[:, here]
            part_ref[:, here] = weighted
            row_inners.append(jnp.sum(raw * weighted, axis=1, keepdims=True))
        row_inner = jnp.concatenate(row_inners, axis=1)
        total = row_inner if total is None else total + row_inner
    first = pl.program_id(0) == 0

    @pl.when(first)
    def _():
        inner_ref[...] = total

    @pl.when(jnp.logical_not(first))
    def _():
        inner_ref[...] += total


def attention_backward(
    hidden_own,
    hidden_other,
    w_out,
    values,
    q_rot,
    k_rot,
    probs,
    queries,
    keys,
    query_gain,
    key_gain,
    scales,
    cosine,
    sine,
    heads,
):
    seq_len, width = queries.shape
    head = width // heads
    group = min(heads, 4)
    column = pl.BlockSpec((seq_len, group * head), lambda h: (0, h))
    gain = pl.BlockSpec((1, group * head), lambda h: (0, h))

    def whole(array):
        return pl.BlockSpec(array.shape, lambda h: (0, 0))

    full = jax.ShapeDtypeStruct((seq_len, width), f32)
    line = jax.ShapeDtypeStruct((heads, 1, head), f32)
    line_spec = pl.BlockSpec((group, 1, head), lambda h: (h, 0, 0))
    sums = jax.ShapeDtypeStruct((seq_len, 2), f32)
    return pl.pallas_call(
        lambda *refs: attention_backward_body(head**-0.5, *refs),
        grid=(heads // group,),
        in_specs=[
            whole(hidden_own),
            whole(hidden_other),
            pl.BlockSpec((group * head, w_out.shape[1]), lambda h: (h, 0)),
            column,
            column,
            column,
            pl.BlockSpec((group, seq_len, seq_len), lambda h: (h, 0, 0)),
            column,
            column,
            gain,
            gain,
        ]
        + [whole(a) for a in (scales, cosine, sine)],
        out_specs=[column, column, column, line_spec, line_spec, whole(sums)],
        out_shape=[
            jax.ShapeDtypeStruct((seq_len, width), bf16),
            full,
            full,
            line,
            line,
            sums,
        ],
        compiler_params=params(20),
        cost_estimate=pl.CostEstimate(
            flops=10 * seq_len * seq_len * width + 2 * seq_len * width * w_out.shape[1],
            transcendentals=0,
            bytes_accessed=seq_len * width * 28
            + heads * seq_len * seq_len * 4
            + 2 * w_out.size
            + 4 * hidden_own.size,
        ),
        name="attention_backward",
    )(
        *in_hbm(hidden_own),
        hidden_other,
        *in_hbm(w_out, values, q_rot, k_rot, probs, queries, keys),
        query_gain,
        key_gain,
        scales,
        cosine,
        sine,
    )


def projection_grads_body(
    width,
    query_part_ref,
    key_part_ref,
    query_ref,
    key_ref,
    value_grad_ref,
    scales_ref,
    inner_ref,
    other_inner_ref,
    stack_ref,
):
    blocks, _, columns = stack_ref.shape
    size = columns // 3
    inner = (inner_ref[...] + other_order(other_inner_ref)) * (1.0 / width)
    for k, (part_ref, raw_ref) in enumerate(
        ((query_part_ref, query_ref), (key_part_ref, key_ref))
    ):
        scale = scales_ref[:, k : k + 1]
        factor = scale * scale * scale * inner[:, k : k + 1]
        for block in range(blocks):
            here = slice(block * size, (block + 1) * size)
            grad = scale * part_ref[:, here] - raw_ref[:, here] * factor
            stack_ref[block, :, k * size : (k + 1) * size] = grad.astype(bf16)
    for block in range(blocks):
        stack_ref[block, :, 2 * size :] = value_grad_ref[:, block * size : (block + 1) * size]


def projection_grads(
    query_part, key_part, queries, keys, value_grad, scales, inners, planes
):
    seq_len, width = queries.shape
    size = width // planes
    steps = 2
    column = pl.BlockSpec((seq_len, width // steps), lambda k: (0, k))
    pair = pl.BlockSpec((seq_len, 2), lambda k: (0, 0))
    return pl.pallas_call(
        lambda *refs: projection_grads_body(2 * width, *refs),
        grid=(steps,),
        in_specs=[column] * 5 + [pair] * 3,
        out_specs=pl.BlockSpec((planes // steps, seq_len, 3 * size), lambda k: (k, 0, 0)),
        out_shape=jax.ShapeDtypeStruct((planes, seq_len, 3 * size), bf16),
        compiler_params=params(10),
        cost_estimate=pl.CostEstimate(
            flops=10 * seq_len * width, transcendentals=0, bytes_accessed=24 * seq_len * width
        ),
        name="projection_grads",
    )(query_part, key_part, queries, keys, value_grad, scales, *inners)


def expert_forward_body(
    rows_hbm,
    gate_own_hbm,
    gate_other_hbm,
    up_own_hbm,
    up_other_hbm,
    down_own_hbm,
    down_other_hbm,
    out_hbm,
    rows_ref,
    gate_ref,
    up_ref,
    down_ref,
    out_ref,
    in_sems,
    out_sems,
):
    count, width = rows_ref.shape
    pieces = 2
    size = count // pieces
    copies = {}
    order = [("rows", 0), ("gate", 0), ("up", 0), ("gate", 1), ("up", 1), ("down", 0), ("down", 1)]
    order += [("rows", k) for k in range(1, pieces)]
    sources = {
        "gate": ((gate_own_hbm, gate_other_hbm), gate_ref),
        "up": ((up_own_hbm, up_other_hbm), up_ref),
        "down": ((down_own_hbm, down_other_hbm), down_ref),
    }
    for number, (name, k) in enumerate(order):
        if name == "rows":
            here = pl.ds(k * size, size)
            copy = pltpu.make_async_copy(rows_hbm.at[here], rows_ref.at[here], in_sems.at[number])
        else:
            source, target = sources[name]
            copy = pltpu.make_async_copy(source[k], target.at[k], in_sems.at[number])
        copy.start()
        copies[name, k] = copy
    outs = []
    for piece in range(pieces):
        here = pl.ds(piece * size, size)
        copies["rows", piece].wait()
        inners = []
        for k in range(2):
            if piece == 0:
                copies["gate", k].wait()
            gate = dot(rows_ref[here, :], gate_ref[k])
            if piece == 0:
                copies["up", k].wait()
            up = dot(rows_ref[here, :], up_ref[k])
            inners.append((gate * jax.nn.sigmoid(gate) * up).astype(bf16))
        if piece == 0:
            copies["down", 0].wait()
            copies["down", 1].wait()
        step = min(512, width)
        for start in range(0, width, step):
            columns = pl.ds(start, step)
            total = dot(inners[0], down_ref[0, :, columns]) + dot(
                inners[1], down_ref[1, :, columns]
            )
            out_ref[here, columns] = total.astype(bf16)
        copy = pltpu.make_async_copy(out_ref.at[here], out_hbm.at[here], out_sems.at[piece])
        copy.start()
        outs.append(copy)
    for copy in outs:
        copy.wait()


def expert_specs(count, width, size):
    whole = pl.BlockSpec((count, width), lambda k: (0, 0), pipeline_mode=pl.Buffered(1))
    into = pl.BlockSpec((width, size), lambda k: (0, k))
    back = pl.BlockSpec((size, width), lambda k: (k, 0))
    return whole, into, back


def expert_forward(rows, gates, ups, downs):
    count, width = rows.shape
    units = gates[0].shape[1]
    return pl.pallas_call(
        expert_forward_body,
        in_specs=[pl.BlockSpec(memory_space=pl.ANY)] * 7,
        out_specs=pl.BlockSpec(memory_space=pl.ANY),
        out_shape=pltpu.HBM((count, width), bf16),
        scratch_shapes=[
            pltpu.VMEM((count, width), bf16),
            pltpu.VMEM((2, width, units), bf16),
            pltpu.VMEM((2, width, units), bf16),
            pltpu.VMEM((2, units, width), bf16),
            pltpu.VMEM((count, width), bf16),
            pltpu.SemaphoreType.DMA((8,)),
            pltpu.SemaphoreType.DMA((2,)),
        ],
        compiler_params=params(44),
        cost_estimate=pl.CostEstimate(
            flops=12 * count * width * units // cheap,
            transcendentals=0,
            bytes_accessed=(count * width * 4 + 12 * width * units) // cheap,
        ),
        name="expert_forward",
    )(*in_hbm(rows, *gates, *ups, *downs))


def expert_backward_body(
    rows_ref,
    slot_grad_ref,
    gate_own_ref,
    gate_other_ref,
    up_own_ref,
    up_other_ref,
    down_own_ref,
    down_other_ref,
    inner_own_ref,
    inner_other_ref,
    gate_grad_own_ref,
    gate_grad_other_ref,
    up_grad_own_ref,
    up_grad_other_ref,
    out_ref,
    total_ref,
):
    step = pl.program_id(0)
    last = pl.num_programs(0) - 1
    for gate_ref, up_ref, down_ref, inner_ref, gate_grad_ref, up_grad_ref in (
        (gate_own_ref, up_own_ref, down_own_ref, inner_own_ref, gate_grad_own_ref, up_grad_own_ref),
        (
            gate_other_ref,
            up_other_ref,
            down_other_ref,
            inner_other_ref,
            gate_grad_other_ref,
            up_grad_other_ref,
        ),
    ):
        gate = dot(rows_ref[...], gate_ref[...])
        up = dot(rows_ref[...], up_ref[...])
        inner_grad = dot_cols(slot_grad_ref[...], down_ref[...])
        sigmoid_gate = jax.nn.sigmoid(gate)
        silu_gate = gate * sigmoid_gate
        inner_ref[...] = (silu_gate * up).astype(bf16)
        up_grad_ref[...] = (inner_grad * silu_gate).astype(bf16)
        gate_grad_ref[...] = (
            inner_grad * up * sigmoid_gate * (1.0 + gate * (1.0 - sigmoid_gate))
        ).astype(bf16)
    width = out_ref.shape[1]
    size = min(512, width)
    for start in range(0, width, size):
        here = pl.ds(start, size)
        part = None
        for grad_ref, w_ref in (
            (gate_grad_own_ref, gate_own_ref),
            (gate_grad_other_ref, gate_other_ref),
            (up_grad_own_ref, up_own_ref),
            (up_grad_other_ref, up_other_ref),
        ):
            term = dot_cols(grad_ref[...], w_ref[here, :])
            part = term if part is None else part + term

        @pl.when(step == 0)
        def _():
            total_ref[:, here] = part

        @pl.when((step > 0) & (step < last))
        def _():
            total_ref[:, here] += part

        @pl.when(step == last)
        def _():
            out_ref[:, here] = (total_ref[:, here] + part).astype(bf16)


def expert_backward(rows, slot_grad, gates, ups, downs):
    count, width = rows.shape
    units = gates[0].shape[1]
    steps = 2
    size = units // steps
    whole, into, back = expert_specs(count, width, size)
    acts = pl.BlockSpec((count, size), lambda k: (0, k))
    return pl.pallas_call(
        expert_backward_body,
        grid=(steps,),
        in_specs=[whole] * 2 + [into] * 4 + [back] * 2,
        out_specs=[acts] * 6 + [pl.BlockSpec((count, width), lambda k: (0, 0))],
        out_shape=[jax.ShapeDtypeStruct((count, units), bf16)] * 6
        + [jax.ShapeDtypeStruct((count, width), bf16)],
        scratch_shapes=[pltpu.VMEM((count, width), f32)],
        compiler_params=params(56),
        cost_estimate=pl.CostEstimate(
            flops=20 * count * width * units // cheap,
            transcendentals=0,
            bytes_accessed=count * width * 6 // cheap,
        ),
        name="expert_backward",
    )(rows, slot_grad, *gates, *ups, *downs)


def put_blocks(out_ref, row, product):
    chips = out_ref.shape[0]
    rows = product.shape[0] // chips
    for k in range(product.shape[1] // lanes):
        piece = product[:, k * lanes : (k + 1) * lanes].reshape(chips, rows, lanes)
        out_ref[:, row : row + rows, :] = piece
        row += rows
    return row


def joined(own_ref, other_ref):
    rows = jnp.concatenate([own_ref[...], other_ref[...]], axis=1)
    return rows.reshape(rows.shape[0] * rows.shape[1], rows.shape[2])


def weight_parcel_body(
    normed_ref, normed_other_ref, grads_ref, parcel_hbm, out_hbm, block_ref, sems
):
    step = pl.program_id(0)
    slot = step % 2
    group, rows = block_ref.shape[1], block_ref.shape[2]

    def copy(at):
        here = out_hbm.at[pl.ds(step * group, group), pl.ds(0, rows)]
        return pltpu.make_async_copy(block_ref.at[at], here, sems.at[at])

    @pl.when(step >= 2)
    def _():
        copy(slot).wait()

    left = joined(normed_ref, normed_other_ref)
    put_blocks(block_ref.at[slot], 0, dot_rows(left, grads_ref[...]).astype(bf16))
    copy(slot).start()

    @pl.when(step == pl.num_programs(0) - 1)
    def _():
        copy(1 - slot).wait()
        copy(slot).wait()


def weight_parcel(normed, grads, parcel):
    planes, half, width = normed[0].shape
    tokens, columns = grads.shape
    chips, height, _ = parcel.shape
    rows = width // chips * columns // lanes
    steps = planes
    left = pl.BlockSpec((planes, half, width // steps), lambda k: (0, 0, k))
    return pl.pallas_call(
        weight_parcel_body,
        grid=(steps,),
        in_specs=[
            left,
            left,
            pl.BlockSpec((tokens, columns), lambda k: (0, 0)),
            pl.BlockSpec(memory_space=pl.ANY),
        ],
        out_specs=pl.BlockSpec(memory_space=pl.ANY),
        out_shape=pltpu.HBM((chips, height, lanes), bf16),
        input_output_aliases={3: 0},
        scratch_shapes=[
            pltpu.VMEM((2, chips // steps, rows, lanes), bf16),
            pltpu.SemaphoreType.DMA((2,)),
        ],
        compiler_params=params(18),
        cost_estimate=pl.CostEstimate(
            flops=2 * tokens * width * columns,
            transcendentals=0,
            bytes_accessed=2 * (tokens * width + grads.size + chips * height * lanes),
        ),
        name="weight_parcel",
    )(*in_hbm(*normed, grads, parcel))


def out_parcel_body(
    start,
    per_chip,
    line,
    place_ref,
    low_ref,
    *refs,
):
    low_other_refs, mixed_refs, refs = refs[:line], refs[line : 2 * line], refs[2 * line :]
    router_ref, moe_ref, moe_other_ref, query_gain_ref, key_gain_ref, counts_ref = refs[:6]
    out_hbm, block_ref, sems = refs[6:]
    step = pl.program_id(0)
    slot = step % 2
    group = block_ref.shape[1]

    def copy(at):
        here = out_hbm.at[pl.ds(step * group, group), pl.ds(start, block_ref.shape[2])]
        return pltpu.make_async_copy(block_ref.at[at], here, sems.at[at])

    @pl.when(step >= 2)
    def _():
        copy(slot).wait()

    total = None
    for shift, mixed_ref in enumerate(mixed_refs):
        source = (place_ref[3] + line - shift) % line
        other = low_other_refs[0][...]
        for k in range(1, line):
            other = jnp.where(source == k, low_other_refs[k][...], other)
        left = jnp.concatenate([low_ref[source], other], axis=0)
        part = dot_rows(left, mixed_ref[...])
        total = part if total is None else total + part
    row = put_blocks(block_ref.at[slot], 0, total.astype(bf16))

    chips, rows, spare = router_ref.shape[0], router_ref.shape[1] // 2, lanes // 2
    core = place_ref[1]
    router = router_ref[:, pl.ds(core * rows, rows), :]
    if router.shape[2] < spare:
        fill = jnp.zeros((chips, rows, spare - router.shape[2]), f32)
        router = jnp.concatenate([router, fill], axis=2)
    moe = moe_ref[...] + moe_other_ref[...]
    span = 2 * rows
    moe = jnp.concatenate([moe[:, k * span : (k + 1) * span] for k in range(chips)], axis=0)
    moe = jnp.where(core == 0, moe[:, :rows], moe[:, rows:])
    heads, head = query_gain_ref.shape[0], query_gain_ref.shape[2]
    chip = lax.broadcasted_iota(jnp.int32, (chips, heads, head), 0) + step * chips
    lane = lax.broadcasted_iota(jnp.int32, (chips, heads, head), 2)
    mine = lane // per_chip == chip
    feature = lax.broadcasted_iota(jnp.int32, (head, spare), 0) % per_chip
    column = lax.broadcasted_iota(jnp.int32, (head, spare), 1)
    first_row = lax.broadcasted_iota(jnp.int32, (chips, heads, spare), 1) == 0
    used = 2 * per_chip + rows + 1
    blocks = []
    for part in range(2):
        block = jnp.zeros((chips * heads, spare), f32)
        for k, gain_ref in enumerate((query_gain_ref, key_gain_ref)):
            values = halves(gain_ref[:, 0, :])[part].astype(f32)
            values = jnp.where(mine, values[None], 0.0).reshape(chips * heads, head).astype(bf16)
            target = jnp.where(column == feature + k * per_chip, 1.0, 0.0).astype(bf16)
            block = block + dot(values, target)
        moe_part = halves(moe)[part].astype(f32)
        count = counts_ref[...] if part == 0 else jnp.zeros((chips, 1), f32)
        vector = jnp.concatenate(
            [jnp.zeros((chips, 2 * per_chip), f32), moe_part, count]
            + [jnp.zeros((chips, spare - used), f32)] * (used < spare),
            axis=1,
        )
        block = block.reshape(chips, heads, spare)
        blocks.append(block + jnp.where(first_row, vector[:, None, :], 0.0))
        if heads < rows // 2:
            blocks.append(jnp.zeros((chips, rows // 2 - heads, spare), f32))
    beside = jnp.concatenate(blocks, axis=1)
    small = jnp.concatenate([router, beside], axis=2).astype(bf16)
    block_ref[slot, :, row:, :] = small
    copy(slot).start()

    @pl.when(step == pl.num_programs(0) - 1)
    def _():
        copy(1 - slot).wait()
        copy(slot).wait()


def out_parcel(place, low, low_other, mixed, router, moe, query_gain, key_gain, counts):
    line, half, width = low.shape
    tokens, part = mixed[0].shape
    chips, router_rows, experts = router.shape
    heads, _, head = query_gain.shape
    room = width // chips * part // lanes
    small_rows = router_rows // 2
    height = 4 * room + small_rows
    steps = line
    group = chips // steps
    gain = pl.BlockSpec((heads, 1, head), lambda k, z: (0, 0, 0))
    vector = pl.BlockSpec((1, width // steps), lambda k, z: (0, k))
    return pl.pallas_call(
        lambda *refs: out_parcel_body(3 * room, head // chips, line, *refs),
        grid_spec=pltpu.PrefetchScalarGridSpec(
            num_scalar_prefetch=1,
            grid=(steps,),
            in_specs=[pl.BlockSpec((line, half, width // steps), lambda k, z: (0, 0, k))]
            + [pl.BlockSpec((half, width // steps), lambda k, z: (0, k))] * line
            + [pl.BlockSpec((tokens, part), lambda k, z: (0, 0))] * line
            + [pl.BlockSpec((group, router_rows, experts), lambda k, z: (k, 0, 0))]
            + [vector, vector, gain, gain, pl.BlockSpec((group, 1), lambda k, z: (k, 0))],
            out_specs=pl.BlockSpec(memory_space=pl.ANY),
            scratch_shapes=[
                pltpu.VMEM((2, group, room + small_rows, lanes), bf16),
                pltpu.SemaphoreType.DMA((2,)),
            ],
        ),
        out_shape=pltpu.HBM((chips, height, lanes), bf16),
        compiler_params=params(18),
        cost_estimate=pl.CostEstimate(
            flops=2 * tokens * width * part // cheap,
            transcendentals=0,
            bytes_accessed=2 * (tokens * width + chips * room * lanes) // cheap,
        ),
        name="out_parcel",
    )(
        place,
        *in_hbm(low),
        *low_other,
        *mixed,
        *in_hbm(router),
        *moe,
        query_gain,
        key_gain,
        counts,
    )


def parcel_sums_body(
    per_chip,
    place_ref,
    parcel_ref,
    w_query_ref,
    w_key_ref,
    w_value_ref,
    own_gain_ref,
    query_ref,
    key_ref,
    value_ref,
    out_ref,
    router_ref,
    query_gain_ref,
    key_gain_ref,
    moe_ref,
    count_ref,
    attn_ref,
    attn_other_ref,
    extra_ref,
    gain_ref,
):
    rows, columns = query_ref.shape
    step = pl.program_id(0)
    blocks = columns // lanes
    row = 3 * blocks * rows
    total = jnp.sum(parcel_ref[:, :row, :].astype(f32), axis=0)
    gain = jnp.zeros((rows, lanes), f32)
    for number, (ref, w_ref) in enumerate(
        ((query_ref, w_query_ref), (key_ref, w_key_ref), (value_ref, w_value_ref))
    ):
        for k in range(blocks):
            here = slice(k * lanes, (k + 1) * lanes)
            first_row = (number * blocks + k) * rows
            piece = total[first_row : first_row + rows, :]
            ref[:, here] = piece
            gain = gain + piece * w_ref[:, here].astype(f32)

    @pl.when(step == 0)
    def _():
        out_ref[...] = jnp.zeros_like(out_ref)
        extra_ref[...] = jnp.zeros_like(extra_ref)
        gain_ref[...] = jnp.zeros_like(gain_ref)

    gain_ref[...] += gain
    extra_ref[...] += jnp.sum(parcel_ref[:, row + blocks * rows :, :].astype(f32), axis=0)
    line = pl.num_programs(0)
    group = parcel_ref.shape[0] // line
    for x in range(line):
        part = parcel_ref[x * group : (x + 1) * group, row : row + blocks * rows, :]
        part = jnp.sum(part.astype(f32), axis=0)
        for k in range(blocks):
            here = slice(x * columns + k * lanes, x * columns + (k + 1) * lanes)
            out_ref[:, here] += part[k * rows : (k + 1) * rows, :]

    @pl.when(step == pl.num_programs(0) - 1)
    def _():
        half = rows // 2
        heads = query_gain_ref.shape[1]
        router_ref[...] = extra_ref[:, : router_ref.shape[1]]
        sums = extra_ref[0:heads, :] + extra_ref[half // 2 : half // 2 + heads, :]
        first_lane = lanes // 2 + 2 * per_chip
        moe_ref[...] = sums[0:1, first_lane : first_lane + half]
        count_ref[...] = sums[0:1, first_lane + half : first_lane + half + 1].astype(jnp.int32)
        sums = sums.T
        query_gain_ref[...] = sums[lanes // 2 : lanes // 2 + per_chip, :]
        key_gain_ref[...] = sums[lanes // 2 + per_chip : first_lane, :]
        attn = jnp.sum(gain_ref[...].T, axis=0, keepdims=True) / own_gain_ref[...]
        first = place_ref[1] == 0
        attn_ref[...] = jnp.where(first, attn[:, :half], attn[:, half:])
        attn_other_ref[...] = jnp.where(first, attn[:, half:], attn[:, :half])


def parcel_sums(place, parcel, weights, own_gain, planes, rows, width, heads, per_chip, experts):
    chips, height, _ = parcel.shape
    part = width // planes
    half = rows // 2
    wide = pl.BlockSpec((rows, part), lambda k, c: (0, k))

    def whole(shape):
        return pl.BlockSpec(shape, lambda k, c: (0, 0))

    small = [(half, experts), (per_chip, heads), (per_chip, heads), (1, half), (1, 1)]
    small += [(1, half), (1, half)]
    kinds = [f32] * 4 + [jnp.int32] + [f32] * 2
    return pl.pallas_call(
        lambda *refs: parcel_sums_body(per_chip, *refs),
        grid_spec=pltpu.PrefetchScalarGridSpec(
            num_scalar_prefetch=1,
            grid=(planes,),
            in_specs=[pl.BlockSpec((chips // planes, height, lanes), lambda k, c: (k, 0, 0))]
            + [pl.BlockSpec((rows, part), lambda k, c: (c[2], k))] * 3
            + [whole((1, rows))],
            out_specs=[wide] * 3 + [whole((rows, width))] + [whole(shape) for shape in small],
            scratch_shapes=[pltpu.VMEM((half, lanes), f32), pltpu.VMEM((rows, lanes), f32)],
        ),
        out_shape=[jax.ShapeDtypeStruct((rows, width), f32)] * 4
        + [jax.ShapeDtypeStruct(shape, kind) for shape, kind in zip(small, kinds)],
        compiler_params=params(14),
        cost_estimate=pl.CostEstimate(
            flops=parcel.size, transcendentals=0, bytes_accessed=2 * parcel.size
        ),
        name="parcel_sums",
    )(place, parcel, *in_hbm(*weights), own_gain)


def expert_weight_grads_body(rows_ref, slot_grad_ref, inner_ref, gate_ref, up_ref, *refs):
    grads = (
        dot_rows(rows_ref[...], gate_ref[...]),
        dot_rows(rows_ref[...], up_ref[...]),
        dot_rows(inner_ref[...], slot_grad_ref[...]),
    )
    others, outs = refs[:-3], refs[-3:]
    for k, (grad, out_ref) in enumerate(zip(grads, outs)):
        if others:
            grad = grad + others[k][...].astype(f32)
        out_ref[...] = grad.astype(out_ref.dtype)


def expert_weight_grads(rows, slot_grad, inner, gate_grad, up_grad, others, kind):
    count, width = rows.shape
    units = inner.shape[1]
    steps = 4
    size = width // steps
    wide = pl.BlockSpec((count, size), lambda k: (0, k))
    narrow = pl.BlockSpec((count, units), lambda k: (0, 0))
    into = pl.BlockSpec((size, units), lambda k: (k, 0))
    back = pl.BlockSpec((units, size), lambda k: (0, k))
    return pl.pallas_call(
        expert_weight_grads_body,
        grid=(steps,),
        in_specs=[wide, wide, narrow, narrow, narrow] + [into, into, back][: len(others)],
        out_specs=[into, into, back],
        out_shape=[
            jax.ShapeDtypeStruct((width, units), kind),
            jax.ShapeDtypeStruct((width, units), kind),
            jax.ShapeDtypeStruct((units, width), kind),
        ],
        compiler_params=params(30),
        cost_estimate=pl.CostEstimate(
            flops=6 * count * width * units // cheap,
            transcendentals=0,
            bytes_accessed=4 * count * width // cheap,
        ),
        name="expert_weight_grads",
    )(*in_hbm(rows, slot_grad, inner, gate_grad, up_grad, *others))


def normed_grad_body(stack_ref, query_ref, key_ref, value_ref, own_ref, other_ref):
    size = query_ref.shape[1]
    total = None
    for k, w_ref in enumerate((query_ref, key_ref, value_ref)):
        part = dot_cols(stack_ref[:, k * size : (k + 1) * size], w_ref[...])
        total = part if total is None else total + part
    half = own_ref.shape[0]
    first = pl.program_id(0) == 0

    @pl.when(first)
    def _():
        own_ref[...] = total[:half]
        other_ref[...] = total[half:]

    @pl.when(jnp.logical_not(first))
    def _():
        own_ref[...] += total[:half]
        other_ref[...] += total[half:]


def normed_grad_of(stack, weights):
    planes, seq_len, columns = stack.shape
    size = columns // 3
    full = weights[0].shape[0]
    half = pl.BlockSpec((seq_len // 2, full), lambda k: (0, 0))
    return pl.pallas_call(
        normed_grad_body,
        grid=(planes,),
        in_specs=[pl.BlockSpec((None, seq_len, columns), lambda k: (k, 0, 0))]
        + [pl.BlockSpec((full, size), lambda k: (0, k))] * 3,
        out_specs=[half] * 2,
        out_shape=[jax.ShapeDtypeStruct((seq_len // 2, full), f32)] * 2,
        compiler_params=params(20),
        cost_estimate=pl.CostEstimate(
            flops=2 * stack.size * full // cheap,
            transcendentals=0,
            bytes_accessed=2 * planes * columns * full // cheap,
        ),
        name="normed_grad",
    )(stack, *in_hbm(*weights))


def pick_body(slots, place_ref, routes_ref, pick_ref, counts_ref):
    core = place_ref[1]
    experts = counts_ref.shape[0]
    seq_len = routes_ref.shape[1]
    half = seq_len // 2
    routes = routes_ref[...]
    routes = jnp.where(
        core == 0, routes, jnp.concatenate([routes[:, half:], routes[:, :half]], axis=1)
    )
    numbers = lax.broadcasted_iota(jnp.int32, (experts, seq_len), 0)
    hits = numbers == routes[0:1, :]
    for k in range(1, routes.shape[0]):
        hits = hits | (numbers == routes[k : k + 1, :])
    hits_float = jnp.where(hits, 1.0, 0.0)
    counts_ref[...] = jnp.sum(hits_float, axis=1, keepdims=True)
    square = (seq_len, seq_len)
    shift = core * half
    earlier = lax.broadcasted_iota(jnp.int32, square, 0) + shift
    place = lax.broadcasted_iota(jnp.int32, square, 1) + shift
    earlier = jnp.where(earlier >= seq_len, earlier - seq_len, earlier)
    place = jnp.where(place >= seq_len, place - seq_len, place)
    before = jnp.where(earlier < place, 1.0, 0.0).astype(bf16)
    rank = jnp.where(hits, dot(hits_float.astype(bf16), before), -1.0)
    slot = lax.broadcasted_iota(jnp.int32, (experts, slots, seq_len), 1) + core * slots
    pick = jnp.where(rank[:, None, :] == slot.astype(f32), 1.0, 0.0)
    pick_ref[...] = pick.reshape(experts * slots, seq_len).astype(bf16)


def pick_of(place, routes, experts, slots):
    seq_len = routes.shape[1]

    def whole(*shape):
        return pl.BlockSpec(shape, lambda k, c: (0, 0))

    return pl.pallas_call(
        lambda *refs: pick_body(slots, *refs),
        grid_spec=pltpu.PrefetchScalarGridSpec(
            num_scalar_prefetch=1,
            grid=(1,),
            in_specs=[whole(*routes.shape)],
            out_specs=[whole(experts * slots, seq_len), whole(experts, 1)],
        ),
        out_shape=[
            jax.ShapeDtypeStruct((experts * slots, seq_len), bf16),
            jax.ShapeDtypeStruct((experts, 1), f32),
        ],
        compiler_params=params(12),
        cost_estimate=pl.CostEstimate(
            flops=1 << 22, transcendentals=0, bytes_accessed=2 * experts * slots * seq_len
        ),
        name="pick",
    )(place, routes)


def slot_rows_body(pick_ref, own_ref, other_ref, out_ref):
    rows = jnp.concatenate([own_ref[...], other_ref[...]], axis=0)
    out_ref[...] = dot(pick_ref[...], rows).astype(bf16)


def slot_rows(pick, own, other, columns):
    count, seq_len = pick.shape
    steps = 2
    size = columns // steps
    rows = pl.BlockSpec((seq_len // 2, size), lambda k: (0, k))
    return pl.pallas_call(
        slot_rows_body,
        grid=(steps,),
        in_specs=[pl.BlockSpec((count, seq_len), lambda k: (0, 0)), rows, rows],
        out_specs=pl.BlockSpec((count, size), lambda k: (0, k)),
        out_shape=pltpu.HBM((count, columns), bf16),
        compiler_params=params(12),
        cost_estimate=pl.CostEstimate(
            flops=2 * count * seq_len * columns,
            transcendentals=0,
            bytes_accessed=2 * (seq_len + count) * columns,
        ),
        name="slot_rows",
    )(pick, *in_hbm(own), other)


def turned_body(value_ref, out_ref):
    out_ref[...] = value_ref[...].T


def turned(value):
    return pl.pallas_call(
        turned_body,
        out_shape=pltpu.HBM(value.shape[::-1], value.dtype),
        compiler_params=params(8),
        cost_estimate=pl.CostEstimate(
            flops=1 << 10, transcendentals=0, bytes_accessed=value.size // cheap
        ),
        name="turned",
    )(value)


def token_sums_body(pick_ref, rows_ref, own_ref, other_ref):
    total = dot(pick_ref[...], rows_ref[...])
    half = own_ref.shape[0]
    own_ref[...] = total[:half]
    other_ref[...] = total[half:].astype(bf16)


def token_sums(pick_back, rows):
    seq_len, count = pick_back.shape
    width = rows.shape[1]
    steps = 2
    half = pl.BlockSpec((seq_len // 2, width // steps), lambda k: (0, k))
    return pl.pallas_call(
        token_sums_body,
        grid=(steps,),
        in_specs=[
            pl.BlockSpec((seq_len, count), lambda k: (0, 0)),
            pl.BlockSpec((count, width // steps), lambda k: (0, k)),
        ],
        out_specs=[half] * 2,
        out_shape=[jax.ShapeDtypeStruct((seq_len // 2, width), kind) for kind in (f32, bf16)],
        compiler_params=params(16),
        cost_estimate=pl.CostEstimate(
            flops=2 * count * seq_len * width,
            transcendentals=0,
            bytes_accessed=2 * count * (seq_len + width) + 4 * seq_len * width,
        ),
        name="token_sums",
    )(*in_hbm(pick_back, rows))


def hidden_grad_body(
    own_ref,
    other_ref,
    logit_high_ref,
    logit_low_ref,
    w_router_ref,
    gain_ref,
    hidden_ref,
    scale_ref,
    cot_ref,
    grad_ref,
    low_ref,
    gain_grad_ref,
):
    w_router = w_router_ref[...]
    moe_in = own_ref[...] + other_ref[...].astype(f32)
    moe_in = moe_in + dot(logit_high_ref[...], w_router)
    moe_in = moe_in + dot(logit_low_ref[...], w_router)
    hidden, scale = hidden_ref[...], scale_ref[...]
    gain_grad_ref[...] = jnp.sum(hidden * scale * moe_in, axis=0, keepdims=True)
    weighted = moe_in * gain_ref[...]
    inner = jnp.mean(hidden * weighted, axis=1, keepdims=True)
    grad = cot_ref[...].astype(f32) + scale * weighted
    grad = grad - hidden * (scale * scale * scale * inner)
    grad_ref[...] = grad
    low_ref[...] = grad.astype(bf16)


def hidden_grad_of(own, other, logit_high, logit_low, w_router, gain, hidden, scale, cot):
    rows, width = own.shape
    return pl.pallas_call(
        hidden_grad_body,
        out_shape=[
            pltpu.HBM((rows, width), f32),
            pltpu.HBM((rows, width), bf16),
            jax.ShapeDtypeStruct((1, width), f32),
        ],
        compiler_params=params(16),
        cost_estimate=pl.CostEstimate(
            flops=20 * rows * width, transcendentals=0, bytes_accessed=20 * rows * width
        ),
        name="hidden_grad",
    )(own, other, logit_high, logit_low, w_router, gain, hidden, scale, cot)


def router_grad_body(normed_ref, high_ref, low_ref, out_ref):
    normed = normed_ref[...]
    out_ref[...] = dot_rows(normed, high_ref[...]) + dot_rows(normed, low_ref[...])


def router_grad_of(normed, high, low):
    return pl.pallas_call(
        router_grad_body,
        out_shape=jax.ShapeDtypeStruct((normed.shape[1], high.shape[1]), f32),
        compiler_params=params(10),
        cost_estimate=pl.CostEstimate(
            flops=1 << 20, transcendentals=0, bytes_accessed=normed.size
        ),
        name="router_grad",
    )(normed, high, low)


def projections_body(
    own_ref,
    other_ref,
    gain_ref,
    w_query_ref,
    w_key_ref,
    w_value_ref,
    normed_own_ref,
    normed_other_ref,
    scale_ref,
    query_ref,
    key_ref,
    value_ref,
    squares_ref,
    normed_ref,
):
    half = own_ref.shape[0]
    step = pl.program_id(0)

    @pl.when(step == 0)
    def _():
        for k, (ref, out_ref) in enumerate(
            ((own_ref, normed_own_ref), (other_ref, normed_other_ref))
        ):
            rows = ref[...].astype(f32)
            scale = rms_scale(rows)
            normed = (rows * scale * gain_ref[...]).astype(bf16)
            out_ref[...] = normed
            normed_ref[k * half : (k + 1) * half, :] = normed
            if k == 0:
                scale_ref[...] = scale

    normed = normed_ref[...]
    query = dot(normed, w_query_ref[...])
    key = dot(normed, w_key_ref[...])
    query_ref[...] = query
    key_ref[...] = key
    value_ref[...] = dot(normed, w_value_ref[...]).astype(bf16)
    squares = jnp.concatenate(
        [jnp.sum(v * v, axis=1, keepdims=True) for v in (query, key)], axis=1
    )

    @pl.when(step == 0)
    def _():
        squares_ref[...] = squares

    @pl.when(step > 0)
    def _():
        squares_ref[...] += squares


def projections(own, other, gain, weights):
    half, width = own.shape
    local_width = weights[0].shape[1]
    steps = 4
    size = local_width // steps

    def whole(*shape):
        return pl.BlockSpec(shape, lambda k: (0, 0))

    column = pl.BlockSpec((2 * half, size), lambda k: (0, k))
    return pl.pallas_call(
        projections_body,
        grid=(steps,),
        in_specs=[whole(half, width), whole(half, width), whole(1, width)]
        + [pl.BlockSpec((width, size), lambda k: (0, k))] * 3,
        out_specs=[whole(half, width)] * 2
        + [whole(half, 1), column, column, column, whole(2 * half, 2)],
        out_shape=[jax.ShapeDtypeStruct((half, width), bf16)] * 2
        + [jax.ShapeDtypeStruct((half, 1), f32)]
        + [jax.ShapeDtypeStruct((2 * half, local_width), kind) for kind in (f32, f32, bf16)]
        + [jax.ShapeDtypeStruct((2 * half, 2), f32)],
        scratch_shapes=[pltpu.VMEM((2 * half, width), bf16)],
        compiler_params=params(22),
        cost_estimate=pl.CostEstimate(
            flops=1 << 20, transcendentals=0, bytes_accessed=width * local_width // cheap
        ),
        name="projections",
    )(*in_hbm(own, other), gain, *in_hbm(*weights))


def branch_body(mixed_ref, w_ref, own_ref, other_ref):
    total = dot(mixed_ref[...], w_ref[...])
    half = own_ref.shape[0]
    own_ref[...] = total[:half]
    other_ref[...] = total[half:]


def branch_of(mixed, w_out):
    seq_len, local_width = mixed.shape
    width = w_out.shape[1]
    steps = 4
    half = pl.BlockSpec((seq_len // 2, width // steps), lambda k: (0, k))
    return pl.pallas_call(
        branch_body,
        grid=(steps,),
        in_specs=[
            pl.BlockSpec((seq_len, local_width), lambda k: (0, 0)),
            pl.BlockSpec((local_width, width // steps), lambda k: (0, k)),
        ],
        out_specs=[half] * 2,
        out_shape=[jax.ShapeDtypeStruct((seq_len // 2, width), f32)] * 2,
        compiler_params=params(12),
        cost_estimate=pl.CostEstimate(
            flops=1 << 20, transcendentals=0, bytes_accessed=width * local_width // cheap
        ),
        name="branch",
    )(mixed, *in_hbm(w_out))


def moe_rows_body(
    own_ref,
    other_ref,
    branch_own_ref,
    branch_other_ref,
    got_own_ref,
    got_other_ref,
    gain_ref,
    w_router_ref,
    pick_ref,
    hidden_ref,
    scale_ref,
    normed_ref,
    probs_ref,
    out_ref,
):
    half = own_ref.shape[0]
    step = pl.program_id(0)

    @pl.when(step == 0)
    def _():
        for k, (ref, branch_ref, got_ref) in enumerate(
            ((own_ref, branch_own_ref, got_own_ref), (other_ref, branch_other_ref, got_other_ref))
        ):
            hidden = ref[...].astype(f32) + (branch_ref[...] + got_ref[...])
            scale = rms_scale(hidden)
            normed_ref[k * half : (k + 1) * half, :] = (hidden * scale * gain_ref[...]).astype(bf16)
            if k == 0:
                hidden_ref[...] = hidden
                scale_ref[...] = scale
        logits = dot_cols(normed_ref[...], w_router_ref[...])
        grown = jnp.exp(logits - jnp.max(logits, axis=1, keepdims=True))
        probs_ref[...] = grown / jnp.sum(grown, axis=1, keepdims=True)

    size = out_ref.shape[1]
    columns = pl.ds(pl.multiple_of(step * size, size), size)
    out_ref[...] = dot(pick_ref[...], normed_ref[:, columns]).astype(bf16)


def moe_rows(own, other, branch, got, gain, w_router, pick):
    half, width = own.shape
    count, seq_len = pick.shape
    experts = w_router.shape[0]
    steps = 4

    def whole(*shape):
        return pl.BlockSpec(shape, lambda k: (0, 0), pipeline_mode=pl.Buffered(1))

    def kept(*shape):
        return pl.BlockSpec(shape, lambda k: (0, 0))

    return pl.pallas_call(
        moe_rows_body,
        grid=(steps,),
        in_specs=[whole(half, width)] * 6
        + [whole(1, width), whole(experts, width), whole(count, seq_len)],
        out_specs=[
            kept(half, width),
            kept(half, 1),
            kept(seq_len, width),
            kept(seq_len, experts),
            pl.BlockSpec((count, width // steps), lambda k: (0, k)),
        ],
        out_shape=[
            pltpu.HBM((half, width), f32),
            jax.ShapeDtypeStruct((half, 1), f32),
            pltpu.HBM((seq_len, width), bf16),
            jax.ShapeDtypeStruct((seq_len, experts), f32),
            pltpu.HBM((count, width), bf16),
        ],
        compiler_params=params(24),
        cost_estimate=pl.CostEstimate(
            flops=1 << 20, transcendentals=0, bytes_accessed=width * count // cheap
        ),
        name="moe_rows",
    )(*in_hbm(own, other), *branch, *got, gain, *in_hbm(w_router, pick))


def local(
    residual_in,
    routes,
    segment_ids,
    gain_attn,
    w_query,
    w_key,
    w_value,
    gain_query,
    gain_key,
    w_out,
    gain_moe,
    w_router,
    w_gate,
    w_up,
    w_down,
    cotangent,
):
    core = lax.axis_index("tp")
    planes = lax.axis_size("z")
    chips = lax.axis_size(rows_of_chips)
    chip = lax.axis_index(rows_of_chips)
    own_rows, width = residual_in.shape
    seq_len, top_count = routes.shape
    local_width = w_query.shape[1]
    local_heads, head_dim = gain_query.shape
    experts = chips
    capacity = seq_len * top_count // experts
    own_slots = capacity // 2
    quarter = local_width // planes
    out_rows = width // chips

    def own_first(value):
        return jnp.where(
            core == 0, value, jnp.concatenate([value[own_rows:], value[:own_rows]], axis=0)
        )

    first_columns = width * 5 // 8
    numbers = jnp.stack([lax.axis_index("z"), core, chip, lax.axis_index("x")])
    cot_other = swap(cotangent)
    pick, counts = pick_of(numbers, routes.T, experts, own_slots)
    cot_slots = slot_rows(pick, cotangent, cot_other, first_columns)
    cot_slots, residual_in, segment_ids = lax.optimization_barrier(
        (cot_slots, residual_in, segment_ids)
    )
    cot_first = all_to_all(
        cot_slots.reshape(experts, own_slots, first_columns), rows_of_chips
    ).reshape(experts * own_slots, first_columns)
    cot = jnp.concatenate([cotangent, cot_other], axis=0)

    place = own_first(jnp.arange(seq_len, dtype=jnp.int32))
    seg = own_first(segment_ids[0])
    same_doc = seg[:, None] == seg[None, :]
    position = place - jnp.min(jnp.where(same_doc, place[None, :], seq_len), axis=1)
    cosine, sine = rope_angles(position, head_dim)
    cosine = jnp.concatenate([cosine, cosine], axis=1)
    sine = jnp.concatenate([-sine, sine], axis=1)
    bias = jnp.where(same_doc & (place[None, :] <= place[:, None]), 0.0, mask_fill)

    other_in = swap(residual_in)
    normed_own, normed_other, scale_attn, queries, key_proj, values, squares = projections(
        residual_in, other_in, gain_attn[None], (w_query, w_key, w_value)
    )
    normed_planes = lax.all_gather(normed_own, "z", axis=0, tiled=False)
    query_gain = gain_query.reshape(1, local_width)
    key_gain = gain_key.reshape(1, local_width)
    q_rot, k_rot, probs, mixed, mixed_parts, scales = attention_forward(
        queries,
        key_proj,
        values,
        query_gain,
        key_gain,
        squares,
        swap(squares),
        cosine,
        sine,
        bias,
        local_heads,
        planes,
    )
    branch = branch_of(mixed, w_out)
    hidden_own, scale_moe, normed_moe, router_probs, moe_slots = moe_rows(
        residual_in,
        other_in,
        branch,
        (swap(branch[1]), swap(branch[0])),
        gain_moe[None],
        w_router.T,
        pick,
    )

    moe_slots, cot_first = lax.optimization_barrier((moe_slots, cot_first))
    arrived = all_to_all(
        moe_slots.reshape(experts, own_slots, width), rows_of_chips
    ).reshape(experts * own_slots, width)
    cot_slots = dot(pick, cot[:, first_columns:]).astype(bf16)
    arrived, cot_slots = lax.optimization_barrier((arrived, cot_slots))
    cot_rest = all_to_all(
        cot_slots.reshape(experts, own_slots, width - first_columns), rows_of_chips
    ).reshape(experts * own_slots, width - first_columns)

    gate_parts = (w_gate[0], swap(w_gate[0]))
    up_parts = (w_up[0], swap(w_up[0]))
    down_parts = (w_down[0], swap(w_down[0]))
    slot_out = expert_forward(arrived, gate_parts, up_parts, down_parts)
    slot_out, arrived, cot_rest, normed_planes = lax.optimization_barrier(
        (slot_out, arrived, cot_rest, normed_planes)
    )
    cot_arrived = jnp.concatenate([cot_first, cot_rest], axis=1)
    returned = all_to_all(
        slot_out.reshape(experts, own_slots, width), rows_of_chips
    ).reshape(experts * own_slots, width)
    slot_probs = jax.nn.softmax(dot(arrived, w_router), axis=-1)
    own_expert = jnp.arange(experts, dtype=jnp.int32) == chip
    slot_weight = jnp.sum(jnp.where(own_expert[None, :], slot_probs, 0.0), axis=1, keepdims=True)
    slot_grad = (slot_weight * cot_arrived.astype(f32)).astype(bf16)
    (
        inner_own,
        inner_other,
        gate_own,
        gate_other,
        up_own,
        up_other,
        slot_in_grad,
    ) = expert_backward(arrived, slot_grad, gate_parts, up_parts, down_parts)
    slot_in_grad, returned = lax.optimization_barrier((slot_in_grad, returned))
    grads_back = all_to_all(
        slot_in_grad.reshape(experts, own_slots, width), rows_of_chips
    ).reshape(experts * own_slots, width)
    normed_planes = (normed_planes, swap(normed_planes))
    number = lax.axis_index("x")
    line = lax.axis_size("x")
    mixed_line = [lax.dynamic_index_in_dim(mixed_parts, number, 0, keepdims=False)]
    for shift in range(1, line):
        part = lax.dynamic_index_in_dim(mixed_parts, (number + shift) % line, 0, keepdims=False)
        mixed_line.append(lax.ppermute(part, "x", [(k, (k + shift) % line) for k in range(line)]))
    others = expert_weight_grads(arrived, slot_grad, inner_other, gate_other, up_other, (), bf16)

    pick_pairs = pick.reshape(experts, own_slots, seq_len)
    weighted = pick_pairs.astype(f32) * router_probs.T[:, None, :]
    weight_high, weight_low = halves(weighted.reshape(experts * own_slots, seq_len))
    moe_part = dot_rows(weight_high, returned) + dot_rows(weight_low, returned)
    moe_own, moe_other = moe_part[:own_rows], moe_part[own_rows:].astype(bf16)
    pair_products = dot_cols(returned, cot).reshape(experts, own_slots, seq_len)
    prob_part = jnp.sum(pair_products * pick_pairs.astype(f32), axis=1).T
    other_part = swap(prob_part)
    prob_grad = prob_part + jnp.concatenate([other_part[own_rows:], other_part[:own_rows]], axis=0)
    logit_grad = router_probs * (
        prob_grad - jnp.sum(router_probs * prob_grad, axis=1, keepdims=True)
    )
    logit_high, logit_low = halves(logit_grad)
    router_grad = router_grad_of(normed_moe, logit_high, logit_low)
    (
        grads_back,
        others,
        moe_own,
        moe_other,
        logit_high,
        logit_low,
        router_grad,
        mixed_line,
        normed_planes,
        pick_back,
    ) = lax.optimization_barrier(
        (
            grads_back,
            others,
            moe_own,
            moe_other,
            logit_high,
            logit_low,
            router_grad,
            mixed_line,
            normed_planes,
            turned(pick),
        )
    )
    moe_own = moe_own + swap(moe_other).astype(f32)
    output = (hidden_own + moe_own).astype(bf16)
    others = [swap(grad) for grad in others]
    grad_w_gate, grad_w_up, grad_w_down = expert_weight_grads(
        arrived, slot_grad, inner_own, gate_own, up_own, others, f32
    )
    moe_in_own, moe_in_other = token_sums(pick_back, grads_back)
    hidden_grad, hidden_low_own, gain_moe_grad = hidden_grad_of(
        moe_in_own,
        swap(moe_in_other),
        logit_high[:own_rows],
        logit_low[:own_rows],
        w_router.T,
        gain_moe[None],
        hidden_own,
        scale_moe,
        cotangent,
    )
    hidden_low_other = swap(hidden_low_own)
    low_line = lax.all_gather(hidden_low_own, "x", axis=0, tiled=False)

    value_grad, query_part, key_part, gain_query_grad, gain_key_grad, inner = attention_backward(
        hidden_low_own,
        hidden_low_other,
        w_out,
        values,
        q_rot,
        k_rot,
        probs,
        queries,
        key_proj,
        query_gain,
        key_gain,
        scales,
        cosine,
        sine,
        local_heads,
    )
    inner_other, gain_moe_other = lax.optimization_barrier((swap(inner), swap(gain_moe_grad)))
    to_planes = projection_grads(
        query_part,
        key_part,
        queries,
        key_proj,
        value_grad,
        scales,
        (inner, inner_other),
        planes,
    )

    grads_planes = all_to_all(to_planes, "z").reshape(planes * seq_len, 3 * quarter)
    low_line, _ = lax.optimization_barrier((low_line, to_planes))
    parcel = out_parcel(
        numbers,
        low_line,
        [swap(low_line[k]) for k in range(line)],
        mixed_line,
        router_grad.reshape(chips, out_rows, experts),
        (gain_moe_grad, gain_moe_other),
        gain_query_grad,
        gain_key_grad,
        counts,
    )
    normed_grad, normed_grad_other = normed_grad_of(to_planes, (w_query, w_key, w_value))
    normed_grad = normed_grad + swap(normed_grad_other)
    in_own = residual_in.astype(f32)
    in_scale = scale_attn
    weighted_attn = normed_grad * gain_attn
    grad_input = (
        hidden_grad
        + in_scale * weighted_attn
        - in_own * in_scale**3 * jnp.mean(in_own * weighted_attn, axis=1, keepdims=True)
    )

    grads_planes, parcel = lax.optimization_barrier((grads_planes, parcel))
    parcel = weight_parcel(normed_planes, grads_planes, parcel)
    parcel, *done = lax.optimization_barrier(
        (
            all_to_all(parcel, rows_of_chips),
            output,
            grad_input,
            grad_w_gate,
            grad_w_up,
            grad_w_down,
        )
    )
    output, grad_input, grad_w_gate, grad_w_up, grad_w_down = done
    per_chip = head_dim // chips
    own_gain = lax.dynamic_slice_in_dim(gain_attn, chip * out_rows, out_rows)[None]
    (
        grad_w_query,
        grad_w_key,
        grad_w_value,
        grad_w_out,
        grad_w_router,
        grad_gain_query,
        grad_gain_key,
        grad_gain_moe,
        count,
        attn_own,
        attn_other,
    ) = parcel_sums(
        numbers,
        parcel,
        (w_query, w_key, w_value),
        own_gain,
        planes,
        out_rows,
        local_width,
        local_heads,
        per_chip,
        experts,
    )
    return (
        output,
        grad_input,
        (attn_own + swap(attn_other))[0],
        grad_w_query,
        grad_w_key,
        grad_w_value,
        grad_gain_query.T,
        grad_gain_key.T,
        grad_w_out.T,
        grad_gain_moe[0],
        grad_w_router,
        grad_w_gate[None],
        grad_w_up[None],
        grad_w_down[None],
        count[0],
    )


def solution(mesh):
    side = round(mesh.shape["ep"] ** (1 / 3))
    cube = Mesh(mesh.devices.reshape(side, side, side, 2), rows_of_chips + ("tp",))
    ep = rows_of_chips
    both = rows_of_chips + ("tp",)
    in_specs = (
        P(both, None),
        P(ep, None),
        P(ep, None),
        P(),
        P(None, "tp"),
        P(None, "tp"),
        P(None, "tp"),
        P("tp", None),
        P("tp", None),
        P("tp", None),
        P(),
        P(),
        P(ep, None, "tp"),
        P(ep, None, "tp"),
        P(ep, "tp", None),
        P(both, None),
    )
    out_specs = (
        P(both, None),
        P(both, None),
        P(both),
        P(ep, "tp"),
        P(ep, "tp"),
        P(ep, "tp"),
        P("tp", ep),
        P("tp", ep),
        P("tp", ep),
        P(both),
        P(both, None),
        P(ep, None, "tp"),
        P(ep, None, "tp"),
        P(ep, "tp", None),
        P(ep),
    )
    return jax.shard_map(local, mesh=cube, in_specs=in_specs, out_specs=out_specs, check_vma=False)
```

```python
import jax
import jax.numpy as jnp
from jax import lax
from jax.experimental import pallas as pl
from jax.experimental.pallas import tpu as pltpu
from jax.sharding import Mesh, PartitionSpec as P

norm_eps = 1e-05
rope_base = 10000.0
mask_fill = -1e30
bf16 = jnp.bfloat16
f32 = jnp.float32
rows_of_chips = ("z", "x", "y")


def swap(value):
    return lax.ppermute(value, "tp", [(0, 1), (1, 0)])


def dot(left, right):
    return lax.dot_general(left, right, (((1,), (0,)), ((), ())), preferred_element_type=f32)


def dot_rows(left, right):
    return lax.dot_general(left, right, (((0,), (0,)), ((), ())), preferred_element_type=f32)


def dot_cols(left, right):
    return lax.dot_general(left, right, (((1,), (1,)), ((), ())), preferred_element_type=f32)


def all_to_all(value, axes):
    return lax.all_to_all(value, axes, split_axis=0, concat_axis=0, tiled=True)


def rms_scale(values):
    return lax.rsqrt(jnp.mean(values * values, axis=-1, keepdims=True) + norm_eps)


def halves(value):
    high = value.astype(bf16)
    return high, (value - high.astype(f32)).astype(bf16)


def rope_angles(positions, head_dim):
    half_dim = head_dim // 2
    exponent = jnp.arange(half_dim, dtype=f32) * (2.0 / head_dim)
    inverse = jnp.power(f32(rope_base), -exponent)
    angles = positions.astype(f32)[:, None] * inverse[None, :]
    return jnp.cos(angles), jnp.sin(angles)


lanes = 128
cheap = 64


def in_hbm(*arrays):
    return [pltpu.with_memory_space_constraint(array, pltpu.HBM) for array in arrays]


def params(megabytes):
    return pltpu.CompilerParams(vmem_limit_bytes=megabytes * 1024 * 1024)


def turn(value, cosine, sine):
    return value * cosine + pltpu.roll(value, value.shape[1] // 2, 1) * sine


def other_order(ref):
    half = ref.shape[0] // 2
    return jnp.concatenate([ref[half:, :], ref[:half, :]], axis=0)


def attention_forward_body(
    scale,
    full_width,
    query_ref,
    key_ref,
    value_ref,
    query_gain_ref,
    key_gain_ref,
    squares_ref,
    other_squares_ref,
    cosine_ref,
    sine_ref,
    bias_ref,
    q_rot_ref,
    k_rot_ref,
    probs_ref,
    mixed_ref,
    parts_ref,
    scales_ref,
):
    cosine, sine, bias = cosine_ref[...], sine_ref[...], bias_ref[...]
    head = cosine.shape[1]
    squares = squares_ref[...] + other_order(other_squares_ref)
    scales = lax.rsqrt(squares * (1.0 / full_width) + norm_eps)
    scales_ref[...] = scales
    for h in range(probs_ref.shape[0]):
        here = slice(h * head, (h + 1) * head)
        query = query_ref[:, here] * scales[:, 0:1] * query_gain_ref[:, here]
        key = key_ref[:, here] * scales[:, 1:2] * key_gain_ref[:, here]
        q_rot = turn(query, cosine, sine).astype(bf16)
        k_rot = turn(key, cosine, sine).astype(bf16)
        q_rot_ref[:, here] = q_rot
        k_rot_ref[:, here] = k_rot
        scores = dot_cols(q_rot, k_rot) * scale + bias
        grown = jnp.exp(scores - jnp.max(scores, axis=1, keepdims=True))
        probs = grown / jnp.sum(grown, axis=1, keepdims=True)
        probs_ref[h] = probs
        mixed_ref[:, here] = dot(probs.astype(bf16), value_ref[:, here]).astype(bf16)
    part = parts_ref.shape[2]
    for k in range(parts_ref.shape[0]):
        parts_ref[k] = mixed_ref[:, k * part : (k + 1) * part]


def attention_forward(
    queries, keys, values, query_gain, key_gain, squares, other, cosine, sine, bias, heads, planes
):
    seq_len, width = queries.shape
    head = width // heads
    group = min(heads, 4)
    column = pl.BlockSpec((seq_len, group * head), lambda h: (0, h))
    gain = pl.BlockSpec((1, group * head), lambda h: (0, h))

    def whole(array):
        return pl.BlockSpec(array.shape, lambda h: (0, 0))

    return pl.pallas_call(
        lambda *refs: attention_forward_body(head**-0.5, 2 * width, *refs),
        grid=(heads // group,),
        in_specs=[column, column, column, gain, gain]
        + [whole(a) for a in (squares, other, cosine, sine, bias)],
        out_specs=[
            column,
            column,
            pl.BlockSpec((group, seq_len, seq_len), lambda h: (h, 0, 0)),
            column,
            pl.BlockSpec(
                (planes * group // heads, seq_len, width // planes), lambda h: (h, 0, 0)
            ),
            whole(squares),
        ],
        out_shape=[
            jax.ShapeDtypeStruct((seq_len, width), bf16),
            jax.ShapeDtypeStruct((seq_len, width), bf16),
            jax.ShapeDtypeStruct((heads, seq_len, seq_len), f32),
            jax.ShapeDtypeStruct((seq_len, width), bf16),
            jax.ShapeDtypeStruct((planes, seq_len, width // planes), bf16),
            jax.ShapeDtypeStruct((seq_len, 2), f32),
        ],
        compiler_params=params(16),
        cost_estimate=pl.CostEstimate(
            flops=4 * seq_len * seq_len * width // cheap,
            transcendentals=0,
            bytes_accessed=seq_len * width * 16 // cheap,
        ),
        name="attention_forward",
    )(queries, keys, values, query_gain, key_gain, squares, other, cosine, sine, bias)


def attention_backward_body(
    scale,
    hidden_own_ref,
    hidden_other_ref,
    w_out_ref,
    value_ref,
    q_rot_ref,
    k_rot_ref,
    probs_ref,
    query_ref,
    key_ref,
    query_gain_ref,
    key_gain_ref,
    scales_ref,
    cosine_ref,
    sine_ref,
    value_grad_ref,
    query_part_ref,
    key_part_ref,
    query_gain_grad_ref,
    key_gain_grad_ref,
    inner_ref,
):
    cosine, sine = cosine_ref[...], sine_ref[...]
    hidden = jnp.concatenate([hidden_own_ref[...], hidden_other_ref[...]], axis=0)
    heads, head = query_gain_grad_ref.shape[0], query_gain_grad_ref.shape[2]
    grad_mixed = dot_cols(hidden, w_out_ref[...]).astype(bf16)
    total = None
    for h in range(heads):
        here = slice(h * head, (h + 1) * head)
        grad = grad_mixed[:, here]
        probs = probs_ref[h]
        grad_probs = dot_cols(grad, value_ref[:, here])
        inner = jnp.sum(probs * grad_probs, axis=1, keepdims=True)
        grad_scores = (probs * (grad_probs - inner)).astype(bf16)
        value_grad_ref[:, here] = dot_rows(probs.astype(bf16), grad).astype(bf16)
        row_inners = []
        for k, (grad_rot, raw_ref, gain_ref, part_ref, gain_grad_ref) in enumerate(
            (
                (
                    dot(grad_scores, k_rot_ref[:, here]),
                    query_ref,
                    query_gain_ref,
                    query_part_ref,
                    query_gain_grad_ref,
                ),
                (
                    dot_rows(grad_scores, q_rot_ref[:, here]),
                    key_ref,
                    key_gain_ref,
                    key_part_ref,
                    key_gain_grad_ref,
                ),
            )
        ):
            grad_normed = turn(grad_rot * scale, cosine, -sine)
            raw = raw_ref[:, here]
            gain_grad_ref[h] = jnp.sum(
                raw * scales_ref[:, k : k + 1] * grad_normed, axis=0, keepdims=True
            )
            weighted = grad_normed * gain_ref[:, here]
            part_ref[:, here] = weighted
            row_inners.append(jnp.sum(raw * weighted, axis=1, keepdims=True))
        row_inner = jnp.concatenate(row_inners, axis=1)
        total = row_inner if total is None else total + row_inner
    first = pl.program_id(0) == 0

    @pl.when(first)
    def _():
        inner_ref[...] = total

    @pl.when(jnp.logical_not(first))
    def _():
        inner_ref[...] += total


def attention_backward(
    hidden_own,
    hidden_other,
    w_out,
    values,
    q_rot,
    k_rot,
    probs,
    queries,
    keys,
    query_gain,
    key_gain,
    scales,
    cosine,
    sine,
    heads,
):
    seq_len, width = queries.shape
    head = width // heads
    group = min(heads, 4)
    column = pl.BlockSpec((seq_len, group * head), lambda h: (0, h))
    gain = pl.BlockSpec((1, group * head), lambda h: (0, h))

    def whole(array):
        return pl.BlockSpec(array.shape, lambda h: (0, 0))

    full = jax.ShapeDtypeStruct((seq_len, width), f32)
    line = jax.ShapeDtypeStruct((heads, 1, head), f32)
    line_spec = pl.BlockSpec((group, 1, head), lambda h: (h, 0, 0))
    sums = jax.ShapeDtypeStruct((seq_len, 2), f32)
    return pl.pallas_call(
        lambda *refs: attention_backward_body(head**-0.5, *refs),
        grid=(heads // group,),
        in_specs=[
            whole(hidden_own),
            whole(hidden_other),
            pl.BlockSpec((group * head, w_out.shape[1]), lambda h: (h, 0)),
            column,
            column,
            column,
            pl.BlockSpec((group, seq_len, seq_len), lambda h: (h, 0, 0)),
            column,
            column,
            gain,
            gain,
        ]
        + [whole(a) for a in (scales, cosine, sine)],
        out_specs=[column, column, column, line_spec, line_spec, whole(sums)],
        out_shape=[
            jax.ShapeDtypeStruct((seq_len, width), bf16),
            full,
            full,
            line,
            line,
            sums,
        ],
        compiler_params=params(20),
        cost_estimate=pl.CostEstimate(
            flops=10 * seq_len * seq_len * width + 2 * seq_len * width * w_out.shape[1],
            transcendentals=0,
            bytes_accessed=seq_len * width * 28
            + heads * seq_len * seq_len * 4
            + 2 * w_out.size
            + 4 * hidden_own.size,
        ),
        name="attention_backward",
    )(
        *in_hbm(hidden_own),
        hidden_other,
        *in_hbm(w_out, values, q_rot, k_rot, probs, queries, keys),
        query_gain,
        key_gain,
        scales,
        cosine,
        sine,
    )


def projection_grads_body(
    width,
    query_part_ref,
    key_part_ref,
    query_ref,
    key_ref,
    value_grad_ref,
    scales_ref,
    inner_ref,
    other_inner_ref,
    stack_ref,
):
    blocks, _, columns = stack_ref.shape
    size = columns // 3
    inner = (inner_ref[...] + other_order(other_inner_ref)) * (1.0 / width)
    for k, (part_ref, raw_ref) in enumerate(
        ((query_part_ref, query_ref), (key_part_ref, key_ref))
    ):
        scale = scales_ref[:, k : k + 1]
        factor = scale * scale * scale * inner[:, k : k + 1]
        for block in range(blocks):
            here = slice(block * size, (block + 1) * size)
            grad = scale * part_ref[:, here] - raw_ref[:, here] * factor
            stack_ref[block, :, k * size : (k + 1) * size] = grad.astype(bf16)
    for block in range(blocks):
        stack_ref[block, :, 2 * size :] = value_grad_ref[:, block * size : (block + 1) * size]


def projection_grads(
    query_part, key_part, queries, keys, value_grad, scales, inners, planes
):
    seq_len, width = queries.shape
    size = width // planes
    steps = 2
    column = pl.BlockSpec((seq_len, width // steps), lambda k: (0, k))
    pair = pl.BlockSpec((seq_len, 2), lambda k: (0, 0))
    return pl.pallas_call(
        lambda *refs: projection_grads_body(2 * width, *refs),
        grid=(steps,),
        in_specs=[column] * 5 + [pair] * 3,
        out_specs=pl.BlockSpec((planes // steps, seq_len, 3 * size), lambda k: (k, 0, 0)),
        out_shape=jax.ShapeDtypeStruct((planes, seq_len, 3 * size), bf16),
        compiler_params=params(10),
        cost_estimate=pl.CostEstimate(
            flops=10 * seq_len * width, transcendentals=0, bytes_accessed=24 * seq_len * width
        ),
        name="projection_grads",
    )(query_part, key_part, queries, keys, value_grad, scales, *inners)


def expert_forward_body(
    rows_hbm,
    gate_own_hbm,
    gate_other_hbm,
    up_own_hbm,
    up_other_hbm,
    down_own_hbm,
    down_other_hbm,
    out_hbm,
    rows_ref,
    gate_ref,
    up_ref,
    down_ref,
    out_ref,
    in_sems,
    out_sems,
):
    count, width = rows_ref.shape
    pieces = 2
    size = count // pieces
    copies = {}
    order = [("rows", 0), ("gate", 0), ("up", 0), ("gate", 1), ("up", 1), ("down", 0), ("down", 1)]
    order += [("rows", k) for k in range(1, pieces)]
    sources = {
        "gate": ((gate_own_hbm, gate_other_hbm), gate_ref),
        "up": ((up_own_hbm, up_other_hbm), up_ref),
        "down": ((down_own_hbm, down_other_hbm), down_ref),
    }
    for number, (name, k) in enumerate(order):
        if name == "rows":
            here = pl.ds(k * size, size)
            copy = pltpu.make_async_copy(rows_hbm.at[here], rows_ref.at[here], in_sems.at[number])
        else:
            source, target = sources[name]
            copy = pltpu.make_async_copy(source[k], target.at[k], in_sems.at[number])
        copy.start()
        copies[name, k] = copy
    outs = []
    for piece in range(pieces):
        here = pl.ds(piece * size, size)
        copies["rows", piece].wait()
        inners = []
        for k in range(2):
            if piece == 0:
                copies["gate", k].wait()
            gate = dot(rows_ref[here, :], gate_ref[k])
            if piece == 0:
                copies["up", k].wait()
            up = dot(rows_ref[here, :], up_ref[k])
            inners.append((gate * jax.nn.sigmoid(gate) * up).astype(bf16))
        if piece == 0:
            copies["down", 0].wait()
            copies["down", 1].wait()
        step = min(512, width)
        for start in range(0, width, step):
            columns = pl.ds(start, step)
            total = dot(inners[0], down_ref[0, :, columns]) + dot(
                inners[1], down_ref[1, :, columns]
            )
            out_ref[here, columns] = total.astype(bf16)
        copy = pltpu.make_async_copy(out_ref.at[here], out_hbm.at[here], out_sems.at[piece])
        copy.start()
        outs.append(copy)
    for copy in outs:
        copy.wait()


def expert_specs(count, width, size):
    whole = pl.BlockSpec((count, width), lambda k: (0, 0), pipeline_mode=pl.Buffered(1))
    into = pl.BlockSpec((width, size), lambda k: (0, k))
    back = pl.BlockSpec((size, width), lambda k: (k, 0))
    return whole, into, back


def expert_forward(rows, gates, ups, downs):
    count, width = rows.shape
    units = gates[0].shape[1]
    return pl.pallas_call(
        expert_forward_body,
        in_specs=[pl.BlockSpec(memory_space=pl.ANY)] * 7,
        out_specs=pl.BlockSpec(memory_space=pl.ANY),
        out_shape=pltpu.HBM((count, width), bf16),
        scratch_shapes=[
            pltpu.VMEM((count, width), bf16),
            pltpu.VMEM((2, width, units), bf16),
            pltpu.VMEM((2, width, units), bf16),
            pltpu.VMEM((2, units, width), bf16),
            pltpu.VMEM((count, width), bf16),
            pltpu.SemaphoreType.DMA((8,)),
            pltpu.SemaphoreType.DMA((2,)),
        ],
        compiler_params=params(44),
        cost_estimate=pl.CostEstimate(
            flops=12 * count * width * units // cheap,
            transcendentals=0,
            bytes_accessed=(count * width * 4 + 12 * width * units) // cheap,
        ),
        name="expert_forward",
    )(*in_hbm(rows, *gates, *ups, *downs))


def expert_backward_body(
    rows_ref,
    slot_grad_ref,
    gate_own_ref,
    gate_other_ref,
    up_own_ref,
    up_other_ref,
    down_own_ref,
    down_other_ref,
    inner_own_ref,
    inner_other_ref,
    gate_grad_own_ref,
    gate_grad_other_ref,
    up_grad_own_ref,
    up_grad_other_ref,
    out_ref,
    total_ref,
):
    step = pl.program_id(0)
    last = pl.num_programs(0) - 1
    for gate_ref, up_ref, down_ref, inner_ref, gate_grad_ref, up_grad_ref in (
        (gate_own_ref, up_own_ref, down_own_ref, inner_own_ref, gate_grad_own_ref, up_grad_own_ref),
        (
            gate_other_ref,
            up_other_ref,
            down_other_ref,
            inner_other_ref,
            gate_grad_other_ref,
            up_grad_other_ref,
        ),
    ):
        gate = dot(rows_ref[...], gate_ref[...])
        up = dot(rows_ref[...], up_ref[...])
        inner_grad = dot_cols(slot_grad_ref[...], down_ref[...])
        sigmoid_gate = jax.nn.sigmoid(gate)
        silu_gate = gate * sigmoid_gate
        inner_ref[...] = (silu_gate * up).astype(bf16)
        up_grad_ref[...] = (inner_grad * silu_gate).astype(bf16)
        gate_grad_ref[...] = (
            inner_grad * up * sigmoid_gate * (1.0 + gate * (1.0 - sigmoid_gate))
        ).astype(bf16)
    width = out_ref.shape[1]
    size = min(512, width)
    for start in range(0, width, size):
        here = pl.ds(start, size)
        part = None
        for grad_ref, w_ref in (
            (gate_grad_own_ref, gate_own_ref),
            (gate_grad_other_ref, gate_other_ref),
            (up_grad_own_ref, up_own_ref),
            (up_grad_other_ref, up_other_ref),
        ):
            term = dot_cols(grad_ref[...], w_ref[here, :])
            part = term if part is None else part + term

        @pl.when(step == 0)
        def _():
            total_ref[:, here] = part

        @pl.when((step > 0) & (step < last))
        def _():
            total_ref[:, here] += part

        @pl.when(step == last)
        def _():
            out_ref[:, here] = (total_ref[:, here] + part).astype(bf16)


def expert_backward(rows, slot_grad, gates, ups, downs):
    count, width = rows.shape
    units = gates[0].shape[1]
    steps = 2
    size = units // steps
    whole, into, back = expert_specs(count, width, size)
    acts = pl.BlockSpec((count, size), lambda k: (0, k))
    return pl.pallas_call(
        expert_backward_body,
        grid=(steps,),
        in_specs=[whole] * 2 + [into] * 4 + [back] * 2,
        out_specs=[acts] * 6 + [pl.BlockSpec((count, width), lambda k: (0, 0))],
        out_shape=[jax.ShapeDtypeStruct((count, units), bf16)] * 6
        + [jax.ShapeDtypeStruct((count, width), bf16)],
        scratch_shapes=[pltpu.VMEM((count, width), f32)],
        compiler_params=params(56),
        cost_estimate=pl.CostEstimate(
            flops=20 * count * width * units // cheap,
            transcendentals=0,
            bytes_accessed=count * width * 6 // cheap,
        ),
        name="expert_backward",
    )(rows, slot_grad, *gates, *ups, *downs)


def put_blocks(out_ref, row, product):
    chips = out_ref.shape[0]
    rows = product.shape[0] // chips
    for k in range(product.shape[1] // lanes):
        piece = product[:, k * lanes : (k + 1) * lanes].reshape(chips, rows, lanes)
        out_ref[:, row : row + rows, :] = piece
        row += rows
    return row


def joined(own_ref, other_ref):
    rows = jnp.concatenate([own_ref[...], other_ref[...]], axis=1)
    return rows.reshape(rows.shape[0] * rows.shape[1], rows.shape[2])


def weight_parcel_body(
    normed_ref, normed_other_ref, grads_ref, parcel_hbm, out_hbm, block_ref, sems
):
    step = pl.program_id(0)
    slot = step % 2
    group, rows = block_ref.shape[1], block_ref.shape[2]

    def copy(at):
        here = out_hbm.at[pl.ds(step * group, group), pl.ds(0, rows)]
        return pltpu.make_async_copy(block_ref.at[at], here, sems.at[at])

    @pl.when(step >= 2)
    def _():
        copy(slot).wait()

    left = joined(normed_ref, normed_other_ref)
    put_blocks(block_ref.at[slot], 0, dot_rows(left, grads_ref[...]).astype(bf16))
    copy(slot).start()

    @pl.when(step == pl.num_programs(0) - 1)
    def _():
        copy(1 - slot).wait()
        copy(slot).wait()


def weight_parcel(normed, grads, parcel):
    planes, half, width = normed[0].shape
    tokens, columns = grads.shape
    chips, height, _ = parcel.shape
    rows = width // chips * columns // lanes
    steps = planes
    left = pl.BlockSpec((planes, half, width // steps), lambda k: (0, 0, k))
    return pl.pallas_call(
        weight_parcel_body,
        grid=(steps,),
        in_specs=[
            left,
            left,
            pl.BlockSpec((tokens, columns), lambda k: (0, 0)),
            pl.BlockSpec(memory_space=pl.ANY),
        ],
        out_specs=pl.BlockSpec(memory_space=pl.ANY),
        out_shape=pltpu.HBM((chips, height, lanes), bf16),
        input_output_aliases={3: 0},
        scratch_shapes=[
            pltpu.VMEM((2, chips // steps, rows, lanes), bf16),
            pltpu.SemaphoreType.DMA((2,)),
        ],
        compiler_params=params(18),
        cost_estimate=pl.CostEstimate(
            flops=2 * tokens * width * columns,
            transcendentals=0,
            bytes_accessed=2 * (tokens * width + grads.size + chips * height * lanes),
        ),
        name="weight_parcel",
    )(*in_hbm(*normed, grads, parcel))


def out_parcel_body(
    start,
    per_chip,
    line,
    place_ref,
    low_ref,
    *refs,
):
    low_other_refs, mixed_refs, refs = refs[:line], refs[line : 2 * line], refs[2 * line :]
    router_ref, moe_ref, moe_other_ref, query_gain_ref, key_gain_ref, counts_ref = refs[:6]
    out_hbm, block_ref, sems = refs[6:]
    step = pl.program_id(0)
    slot = step % 2
    group = block_ref.shape[1]

    def copy(at):
        here = out_hbm.at[pl.ds(step * group, group), pl.ds(start, block_ref.shape[2])]
        return pltpu.make_async_copy(block_ref.at[at], here, sems.at[at])

    @pl.when(step >= 2)
    def _():
        copy(slot).wait()

    total = None
    for shift, mixed_ref in enumerate(mixed_refs):
        source = (place_ref[3] + line - shift) % line
        other = low_other_refs[0][...]
        for k in range(1, line):
            other = jnp.where(source == k, low_other_refs[k][...], other)
        left = jnp.concatenate([low_ref[source], other], axis=0)
        part = dot_rows(left, mixed_ref[...])
        total = part if total is None else total + part
    row = put_blocks(block_ref.at[slot], 0, total.astype(bf16))

    chips, rows, spare = router_ref.shape[0], router_ref.shape[1] // 2, lanes // 2
    core = place_ref[1]
    router = router_ref[:, pl.ds(core * rows, rows), :]
    if router.shape[2] < spare:
        fill = jnp.zeros((chips, rows, spare - router.shape[2]), f32)
        router = jnp.concatenate([router, fill], axis=2)
    moe = moe_ref[...] + moe_other_ref[...]
    span = 2 * rows
    moe = jnp.concatenate([moe[:, k * span : (k + 1) * span] for k in range(chips)], axis=0)
    moe = jnp.where(core == 0, moe[:, :rows], moe[:, rows:])
    heads, head = query_gain_ref.shape[0], query_gain_ref.shape[2]
    chip = lax.broadcasted_iota(jnp.int32, (chips, heads, head), 0) + step * chips
    lane = lax.broadcasted_iota(jnp.int32, (chips, heads, head), 2)
    mine = lane // per_chip == chip
    feature = lax.broadcasted_iota(jnp.int32, (head, spare), 0) % per_chip
    column = lax.broadcasted_iota(jnp.int32, (head, spare), 1)
    first_row = lax.broadcasted_iota(jnp.int32, (chips, heads, spare), 1) == 0
    used = 2 * per_chip + rows + 1
    blocks = []
    for part in range(2):
        block = jnp.zeros((chips * heads, spare), f32)
        for k, gain_ref in enumerate((query_gain_ref, key_gain_ref)):
            values = halves(gain_ref[:, 0, :])[part].astype(f32)
            values = jnp.where(mine, values[None], 0.0).reshape(chips * heads, head).astype(bf16)
            target = jnp.where(column == feature + k * per_chip, 1.0, 0.0).astype(bf16)
            block = block + dot(values, target)
        moe_part = halves(moe)[part].astype(f32)
        count = counts_ref[...] if part == 0 else jnp.zeros((chips, 1), f32)
        vector = jnp.concatenate(
            [jnp.zeros((chips, 2 * per_chip), f32), moe_part, count]
            + [jnp.zeros((chips, spare - used), f32)] * (used < spare),
            axis=1,
        )
        block = block.reshape(chips, heads, spare)
        blocks.append(block + jnp.where(first_row, vector[:, None, :], 0.0))
        if heads < rows // 2:
            blocks.append(jnp.zeros((chips, rows // 2 - heads, spare), f32))
    beside = jnp.concatenate(blocks, axis=1)
    small = jnp.concatenate([router, beside], axis=2).astype(bf16)
    block_ref[slot, :, row:, :] = small
    copy(slot).start()

    @pl.when(step == pl.num_programs(0) - 1)
    def _():
        copy(1 - slot).wait()
        copy(slot).wait()


def out_parcel(place, low, low_other, mixed, router, moe, query_gain, key_gain, counts):
    line, half, width = low.shape
    tokens, part = mixed[0].shape
    chips, router_rows, experts = router.shape
    heads, _, head = query_gain.shape
    room = width // chips * part // lanes
    small_rows = router_rows // 2
    height = 4 * room + small_rows
    steps = line
    group = chips // steps
    gain = pl.BlockSpec((heads, 1, head), lambda k, z: (0, 0, 0))
    vector = pl.BlockSpec((1, width // steps), lambda k, z: (0, k))
    return pl.pallas_call(
        lambda *refs: out_parcel_body(3 * room, head // chips, line, *refs),
        grid_spec=pltpu.PrefetchScalarGridSpec(
            num_scalar_prefetch=1,
            grid=(steps,),
            in_specs=[pl.BlockSpec((line, half, width // steps), lambda k, z: (0, 0, k))]
            + [pl.BlockSpec((half, width // steps), lambda k, z: (0, k))] * line
            + [pl.BlockSpec((tokens, part), lambda k, z: (0, 0))] * line
            + [pl.BlockSpec((group, router_rows, experts), lambda k, z: (k, 0, 0))]
            + [vector, vector, gain, gain, pl.BlockSpec((group, 1), lambda k, z: (k, 0))],
            out_specs=pl.BlockSpec(memory_space=pl.ANY),
            scratch_shapes=[
                pltpu.VMEM((2, group, room + small_rows, lanes), bf16),
                pltpu.SemaphoreType.DMA((2,)),
            ],
        ),
        out_shape=pltpu.HBM((chips, height, lanes), bf16),
        compiler_params=params(18),
        cost_estimate=pl.CostEstimate(
            flops=2 * tokens * width * part // cheap,
            transcendentals=0,
            bytes_accessed=2 * (tokens * width + chips * room * lanes) // cheap,
        ),
        name="out_parcel",
    )(
        place,
        *in_hbm(low),
        *low_other,
        *mixed,
        *in_hbm(router),
        *moe,
        query_gain,
        key_gain,
        counts,
    )


def parcel_sums_body(
    per_chip,
    place_ref,
    parcel_ref,
    w_query_ref,
    w_key_ref,
    w_value_ref,
    own_gain_ref,
    query_ref,
    key_ref,
    value_ref,
    out_ref,
    router_ref,
    query_gain_ref,
    key_gain_ref,
    moe_ref,
    count_ref,
    attn_ref,
    attn_other_ref,
    extra_ref,
    gain_ref,
):
    rows, columns = query_ref.shape
    step = pl.program_id(0)
    blocks = columns // lanes
    row = 3 * blocks * rows
    total = jnp.sum(parcel_ref[:, :row, :].astype(f32), axis=0)
    gain = jnp.zeros((rows, lanes), f32)
    for number, (ref, w_ref) in enumerate(
        ((query_ref, w_query_ref), (key_ref, w_key_ref), (value_ref, w_value_ref))
    ):
        for k in range(blocks):
            here = slice(k * lanes, (k + 1) * lanes)
            first_row = (number * blocks + k) * rows
            piece = total[first_row : first_row + rows, :]
            ref[:, here] = piece
            gain = gain + piece * w_ref[:, here].astype(f32)

    @pl.when(step == 0)
    def _():
        out_ref[...] = jnp.zeros_like(out_ref)
        extra_ref[...] = jnp.zeros_like(extra_ref)
        gain_ref[...] = jnp.zeros_like(gain_ref)

    gain_ref[...] += gain
    extra_ref[...] += jnp.sum(parcel_ref[:, row + blocks * rows :, :].astype(f32), axis=0)
    line = pl.num_programs(0)
    group = parcel_ref.shape[0] // line
    for x in range(line):
        part = parcel_ref[x * group : (x + 1) * group, row : row + blocks * rows, :]
        part = jnp.sum(part.astype(f32), axis=0)
        for k in range(blocks):
            here = slice(x * columns + k * lanes, x * columns + (k + 1) * lanes)
            out_ref[:, here] += part[k * rows : (k + 1) * rows, :]

    @pl.when(step == pl.num_programs(0) - 1)
    def _():
        half = rows // 2
        heads = query_gain_ref.shape[1]
        router_ref[...] = extra_ref[:, : router_ref.shape[1]]
        sums = extra_ref[0:heads, :] + extra_ref[half // 2 : half // 2 + heads, :]
        first_lane = lanes // 2 + 2 * per_chip
        moe_ref[...] = sums[0:1, first_lane : first_lane + half]
        count_ref[...] = sums[0:1, first_lane + half : first_lane + half + 1].astype(jnp.int32)
        sums = sums.T
        query_gain_ref[...] = sums[lanes // 2 : lanes // 2 + per_chip, :]
        key_gain_ref[...] = sums[lanes // 2 + per_chip : first_lane, :]
        attn = jnp.sum(gain_ref[...].T, axis=0, keepdims=True) / own_gain_ref[...]
        first = place_ref[1] == 0
        attn_ref[...] = jnp.where(first, attn[:, :half], attn[:, half:])
        attn_other_ref[...] = jnp.where(first, attn[:, half:], attn[:, :half])


def parcel_sums(place, parcel, weights, own_gain, planes, rows, width, heads, per_chip, experts):
    chips, height, _ = parcel.shape
    part = width // planes
    half = rows // 2
    wide = pl.BlockSpec((rows, part), lambda k, c: (0, k))

    def whole(shape):
        return pl.BlockSpec(shape, lambda k, c: (0, 0))

    small = [(half, experts), (per_chip, heads), (per_chip, heads), (1, half), (1, 1)]
    small += [(1, half), (1, half)]
    kinds = [f32] * 4 + [jnp.int32] + [f32] * 2
    return pl.pallas_call(
        lambda *refs: parcel_sums_body(per_chip, *refs),
        grid_spec=pltpu.PrefetchScalarGridSpec(
            num_scalar_prefetch=1,
            grid=(planes,),
            in_specs=[pl.BlockSpec((chips // planes, height, lanes), lambda k, c: (k, 0, 0))]
            + [pl.BlockSpec((rows, part), lambda k, c: (c[2], k))] * 3
            + [whole((1, rows))],
            out_specs=[wide] * 3 + [whole((rows, width))] + [whole(shape) for shape in small],
            scratch_shapes=[pltpu.VMEM((half, lanes), f32), pltpu.VMEM((rows, lanes), f32)],
        ),
        out_shape=[jax.ShapeDtypeStruct((rows, width), f32)] * 4
        + [jax.ShapeDtypeStruct(shape, kind) for shape, kind in zip(small, kinds)],
        compiler_params=params(14),
        cost_estimate=pl.CostEstimate(
            flops=parcel.size, transcendentals=0, bytes_accessed=2 * parcel.size
        ),
        name="parcel_sums",
    )(place, parcel, *in_hbm(*weights), own_gain)


def expert_weight_grads_body(rows_ref, slot_grad_ref, inner_ref, gate_ref, up_ref, *refs):
    grads = (
        dot_rows(rows_ref[...], gate_ref[...]),
        dot_rows(rows_ref[...], up_ref[...]),
        dot_rows(inner_ref[...], slot_grad_ref[...]),
    )
    others, outs = refs[:-3], refs[-3:]
    for k, (grad, out_ref) in enumerate(zip(grads, outs)):
        if others:
            grad = grad + others[k][...].astype(f32)
        out_ref[...] = grad.astype(out_ref.dtype)


def expert_weight_grads(rows, slot_grad, inner, gate_grad, up_grad, others, kind):
    count, width = rows.shape
    units = inner.shape[1]
    steps = 4
    size = width // steps
    wide = pl.BlockSpec((count, size), lambda k: (0, k))
    narrow = pl.BlockSpec((count, units), lambda k: (0, 0))
    into = pl.BlockSpec((size, units), lambda k: (k, 0))
    back = pl.BlockSpec((units, size), lambda k: (0, k))
    return pl.pallas_call(
        expert_weight_grads_body,
        grid=(steps,),
        in_specs=[wide, wide, narrow, narrow, narrow] + [into, into, back][: len(others)],
        out_specs=[into, into, back],
        out_shape=[
            jax.ShapeDtypeStruct((width, units), kind),
            jax.ShapeDtypeStruct((width, units), kind),
            jax.ShapeDtypeStruct((units, width), kind),
        ],
        compiler_params=params(30),
        cost_estimate=pl.CostEstimate(
            flops=6 * count * width * units // cheap,
            transcendentals=0,
            bytes_accessed=4 * count * width // cheap,
        ),
        name="expert_weight_grads",
    )(*in_hbm(rows, slot_grad, inner, gate_grad, up_grad, *others))


def normed_grad_body(stack_ref, query_ref, key_ref, value_ref, own_ref, other_ref):
    size = query_ref.shape[1]
    total = None
    for k, w_ref in enumerate((query_ref, key_ref, value_ref)):
        part = dot_cols(stack_ref[:, k * size : (k + 1) * size], w_ref[...])
        total = part if total is None else total + part
    half = own_ref.shape[0]
    first = pl.program_id(0) == 0

    @pl.when(first)
    def _():
        own_ref[...] = total[:half]
        other_ref[...] = total[half:]

    @pl.when(jnp.logical_not(first))
    def _():
        own_ref[...] += total[:half]
        other_ref[...] += total[half:]


def normed_grad_of(stack, weights):
    planes, seq_len, columns = stack.shape
    size = columns // 3
    full = weights[0].shape[0]
    half = pl.BlockSpec((seq_len // 2, full), lambda k: (0, 0))
    return pl.pallas_call(
        normed_grad_body,
        grid=(planes,),
        in_specs=[pl.BlockSpec((None, seq_len, columns), lambda k: (k, 0, 0))]
        + [pl.BlockSpec((full, size), lambda k: (0, k))] * 3,
        out_specs=[half] * 2,
        out_shape=[jax.ShapeDtypeStruct((seq_len // 2, full), f32)] * 2,
        compiler_params=params(20),
        cost_estimate=pl.CostEstimate(
            flops=2 * stack.size * full // cheap,
            transcendentals=0,
            bytes_accessed=2 * planes * columns * full // cheap,
        ),
        name="normed_grad",
    )(stack, *in_hbm(*weights))


def pick_body(slots, place_ref, routes_ref, pick_ref, counts_ref):
    core = place_ref[1]
    experts = counts_ref.shape[0]
    seq_len = routes_ref.shape[1]
    half = seq_len // 2
    routes = routes_ref[...]
    routes = jnp.where(
        core == 0, routes, jnp.concatenate([routes[:, half:], routes[:, :half]], axis=1)
    )
    numbers = lax.broadcasted_iota(jnp.int32, (experts, seq_len), 0)
    hits = numbers == routes[0:1, :]
    for k in range(1, routes.shape[0]):
        hits = hits | (numbers == routes[k : k + 1, :])
    hits_float = jnp.where(hits, 1.0, 0.0)
    counts_ref[...] = jnp.sum(hits_float, axis=1, keepdims=True)
    square = (seq_len, seq_len)
    shift = core * half
    earlier = lax.broadcasted_iota(jnp.int32, square, 0) + shift
    place = lax.broadcasted_iota(jnp.int32, square, 1) + shift
    earlier = jnp.where(earlier >= seq_len, earlier - seq_len, earlier)
    place = jnp.where(place >= seq_len, place - seq_len, place)
    before = jnp.where(earlier < place, 1.0, 0.0).astype(bf16)
    rank = jnp.where(hits, dot(hits_float.astype(bf16), before), -1.0)
    slot = lax.broadcasted_iota(jnp.int32, (experts, slots, seq_len), 1) + core * slots
    pick = jnp.where(rank[:, None, :] == slot.astype(f32), 1.0, 0.0)
    pick_ref[...] = pick.reshape(experts * slots, seq_len).astype(bf16)


def pick_of(place, routes, experts, slots):
    seq_len = routes.shape[1]

    def whole(*shape):
        return pl.BlockSpec(shape, lambda k, c: (0, 0))

    return pl.pallas_call(
        lambda *refs: pick_body(slots, *refs),
        grid_spec=pltpu.PrefetchScalarGridSpec(
            num_scalar_prefetch=1,
            grid=(1,),
            in_specs=[whole(*routes.shape)],
            out_specs=[whole(experts * slots, seq_len), whole(experts, 1)],
        ),
        out_shape=[
            jax.ShapeDtypeStruct((experts * slots, seq_len), bf16),
            jax.ShapeDtypeStruct((experts, 1), f32),
        ],
        compiler_params=params(12),
        cost_estimate=pl.CostEstimate(
            flops=1 << 22, transcendentals=0, bytes_accessed=2 * experts * slots * seq_len
        ),
        name="pick",
    )(place, routes)


def slot_rows_body(pick_ref, own_ref, other_ref, out_ref):
    rows = jnp.concatenate([own_ref[...], other_ref[...]], axis=0)
    out_ref[...] = dot(pick_ref[...], rows).astype(bf16)


def slot_rows(pick, own, other, columns):
    count, seq_len = pick.shape
    steps = 3
    size = columns // steps
    rows = pl.BlockSpec((seq_len // 2, size), lambda k: (0, k))
    return pl.pallas_call(
        slot_rows_body,
        grid=(steps,),
        in_specs=[pl.BlockSpec((count, seq_len), lambda k: (0, 0)), rows, rows],
        out_specs=pl.BlockSpec((count, size), lambda k: (0, k)),
        out_shape=pltpu.HBM((count, columns), bf16),
        compiler_params=params(12),
        cost_estimate=pl.CostEstimate(
            flops=2 * count * seq_len * columns,
            transcendentals=0,
            bytes_accessed=2 * (seq_len + count) * columns,
        ),
        name="slot_rows",
    )(pick, *in_hbm(own), other)


def turned_body(value_ref, out_ref):
    out_ref[...] = value_ref[...].T


def turned(value):
    return pl.pallas_call(
        turned_body,
        out_shape=pltpu.HBM(value.shape[::-1], value.dtype),
        compiler_params=params(8),
        cost_estimate=pl.CostEstimate(
            flops=1 << 10, transcendentals=0, bytes_accessed=value.size // cheap
        ),
        name="turned",
    )(value)


def token_sums_body(pick_ref, rows_ref, own_ref, other_ref):
    total = dot(pick_ref[...], rows_ref[...])
    half = own_ref.shape[0]
    own_ref[...] = total[:half]
    other_ref[...] = total[half:].astype(bf16)


def token_sums(pick_back, rows):
    seq_len, count = pick_back.shape
    width = rows.shape[1]
    steps = 2
    half = pl.BlockSpec((seq_len // 2, width // steps), lambda k: (0, k))
    return pl.pallas_call(
        token_sums_body,
        grid=(steps,),
        in_specs=[
            pl.BlockSpec((seq_len, count), lambda k: (0, 0)),
            pl.BlockSpec((count, width // steps), lambda k: (0, k)),
        ],
        out_specs=[half] * 2,
        out_shape=[jax.ShapeDtypeStruct((seq_len // 2, width), kind) for kind in (f32, bf16)],
        compiler_params=params(16),
        cost_estimate=pl.CostEstimate(
            flops=2 * count * seq_len * width,
            transcendentals=0,
            bytes_accessed=2 * count * (seq_len + width) + 4 * seq_len * width,
        ),
        name="token_sums",
    )(*in_hbm(pick_back, rows))


def hidden_grad_body(
    own_ref,
    other_ref,
    logit_high_ref,
    logit_low_ref,
    w_router_ref,
    gain_ref,
    hidden_ref,
    scale_ref,
    cot_ref,
    grad_ref,
    low_ref,
    gain_grad_ref,
):
    w_router = w_router_ref[...]
    moe_in = own_ref[...] + other_ref[...].astype(f32)
    moe_in = moe_in + dot(logit_high_ref[...], w_router)
    moe_in = moe_in + dot(logit_low_ref[...], w_router)
    hidden, scale = hidden_ref[...], scale_ref[...]
    gain_grad_ref[...] = jnp.sum(hidden * scale * moe_in, axis=0, keepdims=True)
    weighted = moe_in * gain_ref[...]
    inner = jnp.mean(hidden * weighted, axis=1, keepdims=True)
    grad = cot_ref[...].astype(f32) + scale * weighted
    grad = grad - hidden * (scale * scale * scale * inner)
    grad_ref[...] = grad
    low_ref[...] = grad.astype(bf16)


def hidden_grad_of(own, other, logit_high, logit_low, w_router, gain, hidden, scale, cot):
    rows, width = own.shape
    return pl.pallas_call(
        hidden_grad_body,
        out_shape=[
            pltpu.HBM((rows, width), f32),
            pltpu.HBM((rows, width), bf16),
            jax.ShapeDtypeStruct((1, width), f32),
        ],
        compiler_params=params(16),
        cost_estimate=pl.CostEstimate(
            flops=20 * rows * width, transcendentals=0, bytes_accessed=20 * rows * width
        ),
        name="hidden_grad",
    )(own, other, logit_high, logit_low, w_router, gain, hidden, scale, cot)


def router_grad_body(normed_ref, high_ref, low_ref, out_ref):
    normed = normed_ref[...]
    out_ref[...] = dot_rows(normed, high_ref[...]) + dot_rows(normed, low_ref[...])


def router_grad_of(normed, high, low):
    return pl.pallas_call(
        router_grad_body,
        out_shape=jax.ShapeDtypeStruct((normed.shape[1], high.shape[1]), f32),
        compiler_params=params(10),
        cost_estimate=pl.CostEstimate(
            flops=1 << 20, transcendentals=0, bytes_accessed=normed.size
        ),
        name="router_grad",
    )(normed, high, low)


def projections_body(
    own_ref,
    other_ref,
    gain_ref,
    w_query_ref,
    w_key_ref,
    w_value_ref,
    normed_own_ref,
    normed_other_ref,
    scale_ref,
    query_ref,
    key_ref,
    value_ref,
    squares_ref,
    normed_ref,
):
    half = own_ref.shape[0]
    step = pl.program_id(0)

    @pl.when(step == 0)
    def _():
        for k, (ref, out_ref) in enumerate(
            ((own_ref, normed_own_ref), (other_ref, normed_other_ref))
        ):
            rows = ref[...].astype(f32)
            scale = rms_scale(rows)
            normed = (rows * scale * gain_ref[...]).astype(bf16)
            out_ref[...] = normed
            normed_ref[k * half : (k + 1) * half, :] = normed
            if k == 0:
                scale_ref[...] = scale

    normed = normed_ref[...]
    query = dot(normed, w_query_ref[...])
    key = dot(normed, w_key_ref[...])
    query_ref[...] = query
    key_ref[...] = key
    value_ref[...] = dot(normed, w_value_ref[...]).astype(bf16)
    squares = jnp.concatenate(
        [jnp.sum(v * v, axis=1, keepdims=True) for v in (query, key)], axis=1
    )

    @pl.when(step == 0)
    def _():
        squares_ref[...] = squares

    @pl.when(step > 0)
    def _():
        squares_ref[...] += squares


def projections(own, other, gain, weights):
    half, width = own.shape
    local_width = weights[0].shape[1]
    steps = 4
    size = local_width // steps

    def whole(*shape):
        return pl.BlockSpec(shape, lambda k: (0, 0))

    column = pl.BlockSpec((2 * half, size), lambda k: (0, k))
    return pl.pallas_call(
        projections_body,
        grid=(steps,),
        in_specs=[whole(half, width), whole(half, width), whole(1, width)]
        + [pl.BlockSpec((width, size), lambda k: (0, k))] * 3,
        out_specs=[whole(half, width)] * 2
        + [whole(half, 1), column, column, column, whole(2 * half, 2)],
        out_shape=[jax.ShapeDtypeStruct((half, width), bf16)] * 2
        + [jax.ShapeDtypeStruct((half, 1), f32)]
        + [jax.ShapeDtypeStruct((2 * half, local_width), kind) for kind in (f32, f32, bf16)]
        + [jax.ShapeDtypeStruct((2 * half, 2), f32)],
        scratch_shapes=[pltpu.VMEM((2 * half, width), bf16)],
        compiler_params=params(22),
        cost_estimate=pl.CostEstimate(
            flops=1 << 20, transcendentals=0, bytes_accessed=width * local_width // cheap
        ),
        name="projections",
    )(*in_hbm(own, other), gain, *in_hbm(*weights))


def branch_body(mixed_ref, w_ref, own_ref, other_ref, own_low_ref, other_low_ref):
    total = dot(mixed_ref[...], w_ref[...])
    half = own_ref.shape[0]
    own_ref[...] = total[:half]
    other_ref[...] = total[half:]
    own_low_ref[...] = total[:half].astype(bf16)
    other_low_ref[...] = total[half:].astype(bf16)


def branch_of(mixed, w_out):
    seq_len, local_width = mixed.shape
    width = w_out.shape[1]
    steps = 4
    half = pl.BlockSpec((seq_len // 2, width // steps), lambda k: (0, k))
    return pl.pallas_call(
        branch_body,
        grid=(steps,),
        in_specs=[
            pl.BlockSpec((seq_len, local_width), lambda k: (0, 0)),
            pl.BlockSpec((local_width, width // steps), lambda k: (0, k)),
        ],
        out_specs=[half] * 4,
        out_shape=[
            jax.ShapeDtypeStruct((seq_len // 2, width), kind) for kind in (f32, f32, bf16, bf16)
        ],
        compiler_params=params(12),
        cost_estimate=pl.CostEstimate(
            flops=1 << 20, transcendentals=0, bytes_accessed=width * local_width // cheap
        ),
        name="branch",
    )(mixed, *in_hbm(w_out))


def moe_rows_body(
    own_ref,
    other_ref,
    branch_own_ref,
    branch_other_ref,
    got_own_ref,
    got_other_ref,
    gain_ref,
    w_router_ref,
    pick_ref,
    hidden_ref,
    scale_ref,
    normed_ref,
    probs_ref,
    out_ref,
):
    half = own_ref.shape[0]
    step = pl.program_id(0)

    @pl.when(step == 0)
    def _():
        for k, (ref, branch_ref, got_ref) in enumerate(
            ((own_ref, branch_own_ref, got_own_ref), (other_ref, branch_other_ref, got_other_ref))
        ):
            hidden = ref[...].astype(f32) + (branch_ref[...] + got_ref[...].astype(f32))
            scale = rms_scale(hidden)
            normed_ref[k * half : (k + 1) * half, :] = (hidden * scale * gain_ref[...]).astype(bf16)
            if k == 0:
                hidden_ref[...] = hidden
                scale_ref[...] = scale
        logits = dot_cols(normed_ref[...], w_router_ref[...])
        grown = jnp.exp(logits - jnp.max(logits, axis=1, keepdims=True))
        probs_ref[...] = grown / jnp.sum(grown, axis=1, keepdims=True)

    size = out_ref.shape[1]
    columns = pl.ds(pl.multiple_of(step * size, size), size)
    out_ref[...] = dot(pick_ref[...], normed_ref[:, columns]).astype(bf16)


def moe_rows(own, other, branch, got, gain, w_router, pick):
    half, width = own.shape
    count, seq_len = pick.shape
    experts = w_router.shape[0]
    steps = 4

    def whole(*shape):
        return pl.BlockSpec(shape, lambda k: (0, 0), pipeline_mode=pl.Buffered(1))

    def kept(*shape):
        return pl.BlockSpec(shape, lambda k: (0, 0))

    return pl.pallas_call(
        moe_rows_body,
        grid=(steps,),
        in_specs=[whole(half, width)] * 6
        + [whole(1, width), whole(experts, width), whole(count, seq_len)],
        out_specs=[
            kept(half, width),
            kept(half, 1),
            kept(seq_len, width),
            kept(seq_len, experts),
            pl.BlockSpec((count, width // steps), lambda k: (0, k)),
        ],
        out_shape=[
            pltpu.HBM((half, width), f32),
            jax.ShapeDtypeStruct((half, 1), f32),
            pltpu.HBM((seq_len, width), bf16),
            jax.ShapeDtypeStruct((seq_len, experts), f32),
            pltpu.HBM((count, width), bf16),
        ],
        compiler_params=params(24),
        cost_estimate=pl.CostEstimate(
            flops=1 << 20, transcendentals=0, bytes_accessed=width * count // cheap
        ),
        name="moe_rows",
    )(*in_hbm(own, other), *branch, *got, gain, *in_hbm(w_router, pick))


def local(
    residual_in,
    routes,
    segment_ids,
    gain_attn,
    w_query,
    w_key,
    w_value,
    gain_query,
    gain_key,
    w_out,
    gain_moe,
    w_router,
    w_gate,
    w_up,
    w_down,
    cotangent,
):
    core = lax.axis_index("tp")
    planes = lax.axis_size("z")
    chips = lax.axis_size(rows_of_chips)
    chip = lax.axis_index(rows_of_chips)
    own_rows, width = residual_in.shape
    seq_len, top_count = routes.shape
    local_width = w_query.shape[1]
    local_heads, head_dim = gain_query.shape
    experts = chips
    capacity = seq_len * top_count // experts
    own_slots = capacity // 2
    quarter = local_width // planes
    out_rows = width // chips

    def own_first(value):
        return jnp.where(
            core == 0, value, jnp.concatenate([value[own_rows:], value[:own_rows]], axis=0)
        )

    first_columns = width * 9 // 16
    numbers = jnp.stack([lax.axis_index("z"), core, chip, lax.axis_index("x")])
    cot_other = swap(cotangent)
    pick, counts = pick_of(numbers, routes.T, experts, own_slots)
    cot_slots = slot_rows(pick, cotangent, cot_other, first_columns)
    cot_slots, residual_in, segment_ids = lax.optimization_barrier(
        (cot_slots, residual_in, segment_ids)
    )
    cot_first = all_to_all(
        cot_slots.reshape(experts, own_slots, first_columns), rows_of_chips
    ).reshape(experts * own_slots, first_columns)
    cot = jnp.concatenate([cotangent, cot_other], axis=0)

    place = own_first(jnp.arange(seq_len, dtype=jnp.int32))
    seg = own_first(segment_ids[0])
    same_doc = seg[:, None] == seg[None, :]
    position = place - jnp.min(jnp.where(same_doc, place[None, :], seq_len), axis=1)
    cosine, sine = rope_angles(position, head_dim)
    cosine = jnp.concatenate([cosine, cosine], axis=1)
    sine = jnp.concatenate([-sine, sine], axis=1)
    bias = jnp.where(same_doc & (place[None, :] <= place[:, None]), 0.0, mask_fill)

    other_in = swap(residual_in)
    normed_own, normed_other, scale_attn, queries, key_proj, values, squares = projections(
        residual_in, other_in, gain_attn[None], (w_query, w_key, w_value)
    )
    normed_planes = lax.all_gather(normed_own, "z", axis=0, tiled=False)
    query_gain = gain_query.reshape(1, local_width)
    key_gain = gain_key.reshape(1, local_width)
    q_rot, k_rot, probs, mixed, mixed_parts, scales = attention_forward(
        queries,
        key_proj,
        values,
        query_gain,
        key_gain,
        squares,
        swap(squares),
        cosine,
        sine,
        bias,
        local_heads,
        planes,
    )
    branch = branch_of(mixed, w_out)
    hidden_own, scale_moe, normed_moe, router_probs, moe_slots = moe_rows(
        residual_in,
        other_in,
        branch[:2],
        (swap(branch[3]), swap(branch[2])),
        gain_moe[None],
        w_router.T,
        pick,
    )

    moe_slots, cot_first = lax.optimization_barrier((moe_slots, cot_first))
    arrived = all_to_all(
        moe_slots.reshape(experts, own_slots, width), rows_of_chips
    ).reshape(experts * own_slots, width)
    cot_slots = dot(pick, cot[:, first_columns:]).astype(bf16)
    arrived, cot_slots = lax.optimization_barrier((arrived, cot_slots))
    cot_rest = all_to_all(
        cot_slots.reshape(experts, own_slots, width - first_columns), rows_of_chips
    ).reshape(experts * own_slots, width - first_columns)

    gate_parts = (w_gate[0], swap(w_gate[0]))
    up_parts = (w_up[0], swap(w_up[0]))
    down_parts = (w_down[0], swap(w_down[0]))
    slot_out = expert_forward(arrived, gate_parts, up_parts, down_parts)
    slot_out, arrived, cot_rest, normed_planes = lax.optimization_barrier(
        (slot_out, arrived, cot_rest, normed_planes)
    )
    cot_arrived = jnp.concatenate([cot_first, cot_rest], axis=1)
    returned = all_to_all(
        slot_out.reshape(experts, own_slots, width), rows_of_chips
    ).reshape(experts * own_slots, width)
    slot_probs = jax.nn.softmax(dot(arrived, w_router), axis=-1)
    own_expert = jnp.arange(experts, dtype=jnp.int32) == chip
    slot_weight = jnp.sum(jnp.where(own_expert[None, :], slot_probs, 0.0), axis=1, keepdims=True)
    slot_grad = (slot_weight * cot_arrived.astype(f32)).astype(bf16)
    (
        inner_own,
        inner_other,
        gate_own,
        gate_other,
        up_own,
        up_other,
        slot_in_grad,
    ) = expert_backward(arrived, slot_grad, gate_parts, up_parts, down_parts)
    slot_in_grad, returned = lax.optimization_barrier((slot_in_grad, returned))
    grads_back = all_to_all(
        slot_in_grad.reshape(experts, own_slots, width), rows_of_chips
    ).reshape(experts * own_slots, width)
    normed_planes = (normed_planes, swap(normed_planes))
    number = lax.axis_index("x")
    line = lax.axis_size("x")
    mixed_line = [lax.dynamic_index_in_dim(mixed_parts, number, 0, keepdims=False)]
    for shift in range(1, line):
        part = lax.dynamic_index_in_dim(mixed_parts, (number + shift) % line, 0, keepdims=False)
        mixed_line.append(lax.ppermute(part, "x", [(k, (k + shift) % line) for k in range(line)]))
    others = expert_weight_grads(arrived, slot_grad, inner_other, gate_other, up_other, (), bf16)

    pick_pairs = pick.reshape(experts, own_slots, seq_len)
    weighted = pick_pairs.astype(f32) * router_probs.T[:, None, :]
    weight_high, weight_low = halves(weighted.reshape(experts * own_slots, seq_len))
    moe_part = dot_rows(weight_high, returned) + dot_rows(weight_low, returned)
    moe_own, moe_other = moe_part[:own_rows], moe_part[own_rows:].astype(bf16)
    pair_products = dot_cols(returned, cot).reshape(experts, own_slots, seq_len)
    prob_part = jnp.sum(pair_products * pick_pairs.astype(f32), axis=1).T
    other_part = swap(prob_part)
    prob_grad = prob_part + jnp.concatenate([other_part[own_rows:], other_part[:own_rows]], axis=0)
    logit_grad = router_probs * (
        prob_grad - jnp.sum(router_probs * prob_grad, axis=1, keepdims=True)
    )
    logit_high, logit_low = halves(logit_grad)
    router_grad = router_grad_of(normed_moe, logit_high, logit_low)
    (
        grads_back,
        others,
        moe_own,
        moe_other,
        logit_high,
        logit_low,
        router_grad,
        mixed_line,
        normed_planes,
        pick_back,
    ) = lax.optimization_barrier(
        (
            grads_back,
            others,
            moe_own,
            moe_other,
            logit_high,
            logit_low,
            router_grad,
            mixed_line,
            normed_planes,
            turned(pick),
        )
    )
    moe_own = moe_own + swap(moe_other).astype(f32)
    output = (hidden_own + moe_own).astype(bf16)
    others = [swap(grad) for grad in others]
    grad_w_gate, grad_w_up, grad_w_down = expert_weight_grads(
        arrived, slot_grad, inner_own, gate_own, up_own, others, f32
    )
    moe_in_own, moe_in_other = token_sums(pick_back, grads_back)
    hidden_grad, hidden_low_own, gain_moe_grad = hidden_grad_of(
        moe_in_own,
        swap(moe_in_other),
        logit_high[:own_rows],
        logit_low[:own_rows],
        w_router.T,
        gain_moe[None],
        hidden_own,
        scale_moe,
        cotangent,
    )
    hidden_low_other = swap(hidden_low_own)
    low_line = lax.all_gather(hidden_low_own, "x", axis=0, tiled=False)

    value_grad, query_part, key_part, gain_query_grad, gain_key_grad, inner = attention_backward(
        hidden_low_own,
        hidden_low_other,
        w_out,
        values,
        q_rot,
        k_rot,
        probs,
        queries,
        key_proj,
        query_gain,
        key_gain,
        scales,
        cosine,
        sine,
        local_heads,
    )
    inner_other, gain_moe_other = lax.optimization_barrier((swap(inner), swap(gain_moe_grad)))
    to_planes = projection_grads(
        query_part,
        key_part,
        queries,
        key_proj,
        value_grad,
        scales,
        (inner, inner_other),
        planes,
    )

    grads_planes = all_to_all(to_planes, "z").reshape(planes * seq_len, 3 * quarter)
    low_line, _ = lax.optimization_barrier((low_line, to_planes))
    parcel = out_parcel(
        numbers,
        low_line,
        [swap(low_line[k]) for k in range(line)],
        mixed_line,
        router_grad.reshape(chips, out_rows, experts),
        (gain_moe_grad, gain_moe_other),
        gain_query_grad,
        gain_key_grad,
        counts,
    )
    normed_grad, normed_grad_other = normed_grad_of(to_planes, (w_query, w_key, w_value))
    normed_grad = normed_grad + swap(normed_grad_other)
    in_own = residual_in.astype(f32)
    in_scale = scale_attn
    weighted_attn = normed_grad * gain_attn
    grad_input = (
        hidden_grad
        + in_scale * weighted_attn
        - in_own * in_scale**3 * jnp.mean(in_own * weighted_attn, axis=1, keepdims=True)
    )

    grads_planes, parcel = lax.optimization_barrier((grads_planes, parcel))
    parcel = weight_parcel(normed_planes, grads_planes, parcel)
    parcel, *done = lax.optimization_barrier(
        (
            all_to_all(parcel, rows_of_chips),
            output,
            grad_input,
            grad_w_gate,
            grad_w_up,
            grad_w_down,
        )
    )
    output, grad_input, grad_w_gate, grad_w_up, grad_w_down = done
    per_chip = head_dim // chips
    own_gain = lax.dynamic_slice_in_dim(gain_attn, chip * out_rows, out_rows)[None]
    (
        grad_w_query,
        grad_w_key,
        grad_w_value,
        grad_w_out,
        grad_w_router,
        grad_gain_query,
        grad_gain_key,
        grad_gain_moe,
        count,
        attn_own,
        attn_other,
    ) = parcel_sums(
        numbers,
        parcel,
        (w_query, w_key, w_value),
        own_gain,
        planes,
        out_rows,
        local_width,
        local_heads,
        per_chip,
        experts,
    )
    return (
        output,
        grad_input,
        (attn_own + swap(attn_other))[0],
        grad_w_query,
        grad_w_key,
        grad_w_value,
        grad_gain_query.T,
        grad_gain_key.T,
        grad_w_out.T,
        grad_gain_moe[0],
        grad_w_router,
        grad_w_gate[None],
        grad_w_up[None],
        grad_w_down[None],
        count[0],
    )


def solution(mesh):
    side = round(mesh.shape["ep"] ** (1 / 3))
    cube = Mesh(mesh.devices.reshape(side, side, side, 2), rows_of_chips + ("tp",))
    ep = rows_of_chips
    both = rows_of_chips + ("tp",)
    in_specs = (
        P(both, None),
        P(ep, None),
        P(ep, None),
        P(),
        P(None, "tp"),
        P(None, "tp"),
        P(None, "tp"),
        P("tp", None),
        P("tp", None),
        P("tp", None),
        P(),
        P(),
        P(ep, None, "tp"),
        P(ep, None, "tp"),
        P(ep, "tp", None),
        P(both, None),
    )
    out_specs = (
        P(both, None),
        P(both, None),
        P(both),
        P(ep, "tp"),
        P(ep, "tp"),
        P(ep, "tp"),
        P("tp", ep),
        P("tp", ep),
        P("tp", ep),
        P(both),
        P(both, None),
        P(ep, None, "tp"),
        P(ep, None, "tp"),
        P(ep, "tp", None),
        P(ep),
    )
    return jax.shard_map(local, mesh=cube, in_specs=in_specs, out_specs=out_specs, check_vma=False)
```
